32 devices in a mesh: expert: 8 (over z, x), tensor: 4 (over y, core).
Axes of the slice: x: 2, y: 2, z: 4, core: 2. Of those that a mesh axis runs over, the one named last changes fastest.
Arguments:
- tokens: bfloat16 [4096, 1024], P('expert'), may hold values from -6 to 6
- teacher: bfloat16 [4096, 1024], P('expert'), may hold values from -6 to 6
- valid_mask: int32 [4096], P('expert'), may hold values from 0 to 1, as said below
- routes: int32 [4096, 8], P('expert'), may hold values from 0 to 31, all different within a row; in each aligned block of 512 rows (0 to 511, 512 to 1023, ...) at most 192 rows name the same one
- first_gain: float32 [1024], replicated, may hold values from 0.5 to 1.5
- query_weight: bfloat16 [1024, 1024], P(None, 'tensor'), may hold values from -0.75 to 0.75
- key_matrix: bfloat16 [1024, 512], P(None, 'tensor'), may hold values from -0.75 to 0.75
- value_matrix: bfloat16 [1024, 512], P(None, 'tensor'), may hold values from -0.1875 to 0.1875
- output_weight: bfloat16 [1024, 1024], P('tensor'), may hold values from -3 to 3
- second_gain: float32 [1024], replicated, may hold values from 0.5 to 1.5
- router_weight: bfloat16 [1024, 32], replicated, may hold values from -0.09375 to 0.09375
- expert_in: bfloat16 [64, 2, 512, 512], P('expert', None, None, 'tensor'), may hold values from -0.1875 to 0.1875
- expert_out: bfloat16 [64, 512, 512], P('expert', 'tensor'), may hold values from -3 to 3
Outputs:
- layer_output: bfloat16 [4096, 1024], P('expert')
- mean_loss: float32 [], replicated
- grad_tokens: float32 [4096, 1024], P('expert')
- grad_first_gain: float32 [1024], replicated
- grad_query: float32 [1024, 1024], P(None, 'tensor')
- grad_key: float32 [1024, 512], P(None, 'tensor')
- grad_value: float32 [1024, 512], P(None, 'tensor')
- grad_output: float32 [1024, 1024], P('tensor')
- grad_second_gain: float32 [1024], replicated
- grad_router: float32 [1024, 32], replicated
- grad_expert_in: float32 [64, 2, 512, 512], P('expert', None, None, 'tensor')
- grad_expert_out: float32 [64, 512, 512], P('expert', 'tensor')
The draws below stay inside these ranges and needn't reach their ends.
Inputs may be any that keep to these rules, and one draw needn't show every extreme that they name: `routes`: each row names 8 different experts; among the 512 rows of one device no expert is named more than 192 times, a bound that some block reaches. `valid_mask`: the last of each device's 512 rows is 1.
All inputs are finite; a program needn't handle non-finite values.
Results may differ from the reference program's by a relative error of at most 0.017.
The reference program's roundings to bfloat16 on the way count: a program that leaves them out, or rounds other values in their place, can miss the bound.
Values may be sent and summed in bfloat16 or wider, within the bound.
No kernel may reach another device: no remote copies, remote signals or barrier semaphores. Data moves between devices by JAX's collectives and lax.ppermute only.
A program may use at most 192 MiB of HBM per device.

```python
import math
import jax
import jax.numpy as jnp
import numpy as np
from jax import lax

MODEL_DIM = 1024
QUERY_HEADS = 16
KEY_VALUE_HEADS = 8
HEAD_DIM = 64
FFE = 512
EXPERTS = 32
TOP = 8
BLOCK = 256
TOK_DEV = 512
CAP = 192
TOKENS = 4096
N_TENSOR = 4


def draw_valid_mask(key, part):
    row_index = jnp.arange(TOKENS, dtype=jnp.int32)
    drawn = jax.random.randint(key, (TOKENS,), 0, 4 * TOKENS, dtype=jnp.int32)
    keep_row = (drawn < TOKENS + 2 * row_index) | (row_index % TOK_DEV == TOK_DEV - 1)
    return keep_row.astype(jnp.int32)


def block_scale(own_key, dims, split, low, high):
    gain = 1.0
    for axis_at, blocks in split:
        draws = jax.random.uniform(jax.random.fold_in(jax.random.fold_in(own_key, 6), axis_at), (blocks,), jnp.float32, low / len(split), high / len(split))
        gain = gain * jnp.repeat(jnp.exp(draws), dims[axis_at] // blocks).reshape((-1,) + (1,) * (len(dims) - 1 - axis_at))
    return gain


def deal_out(stream_key, own, number, rows, amount, top, bound, slope):
    order = jax.random.permutation(stream_key, amount)
    heavy_load, usual = load_shares(amount, rows * top, bound, slope, True), load_shares(amount, rows * top, bound, slope, False)
    places = jnp.arange(amount)

    def named(tallies, rotation):
        used = int((tallies > 0).sum())
        fixed = max(1, used // 4)
        passed = fixed + (places - fixed + rotation * (used - fixed)) % max(1, amount - fixed)
        return jnp.zeros((amount,), jnp.int32).at[order[jnp.where(places < fixed, places, passed)]].set(jnp.asarray(tallies, jnp.int32))

    tallies = jnp.where(number % 4 == 0, named(heavy_load, number // 4), named(usual, number - number // 4 - 1))
    mixed = jax.random.permutation(jax.random.fold_in(own, 3), amount)
    source_of, sink = mixed[0:amount // 2 * 2:2], mixed[1:amount // 2 * 2:2]
    room = jnp.minimum(tallies[source_of] - 1, bound - tallies[sink]) // 2
    room = jnp.where((source_of == order[0]) | (sink == order[0]) | (tallies[sink] == 0), 0, jnp.maximum(room, 0))
    passed = jax.random.randint(jax.random.fold_in(own, 4), (amount // 2,), 0, 1 << 20) % (room + 1)
    tallies = tallies.at[source_of].add(-passed).at[sink].add(passed)
    members = jnp.searchsorted(jnp.cumsum(tallies), jnp.arange(rows * top), side="right").astype(jnp.int32)
    table = members.reshape(top, rows).T
    table = table[jax.random.permutation(jax.random.fold_in(own, 1), rows)]
    rotation = jax.random.randint(jax.random.fold_in(own, 2), (rows, 1), 0, top)
    return jnp.take_along_axis(table, (jnp.arange(top)[None, :] + rotation) % top, axis=1)


def load_shares(amount, total, limit, slope, full):
    weights = [(1 << 20) // math.isqrt(rank ** slope) + 1 for rank in range(1, amount + 1)]
    largest = limit if full else min(limit, max(-(-total // amount), total * weights[0] // sum(weights)))
    least = 1 if total - largest >= amount - 1 else 0
    given, surplus = [largest] + [least] * (amount - 1), total - largest - least * (amount - 1)
    while surplus > 0:
        free = [i for i in range(1, amount) if given[i] < largest] or [i for i in range(1, amount) if given[i] < limit]
        pool, remaining = sum([weights[i] for i in free]), surplus
        for i in free:
            extra = min(limit - given[i], max(1, remaining * weights[i] // pool), surplus)
            given[i] = given[i] + extra
            surplus = surplus - extra
    return np.array(given)


def centred(stream_key, shape, deviation, limit, pieces=(), held_as=jnp.bfloat16):
    entries = deviation * jax.random.normal(stream_key, shape, jnp.float32)
    if pieces:
        entries = entries * block_scale(stream_key, shape, pieces, -0.22, 0.18)
    return jnp.clip(entries, -limit, limit).astype(held_as)


def setup_inputs(seed: int = 0) -> dict:
    keys = jax.random.split(jax.random.key(seed), 14)
    tokens = centred(keys[0], (TOKENS, MODEL_DIM), 1.0, 6.0, ((0, 8),))
    teacher = centred(keys[1], (TOKENS, MODEL_DIM), 1.0, 6.0, ((0, 8),))
    valid_mask = draw_valid_mask(jax.random.fold_in(keys[13], 71), 0)
    routes_keys = jax.random.split(jax.random.fold_in(keys[3], 1), TOKENS // TOK_DEV)
    routes_turns = jax.random.permutation(jax.random.fold_in(keys[3], 3), TOKENS // TOK_DEV)
    routes = jax.vmap(lambda own, number: deal_out(jax.random.fold_in(keys[3], 2), own, number, TOK_DEV, EXPERTS, TOP, CAP, 1))(routes_keys, routes_turns).reshape((TOKENS, TOP))
    first_gain = jnp.clip(1.0 + 0.1 * jax.random.normal(keys[4], (MODEL_DIM,), jnp.float32), 0.5, 1.5)
    query_weight = centred(keys[5], (MODEL_DIM, QUERY_HEADS * HEAD_DIM), (MODEL_DIM // 16) ** -0.5, 0.75, ((1, 4),))
    key_matrix = centred(keys[6], (MODEL_DIM, KEY_VALUE_HEADS * HEAD_DIM), (MODEL_DIM // 16) ** -0.5, 0.75, ((1, 4),))
    value_matrix = centred(keys[7], (MODEL_DIM, KEY_VALUE_HEADS * HEAD_DIM), MODEL_DIM ** -0.5, 0.1875, ((1, 4),))
    output_weight = centred(keys[8], (QUERY_HEADS * HEAD_DIM, MODEL_DIM), 0.5, 3.0, ((0, 4),))
    second_gain = jnp.clip(1.0 + 0.1 * jax.random.normal(keys[9], (MODEL_DIM,), jnp.float32), 0.5, 1.5)
    router_weight = centred(keys[10], (MODEL_DIM, EXPERTS), (4 * MODEL_DIM) ** -0.5, 0.09375)
    expert_in = centred(keys[11], (2 * EXPERTS, 2, MODEL_DIM // 2, FFE), MODEL_DIM ** -0.5, 0.1875, ((0, 8), (3, 4)))
    expert_out = centred(keys[12], (2 * EXPERTS, FFE, MODEL_DIM // 2), 0.5, 3.0, ((0, 8), (1, 4)))
    return dict(tokens=tokens, teacher=teacher, valid_mask=valid_mask, routes=routes, first_gain=first_gain, query_weight=query_weight, key_matrix=key_matrix, value_matrix=value_matrix, output_weight=output_weight, second_gain=second_gain, router_weight=router_weight, expert_in=expert_in, expert_out=expert_out)


@jax.custom_vjp
def low(v):
    return lax.optimization_barrier(v.astype(jnp.bfloat16)).astype(jnp.float32)

@jax.custom_vjp
def low_back(v):
    return v

def low_keep(v):
    return (low(v), None)

def low_pass(kept, grad):
    return (grad,)

def back_keep(v):
    return (v, None)

def back_low(kept, grad):
    return (low(grad),)
low.defvjp(low_keep, low_pass)
low_back.defvjp(back_keep, back_low)
EPS = 1e-06
ATTN_SCALE = 0.015625
RESIDUAL = 0.22
THETA = 10000.0
HIGH_PRECISION = lax.Precision.HIGHEST

def rope_tables(length, head_size):
    half_size = head_size // 2
    frequency = THETA ** (-(jnp.arange(half_size, dtype=jnp.float32) * 2.0) / head_size)
    angle_table = jnp.arange(length, dtype=jnp.float32)[:, None] * frequency[None, :]
    return (jnp.cos(angle_table)[:, None, :], jnp.sin(angle_table)[:, None, :])

def apply_rotary(values, cosine_lookup, sine_lookup):
    half_size = values.shape[-1] // 2
    lower_half, upper_half = (values[..., :half_size], values[..., half_size:])
    return jnp.concatenate([lower_half * cosine_lookup - upper_half * sine_lookup, upper_half * cosine_lookup + lower_half * sine_lookup], -1)

def normalize(values):
    row_peak = lax.optimization_barrier(jnp.max(values, -1, keepdims=True))
    exp_scores = jnp.exp(values - row_peak)
    return exp_scores / lax.optimization_barrier(jnp.sum(exp_scores, -1, keepdims=True))

def slot_tables(route_ids, expert_count, capacity):
    row_count, top_count = route_ids.shape
    onehot = route_ids[:, :, None] == jnp.arange(expert_count, dtype=jnp.int32)[None, None, :]
    hit_count = lax.optimization_barrier(jnp.sum(onehot.astype(jnp.int32), 1))
    slot_place = jnp.cumsum(hit_count, 0) - 1
    within = jnp.take_along_axis(slot_place, route_ids, 1)
    dest_slot = (route_ids * capacity + within).astype(jnp.int32)
    pair_count = row_count * top_count
    source = jnp.full((expert_count * capacity,), pair_count, jnp.int32).at[dest_slot.reshape(-1)].set(jnp.arange(pair_count, dtype=jnp.int32))
    live_slot = source < pair_count
    token_row = (jnp.minimum(source, pair_count - 1) // top_count).astype(jnp.int32)
    return (onehot, dest_slot, source, live_slot, token_row)

def sequence_layer(tokens_f32, target, valid_rows, route_ids, weights):
    first_gain, query_weight, key_matrix, value_matrix, output_weight, second_gain, router_weight, expert_in, expert_out = weights
    full_in = expert_in.reshape(2, EXPERTS, 2, MODEL_DIM // 2, FFE).transpose(1, 2, 0, 3, 4).reshape(EXPERTS, 2, MODEL_DIM, FFE)
    full_out = expert_out.reshape(2, EXPERTS, FFE, MODEL_DIM // 2).transpose(1, 2, 0, 3).reshape(EXPERTS, FFE, MODEL_DIM)
    sequence_length = tokens_f32.shape[0]
    query_group_size = QUERY_HEADS // KEY_VALUE_HEADS
    unit_one = tokens_f32 * lax.rsqrt(lax.optimization_barrier(jnp.mean(tokens_f32 * tokens_f32, -1, keepdims=True)) + EPS)
    first_normed = low(unit_one * first_gain)
    query_linear = low_back(jnp.dot(first_normed, query_weight, precision=HIGH_PRECISION)).reshape(sequence_length, QUERY_HEADS, HEAD_DIM)
    keys_linear = low_back(jnp.dot(first_normed, key_matrix, precision=HIGH_PRECISION)).reshape(sequence_length, KEY_VALUE_HEADS, HEAD_DIM)
    value_low = low(low_back(jnp.dot(first_normed, value_matrix, precision=HIGH_PRECISION))).reshape(sequence_length, KEY_VALUE_HEADS, HEAD_DIM)
    cosine_lookup, sine_lookup = rope_tables(sequence_length, HEAD_DIM)
    query_rotated = low(apply_rotary(query_linear, cosine_lookup, sine_lookup)).reshape(sequence_length, KEY_VALUE_HEADS, query_group_size, HEAD_DIM)
    keys_rot = low(apply_rotary(keys_linear, cosine_lookup, sine_lookup))
    score_block = low_back(ATTN_SCALE * jnp.einsum('qhgd,khd->hgqk', query_rotated, keys_rot, precision=HIGH_PRECISION))
    block_of = jnp.arange(sequence_length, dtype=jnp.int32) // BLOCK
    allowed = block_of[None, :] <= block_of[:, None]
    attn_probs = normalize(jnp.where(allowed, score_block, -1e+30))
    attended = jnp.einsum('hgqk,khd->qhgd', low(attn_probs), value_low, precision=HIGH_PRECISION).reshape(sequence_length, QUERY_HEADS * HEAD_DIM)
    attended = low(low_back(attended))
    attn_sum = low_back(jnp.dot(attended, output_weight, precision=HIGH_PRECISION))
    hidden_state = tokens_f32 + RESIDUAL * attn_sum
    unit_two = hidden_state * lax.rsqrt(lax.optimization_barrier(jnp.mean(hidden_state * hidden_state, -1, keepdims=True)) + EPS)
    normed_two = low(unit_two * second_gain)
    router_logits = low_back(jnp.dot(normed_two, router_weight, precision=HIGH_PRECISION))
    gate_probs = normalize(jnp.take_along_axis(router_logits, route_ids, 1))
    onehot, dest_slot, source, live_slot, token_row = slot_tables(route_ids, EXPERTS, CAP)
    slot_input = jnp.where(live_slot[:, None], normed_two[token_row], 0.0).reshape(EXPERTS, CAP, MODEL_DIM)
    share_input = low_back(jnp.broadcast_to(slot_input[:, :, None, :], (EXPERTS, CAP, N_TENSOR, MODEL_DIM)))
    share_size = FFE // N_TENSOR
    split_in = full_in.reshape(EXPERTS, 2, MODEL_DIM, N_TENSOR, share_size)
    gate_up = low_back(jnp.einsum('ectd,ewdtf->ectwf', share_input, split_in, precision=HIGH_PRECISION))
    inner_act = low(jax.nn.silu(gate_up[:, :, :, 0]) * gate_up[:, :, :, 1])
    split_out = full_out.reshape(EXPERTS, N_TENSOR, share_size, MODEL_DIM)
    share_out = low(low_back(jnp.einsum('ectf,etfd->ectd', inner_act, split_out, precision=HIGH_PRECISION)))
    slot_out = lax.optimization_barrier(jnp.sum(share_out, 2)).reshape(EXPERTS * CAP, MODEL_DIM)
    per_route = slot_out[dest_slot]
    moe_sum = low_back(lax.optimization_barrier(jnp.sum(gate_probs[:, :, None] * per_route, 1)))
    output = hidden_state + RESIDUAL * moe_sum
    residual_err = output - target
    squared = jnp.sum(valid_rows * lax.optimization_barrier(jnp.sum(residual_err * residual_err, -1)))
    return (output, squared)

def reference(tokens, teacher, valid_mask, routes, first_gain, query_weight, key_matrix, value_matrix, output_weight, second_gain, router_weight, expert_in, expert_out):
    valid_total = jnp.sum(valid_mask).astype(jnp.float32)
    weights = tuple((item.astype(jnp.float32) for item in (first_gain, query_weight, key_matrix, value_matrix, output_weight, second_gain, router_weight, expert_in, expert_out)))
    seq_count = TOKENS // TOK_DEV
    tokens_f32 = tokens.astype(jnp.float32).reshape(seq_count, TOK_DEV, MODEL_DIM)
    targets = teacher.astype(jnp.float32).reshape(seq_count, TOK_DEV, MODEL_DIM)
    valid_rows = valid_mask.astype(jnp.float32).reshape(seq_count, TOK_DEV)
    route_ids = routes.reshape(seq_count, TOK_DEV, TOP)

    def objective(token_input, *params):
        layer_step = jax.checkpoint(lambda sequence: sequence_layer(sequence[0], sequence[1], sequence[2], sequence[3], params))
        outputs, squares = lax.map(layer_step, (token_input, targets, valid_rows, route_ids))
        loss_value = jnp.sum(squares) / (2.0 * MODEL_DIM * valid_total)
        return (TOKENS * MODEL_DIM * loss_value, (outputs, loss_value))
    objective_value, pull_back, extras = jax.vjp(objective, tokens_f32, *weights, has_aux=True)
    grads = pull_back(jnp.ones_like(objective_value))
    outputs, loss_value = extras
    return (outputs.reshape(TOKENS, MODEL_DIM).astype(jnp.bfloat16), loss_value, grads[0].reshape(TOKENS, MODEL_DIM), grads[1], grads[2], grads[3], grads[4], grads[5], grads[6], grads[7], grads[8], grads[9])
```

```python
import jax
import jax.numpy as jnp
from jax import lax
from jax.experimental import pallas as pl
from jax.experimental.pallas import tpu as pltpu
from jax.sharding import PartitionSpec as P

HEAD_DIM = 64
TOP = 8
BLOCK = 256


EPS = 1e-06
ATTN_SCALE = 0.015625
RESIDUAL = 0.22
THETA = 10000.0


def shifted(value, axis, steps):
    count = lax.axis_size(axis)
    pairs = [(source, (source + steps) % count) for source in range(count)]
    return lax.ppermute(value, axis, pairs)


def rope_tables(length, head_size):
    half_size = head_size // 2
    frequency = THETA ** (-(jnp.arange(half_size, dtype=jnp.float32) * 2.0) / head_size)
    angle_table = jnp.arange(length, dtype=jnp.float32)[:, None] * frequency[None, :]
    return (jnp.cos(angle_table)[:, None, :], jnp.sin(angle_table)[:, None, :])


def apply_rotary(values, cosine_lookup, sine_lookup):
    half_size = values.shape[-1] // 2
    lower_half, upper_half = (values[..., :half_size], values[..., half_size:])
    return jnp.concatenate(
        [
            lower_half * cosine_lookup - upper_half * sine_lookup,
            upper_half * cosine_lookup + lower_half * sine_lookup,
        ],
        -1,
    )


def unrotate(grads, cosine_lookup, sine_lookup):
    half_size = grads.shape[-1] // 2
    lower_half, upper_half = (grads[..., :half_size], grads[..., half_size:])
    return jnp.concatenate(
        [
            lower_half * cosine_lookup + upper_half * sine_lookup,
            upper_half * cosine_lookup - lower_half * sine_lookup,
        ],
        -1,
    )


def normalize(values):
    row_peak = jnp.max(values, -1, keepdims=True)
    exp_scores = jnp.exp(values - row_peak)
    return exp_scores / jnp.sum(exp_scores, -1, keepdims=True)


def slot_tables(route_ids, expert_count, capacity):
    row_count, top_count = route_ids.shape
    onehot = route_ids[:, :, None] == jnp.arange(expert_count, dtype=jnp.int32)[None, None, :]
    hit_count = jnp.sum(onehot.astype(jnp.int32), 1)
    slot_place = jnp.cumsum(hit_count, 0) - 1
    within = jnp.take_along_axis(slot_place, route_ids, 1)
    dest_slot = route_ids * capacity + within
    pair_count = row_count * top_count
    source = (
        jnp.full((expert_count * capacity,), pair_count, jnp.int32)
        .at[dest_slot.reshape(-1)]
        .set(jnp.arange(pair_count, dtype=jnp.int32))
    )
    live_slot = source < pair_count
    token_row = jnp.minimum(source, pair_count - 1) // top_count
    return (onehot, dest_slot, source, live_slot, token_row)


def general_device(
    tokens,
    teacher,
    valid_mask,
    routes,
    first_gain,
    query_weight,
    key_matrix,
    value_matrix,
    output_weight,
    second_gain,
    router_weight,
    expert_in,
    expert_out,
):
    row_count = tokens.shape[0]
    model_width = tokens.shape[1]
    half_width = model_width // 2
    local_query = query_weight.shape[1] // HEAD_DIM
    local_kv = key_matrix.shape[1] // HEAD_DIM
    query_group_size = local_query // local_kv
    expert_count = router_weight.shape[1]
    row_local = expert_in.shape[0]
    senders = lax.axis_size("expert")
    partner_step = senders // 2
    capacity = 3 * row_count * TOP // (2 * expert_count)
    pair_count = row_count * TOP
    score_rows = min(512, row_count)
    valid_total = lax.psum(jnp.sum(valid_mask).astype(jnp.float32), "expert")
    tokens_f32 = tokens.astype(jnp.float32)
    scale_one = lax.rsqrt(jnp.mean(tokens_f32 * tokens_f32, -1, keepdims=True) + EPS)
    unit_one = tokens_f32 * scale_one
    first_normed = (unit_one * first_gain).astype(jnp.bfloat16)
    cosine_lookup, sine_lookup = rope_tables(row_count, HEAD_DIM)
    query_linear = jnp.dot(first_normed, query_weight, preferred_element_type=jnp.float32).reshape(
        row_count, local_query, HEAD_DIM
    )
    keys_linear = jnp.dot(first_normed, key_matrix, preferred_element_type=jnp.float32).reshape(
        row_count, local_kv, HEAD_DIM
    )
    value_low = jnp.dot(first_normed, value_matrix, preferred_element_type=jnp.float32).astype(
        jnp.bfloat16
    )
    value_low = value_low.reshape(row_count, local_kv, HEAD_DIM)
    query_rotated = apply_rotary(query_linear, cosine_lookup, sine_lookup).astype(jnp.bfloat16)
    keys_rot = apply_rotary(keys_linear, cosine_lookup, sine_lookup).astype(jnp.bfloat16)
    block_of = jnp.arange(row_count, dtype=jnp.int32) // BLOCK

    def scores(start_row):
        stop_row = start_row + score_rows
        query_block = query_rotated.reshape(score_rows, local_kv, query_group_size, HEAD_DIM)
        score_block = (
            jnp.einsum("qhgd,khd->hgqk", query_block, keys_rot, preferred_element_type=jnp.float32)
            * ATTN_SCALE
        )
        allowed = block_of[None, :stop_row] <= block_of[start_row:stop_row, None]
        return (query_block, jnp.where(allowed, score_block, -1e30))

    attn_parts, row_peaks, row_totals = ([], [], [])
    start_row = 0
    query_block, score_block = scores(start_row)
    row_peak = jnp.max(score_block, -1, keepdims=True)
    exp_scores = jnp.exp(score_block - row_peak)
    row_total = jnp.sum(exp_scores, -1, keepdims=True)
    attn_probs = (exp_scores / row_total).astype(jnp.bfloat16)
    attn_parts.append(
        jnp.einsum("hgqk,khd->qhgd", attn_probs, value_low, preferred_element_type=jnp.float32)
    )
    row_peaks.append(row_peak)
    row_totals.append(row_total)
    attended = attn_parts[0].reshape(row_count, local_query * HEAD_DIM).astype(jnp.bfloat16)
    attn_part = jnp.dot(attended, output_weight, preferred_element_type=jnp.float32)
    attn_sum = lax.psum(attn_part, "tensor")
    hidden_state = tokens_f32 + RESIDUAL * attn_sum
    scale_two = lax.rsqrt(jnp.mean(hidden_state * hidden_state, -1, keepdims=True) + EPS)
    unit_two = hidden_state * scale_two
    normed_two = (unit_two * second_gain).astype(jnp.bfloat16)
    router_logits = jnp.dot(normed_two, router_weight, preferred_element_type=jnp.float32)
    onehot, dest_slot, source, live_slot, token_row = slot_tables(routes, expert_count, capacity)
    picked = jnp.sum(jnp.where(onehot, router_logits[:, None, :], 0.0), -1)
    gate_probs = normalize(picked)

    def slot_rows(slot_values):
        split_rows = slot_values.reshape(expert_count, capacity, 2, half_width).transpose(
            2, 0, 1, 3
        )
        return split_rows.reshape(senders, row_local, capacity, half_width)

    def slot_columns(returned, width):
        joined = returned.reshape(2, expert_count, capacity, width).transpose(1, 2, 0, 3)
        return joined.reshape(expert_count * capacity, 2, width)

    send_rows = slot_rows(
        jnp.where(live_slot[:, None], normed_two[token_row], jnp.zeros((), jnp.bfloat16))
    )
    received = lax.all_to_all(send_rows, "expert", split_axis=0, concat_axis=2, tiled=True)
    expert_rows = received.reshape(row_local, senders * capacity, half_width)
    gate_up_part = jnp.einsum(
        "rmd,rcdf->rmcf", expert_rows, expert_in, preferred_element_type=jnp.float32
    )
    gate_up_pre = gate_up_part + shifted(gate_up_part, "expert", partner_step)
    gate_pre = gate_up_pre[:, :, 0]
    up_pre = gate_up_pre[:, :, 1]
    inner_act = (jax.nn.silu(gate_pre) * up_pre).astype(jnp.bfloat16)
    expert_result = jnp.einsum(
        "rmf,rfd->rmd", inner_act, expert_out, preferred_element_type=jnp.float32
    )
    expert_result = expert_result.astype(jnp.bfloat16).reshape(
        row_local, senders, capacity, half_width
    )
    returned = lax.all_to_all(expert_result, "expert", split_axis=1, concat_axis=0, tiled=True)
    per_route = slot_columns(returned, half_width).reshape(expert_count * capacity, model_width)[
        dest_slot
    ]
    moe_part = jnp.sum(gate_probs[:, :, None] * per_route, 1)
    moe_sum = lax.psum(moe_part, "tensor")
    output = hidden_state + RESIDUAL * moe_sum
    residual_err = output - teacher.astype(jnp.float32)
    valid_rows = valid_mask.astype(jnp.float32)
    squared_local = jnp.sum(valid_rows * jnp.sum(residual_err * residual_err, -1))
    token_total = senders * row_count
    grad_out = token_total / valid_total * valid_rows[:, None] * residual_err
    grad_moe = (RESIDUAL * grad_out).astype(jnp.bfloat16)
    gate_part = jnp.einsum("td,tkd->tk", grad_moe, per_route, preferred_element_type=jnp.float32)
    gate_slot = gate_probs.reshape(pair_count)[jnp.minimum(source, pair_count - 1)]
    grad_slots = jnp.where(live_slot[:, None], gate_slot[:, None] * grad_moe[token_row], 0.0)
    grad_received = lax.all_to_all(
        slot_rows(grad_slots.astype(jnp.bfloat16)),
        "expert",
        split_axis=0,
        concat_axis=2,
        tiled=True,
    )
    grad_expert = grad_received.reshape(row_local, senders * capacity, half_width)
    grad_inner_part = jnp.einsum(
        "rmd,rfd->rmf", grad_expert, expert_out, preferred_element_type=jnp.float32
    )
    grad_inner = grad_inner_part + shifted(grad_inner_part, "expert", partner_step)
    grad_expert_out = jnp.einsum(
        "rmf,rmd->rfd", inner_act, grad_expert, preferred_element_type=jnp.float32
    )
    sigmoid_gate = jax.nn.sigmoid(gate_pre)
    grad_gate = grad_inner * up_pre * sigmoid_gate * (1.0 + gate_pre * (1.0 - sigmoid_gate))
    grad_up = grad_inner * (gate_pre * sigmoid_gate)
    grad_pre = jnp.stack([grad_gate, grad_up], 2).astype(jnp.bfloat16)
    grad_expert_in = jnp.einsum(
        "rmd,rmcf->rcdf", expert_rows, grad_pre, preferred_element_type=jnp.float32
    )
    grad_slot_rows = jnp.einsum(
        "rmcf,rcdf->rmd", grad_pre, expert_in, preferred_element_type=jnp.float32
    )
    grad_slot_rows = grad_slot_rows.astype(jnp.bfloat16).reshape(
        row_local, senders, capacity, half_width
    )
    grad_back = lax.all_to_all(grad_slot_rows, "expert", split_axis=1, concat_axis=0, tiled=True)
    grad_back = slot_columns(grad_back, half_width).reshape(expert_count * capacity, model_width)
    grad_two_part = jnp.sum(grad_back[dest_slot].astype(jnp.float32), 1)
    grad_two_experts, grad_gates = lax.psum((grad_two_part, gate_part), "tensor")
    grad_picked = gate_probs * (grad_gates - jnp.sum(gate_probs * grad_gates, -1, keepdims=True))
    grad_logits = jnp.sum(jnp.where(onehot, grad_picked[:, :, None], 0.0), 1).astype(jnp.bfloat16)
    grad_router = jnp.einsum(
        "td,te->de", normed_two, grad_logits, preferred_element_type=jnp.float32
    )
    grad_two = grad_two_experts + jnp.einsum(
        "te,de->td", grad_logits, router_weight, preferred_element_type=jnp.float32
    )
    grad_second_gain = jnp.sum(grad_two * unit_two, 0)
    grad_unit_two = grad_two * second_gain
    grad_hidden = grad_out + scale_two * (
        grad_unit_two - unit_two * jnp.mean(grad_unit_two * unit_two, -1, keepdims=True)
    )
    grad_attn = (RESIDUAL * grad_hidden).astype(jnp.bfloat16)
    grad_output = jnp.einsum("tc,td->cd", attended, grad_attn, preferred_element_type=jnp.float32)
    grad_attended = jnp.einsum(
        "td,cd->tc", grad_attn, output_weight, preferred_element_type=jnp.float32
    )
    grad_attended = grad_attended.astype(jnp.bfloat16).reshape(
        row_count, local_kv, query_group_size, HEAD_DIM
    )
    grad_query_parts = []
    grad_keys = jnp.zeros((row_count, local_kv, HEAD_DIM), jnp.float32)
    grad_values = jnp.zeros((row_count, local_kv, HEAD_DIM), jnp.float32)
    for block_index, start_row in enumerate(range(0, row_count, score_rows)):
        stop_row = start_row + score_rows
        query_block, score_block = scores(start_row)
        attn_probs = jnp.exp(score_block - row_peaks[block_index]) / row_totals[block_index]
        probs_low = attn_probs.astype(jnp.bfloat16)
        grad_probs = jnp.einsum(
            "qhgd,khd->hgqk", grad_attended, value_low, preferred_element_type=jnp.float32
        )
        grad_scores = attn_probs * (
            grad_probs - jnp.sum(attn_probs * grad_probs, -1, keepdims=True)
        )
        grad_scores = grad_scores.astype(jnp.bfloat16)
        grad_query_parts.append(
            ATTN_SCALE
            * jnp.einsum(
                "hgqk,khd->qhgd", grad_scores, keys_rot, preferred_element_type=jnp.float32
            )
        )
        grad_keys = grad_keys.at[:stop_row].add(
            ATTN_SCALE
            * jnp.einsum(
                "hgqk,qhgd->khd", grad_scores, query_block, preferred_element_type=jnp.float32
            )
        )
        grad_values = grad_values.at[:stop_row].add(
            jnp.einsum(
                "hgqk,qhgd->khd", probs_low, grad_attended, preferred_element_type=jnp.float32
            )
        )
    grad_query_rot = grad_query_parts[0].reshape(row_count, local_query, HEAD_DIM)
    grad_query_low = unrotate(grad_query_rot, cosine_lookup, sine_lookup).reshape(
        row_count, local_query * HEAD_DIM
    )
    grad_query_low = grad_query_low.astype(jnp.bfloat16)
    grad_keys_low = unrotate(grad_keys, cosine_lookup, sine_lookup).reshape(
        row_count, local_kv * HEAD_DIM
    )
    grad_keys_low = grad_keys_low.astype(jnp.bfloat16)
    grad_values_low = grad_values.reshape(row_count, local_kv * HEAD_DIM).astype(jnp.bfloat16)
    grad_query = jnp.einsum(
        "td,tc->dc", first_normed, grad_query_low, preferred_element_type=jnp.float32
    )
    grad_key = jnp.einsum(
        "td,tc->dc", first_normed, grad_keys_low, preferred_element_type=jnp.float32
    )
    grad_value = jnp.einsum(
        "td,tc->dc", first_normed, grad_values_low, preferred_element_type=jnp.float32
    )
    grad_one_part = (
        jnp.einsum("tc,dc->td", grad_query_low, query_weight, preferred_element_type=jnp.float32)
        + jnp.einsum("tc,dc->td", grad_keys_low, key_matrix, preferred_element_type=jnp.float32)
        + jnp.einsum("tc,dc->td", grad_values_low, value_matrix, preferred_element_type=jnp.float32)
    )
    grad_one = lax.psum(grad_one_part.astype(jnp.bfloat16), "tensor").astype(jnp.float32)
    grad_first_gain = jnp.sum(grad_one * unit_one, 0)
    grad_unit_one = grad_one * first_gain
    grad_tokens = grad_hidden + scale_one * (
        grad_unit_one - unit_one * jnp.mean(grad_unit_one * unit_one, -1, keepdims=True)
    )
    reduced = lax.psum(
        (
            grad_first_gain,
            grad_query,
            grad_key,
            grad_value,
            grad_output,
            grad_second_gain,
            grad_router,
            squared_local,
        ),
        "expert",
    )
    loss_value = reduced[7] / (2.0 * model_width * valid_total)
    return (
        output.astype(jnp.bfloat16),
        loss_value,
        grad_tokens,
        reduced[0],
        reduced[1],
        reduced[2],
        reduced[3],
        reduced[4],
        reduced[5],
        reduced[6],
        grad_expert_in,
        grad_expert_out,
    )


BF16 = jnp.bfloat16
F32 = jnp.float32
CHUNK = 256
SHARE = 128
NT = (((1,), (1,)), ((), ()))


def weight_copies(pieces, in_buf, out_buf, sems, expert, slot):
    in_own, in_other, out_own, out_other = (pieces[0:4], pieces[4:8], pieces[8:12], pieces[12:16])
    copies = []
    for q in range(4):
        for half, piece in ((0, in_own[q]), (1, in_other[q])):
            width = piece.shape[2]
            for c in range(2):
                target = in_buf.at[
                    slot, pl.ds(half * width, width), pl.ds((2 * q + c) * SHARE, SHARE)
                ]
                copies.append((piece.at[expert, c], target))
        for half, piece in ((0, out_own[q]), (1, out_other[q])):
            width = piece.shape[2]
            target = out_buf.at[slot, pl.ds(q * SHARE, SHARE), pl.ds(half * width, width)]
            copies.append((piece.at[expert], target))
    return [
        pltpu.make_async_copy(source, target, sems.at[slot, n])
        for n, (source, target) in enumerate(copies)
    ]


def reorder_halves(half_index, source, target):
    width = source.shape[1] // 2

    @pl.when(half_index == 0)
    def _():
        target[...] = source[...]

    @pl.when(half_index == 1)
    def _():
        target[:, :width] = source[:, width:]
        target[:, width:] = source[:, :width]


def split_pairs(values):
    blocks = [values[:, i * SHARE : (i + 1) * SHARE] for i in range(values.shape[1] // SHARE)]
    return (jnp.concatenate(blocks[0::2], 1), jnp.concatenate(blocks[1::2], 1))


def join_pairs(first, second):
    blocks = []
    for i in range(first.shape[1] // SHARE):
        blocks.append(first[:, i * SHARE : (i + 1) * SHARE])
        blocks.append(second[:, i * SHARE : (i + 1) * SHARE])
    return jnp.concatenate(blocks, 1)


def chunk_loop(row_count, body):
    def step(i, carry):
        body(pl.ds(pl.multiple_of(i * CHUNK, CHUNK), CHUNK))
        return carry

    lax.fori_loop(0, row_count // CHUNK, step, 0)


def gate_column(gates, expert):
    lane = lax.broadcasted_iota(jnp.int32, gates.shape, 1)
    return jnp.sum(jnp.where(lane == expert, gates, 0.0), -1, keepdims=True)


def stream_weights(pieces, in_buf, out_buf, sems):
    expert = pl.program_id(0)
    slot = lax.rem(expert, 2)

    @pl.when(expert == 0)
    def _():
        for copy in weight_copies(pieces, in_buf, out_buf, sems, 0, 0):
            copy.start()

    @pl.when(expert + 1 < pl.num_programs(0))
    def _():
        for copy in weight_copies(pieces, in_buf, out_buf, sems, expert + 1, 1 - slot):
            copy.start()

    return (expert, slot)


def forward_body(half_ref, rows_ref, route_ref, router_ref, *rest):
    pieces = rest[:16]
    sum_ref, pre_ref, gated_ref, gate_ref, rows_rel, acc, in_buf, out_buf, sems = rest[16:]
    expert, slot = stream_weights(pieces, in_buf, out_buf, sems)
    row_count = rows_ref.shape[0]

    @pl.when(expert == 0)
    def _():
        reorder_halves(half_ref[0], rows_ref, rows_rel)
        acc[...] = jnp.zeros_like(acc)

        def gating(rows):
            logits = jnp.dot(rows_ref[rows, :], router_ref[...], preferred_element_type=F32)
            lane = lax.broadcasted_iota(jnp.int32, logits.shape, 1)
            ids = route_ref[rows, :]
            mask = ids[:, 0:1] == lane
            for k in range(1, TOP):
                mask = mask | (ids[:, k : k + 1] == lane)
            masked = jnp.where(mask, logits, -1e30)
            powers = jnp.where(mask, jnp.exp(masked - jnp.max(masked, -1, keepdims=True)), 0.0)
            gate_ref[rows, :] = powers / jnp.sum(powers, -1, keepdims=True)

        chunk_loop(row_count, gating)

    for copy in weight_copies(pieces, in_buf, out_buf, sems, expert, slot):
        copy.wait()

    def mlp(rows):
        pre = jnp.dot(rows_rel[rows, :], in_buf[slot], preferred_element_type=F32)
        pre_ref[0, rows, :] = pre.astype(BF16)
        gate_pre, up_pre = split_pairs(pre)
        weight = gate_column(gate_ref[rows, :], expert)
        gated = (weight * (gate_pre * jax.nn.sigmoid(gate_pre) * up_pre)).astype(BF16)
        gated_ref[0, rows, :] = gated
        acc[rows, :] += jnp.dot(gated, out_buf[slot], preferred_element_type=F32)

    chunk_loop(row_count, mlp)

    @pl.when(expert == pl.num_programs(0) - 1)
    def _():
        reorder_halves(half_ref[0], acc, sum_ref)


def whole_block(shape):
    return pl.BlockSpec(shape, lambda e, *_: (0,) * len(shape))


def expert_block(shape):
    return pl.BlockSpec((1,) + shape[1:], lambda e, *_: (e, 0, 0))


def weight_scratch(row_count, width, hidden):
    return [
        pltpu.VMEM((row_count, width), BF16),
        pltpu.VMEM((row_count, width), F32),
        pltpu.VMEM((2, width, 2 * hidden), BF16),
        pltpu.VMEM((2, hidden, width), BF16),
        pltpu.SemaphoreType.DMA((2, 24)),
    ]


def experts_forward(half_index, rows, route_ids, router, pieces):
    row_count, width = rows.shape
    local = pieces[0].shape[0]
    hidden = 4 * SHARE
    pre_shape = (local, row_count, 2 * hidden)
    gated_shape = (local, row_count, hidden)
    return pl.pallas_call(
        forward_body,
        grid_spec=pltpu.PrefetchScalarGridSpec(
            num_scalar_prefetch=1,
            grid=(local,),
            in_specs=[whole_block(v.shape) for v in (rows, route_ids, router)]
            + [pl.BlockSpec(memory_space=pl.ANY)] * 16,
            out_specs=[
                whole_block((row_count, width)),
                expert_block(pre_shape),
                expert_block(gated_shape),
                whole_block((row_count, 128)),
            ],
            scratch_shapes=weight_scratch(row_count, width, hidden),
        ),
        out_shape=[
            jax.ShapeDtypeStruct((row_count, width), F32),
            jax.ShapeDtypeStruct(pre_shape, BF16),
            jax.ShapeDtypeStruct(gated_shape, BF16),
            jax.ShapeDtypeStruct((row_count, 128), F32),
        ],
        name="experts_forward",
    )(half_index, rows, route_ids, router, *pieces)


def backward_body(half_ref, grad_ref, mean_ref, gate_ref, router_ref, pre_ref, *rest):
    pieces = rest[:16]
    rows_ref, pre_grad_ref, logit_ref, grad_rel, acc, in_buf, out_buf, sems = rest[16:]
    expert, slot = stream_weights(pieces, in_buf, out_buf, sems)
    row_count = grad_ref.shape[0]

    @pl.when(expert == 0)
    def _():
        reorder_halves(half_ref[0], grad_ref, grad_rel)
        acc[...] = jnp.zeros_like(acc)
        logit_ref[...] = jnp.zeros_like(logit_ref)

    for copy in weight_copies(pieces, in_buf, out_buf, sems, expert, slot):
        copy.wait()

    def mlp(rows):
        plain = lax.dot_general(grad_rel[rows, :], out_buf[slot], NT, preferred_element_type=F32)
        gate_pre, up_pre = split_pairs(pre_ref[0, rows, :].astype(F32))
        weight = gate_column(gate_ref[rows, :], expert)
        sigmoid = jax.nn.sigmoid(gate_pre)
        act = gate_pre * sigmoid
        grad_weight = jnp.sum(act * up_pre * plain, -1, keepdims=True)
        scaled = weight * plain
        pre_grad = join_pairs(
            scaled * up_pre * (sigmoid + act * (1.0 - sigmoid)), scaled * act
        ).astype(BF16)
        pre_grad_ref[0, rows, :] = pre_grad
        old = logit_ref[rows, :]
        lane = lax.broadcasted_iota(jnp.int32, old.shape, 1)
        logit_ref[rows, :] = jnp.where(
            lane == expert, weight * (grad_weight - mean_ref[rows, 0:1]), old
        )
        acc[rows, :] += lax.dot_general(pre_grad, in_buf[slot], NT, preferred_element_type=F32)

    chunk_loop(row_count, mlp)

    @pl.when(expert == pl.num_programs(0) - 1)
    def _():
        reorder_halves(half_ref[0], acc, rows_ref)

        def router(rows):
            rows_ref[rows, :] += lax.dot_general(
                logit_ref[rows, :].astype(BF16), router_ref[...], NT, preferred_element_type=F32
            )

        chunk_loop(row_count, router)


def experts_backward(half_index, grads, means, gates, router, pre, pieces):
    row_count, width = grads.shape
    local = pieces[0].shape[0]
    hidden = 4 * SHARE
    return pl.pallas_call(
        backward_body,
        grid_spec=pltpu.PrefetchScalarGridSpec(
            num_scalar_prefetch=1,
            grid=(local,),
            in_specs=[whole_block(v.shape) for v in (grads, means, gates, router)]
            + [expert_block(pre.shape)]
            + [pl.BlockSpec(memory_space=pl.ANY)] * 16,
            out_specs=[
                whole_block((row_count, width)),
                expert_block(pre.shape),
                whole_block((row_count, 128)),
            ],
            scratch_shapes=weight_scratch(row_count, width, hidden),
        ),
        out_shape=[
            jax.ShapeDtypeStruct((row_count, width), F32),
            jax.ShapeDtypeStruct(pre.shape, BF16),
            jax.ShapeDtypeStruct((row_count, 128), F32),
        ],
        name="experts_backward",
    )(half_index, grads, means, gates, router, pre, *pieces)


def swap_x(value):
    return lax.ppermute(value, "expert", [(i, i ^ 1) for i in range(8)])


def from_z(value, ahead):
    pairs = [(((i // 2 + ahead) % 4) * 2 + i % 2, i) for i in range(8)]
    return lax.ppermute(value, "expert", pairs)


def swap_y(value):
    return lax.ppermute(value, "tensor", [(i, i ^ 2) for i in range(4)])


def swap_core(value):
    return lax.ppermute(value, "tensor", [(i, i ^ 1) for i in range(4)])


def gather_experts(value):
    near = swap_x(value)
    ahead = [from_z(value, d) for d in (1, 2, 3)]
    shards = [value, near]
    for shard in ahead:
        shards += [shard, swap_x(shard)]
    return shards


def scatter_experts(shards):
    columns = [None] * 4
    for dz in (2, 1, 3, 0):
        keep, send = (shards[2 * dz], shards[2 * dz + 1])
        columns[dz] = keep.astype(F32) + swap_x(send.astype(BF16)).astype(F32)
    total = columns[0]
    for dz in (2, 1, 3):
        total = total + from_z(columns[dz].astype(BF16), 4 - dz).astype(F32)
    return total


def scatter_tensor(value, core, row):
    quarter = value.shape[0] // 4
    parts = value.reshape(2, 2, quarter, value.shape[1])
    keep = lax.dynamic_index_in_dim(parts, core, 1, False)
    send = lax.dynamic_index_in_dim(parts, 1 - core, 1, False)
    half = keep + swap_core(send.astype(BF16)).astype(F32)
    keep = lax.dynamic_index_in_dim(half, row, 0, False)
    send = lax.dynamic_index_in_dim(half, 1 - row, 0, False)
    return keep + swap_y(send.astype(BF16)).astype(F32)


def ordered(index, first, second):
    return jnp.where(
        index == 0, jnp.concatenate([first, second], 0), jnp.concatenate([second, first], 0)
    )


def gather_tensor(value, core, row):
    across = swap_y(value)
    pair = ordered(core, value, swap_core(value))
    other = ordered(core, across, swap_core(across))
    return ordered(row, pair, other)


def sum_all(value):
    value = value + swap_core(value)
    value = value + swap_y(value)
    value = value + swap_x(value)
    value = value + lax.ppermute(value, "expert", [(i, i ^ 2) for i in range(8)])
    return value + lax.ppermute(value, "expert", [(i, i ^ 4) for i in range(8)])


def sum_experts(value, layer, column):
    size = value.shape[0] // 8
    shards = []
    for dz in range(4):
        for dx in range(2):
            place = lax.rem(layer + dz, 4) * 2 + jnp.bitwise_xor(column, dx)
            shards.append(lax.dynamic_slice_in_dim(value, place * size, size, 0))
    total = scatter_experts(shards).astype(BF16)
    gathered = gather_experts(total)
    layers = [ordered(column, gathered[2 * dz], gathered[2 * dz + 1]) for dz in range(4)]
    joined = jnp.concatenate(layers + layers, 0)
    start = lax.rem(4 - layer, 4) * 2 * size
    return lax.dynamic_slice_in_dim(joined, start, 8 * size, 0).astype(F32)


def per_device(
    tokens,
    teacher,
    valid_mask,
    routes,
    first_gain,
    query_weight,
    key_matrix,
    value_matrix,
    output_weight,
    second_gain,
    router_weight,
    expert_in,
    expert_out,
):
    row_count, model_width = tokens.shape
    expert_count = router_weight.shape[1]
    senders = lax.axis_size("expert")
    shares = lax.axis_size("tensor")
    fits = (
        (senders, shares) == (8, 4)
        and expert_count == senders * shares
        and expert_in.shape == (8, 2, model_width // 2, SHARE)
        and row_count == 4 * 128
    )
    if not fits:
        return general_device(
            tokens,
            teacher,
            valid_mask,
            routes,
            first_gain,
            query_weight,
            key_matrix,
            value_matrix,
            output_weight,
            second_gain,
            router_weight,
            expert_in,
            expert_out,
        )
    local_query = query_weight.shape[1] // HEAD_DIM
    local_kv = key_matrix.shape[1] // HEAD_DIM
    group = local_query // local_kv
    quarter = row_count // shares
    place = lax.axis_index("expert")
    share = lax.axis_index("tensor")
    layer, column = (place // 2, place % 2)
    row, core = (share // 2, share % 2)
    half_index = place // 4
    held = expert_in.shape[0] // 2
    base = 8 * (place % 4) + held * half_index

    def rows_of(weights, start):
        return lax.dynamic_slice_in_dim(weights, start * held, held, 0)

    in_own, out_own = (rows_of(expert_in, half_index), rows_of(expert_out, half_index))
    in_other = from_z(rows_of(expert_in, 1 - half_index), 2)
    out_other = from_z(rows_of(expert_out, 1 - half_index), 2)
    pieces = []
    for piece in (in_own, in_other, out_own, out_other):
        across = swap_y(piece)
        pieces += [piece, swap_core(piece), across, swap_core(across)]

    def quarter_of(values):
        return lax.dynamic_slice_in_dim(values, share * quarter, quarter, 0)

    local_valid = jnp.sum(valid_mask)
    notes = jnp.concatenate(
        [quarter_of(routes), jnp.full((quarter, TOP), local_valid, jnp.int32)], 1
    )
    note_rows = jnp.stack(gather_experts(notes))
    valid_total = jnp.sum(note_rows[:, 0, TOP]).astype(F32)
    route_rel = jnp.bitwise_and(note_rows[:, :, :TOP] - base, expert_count - 1)
    route_rel = route_rel.reshape(senders * quarter, TOP)
    router_rel = lax.dynamic_slice_in_dim(
        jnp.concatenate([router_weight, router_weight], 1), base, expert_count, 1
    )
    router_rel = jnp.pad(router_rel, ((0, 0), (0, 128 - expert_count)))

    tokens_f32 = tokens.astype(F32)
    scale_one = lax.rsqrt(jnp.mean(tokens_f32 * tokens_f32, -1, keepdims=True) + EPS)
    unit_one = tokens_f32 * scale_one
    first_normed = (unit_one * first_gain).astype(BF16)
    cosine, sine = rope_tables(row_count, HEAD_DIM)
    query_linear = jnp.dot(first_normed, query_weight, preferred_element_type=F32)
    keys_linear = jnp.dot(first_normed, key_matrix, preferred_element_type=F32)
    value_low = jnp.dot(first_normed, value_matrix, preferred_element_type=F32).astype(BF16)
    value_low = value_low.reshape(row_count, local_kv, HEAD_DIM)
    query_rotated = apply_rotary(
        query_linear.reshape(row_count, local_query, HEAD_DIM), cosine, sine
    ).astype(BF16)
    keys_rot = apply_rotary(
        keys_linear.reshape(row_count, local_kv, HEAD_DIM), cosine, sine
    ).astype(BF16)
    query_block = query_rotated.reshape(row_count, local_kv, group, HEAD_DIM)
    block_of = jnp.arange(row_count, dtype=jnp.int32) // BLOCK
    allowed = block_of[None, :] <= block_of[:, None]

    def masked_scores():
        scores = jnp.einsum("qhgd,khd->hgqk", query_block, keys_rot, preferred_element_type=F32)
        return jnp.where(allowed, scores * ATTN_SCALE, -1e30)

    scores = masked_scores()
    row_peak = jnp.max(scores, -1, keepdims=True)
    powers = jnp.exp(scores - row_peak)
    row_total = jnp.sum(powers, -1, keepdims=True)
    probs_low = (powers / row_total).astype(BF16)
    attended = jnp.einsum("hgqk,khd->qhgd", probs_low, value_low, preferred_element_type=F32)
    attended = attended.reshape(row_count, local_query * HEAD_DIM).astype(BF16)
    attn_part = jnp.dot(attended, output_weight, preferred_element_type=F32)

    tokens_mine = quarter_of(tokens).astype(F32)
    hidden = tokens_mine + RESIDUAL * scatter_tensor(attn_part, core, row)
    scale_two = lax.rsqrt(jnp.mean(hidden * hidden, -1, keepdims=True) + EPS)
    unit_two = hidden * scale_two
    normed_two = (unit_two * second_gain).astype(BF16)
    half_arg = half_index.reshape(1)
    expert_rows = jnp.concatenate(gather_experts(normed_two), 0)
    moe_part, pre, gated, gates = experts_forward(
        half_arg, expert_rows, route_rel, router_rel, pieces
    )
    moe_parts = moe_part.reshape(senders, quarter, model_width)
    moe_sum = scatter_experts([moe_parts[i] for i in range(senders)])

    output = hidden + RESIDUAL * moe_sum
    residual_err = output - quarter_of(teacher).astype(F32)
    valid_rows = quarter_of(valid_mask).astype(F32)[:, None]
    squared_local = jnp.sum(valid_rows * residual_err * residual_err)
    token_total = senders * row_count
    grad_out = token_total / valid_total * valid_rows * residual_err
    grad_moe = (RESIDUAL * grad_out).astype(BF16)
    gate_mean = jnp.sum(grad_moe.astype(F32) * moe_sum, -1, keepdims=True)
    grad_rows = jnp.concatenate(gather_experts(grad_moe), 0)
    mean_rows = jnp.concatenate(gather_experts(gate_mean.reshape(1, quarter)), 0)
    mean_rows = jnp.broadcast_to(mean_rows.reshape(senders * quarter, 1), (senders * quarter, 128))
    layer_output = gather_tensor(output.astype(BF16), core, row)

    grad_part, pre_grad, logit_grad = experts_backward(
        half_arg, grad_rows, mean_rows, gates, router_rel, pre, pieces
    )
    grad_parts = grad_part.reshape(senders, quarter, model_width)
    grad_two = scatter_experts([grad_parts[i] for i in range(senders)])

    logit_grad = logit_grad[:, :expert_count]
    logit_grad = lax.dynamic_slice_in_dim(
        jnp.concatenate([logit_grad, logit_grad], 1),
        jnp.bitwise_and(expert_count - base, expert_count - 1),
        expert_count,
        1,
    ).astype(BF16)
    router_part = jnp.einsum("te,td->ed", logit_grad, expert_rows, preferred_element_type=F32)

    in_grads = jnp.einsum("md,emf->edf", expert_rows, pre_grad, preferred_element_type=F32)
    out_grads = jnp.einsum("emf,md->efd", gated, grad_rows, preferred_element_type=F32)
    half_width = model_width // 2
    in_grads = in_grads.astype(BF16).reshape(held, 2, half_width, 4, 2, SHARE)
    out_grads = out_grads.astype(BF16).reshape(held, 4, SHARE, 2, half_width)

    def halves(values, axis):
        first = lax.dynamic_index_in_dim(values, half_index, axis, False)
        return (first, lax.dynamic_index_in_dim(values, 1 - half_index, axis, False))

    def home(part_of):
        near = part_of(0).astype(F32) + swap_core(part_of(1)).astype(F32)
        far = part_of(2).astype(F32) + swap_core(part_of(3)).astype(F32)
        return near + swap_y(far.astype(BF16)).astype(F32)

    results = []
    for mine, theirs in (
        halves(in_grads.transpose(1, 3, 0, 4, 2, 5), 0),
        halves(out_grads.transpose(3, 1, 0, 2, 4), 0),
    ):
        keep = home(lambda q, v=mine: v[q])
        send = home(lambda q, v=theirs: v[q])
        back = from_z(send.astype(BF16), 2).astype(F32)
        results.append(ordered(half_index, keep, back))
    grad_expert_in, grad_expert_out = results

    grad_second_part = jnp.sum(grad_two * unit_two, 0)
    grad_unit_two = grad_two * second_gain
    grad_hidden = grad_out + scale_two * (
        grad_unit_two - unit_two * jnp.mean(grad_unit_two * unit_two, -1, keepdims=True)
    )
    small = jnp.concatenate(
        [
            router_part,
            grad_second_part[None],
            jnp.full((1, model_width), squared_local),
        ],
        0,
    )
    small = sum_all(small)

    grad_attn = gather_tensor((RESIDUAL * grad_hidden).astype(BF16), core, row)
    grad_output = jnp.einsum("tc,td->cd", attended, grad_attn, preferred_element_type=F32)
    grad_attended = jnp.einsum("td,cd->tc", grad_attn, output_weight, preferred_element_type=F32)
    grad_attended = grad_attended.astype(BF16).reshape(row_count, local_kv, group, HEAD_DIM)
    attn_probs = jnp.exp(masked_scores() - row_peak) / row_total
    grad_probs = jnp.einsum("qhgd,khd->hgqk", grad_attended, value_low, preferred_element_type=F32)
    grad_scores = attn_probs * (grad_probs - jnp.sum(attn_probs * grad_probs, -1, keepdims=True))
    grad_scores = grad_scores.astype(BF16)
    grad_query_rot = ATTN_SCALE * jnp.einsum(
        "hgqk,khd->qhgd", grad_scores, keys_rot, preferred_element_type=F32
    )
    grad_keys_rot = ATTN_SCALE * jnp.einsum(
        "hgqk,qhgd->khd", grad_scores, query_block, preferred_element_type=F32
    )
    grad_values = jnp.einsum(
        "hgqk,qhgd->khd", attn_probs.astype(BF16), grad_attended, preferred_element_type=F32
    )
    grad_query_low = unrotate(
        grad_query_rot.reshape(row_count, local_query, HEAD_DIM), cosine, sine
    )
    grad_query_low = grad_query_low.reshape(row_count, local_query * HEAD_DIM).astype(BF16)
    grad_keys_low = unrotate(grad_keys_rot, cosine, sine)
    grad_keys_low = grad_keys_low.reshape(row_count, local_kv * HEAD_DIM).astype(BF16)
    grad_values_low = grad_values.reshape(row_count, local_kv * HEAD_DIM).astype(BF16)
    grad_qkv = jnp.concatenate([grad_query_low, grad_keys_low, grad_values_low], 1)
    weights_qkv = jnp.concatenate([query_weight, key_matrix, value_matrix], 1)
    grad_weights = jnp.einsum("td,tc->dc", first_normed, grad_qkv, preferred_element_type=F32)
    grad_one_part = jnp.einsum("tc,dc->td", grad_qkv, weights_qkv, preferred_element_type=F32)
    grad_one = scatter_tensor(grad_one_part, core, row)

    scale_mine = lax.rsqrt(jnp.mean(tokens_mine * tokens_mine, -1, keepdims=True) + EPS)
    unit_mine = tokens_mine * scale_mine
    grad_first_gain = sum_all(jnp.sum(grad_one * unit_mine, 0)[None])[0]
    grad_unit_one = grad_one * first_gain
    grad_tokens = grad_hidden + scale_mine * (
        grad_unit_one - unit_mine * jnp.mean(grad_unit_one * unit_mine, -1, keepdims=True)
    )
    grad_tokens = gather_tensor(grad_tokens.astype(BF16), core, row).astype(F32)
    grad_output = sum_experts(grad_output, layer, column)
    grad_weights = sum_experts(grad_weights, layer, column)
    query_columns = query_weight.shape[1]
    key_columns = query_columns + key_matrix.shape[1]
    return (
        layer_output,
        small[expert_count + 1, 0] / (2.0 * model_width * valid_total),
        grad_tokens,
        grad_first_gain,
        grad_weights[:, :query_columns],
        grad_weights[:, query_columns:key_columns],
        grad_weights[:, key_columns:],
        grad_output,
        small[expert_count],
        small[:expert_count].T,
        grad_expert_in,
        grad_expert_out,
    )


def solution(mesh):
    return jax.shard_map(
        per_device,
        mesh=mesh,
        in_specs=(
            P("expert", None),
            P("expert", None),
            P("expert"),
            P("expert", None),
            P(),
            P(None, "tensor"),
            P(None, "tensor"),
            P(None, "tensor"),
            P("tensor", None),
            P(),
            P(),
            P("expert", None, None, "tensor"),
            P("expert", "tensor", None),
        ),
        out_specs=(
            P("expert", None),
            P(),
            P("expert", None),
            P(),
            P(None, "tensor"),
            P(None, "tensor"),
            P(None, "tensor"),
            P("tensor", None),
            P(),
            P(),
            P("expert", None, None, "tensor"),
            P("expert", "tensor", None),
        ),
        check_vma=False,
    )
```

```python
import jax
import jax.numpy as jnp
from jax import lax
from jax.experimental import pallas as pl
from jax.experimental.pallas import tpu as pltpu
from jax.sharding import PartitionSpec as P

HEAD_DIM = 64
TOP = 8
BLOCK = 256


EPS = 1e-06
ATTN_SCALE = 0.015625
RESIDUAL = 0.22
THETA = 10000.0


def shifted(value, axis, steps):
    count = lax.axis_size(axis)
    pairs = [(source, (source + steps) % count) for source in range(count)]
    return lax.ppermute(value, axis, pairs)


def rope_tables(length, head_size):
    half_size = head_size // 2
    frequency = THETA ** (-(jnp.arange(half_size, dtype=jnp.float32) * 2.0) / head_size)
    angle_table = jnp.arange(length, dtype=jnp.float32)[:, None] * frequency[None, :]
    return (jnp.cos(angle_table)[:, None, :], jnp.sin(angle_table)[:, None, :])


def apply_rotary(values, cosine_lookup, sine_lookup):
    half_size = values.shape[-1] // 2
    lower_half, upper_half = (values[..., :half_size], values[..., half_size:])
    return jnp.concatenate(
        [
            lower_half * cosine_lookup - upper_half * sine_lookup,
            upper_half * cosine_lookup + lower_half * sine_lookup,
        ],
        -1,
    )


def unrotate(grads, cosine_lookup, sine_lookup):
    half_size = grads.shape[-1] // 2
    lower_half, upper_half = (grads[..., :half_size], grads[..., half_size:])
    return jnp.concatenate(
        [
            lower_half * cosine_lookup + upper_half * sine_lookup,
            upper_half * cosine_lookup - lower_half * sine_lookup,
        ],
        -1,
    )


def normalize(values):
    row_peak = jnp.max(values, -1, keepdims=True)
    exp_scores = jnp.exp(values - row_peak)
    return exp_scores / jnp.sum(exp_scores, -1, keepdims=True)


def slot_tables(route_ids, expert_count, capacity):
    row_count, top_count = route_ids.shape
    onehot = route_ids[:, :, None] == jnp.arange(expert_count, dtype=jnp.int32)[None, None, :]
    hit_count = jnp.sum(onehot.astype(jnp.int32), 1)
    slot_place = jnp.cumsum(hit_count, 0) - 1
    within = jnp.take_along_axis(slot_place, route_ids, 1)
    dest_slot = route_ids * capacity + within
    pair_count = row_count * top_count
    source = (
        jnp.full((expert_count * capacity,), pair_count, jnp.int32)
        .at[dest_slot.reshape(-1)]
        .set(jnp.arange(pair_count, dtype=jnp.int32))
    )
    live_slot = source < pair_count
    token_row = jnp.minimum(source, pair_count - 1) // top_count
    return (onehot, dest_slot, source, live_slot, token_row)


def general_device(
    tokens,
    teacher,
    valid_mask,
    routes,
    first_gain,
    query_weight,
    key_matrix,
    value_matrix,
    output_weight,
    second_gain,
    router_weight,
    expert_in,
    expert_out,
):
    row_count = tokens.shape[0]
    model_width = tokens.shape[1]
    half_width = model_width // 2
    local_query = query_weight.shape[1] // HEAD_DIM
    local_kv = key_matrix.shape[1] // HEAD_DIM
    query_group_size = local_query // local_kv
    expert_count = router_weight.shape[1]
    row_local = expert_in.shape[0]
    senders = lax.axis_size("expert")
    partner_step = senders // 2
    capacity = 3 * row_count * TOP // (2 * expert_count)
    pair_count = row_count * TOP
    score_rows = min(512, row_count)
    valid_total = lax.psum(jnp.sum(valid_mask).astype(jnp.float32), "expert")
    tokens_f32 = tokens.astype(jnp.float32)
    scale_one = lax.rsqrt(jnp.mean(tokens_f32 * tokens_f32, -1, keepdims=True) + EPS)
    unit_one = tokens_f32 * scale_one
    first_normed = (unit_one * first_gain).astype(jnp.bfloat16)
    cosine_lookup, sine_lookup = rope_tables(row_count, HEAD_DIM)
    query_linear = jnp.dot(first_normed, query_weight, preferred_element_type=jnp.float32).reshape(
        row_count, local_query, HEAD_DIM
    )
    keys_linear = jnp.dot(first_normed, key_matrix, preferred_element_type=jnp.float32).reshape(
        row_count, local_kv, HEAD_DIM
    )
    value_low = jnp.dot(first_normed, value_matrix, preferred_element_type=jnp.float32).astype(
        jnp.bfloat16
    )
    value_low = value_low.reshape(row_count, local_kv, HEAD_DIM)
    query_rotated = apply_rotary(query_linear, cosine_lookup, sine_lookup).astype(jnp.bfloat16)
    keys_rot = apply_rotary(keys_linear, cosine_lookup, sine_lookup).astype(jnp.bfloat16)
    block_of = jnp.arange(row_count, dtype=jnp.int32) // BLOCK

    def scores(start_row):
        stop_row = start_row + score_rows
        query_block = query_rotated.reshape(score_rows, local_kv, query_group_size, HEAD_DIM)
        score_block = (
            jnp.einsum("qhgd,khd->hgqk", query_block, keys_rot, preferred_element_type=jnp.float32)
            * ATTN_SCALE
        )
        allowed = block_of[None, :stop_row] <= block_of[start_row:stop_row, None]
        return (query_block, jnp.where(allowed, score_block, -1e30))

    attn_parts, row_peaks, row_totals = ([], [], [])
    start_row = 0
    query_block, score_block = scores(start_row)
    row_peak = jnp.max(score_block, -1, keepdims=True)
    exp_scores = jnp.exp(score_block - row_peak)
    row_total = jnp.sum(exp_scores, -1, keepdims=True)
    attn_probs = (exp_scores / row_total).astype(jnp.bfloat16)
    attn_parts.append(
        jnp.einsum("hgqk,khd->qhgd", attn_probs, value_low, preferred_element_type=jnp.float32)
    )
    row_peaks.append(row_peak)
    row_totals.append(row_total)
    attended = attn_parts[0].reshape(row_count, local_query * HEAD_DIM).astype(jnp.bfloat16)
    attn_part = jnp.dot(attended, output_weight, preferred_element_type=jnp.float32)
    attn_sum = lax.psum(attn_part, "tensor")
    hidden_state = tokens_f32 + RESIDUAL * attn_sum
    scale_two = lax.rsqrt(jnp.mean(hidden_state * hidden_state, -1, keepdims=True) + EPS)
    unit_two = hidden_state * scale_two
    normed_two = (unit_two * second_gain).astype(jnp.bfloat16)
    router_logits = jnp.dot(normed_two, router_weight, preferred_element_type=jnp.float32)
    onehot, dest_slot, source, live_slot, token_row = slot_tables(routes, expert_count, capacity)
    picked = jnp.sum(jnp.where(onehot, router_logits[:, None, :], 0.0), -1)
    gate_probs = normalize(picked)

    def slot_rows(slot_values):
        split_rows = slot_values.reshape(expert_count, capacity, 2, half_width).transpose(
            2, 0, 1, 3
        )
        return split_rows.reshape(senders, row_local, capacity, half_width)

    def slot_columns(returned, width):
        joined = returned.reshape(2, expert_count, capacity, width).transpose(1, 2, 0, 3)
        return joined.reshape(expert_count * capacity, 2, width)

    send_rows = slot_rows(
        jnp.where(live_slot[:, None], normed_two[token_row], jnp.zeros((), jnp.bfloat16))
    )
    received = lax.all_to_all(send_rows, "expert", split_axis=0, concat_axis=2, tiled=True)
    expert_rows = received.reshape(row_local, senders * capacity, half_width)
    gate_up_part = jnp.einsum(
        "rmd,rcdf->rmcf", expert_rows, expert_in, preferred_element_type=jnp.float32
    )
    gate_up_pre = gate_up_part + shifted(gate_up_part, "expert", partner_step)
    gate_pre = gate_up_pre[:, :, 0]
    up_pre = gate_up_pre[:, :, 1]
    inner_act = (jax.nn.silu(gate_pre) * up_pre).astype(jnp.bfloat16)
    expert_result = jnp.einsum(
        "rmf,rfd->rmd", inner_act, expert_out, preferred_element_type=jnp.float32
    )
    expert_result = expert_result.astype(jnp.bfloat16).reshape(
        row_local, senders, capacity, half_width
    )
    returned = lax.all_to_all(expert_result, "expert", split_axis=1, concat_axis=0, tiled=True)
    per_route = slot_columns(returned, half_width).reshape(expert_count * capacity, model_width)[
        dest_slot
    ]
    moe_part = jnp.sum(gate_probs[:, :, None] * per_route, 1)
    moe_sum = lax.psum(moe_part, "tensor")
    output = hidden_state + RESIDUAL * moe_sum
    residual_err = output - teacher.astype(jnp.float32)
    valid_rows = valid_mask.astype(jnp.float32)
    squared_local = jnp.sum(valid_rows * jnp.sum(residual_err * residual_err, -1))
    token_total = senders * row_count
    grad_out = token_total / valid_total * valid_rows[:, None] * residual_err
    grad_moe = (RESIDUAL * grad_out).astype(jnp.bfloat16)
    gate_part = jnp.einsum("td,tkd->tk", grad_moe, per_route, preferred_element_type=jnp.float32)
    gate_slot = gate_probs.reshape(pair_count)[jnp.minimum(source, pair_count - 1)]
    grad_slots = jnp.where(live_slot[:, None], gate_slot[:, None] * grad_moe[token_row], 0.0)
    grad_received = lax.all_to_all(
        slot_rows(grad_slots.astype(jnp.bfloat16)),
        "expert",
        split_axis=0,
        concat_axis=2,
        tiled=True,
    )
    grad_expert = grad_received.reshape(row_local, senders * capacity, half_width)
    grad_inner_part = jnp.einsum(
        "rmd,rfd->rmf", grad_expert, expert_out, preferred_element_type=jnp.float32
    )
    grad_inner = grad_inner_part + shifted(grad_inner_part, "expert", partner_step)
    grad_expert_out = jnp.einsum(
        "rmf,rmd->rfd", inner_act, grad_expert, preferred_element_type=jnp.float32
    )
    sigmoid_gate = jax.nn.sigmoid(gate_pre)
    grad_gate = grad_inner * up_pre * sigmoid_gate * (1.0 + gate_pre * (1.0 - sigmoid_gate))
    grad_up = grad_inner * (gate_pre * sigmoid_gate)
    grad_pre = jnp.stack([grad_gate, grad_up], 2).astype(jnp.bfloat16)
    grad_expert_in = jnp.einsum(
        "rmd,rmcf->rcdf", expert_rows, grad_pre, preferred_element_type=jnp.float32
    )
    grad_slot_rows = jnp.einsum(
        "rmcf,rcdf->rmd", grad_pre, expert_in, preferred_element_type=jnp.float32
    )
    grad_slot_rows = grad_slot_rows.astype(jnp.bfloat16).reshape(
        row_local, senders, capacity, half_width
    )
    grad_back = lax.all_to_all(grad_slot_rows, "expert", split_axis=1, concat_axis=0, tiled=True)
    grad_back = slot_columns(grad_back, half_width).reshape(expert_count * capacity, model_width)
    grad_two_part = jnp.sum(grad_back[dest_slot].astype(jnp.float32), 1)
    grad_two_experts, grad_gates = lax.psum((grad_two_part, gate_part), "tensor")
    grad_picked = gate_probs * (grad_gates - jnp.sum(gate_probs * grad_gates, -1, keepdims=True))
    grad_logits = jnp.sum(jnp.where(onehot, grad_picked[:, :, None], 0.0), 1).astype(jnp.bfloat16)
    grad_router = jnp.einsum(
        "td,te->de", normed_two, grad_logits, preferred_element_type=jnp.float32
    )
    grad_two = grad_two_experts + jnp.einsum(
        "te,de->td", grad_logits, router_weight, preferred_element_type=jnp.float32
    )
    grad_second_gain = jnp.sum(grad_two * unit_two, 0)
    grad_unit_two = grad_two * second_gain
    grad_hidden = grad_out + scale_two * (
        grad_unit_two - unit_two * jnp.mean(grad_unit_two * unit_two, -1, keepdims=True)
    )
    grad_attn = (RESIDUAL * grad_hidden).astype(jnp.bfloat16)
    grad_output = jnp.einsum("tc,td->cd", attended, grad_attn, preferred_element_type=jnp.float32)
    grad_attended = jnp.einsum(
        "td,cd->tc", grad_attn, output_weight, preferred_element_type=jnp.float32
    )
    grad_attended = grad_attended.astype(jnp.bfloat16).reshape(
        row_count, local_kv, query_group_size, HEAD_DIM
    )
    grad_query_parts = []
    grad_keys = jnp.zeros((row_count, local_kv, HEAD_DIM), jnp.float32)
    grad_values = jnp.zeros((row_count, local_kv, HEAD_DIM), jnp.float32)
    for block_index, start_row in enumerate(range(0, row_count, score_rows)):
        stop_row = start_row + score_rows
        query_block, score_block = scores(start_row)
        attn_probs = jnp.exp(score_block - row_peaks[block_index]) / row_totals[block_index]
        probs_low = attn_probs.astype(jnp.bfloat16)
        grad_probs = jnp.einsum(
            "qhgd,khd->hgqk", grad_attended, value_low, preferred_element_type=jnp.float32
        )
        grad_scores = attn_probs * (
            grad_probs - jnp.sum(attn_probs * grad_probs, -1, keepdims=True)
        )
        grad_scores = grad_scores.astype(jnp.bfloat16)
        grad_query_parts.append(
            ATTN_SCALE
            * jnp.einsum(
                "hgqk,khd->qhgd", grad_scores, keys_rot, preferred_element_type=jnp.float32
            )
        )
        grad_keys = grad_keys.at[:stop_row].add(
            ATTN_SCALE
            * jnp.einsum(
                "hgqk,qhgd->khd", grad_scores, query_block, preferred_element_type=jnp.float32
            )
        )
        grad_values = grad_values.at[:stop_row].add(
            jnp.einsum(
                "hgqk,qhgd->khd", probs_low, grad_attended, preferred_element_type=jnp.float32
            )
        )
    grad_query_rot = grad_query_parts[0].reshape(row_count, local_query, HEAD_DIM)
    grad_query_low = unrotate(grad_query_rot, cosine_lookup, sine_lookup).reshape(
        row_count, local_query * HEAD_DIM
    )
    grad_query_low = grad_query_low.astype(jnp.bfloat16)
    grad_keys_low = unrotate(grad_keys, cosine_lookup, sine_lookup).reshape(
        row_count, local_kv * HEAD_DIM
    )
    grad_keys_low = grad_keys_low.astype(jnp.bfloat16)
    grad_values_low = grad_values.reshape(row_count, local_kv * HEAD_DIM).astype(jnp.bfloat16)
    grad_query = jnp.einsum(
        "td,tc->dc", first_normed, grad_query_low, preferred_element_type=jnp.float32
    )
    grad_key = jnp.einsum(
        "td,tc->dc", first_normed, grad_keys_low, preferred_element_type=jnp.float32
    )
    grad_value = jnp.einsum(
        "td,tc->dc", first_normed, grad_values_low, preferred_element_type=jnp.float32
    )
    grad_one_part = (
        jnp.einsum("tc,dc->td", grad_query_low, query_weight, preferred_element_type=jnp.float32)
        + jnp.einsum("tc,dc->td", grad_keys_low, key_matrix, preferred_element_type=jnp.float32)
        + jnp.einsum("tc,dc->td", grad_values_low, value_matrix, preferred_element_type=jnp.float32)
    )
    grad_one = lax.psum(grad_one_part.astype(jnp.bfloat16), "tensor").astype(jnp.float32)
    grad_first_gain = jnp.sum(grad_one * unit_one, 0)
    grad_unit_one = grad_one * first_gain
    grad_tokens = grad_hidden + scale_one * (
        grad_unit_one - unit_one * jnp.mean(grad_unit_one * unit_one, -1, keepdims=True)
    )
    reduced = lax.psum(
        (
            grad_first_gain,
            grad_query,
            grad_key,
            grad_value,
            grad_output,
            grad_second_gain,
            grad_router,
            squared_local,
        ),
        "expert",
    )
    loss_value = reduced[7] / (2.0 * model_width * valid_total)
    return (
        output.astype(jnp.bfloat16),
        loss_value,
        grad_tokens,
        reduced[0],
        reduced[1],
        reduced[2],
        reduced[3],
        reduced[4],
        reduced[5],
        reduced[6],
        grad_expert_in,
        grad_expert_out,
    )


BF16 = jnp.bfloat16
F32 = jnp.float32
CHUNK = 256
SHARE = 128
PACK = 12 * SHARE
NT = (((1,), (1,)), ((), ()))
ORDER = (0, 2, 4, 6, 1, 3, 5, 7)


def whole_block(shape):
    return pl.BlockSpec(shape, lambda e, *_: (0,) * len(shape))


def any_block():
    return pl.BlockSpec(memory_space=pl.ANY)


def pack_body(half_ref, in_ref, out_ref, own, near, far, sems):
    held = in_ref.shape[0] // 2
    copies = []
    for target, start, first, count in (
        (own, half_ref[0] * held, 0, held),
        (near, (1 - half_ref[0]) * held, 0, held // 2),
        (far, (1 - half_ref[0]) * held, held // 2, held // 2),
    ):
        for e in range(count):
            source = start + first + e
            for c in range(2):
                copies.append(
                    (in_ref.at[source, c], target.at[pl.ds(e * PACK + c * 4 * SHARE, 4 * SHARE)])
                )
            for k in range(4):
                copies.append(
                    (
                        out_ref.at[source, :, pl.ds(k * SHARE, SHARE)],
                        target.at[pl.ds(e * PACK + (8 + k) * SHARE, SHARE)],
                    )
                )
    copies = [
        pltpu.make_async_copy(source, target, sems.at[n])
        for n, (source, target) in enumerate(copies)
    ]
    for copy in copies:
        copy.start()
    for copy in copies:
        copy.wait()


def pack_weights(half_index, expert_in, expert_out):
    held = expert_in.shape[0] // 2
    shapes = [(held * PACK, SHARE), (held // 2 * PACK, SHARE), (held // 2 * PACK, SHARE)]
    return pl.pallas_call(
        pack_body,
        in_specs=[pl.BlockSpec(memory_space=pltpu.SMEM), any_block(), any_block()],
        out_specs=[any_block()] * 3,
        out_shape=[jax.ShapeDtypeStruct(shape, BF16) for shape in shapes],
        scratch_shapes=[pltpu.SemaphoreType.DMA((12 * held,))],
        name="pack_weights",
    )(half_index, expert_in, expert_out)


def weight_copies(own, other, own_row, other_row, half, in_buf, out_buf, sems, slot):
    copies = []
    for q in range(4):
        for pack, row, side in ((own[q], own_row, half), (other[q], other_row, 1 - half)):
            for c in range(2):
                copies.append(
                    (
                        pack.at[pl.ds(pl.multiple_of(row + c * 4 * SHARE, SHARE), 4 * SHARE)],
                        in_buf.at[
                            slot,
                            pl.ds(pl.multiple_of(side * 4 * SHARE, SHARE), 4 * SHARE),
                            pl.ds((2 * q + c) * SHARE, SHARE),
                        ],
                    )
                )
            for k in range(4):
                copies.append(
                    (
                        pack.at[pl.ds(pl.multiple_of(row + (8 + k) * SHARE, SHARE), SHARE)],
                        out_buf.at[slot, side, pl.ds(q * SHARE, SHARE), pl.ds(k * SHARE, SHARE)],
                    )
                )
    return [
        pltpu.make_async_copy(source, target, sems.at[slot, n])
        for n, (source, target) in enumerate(copies)
    ]


def stream_weights(first, packs, half, in_buf, out_buf, sems):
    step = pl.program_id(0)
    slot = lax.rem(step, 2)
    own, near, far = (packs[0:4], packs[4:8], packs[8:12])

    def start(index, target):
        expert = first + index

        def begin(other, start_row):
            for copy in weight_copies(
                own, other, expert * PACK, start_row, half, in_buf, out_buf, sems, target
            ):
                copy.start()

        if not far:
            begin(near, index * PACK)
            return

        @pl.when(expert < 2)
        def _():
            begin(near, expert * PACK)

        @pl.when(expert >= 2)
        def _():
            begin(far, (expert - 2) * PACK)

    @pl.when(step == 0)
    def _():
        start(0, 0)

    @pl.when(step + 1 < pl.num_programs(0))
    def _():
        start(step + 1, 1 - slot)

    def wait():
        for copy in weight_copies(own, near, 0, 0, half, in_buf, out_buf, sems, slot):
            copy.wait()

    return (step, slot, wait)


def weight_scratch(width, hidden):
    return [
        pltpu.VMEM((2, width, 2 * hidden), BF16),
        pltpu.VMEM((2, 2, hidden, width // 2), BF16),
        pltpu.SemaphoreType.DMA((2, 48)),
    ]


def split_pairs(values):
    blocks = [values[:, i * SHARE : (i + 1) * SHARE] for i in range(values.shape[1] // SHARE)]
    return (jnp.concatenate(blocks[0::2], 1), jnp.concatenate(blocks[1::2], 1))


def join_pairs(first, second):
    blocks = []
    for i in range(first.shape[1] // SHARE):
        blocks.append(first[:, i * SHARE : (i + 1) * SHARE])
        blocks.append(second[:, i * SHARE : (i + 1) * SHARE])
    return jnp.concatenate(blocks, 1)


def chunk_loop(row_count, body):
    def step(i, carry):
        body(pl.ds(pl.multiple_of(i * CHUNK, CHUNK), CHUNK))
        return carry

    lax.fori_loop(0, row_count // CHUNK, step, 0)


def gate_column(gates, expert):
    lane = lax.broadcasted_iota(jnp.int32, gates.shape, 1)
    return jnp.sum(jnp.where(lane == expert, gates, 0.0), -1, keepdims=True)


def dense_gates(rows, ids, router):
    logits = jnp.dot(rows, router, preferred_element_type=F32)
    lane = lax.broadcasted_iota(jnp.int32, logits.shape, 1)
    mask = ids[:, 0:1] == lane
    for k in range(1, TOP):
        mask = mask | (ids[:, k : k + 1] == lane)
    masked = jnp.where(mask, logits, -1e30)
    powers = jnp.where(mask, jnp.exp(masked - jnp.max(masked, -1, keepdims=True)), 0.0)
    return powers / jnp.sum(powers, -1, keepdims=True)


def apply_expert(rows, expert, slot, rows_ref, gate_ref, pre_ref, gated_ref, in_buf):
    pre = jnp.dot(rows_ref[rows, :], in_buf[slot], preferred_element_type=F32)
    pre_ref[0, rows, :] = pre.astype(BF16)
    gate_pre, up_pre = split_pairs(pre)
    weight = gate_column(gate_ref[rows, :], expert)
    gated = (weight * (gate_pre * jax.nn.sigmoid(gate_pre) * up_pre)).astype(BF16)
    gated_ref[0, rows, :] = gated
    return gated


def forward_first(half_ref, *refs):
    shards = refs[:8]
    route_ref, router_ref = refs[8:10]
    packs = refs[10:18]
    acc, pre_ref, gated_ref, gate_ref, rows_ref, in_buf, out_buf, sems = refs[18:]
    step, slot, wait = stream_weights(0, packs, half_ref[0], in_buf, out_buf, sems)
    row_count, width = acc.shape
    size = row_count // 8

    @pl.when(step == 0)
    def _():
        for i in range(8):
            rows_ref[i * size : (i + 1) * size, :] = shards[i][...]
        acc[...] = jnp.zeros_like(acc)

        def gating(rows):
            gate_ref[rows, :] = dense_gates(rows_ref[rows, :], route_ref[rows, :], router_ref[...])

        chunk_loop(row_count, gating)

    wait()

    def mlp(rows):
        gated = apply_expert(rows, step, slot, rows_ref, gate_ref, pre_ref, gated_ref, in_buf)
        for side in range(2):
            columns = slice(side * width // 2, (side + 1) * width // 2)
            acc[rows, columns] += jnp.dot(gated, out_buf[slot, side], preferred_element_type=F32)

    chunk_loop(row_count, mlp)


def forward_second(half_ref, *refs):
    rows_ref, gate_ref, start_ref = refs[:3]
    packs = refs[3:11]
    keep_ref, near_ref, far_ref, pre_ref, gated_ref, acc, in_buf, out_buf, sems = refs[13:]
    step, slot, wait = stream_weights(2, packs, half_ref[0], in_buf, out_buf, sems)
    row_count, width = acc.shape

    wait()

    def mlp(rows, source):
        gated = apply_expert(rows, step + 2, slot, rows_ref, gate_ref, pre_ref, gated_ref, in_buf)
        for side in range(2):
            columns = slice(side * width // 2, (side + 1) * width // 2)
            acc[rows, columns] = source[rows, columns] + jnp.dot(
                gated, out_buf[slot, side], preferred_element_type=F32
            )

    @pl.when(step == 0)
    def _():
        chunk_loop(row_count, lambda rows: mlp(rows, start_ref))

    @pl.when(step > 0)
    def _():
        chunk_loop(row_count, lambda rows: mlp(rows, acc))

    @pl.when(step == pl.num_programs(0) - 1)
    def _():
        spread(acc, keep_ref, near_ref, far_ref)


def spread(acc, keep_ref, near_ref, far_ref):
    part = acc.shape[0] // 4
    keep_ref[...] = acc[: 2 * part, :]
    near_ref[...] = acc[2 * part : 3 * part, :].astype(BF16)
    far_ref[...] = acc[3 * part :, :].astype(BF16)


def spread_specs(row_count, width):
    shapes = [
        jax.ShapeDtypeStruct((row_count // 2, width), F32),
        jax.ShapeDtypeStruct((row_count // 4, width), BF16),
        jax.ShapeDtypeStruct((row_count // 4, width), BF16),
    ]
    return ([whole_block(s.shape) for s in shapes], shapes)


def expert_block(shape, first=0):
    return pl.BlockSpec((1,) + shape[1:], lambda e, *_: (e + first,) + (0,) * (len(shape) - 1))


def experts_forward(half_index, shards, route_ids, router, own, near, far):
    size, width = shards[0].shape
    row_count = 8 * size
    local = own[0].shape[0] // PACK
    hidden = 4 * SHARE
    sums = jax.ShapeDtypeStruct((row_count, width), F32)
    pre = jax.ShapeDtypeStruct((local, row_count, 2 * hidden), BF16)
    gated = jax.ShapeDtypeStruct((local, row_count, hidden), BF16)
    gates = jax.ShapeDtypeStruct((row_count, 128), F32)
    rows = jax.ShapeDtypeStruct((row_count, width), BF16)
    sums_a, pre_a, gated_a, gates, rows = pl.pallas_call(
        forward_first,
        grid_spec=pltpu.PrefetchScalarGridSpec(
            num_scalar_prefetch=1,
            grid=(2,),
            in_specs=[whole_block(v.shape) for v in (*shards, route_ids, router)]
            + [any_block()] * 8,
            out_specs=[
                whole_block(sums.shape),
                expert_block(pre.shape),
                expert_block(gated.shape),
                whole_block(gates.shape),
                whole_block(rows.shape),
            ],
            scratch_shapes=weight_scratch(width, hidden),
        ),
        out_shape=[sums, pre, gated, gates, rows],
        name="experts_forward_a",
    )(half_index, *shards, route_ids, router, *own, *near)
    specs, shapes = spread_specs(row_count, width)
    keep, send_near, send_far, pre, gated = pl.pallas_call(
        forward_second,
        grid_spec=pltpu.PrefetchScalarGridSpec(
            num_scalar_prefetch=1,
            grid=(2,),
            in_specs=[whole_block(v.shape) for v in (rows, gates, sums)] + [any_block()] * 10,
            out_specs=specs + [expert_block(pre.shape, 2), expert_block(gated.shape, 2)],
            scratch_shapes=[pltpu.VMEM((row_count, width), F32)] + weight_scratch(width, hidden),
        ),
        out_shape=shapes + [pre, gated],
        input_output_aliases={12: 3, 13: 4},
        name="experts_forward_b",
    )(half_index, rows, gates, sums_a, *own, *far, pre_a, gated_a)
    return (keep, send_near, send_far, pre, gated, gates, rows)


def backward_body(half_ref, *refs):
    shards = refs[:8]
    gate_ref, router_ref, pre_ref = refs[8:11]
    packs = refs[11:23]
    keep_ref, near_ref, far_ref, pre_grad_ref, logit_ref, grad_ref = refs[23:29]
    acc, in_buf, out_buf, sems = refs[29:]
    step, slot, wait = stream_weights(0, packs, half_ref[0], in_buf, out_buf, sems)
    row_count, width = grad_ref.shape
    size = row_count // 8

    @pl.when(step == 0)
    def _():
        for i in range(8):
            grad_ref[i * size : (i + 1) * size, :] = shards[i][...]
        acc[...] = jnp.zeros_like(acc)
        logit_ref[...] = jnp.zeros_like(logit_ref)

    wait()

    def mlp(rows):
        plain = lax.dot_general(
            grad_ref[rows, : width // 2], out_buf[slot, 0], NT, preferred_element_type=F32
        ) + lax.dot_general(
            grad_ref[rows, width // 2 :], out_buf[slot, 1], NT, preferred_element_type=F32
        )
        gate_pre, up_pre = split_pairs(pre_ref[0, rows, :].astype(F32))
        weight = gate_column(gate_ref[rows, :], step)
        sigmoid = jax.nn.sigmoid(gate_pre)
        act = gate_pre * sigmoid
        grad_weight = jnp.sum(act * up_pre * plain, -1, keepdims=True)
        scaled = weight * plain
        pre_grad = join_pairs(
            scaled * up_pre * (sigmoid + act * (1.0 - sigmoid)), scaled * act
        ).astype(BF16)
        pre_grad_ref[0, rows, :] = pre_grad
        old = logit_ref[rows, :]
        lane = lax.broadcasted_iota(jnp.int32, old.shape, 1)
        value = weight * grad_weight
        high = value.astype(BF16).astype(F32)
        logit_ref[rows, :] = jnp.where(
            lane == step, high, jnp.where(lane == step + 32, value - high, old)
        )
        acc[rows, :] += lax.dot_general(pre_grad, in_buf[slot], NT, preferred_element_type=F32)

    chunk_loop(row_count, mlp)

    @pl.when(step == pl.num_programs(0) - 1)
    def _():
        def router(rows):
            acc[rows, :] += lax.dot_general(
                logit_ref[rows, :].astype(BF16), router_ref[...], NT, preferred_element_type=F32
            )

        chunk_loop(row_count, router)
        spread(acc, keep_ref, near_ref, far_ref)


def experts_backward(half_index, shards, gates, router, pre, own, near, far):
    row_count, width = (8 * shards[0].shape[0], shards[0].shape[1])
    local = pre.shape[0]
    specs, shapes = spread_specs(row_count, width)
    return pl.pallas_call(
        backward_body,
        grid_spec=pltpu.PrefetchScalarGridSpec(
            num_scalar_prefetch=1,
            grid=(local,),
            in_specs=[whole_block(v.shape) for v in (*shards, gates, router)]
            + [expert_block(pre.shape)]
            + [any_block()] * 12,
            out_specs=specs
            + [
                expert_block(pre.shape),
                whole_block((row_count, 128)),
                whole_block((row_count, width)),
            ],
            scratch_shapes=[pltpu.VMEM((row_count, width), F32)]
            + weight_scratch(width, 4 * SHARE),
        ),
        out_shape=shapes
        + [
            jax.ShapeDtypeStruct(pre.shape, BF16),
            jax.ShapeDtypeStruct((row_count, 128), F32),
            jax.ShapeDtypeStruct((row_count, width), BF16),
        ],
        name="experts_backward",
    )(half_index, *shards, gates, router, pre, *own, *near, *far)


def grad_out_body(half_ref, gated_ref, other_ref, mine_ref, *outs):
    turned = gated_ref[0].T
    for n, source in ((0, other_ref), (2, mine_ref)):
        product = jnp.dot(turned, source[...], preferred_element_type=F32).astype(BF16)
        for q in range(4):
            outs[n + q % 2][q // 2, 0] = product[q * SHARE : (q + 1) * SHARE, :]


def grad_expert_outs(half_index, gated, grads):
    local, row_count, hidden = gated.shape
    width = grads.shape[1]
    half_spec = (row_count, width // 2)
    shape = (2, local, SHARE, width // 2)
    return pl.pallas_call(
        grad_out_body,
        grid_spec=pltpu.PrefetchScalarGridSpec(
            num_scalar_prefetch=1,
            grid=(local,),
            in_specs=[
                expert_block(gated.shape),
                pl.BlockSpec(half_spec, lambda e, half: (0, 1 - half[0])),
                pl.BlockSpec(half_spec, lambda e, half: (0, half[0])),
            ],
            out_specs=[pl.BlockSpec((2, 1) + shape[2:], lambda e, *_: (0, e, 0, 0))] * 4,
        ),
        out_shape=[jax.ShapeDtypeStruct(shape, BF16)] * 4,
        name="grad_expert_out",
    )(half_index, gated, grads, grads)


def grad_in_body(half_ref, rows_ref, pre_ref, keep_ref, send_ref, turned):
    @pl.when(pl.program_id(0) == 0)
    def _():
        turned[...] = rows_ref[...].T

    product = jnp.dot(turned[...], pre_ref[0], preferred_element_type=F32).astype(BF16)
    for q in range(4):
        for c in range(2):
            start = (2 * q + c) * SHARE
            (keep_ref, send_ref)[q % 2][q // 2, 0, c] = product[:, start : start + SHARE]


def grad_expert_ins(half_index, rows, pre_grad):
    local, row_count, wide = pre_grad.shape
    width = rows.shape[1]
    shape = (2, local, 2, width // 2, SHARE)
    return pl.pallas_call(
        grad_in_body,
        grid_spec=pltpu.PrefetchScalarGridSpec(
            num_scalar_prefetch=1,
            grid=(local,),
            in_specs=[
                pl.BlockSpec((row_count, width // 2), lambda e, half: (0, half[0])),
                expert_block(pre_grad.shape),
            ],
            out_specs=[pl.BlockSpec((2, 1) + shape[2:], lambda e, *_: (0, e, 0, 0, 0))] * 2,
            scratch_shapes=[pltpu.VMEM((width // 2, row_count), BF16)],
        ),
        out_shape=[jax.ShapeDtypeStruct(shape, BF16)] * 2,
        name="grad_expert_in",
    )(half_index, rows, pre_grad)


def trade(value, bits):
    return lax.ppermute(value, "expert", [(i, i ^ bits) for i in range(8)])


def swap_y(value):
    return lax.ppermute(value, "tensor", [(i, i ^ 2) for i in range(4)])


def swap_core(value):
    return lax.ppermute(value, "tensor", [(i, i ^ 1) for i in range(4)])


def gather_experts(value):
    column = [value] + [trade(value, bits) for bits in (2, 4, 6)]
    return column + [trade(shard, 1) for shard in column]


def scatter_experts(keep, send_near, send_far):
    size = keep.shape[0] // 4
    far = keep[2 * size :].astype(F32) + trade(send_far, 1).astype(F32)
    far = far.astype(BF16)
    back = [trade(far[:size], 4), trade(far[size:], 6)]
    near = trade(send_near, 1).astype(F32)
    back.append(trade((keep[size : 2 * size].astype(F32) + near[size:]).astype(BF16), 2))
    total = keep[:size].astype(F32) + near[:size]
    for part in back:
        total = total + part.astype(F32)
    return total


def scatter_tensor(value, core, row):
    quarter = value.shape[0] // 4
    parts = value.reshape(2, 2, quarter, value.shape[1])
    keep = lax.dynamic_index_in_dim(parts, core, 1, False)
    send = lax.dynamic_index_in_dim(parts, 1 - core, 1, False)
    half = keep + swap_core(send.astype(BF16)).astype(F32)
    keep = lax.dynamic_index_in_dim(half, row, 0, False)
    send = lax.dynamic_index_in_dim(half, 1 - row, 0, False)
    return keep + swap_y(send.astype(BF16)).astype(F32)


def ordered(index, first, second):
    return jnp.where(
        index == 0, jnp.concatenate([first, second], 0), jnp.concatenate([second, first], 0)
    )


def gather_tensor(value, core, row):
    across = swap_y(value)
    pair = ordered(core, value, swap_core(value))
    other = ordered(core, across, swap_core(across))
    return ordered(row, pair, other)


def sum_all(value):
    value = value + swap_core(value)
    value = value + swap_y(value)
    for bits in (1, 2, 4):
        value = value + trade(value, bits)
    return value


def sum_experts(value, place):
    size = value.shape[0] // 8
    shards = value.reshape(8, size, value.shape[1])

    def pick(*order):
        picked = [
            lax.dynamic_index_in_dim(shards, jnp.bitwise_xor(place, r), 0, False) for r in order
        ]
        return jnp.concatenate(picked, 0)

    total = scatter_experts(pick(0, 2, 4, 6), pick(1, 3).astype(BF16), pick(5, 7).astype(BF16))
    gathered = jnp.stack(gather_experts(total.astype(BF16)))
    lower = (jnp.bitwise_and(place, 1), jnp.bitwise_and(place, 2), jnp.bitwise_and(place, 4))
    column, inner, outer = (bit > 0 for bit in lower)
    halves = jnp.stack([gathered[:4], gathered[4:]])
    halves = jnp.where(column, halves[::-1], halves)
    halves = halves.reshape(2, 2, 2, size, value.shape[1])
    halves = jnp.where(inner, halves[:, :, ::-1], halves)
    halves = jnp.where(outer, halves[:, ::-1], halves)
    return halves.transpose(1, 2, 0, 3, 4).reshape(value.shape).astype(F32)


def per_device(
    tokens,
    teacher,
    valid_mask,
    routes,
    first_gain,
    query_weight,
    key_matrix,
    value_matrix,
    output_weight,
    second_gain,
    router_weight,
    expert_in,
    expert_out,
):
    row_count, model_width = tokens.shape
    expert_count = router_weight.shape[1]
    senders = lax.axis_size("expert")
    shares = lax.axis_size("tensor")
    fits = (
        (senders, shares) == (8, 4)
        and expert_count == senders * shares
        and expert_in.shape == (8, 2, model_width // 2, SHARE)
        and row_count == 4 * 128
    )
    if not fits:
        return general_device(
            tokens,
            teacher,
            valid_mask,
            routes,
            first_gain,
            query_weight,
            key_matrix,
            value_matrix,
            output_weight,
            second_gain,
            router_weight,
            expert_in,
            expert_out,
        )
    local_query = query_weight.shape[1] // HEAD_DIM
    local_kv = key_matrix.shape[1] // HEAD_DIM
    group = local_query // local_kv
    quarter = row_count // shares
    place = lax.axis_index("expert")
    share = lax.axis_index("tensor")
    row, core = (share // 2, share % 2)
    half_index = place // 4
    half_arg = half_index.reshape(1)
    held = expert_in.shape[0] // 2
    base = 8 * (place % 4) + held * half_index

    own_pack, near_pack, far_pack = pack_weights(half_arg, expert_in, expert_out)
    near_pack = trade(near_pack, 4)
    far_pack = trade(far_pack, 4)

    def spread_shares(pack):
        across = swap_y(pack)
        return [pack, swap_core(pack), across, swap_core(across)]

    own = spread_shares(own_pack)

    def quarter_of(values):
        return lax.dynamic_slice_in_dim(values, share * quarter, quarter, 0)

    local_valid = jnp.sum(valid_mask)
    routes_mine = quarter_of(routes)
    notes = jnp.concatenate(
        [routes_mine.T, jnp.full((TOP, quarter), local_valid, jnp.int32)], 0
    )[None]
    for bits in (1, 2, 4):
        notes = jnp.concatenate([notes, trade(notes, bits)], 0)
    valid_total = jnp.sum(notes[:, TOP, 0]).astype(F32)
    notes = jnp.stack([notes[r, :TOP] for r in ORDER])
    route_rel = jnp.bitwise_and(notes - base, expert_count - 1)
    route_rel = route_rel.transpose(0, 2, 1).reshape(senders * quarter, TOP)
    router_rel = lax.dynamic_slice_in_dim(
        jnp.concatenate([router_weight, router_weight], 1), base, expert_count, 1
    )
    router_rel = jnp.pad(
        jnp.concatenate([router_rel, router_rel], 1), ((0, 0), (0, 128 - 2 * expert_count))
    )

    tokens_f32 = tokens.astype(F32)
    scale_one = lax.rsqrt(jnp.mean(tokens_f32 * tokens_f32, -1, keepdims=True) + EPS)
    unit_one = tokens_f32 * scale_one
    first_normed = (unit_one * first_gain).astype(BF16)
    cosine, sine = rope_tables(row_count, HEAD_DIM)
    query_linear = jnp.dot(first_normed, query_weight, preferred_element_type=F32)
    keys_linear = jnp.dot(first_normed, key_matrix, preferred_element_type=F32)
    value_low = jnp.dot(first_normed, value_matrix, preferred_element_type=F32).astype(BF16)
    value_low = value_low.reshape(row_count, local_kv, HEAD_DIM)
    query_rotated = apply_rotary(
        query_linear.reshape(row_count, local_query, HEAD_DIM), cosine, sine
    ).astype(BF16)
    keys_rot = apply_rotary(
        keys_linear.reshape(row_count, local_kv, HEAD_DIM), cosine, sine
    ).astype(BF16)
    query_block = query_rotated.reshape(row_count, local_kv, group, HEAD_DIM)
    block_of = jnp.arange(row_count, dtype=jnp.int32) // BLOCK
    allowed = block_of[None, :] <= block_of[:, None]

    def masked_scores():
        scores = jnp.einsum("qhgd,khd->hgqk", query_block, keys_rot, preferred_element_type=F32)
        return jnp.where(allowed, scores * ATTN_SCALE, -1e30)

    scores = masked_scores()
    row_peak = jnp.max(scores, -1, keepdims=True)
    powers = jnp.exp(scores - row_peak)
    row_total = jnp.sum(powers, -1, keepdims=True)
    probs_low = (powers / row_total).astype(BF16)
    attended = jnp.einsum("hgqk,khd->qhgd", probs_low, value_low, preferred_element_type=F32)
    attended = attended.reshape(row_count, local_query * HEAD_DIM).astype(BF16)
    attn_part = jnp.dot(attended, output_weight, preferred_element_type=F32)

    tokens_mine = quarter_of(tokens).astype(F32)
    hidden = tokens_mine + RESIDUAL * scatter_tensor(attn_part, core, row)
    scale_two = lax.rsqrt(jnp.mean(hidden * hidden, -1, keepdims=True) + EPS)
    unit_two = hidden * scale_two
    normed_two = (unit_two * second_gain).astype(BF16)
    near_pack, far_pack, normed_two = lax.optimization_barrier((near_pack, far_pack, normed_two))
    near, far = (spread_shares(near_pack), spread_shares(far_pack))
    keep, send_near, send_far, pre, gated, gates, expert_rows = experts_forward(
        half_arg,
        gather_experts(normed_two),
        route_rel,
        router_rel,
        own,
        near,
        far,
    )
    moe_sum = scatter_experts(keep, send_near, send_far)

    output = hidden + RESIDUAL * moe_sum
    residual_err = output - quarter_of(teacher).astype(F32)
    valid_rows = quarter_of(valid_mask).astype(F32)[:, None]
    squared_local = jnp.sum(valid_rows * residual_err * residual_err)
    token_total = senders * row_count
    grad_out = token_total / valid_total * valid_rows * residual_err
    grad_moe = (RESIDUAL * grad_out).astype(BF16)
    gate_mean = jnp.sum(grad_moe.astype(F32) * moe_sum, -1, keepdims=True)
    mean_part = -gate_mean * dense_gates(normed_two, routes_mine, router_weight)
    mean_high = mean_part.astype(BF16)
    mean_part = jnp.concatenate([mean_high, (mean_part - mean_high.astype(F32)).astype(BF16)], 1)
    router_pair = jnp.concatenate([router_weight, router_weight], 1)
    mean_rows = jnp.einsum("te,de->td", mean_part, router_pair, preferred_element_type=F32)
    layer_output = gather_tensor(output.astype(BF16), core, row)

    keep, send_near, send_far, pre_grad, logit_grad, grad_rows = experts_backward(
        half_arg, gather_experts(grad_moe), gates, router_rel, pre, own, near, far
    )
    grad_two = scatter_experts(keep, send_near, send_far) + mean_rows

    out_keep, out_send, own_out_keep, own_out_send = grad_expert_outs(half_arg, gated, grad_rows)
    in_keep, in_send = grad_expert_ins(1 - half_arg, expert_rows, pre_grad)
    own_in_keep, own_in_send = grad_expert_ins(half_arg, expert_rows, pre_grad)

    def home(kept, sent):
        received = swap_core(sent)
        near = kept[0].astype(F32) + received[0].astype(F32)
        far = kept[1].astype(F32) + received[1].astype(F32)
        return near + swap_y(far.astype(BF16)).astype(F32)

    back_out = trade(home(out_keep, out_send).astype(BF16), 4).astype(F32)
    back_in = trade(home(in_keep, in_send).astype(BF16), 4).astype(F32)
    grad_expert_out = ordered(half_index, home(own_out_keep, own_out_send), back_out)
    grad_expert_in = ordered(half_index, home(own_in_keep, own_in_send), back_in)

    router_part = jnp.einsum(
        "te,td->ed", logit_grad.astype(BF16), expert_rows, preferred_element_type=F32
    )
    router_part = router_part[:expert_count] + router_part[expert_count : 2 * expert_count]
    router_part = lax.dynamic_slice_in_dim(
        jnp.concatenate([router_part, router_part], 0),
        jnp.bitwise_and(expert_count - base, expert_count - 1),
        expert_count,
        0,
    )
    mean_router = jnp.einsum("te,td->ed", mean_part, normed_two, preferred_element_type=F32)
    router_part = router_part + mean_router[:expert_count] + mean_router[expert_count:]

    grad_second_part = jnp.sum(grad_two * unit_two, 0)
    grad_unit_two = grad_two * second_gain
    grad_hidden = grad_out + scale_two * (
        grad_unit_two - unit_two * jnp.mean(grad_unit_two * unit_two, -1, keepdims=True)
    )
    small = jnp.concatenate(
        [
            router_part,
            grad_second_part[None],
            jnp.full((1, model_width), squared_local),
        ],
        0,
    )
    small = sum_all(small)

    grad_attn = gather_tensor((RESIDUAL * grad_hidden).astype(BF16), core, row)
    grad_output = jnp.einsum("tc,td->cd", attended, grad_attn, preferred_element_type=F32)
    grad_attended = jnp.einsum("td,cd->tc", grad_attn, output_weight, preferred_element_type=F32)
    grad_attended = grad_attended.astype(BF16).reshape(row_count, local_kv, group, HEAD_DIM)
    attn_probs = jnp.exp(masked_scores() - row_peak) / row_total
    grad_probs = jnp.einsum("qhgd,khd->hgqk", grad_attended, value_low, preferred_element_type=F32)
    grad_scores = attn_probs * (grad_probs - jnp.sum(attn_probs * grad_probs, -1, keepdims=True))
    grad_scores = grad_scores.astype(BF16)
    grad_query_rot = ATTN_SCALE * jnp.einsum(
        "hgqk,khd->qhgd", grad_scores, keys_rot, preferred_element_type=F32
    )
    grad_keys_rot = ATTN_SCALE * jnp.einsum(
        "hgqk,qhgd->khd", grad_scores, query_block, preferred_element_type=F32
    )
    grad_values = jnp.einsum(
        "hgqk,qhgd->khd", attn_probs.astype(BF16), grad_attended, preferred_element_type=F32
    )
    grad_query_low = unrotate(
        grad_query_rot.reshape(row_count, local_query, HEAD_DIM), cosine, sine
    )
    grad_query_low = grad_query_low.reshape(row_count, local_query * HEAD_DIM).astype(BF16)
    grad_keys_low = unrotate(grad_keys_rot, cosine, sine)
    grad_keys_low = grad_keys_low.reshape(row_count, local_kv * HEAD_DIM).astype(BF16)
    grad_values_low = grad_values.reshape(row_count, local_kv * HEAD_DIM).astype(BF16)
    grad_qkv = jnp.concatenate([grad_query_low, grad_keys_low, grad_values_low], 1)
    weights_qkv = jnp.concatenate([query_weight, key_matrix, value_matrix], 1)
    grad_weights = jnp.einsum("td,tc->dc", first_normed, grad_qkv, preferred_element_type=F32)
    grad_one_part = jnp.einsum("tc,dc->td", grad_qkv, weights_qkv, preferred_element_type=F32)
    grad_one = scatter_tensor(grad_one_part, core, row)

    scale_mine = lax.rsqrt(jnp.mean(tokens_mine * tokens_mine, -1, keepdims=True) + EPS)
    unit_mine = tokens_mine * scale_mine
    grad_first_gain = sum_all(jnp.sum(grad_one * unit_mine, 0)[None])[0]
    grad_unit_one = grad_one * first_gain
    grad_tokens = grad_hidden + scale_mine * (
        grad_unit_one - unit_mine * jnp.mean(grad_unit_one * unit_mine, -1, keepdims=True)
    )
    grad_tokens = gather_tensor(grad_tokens.astype(BF16), core, row).astype(F32)
    grad_output = sum_experts(grad_output, place)
    grad_weights = sum_experts(grad_weights, place)
    query_columns = query_weight.shape[1]
    key_columns = query_columns + key_matrix.shape[1]
    return (
        layer_output,
        small[expert_count + 1, 0] / (2.0 * model_width * valid_total),
        grad_tokens,
        grad_first_gain,
        grad_weights[:, :query_columns],
        grad_weights[:, query_columns:key_columns],
        grad_weights[:, key_columns:],
        grad_output,
        small[expert_count],
        small[:expert_count].T,
        grad_expert_in,
        grad_expert_out,
    )


def solution(mesh):
    return jax.shard_map(
        per_device,
        mesh=mesh,
        in_specs=(
            P("expert", None),
            P("expert", None),
            P("expert"),
            P("expert", None),
            P(),
            P(None, "tensor"),
            P(None, "tensor"),
            P(None, "tensor"),
            P("tensor", None),
            P(),
            P(),
            P("expert", None, None, "tensor"),
            P("expert", "tensor", None),
        ),
        out_specs=(
            P("expert", None),
            P(),
            P("expert", None),
            P(),
            P(None, "tensor"),
            P(None, "tensor"),
            P(None, "tensor"),
            P("tensor", None),
            P(),
            P(),
            P("expert", None, None, "tensor"),
            P("expert", "tensor", None),
        ),
        check_vma=False,
    )
```

```python
import jax
import jax.numpy as jnp
from jax import lax
from jax.experimental import pallas as pl
from jax.experimental.pallas import tpu as pltpu
from jax.sharding import PartitionSpec as P

HEAD_DIM = 64
TOP = 8
BLOCK = 256


EPS = 1e-06
ATTN_SCALE = 0.015625
RESIDUAL = 0.22
THETA = 10000.0


def shifted(value, axis, steps):
    count = lax.axis_size(axis)
    pairs = [(source, (source + steps) % count) for source in range(count)]
    return lax.ppermute(value, axis, pairs)


def rope_tables(length, head_size):
    half_size = head_size // 2
    frequency = THETA ** (-(jnp.arange(half_size, dtype=jnp.float32) * 2.0) / head_size)
    angle_table = jnp.arange(length, dtype=jnp.float32)[:, None] * frequency[None, :]
    return (jnp.cos(angle_table)[:, None, :], jnp.sin(angle_table)[:, None, :])


def apply_rotary(values, cosine_lookup, sine_lookup):
    half_size = values.shape[-1] // 2
    lower_half, upper_half = (values[..., :half_size], values[..., half_size:])
    return jnp.concatenate(
        [
            lower_half * cosine_lookup - upper_half * sine_lookup,
            upper_half * cosine_lookup + lower_half * sine_lookup,
        ],
        -1,
    )


def unrotate(grads, cosine_lookup, sine_lookup):
    half_size = grads.shape[-1] // 2
    lower_half, upper_half = (grads[..., :half_size], grads[..., half_size:])
    return jnp.concatenate(
        [
            lower_half * cosine_lookup + upper_half * sine_lookup,
            upper_half * cosine_lookup - lower_half * sine_lookup,
        ],
        -1,
    )


def normalize(values):
    row_peak = jnp.max(values, -1, keepdims=True)
    exp_scores = jnp.exp(values - row_peak)
    return exp_scores / jnp.sum(exp_scores, -1, keepdims=True)


def slot_tables(route_ids, expert_count, capacity):
    row_count, top_count = route_ids.shape
    onehot = route_ids[:, :, None] == jnp.arange(expert_count, dtype=jnp.int32)[None, None, :]
    hit_count = jnp.sum(onehot.astype(jnp.int32), 1)
    slot_place = jnp.cumsum(hit_count, 0) - 1
    within = jnp.take_along_axis(slot_place, route_ids, 1)
    dest_slot = route_ids * capacity + within
    pair_count = row_count * top_count
    source = (
        jnp.full((expert_count * capacity,), pair_count, jnp.int32)
        .at[dest_slot.reshape(-1)]
        .set(jnp.arange(pair_count, dtype=jnp.int32))
    )
    live_slot = source < pair_count
    token_row = jnp.minimum(source, pair_count - 1) // top_count
    return (onehot, dest_slot, source, live_slot, token_row)


def general_device(
    tokens,
    teacher,
    valid_mask,
    routes,
    first_gain,
    query_weight,
    key_matrix,
    value_matrix,
    output_weight,
    second_gain,
    router_weight,
    expert_in,
    expert_out,
):
    row_count = tokens.shape[0]
    model_width = tokens.shape[1]
    half_width = model_width // 2
    local_query = query_weight.shape[1] // HEAD_DIM
    local_kv = key_matrix.shape[1] // HEAD_DIM
    query_group_size = local_query // local_kv
    expert_count = router_weight.shape[1]
    row_local = expert_in.shape[0]
    senders = lax.axis_size("expert")
    partner_step = senders // 2
    capacity = 3 * row_count * TOP // (2 * expert_count)
    pair_count = row_count * TOP
    score_rows = min(512, row_count)
    valid_total = lax.psum(jnp.sum(valid_mask).astype(jnp.float32), "expert")
    tokens_f32 = tokens.astype(jnp.float32)
    scale_one = lax.rsqrt(jnp.mean(tokens_f32 * tokens_f32, -1, keepdims=True) + EPS)
    unit_one = tokens_f32 * scale_one
    first_normed = (unit_one * first_gain).astype(jnp.bfloat16)
    cosine_lookup, sine_lookup = rope_tables(row_count, HEAD_DIM)
    query_linear = jnp.dot(first_normed, query_weight, preferred_element_type=jnp.float32).reshape(
        row_count, local_query, HEAD_DIM
    )
    keys_linear = jnp.dot(first_normed, key_matrix, preferred_element_type=jnp.float32).reshape(
        row_count, local_kv, HEAD_DIM
    )
    value_low = jnp.dot(first_normed, value_matrix, preferred_element_type=jnp.float32).astype(
        jnp.bfloat16
    )
    value_low = value_low.reshape(row_count, local_kv, HEAD_DIM)
    query_rotated = apply_rotary(query_linear, cosine_lookup, sine_lookup).astype(jnp.bfloat16)
    keys_rot = apply_rotary(keys_linear, cosine_lookup, sine_lookup).astype(jnp.bfloat16)
    block_of = jnp.arange(row_count, dtype=jnp.int32) // BLOCK

    def scores(start_row):
        stop_row = start_row + score_rows
        query_block = query_rotated.reshape(score_rows, local_kv, query_group_size, HEAD_DIM)
        score_block = (
            jnp.einsum("qhgd,khd->hgqk", query_block, keys_rot, preferred_element_type=jnp.float32)
            * ATTN_SCALE
        )
        allowed = block_of[None, :stop_row] <= block_of[start_row:stop_row, None]
        return (query_block, jnp.where(allowed, score_block, -1e30))

    attn_parts, row_peaks, row_totals = ([], [], [])
    start_row = 0
    query_block, score_block = scores(start_row)
    row_peak = jnp.max(score_block, -1, keepdims=True)
    exp_scores = jnp.exp(score_block - row_peak)
    row_total = jnp.sum(exp_scores, -1, keepdims=True)
    attn_probs = (exp_scores / row_total).astype(jnp.bfloat16)
    attn_parts.append(
        jnp.einsum("hgqk,khd->qhgd", attn_probs, value_low, preferred_element_type=jnp.float32)
    )
    row_peaks.append(row_peak)
    row_totals.append(row_total)
    attended = attn_parts[0].reshape(row_count, local_query * HEAD_DIM).astype(jnp.bfloat16)
    attn_part = jnp.dot(attended, output_weight, preferred_element_type=jnp.float32)
    attn_sum = lax.psum(attn_part, "tensor")
    hidden_state = tokens_f32 + RESIDUAL * attn_sum
    scale_two = lax.rsqrt(jnp.mean(hidden_state * hidden_state, -1, keepdims=True) + EPS)
    unit_two = hidden_state * scale_two
    normed_two = (unit_two * second_gain).astype(jnp.bfloat16)
    router_logits = jnp.dot(normed_two, router_weight, preferred_element_type=jnp.float32)
    onehot, dest_slot, source, live_slot, token_row = slot_tables(routes, expert_count, capacity)
    picked = jnp.sum(jnp.where(onehot, router_logits[:, None, :], 0.0), -1)
    gate_probs = normalize(picked)

    def slot_rows(slot_values):
        split_rows = slot_values.reshape(expert_count, capacity, 2, half_width).transpose(
            2, 0, 1, 3
        )
        return split_rows.reshape(senders, row_local, capacity, half_width)

    def slot_columns(returned, width):
        joined = returned.reshape(2, expert_count, capacity, width).transpose(1, 2, 0, 3)
        return joined.reshape(expert_count * capacity, 2, width)

    send_rows = slot_rows(
        jnp.where(live_slot[:, None], normed_two[token_row], jnp.zeros((), jnp.bfloat16))
    )
    received = lax.all_to_all(send_rows, "expert", split_axis=0, concat_axis=2, tiled=True)
    expert_rows = received.reshape(row_local, senders * capacity, half_width)
    gate_up_part = jnp.einsum(
        "rmd,rcdf->rmcf", expert_rows, expert_in, preferred_element_type=jnp.float32
    )
    gate_up_pre = gate_up_part + shifted(gate_up_part, "expert", partner_step)
    gate_pre = gate_up_pre[:, :, 0]
    up_pre = gate_up_pre[:, :, 1]
    inner_act = (jax.nn.silu(gate_pre) * up_pre).astype(jnp.bfloat16)
    expert_result = jnp.einsum(
        "rmf,rfd->rmd", inner_act, expert_out, preferred_element_type=jnp.float32
    )
    expert_result = expert_result.astype(jnp.bfloat16).reshape(
        row_local, senders, capacity, half_width
    )
    returned = lax.all_to_all(expert_result, "expert", split_axis=1, concat_axis=0, tiled=True)
    per_route = slot_columns(returned, half_width).reshape(expert_count * capacity, model_width)[
        dest_slot
    ]
    moe_part = jnp.sum(gate_probs[:, :, None] * per_route, 1)
    moe_sum = lax.psum(moe_part, "tensor")
    output = hidden_state + RESIDUAL * moe_sum
    residual_err = output - teacher.astype(jnp.float32)
    valid_rows = valid_mask.astype(jnp.float32)
    squared_local = jnp.sum(valid_rows * jnp.sum(residual_err * residual_err, -1))
    token_total = senders * row_count
    grad_out = token_total / valid_total * valid_rows[:, None] * residual_err
    grad_moe = (RESIDUAL * grad_out).astype(jnp.bfloat16)
    gate_part = jnp.einsum("td,tkd->tk", grad_moe, per_route, preferred_element_type=jnp.float32)
    gate_slot = gate_probs.reshape(pair_count)[jnp.minimum(source, pair_count - 1)]
    grad_slots = jnp.where(live_slot[:, None], gate_slot[:, None] * grad_moe[token_row], 0.0)
    grad_received = lax.all_to_all(
        slot_rows(grad_slots.astype(jnp.bfloat16)),
        "expert",
        split_axis=0,
        concat_axis=2,
        tiled=True,
    )
    grad_expert = grad_received.reshape(row_local, senders * capacity, half_width)
    grad_inner_part = jnp.einsum(
        "rmd,rfd->rmf", grad_expert, expert_out, preferred_element_type=jnp.float32
    )
    grad_inner = grad_inner_part + shifted(grad_inner_part, "expert", partner_step)
    grad_expert_out = jnp.einsum(
        "rmf,rmd->rfd", inner_act, grad_expert, preferred_element_type=jnp.float32
    )
    sigmoid_gate = jax.nn.sigmoid(gate_pre)
    grad_gate = grad_inner * up_pre * sigmoid_gate * (1.0 + gate_pre * (1.0 - sigmoid_gate))
    grad_up = grad_inner * (gate_pre * sigmoid_gate)
    grad_pre = jnp.stack([grad_gate, grad_up], 2).astype(jnp.bfloat16)
    grad_expert_in = jnp.einsum(
        "rmd,rmcf->rcdf", expert_rows, grad_pre, preferred_element_type=jnp.float32
    )
    grad_slot_rows = jnp.einsum(
        "rmcf,rcdf->rmd", grad_pre, expert_in, preferred_element_type=jnp.float32
    )
    grad_slot_rows = grad_slot_rows.astype(jnp.bfloat16).reshape(
        row_local, senders, capacity, half_width
    )
    grad_back = lax.all_to_all(grad_slot_rows, "expert", split_axis=1, concat_axis=0, tiled=True)
    grad_back = slot_columns(grad_back, half_width).reshape(expert_count * capacity, model_width)
    grad_two_part = jnp.sum(grad_back[dest_slot].astype(jnp.float32), 1)
    grad_two_experts, grad_gates = lax.psum((grad_two_part, gate_part), "tensor")
    grad_picked = gate_probs * (grad_gates - jnp.sum(gate_probs * grad_gates, -1, keepdims=True))
    grad_logits = jnp.sum(jnp.where(onehot, grad_picked[:, :, None], 0.0), 1).astype(jnp.bfloat16)
    grad_router = jnp.einsum(
        "td,te->de", normed_two, grad_logits, preferred_element_type=jnp.float32
    )
    grad_two = grad_two_experts + jnp.einsum(
        "te,de->td", grad_logits, router_weight, preferred_element_type=jnp.float32
    )
    grad_second_gain = jnp.sum(grad_two * unit_two, 0)
    grad_unit_two = grad_two * second_gain
    grad_hidden = grad_out + scale_two * (
        grad_unit_two - unit_two * jnp.mean(grad_unit_two * unit_two, -1, keepdims=True)
    )
    grad_attn = (RESIDUAL * grad_hidden).astype(jnp.bfloat16)
    grad_output = jnp.einsum("tc,td->cd", attended, grad_attn, preferred_element_type=jnp.float32)
    grad_attended = jnp.einsum(
        "td,cd->tc", grad_attn, output_weight, preferred_element_type=jnp.float32
    )
    grad_attended = grad_attended.astype(jnp.bfloat16).reshape(
        row_count, local_kv, query_group_size, HEAD_DIM
    )
    grad_query_parts = []
    grad_keys = jnp.zeros((row_count, local_kv, HEAD_DIM), jnp.float32)
    grad_values = jnp.zeros((row_count, local_kv, HEAD_DIM), jnp.float32)
    for block_index, start_row in enumerate(range(0, row_count, score_rows)):
        stop_row = start_row + score_rows
        query_block, score_block = scores(start_row)
        attn_probs = jnp.exp(score_block - row_peaks[block_index]) / row_totals[block_index]
        probs_low = attn_probs.astype(jnp.bfloat16)
        grad_probs = jnp.einsum(
            "qhgd,khd->hgqk", grad_attended, value_low, preferred_element_type=jnp.float32
        )
        grad_scores = attn_probs * (
            grad_probs - jnp.sum(attn_probs * grad_probs, -1, keepdims=True)
        )
        grad_scores = grad_scores.astype(jnp.bfloat16)
        grad_query_parts.append(
            ATTN_SCALE
            * jnp.einsum(
                "hgqk,khd->qhgd", grad_scores, keys_rot, preferred_element_type=jnp.float32
            )
        )
        grad_keys = grad_keys.at[:stop_row].add(
            ATTN_SCALE
            * jnp.einsum(
                "hgqk,qhgd->khd", grad_scores, query_block, preferred_element_type=jnp.float32
            )
        )
        grad_values = grad_values.at[:stop_row].add(
            jnp.einsum(
                "hgqk,qhgd->khd", probs_low, grad_attended, preferred_element_type=jnp.float32
            )
        )
    grad_query_rot = grad_query_parts[0].reshape(row_count, local_query, HEAD_DIM)
    grad_query_low = unrotate(grad_query_rot, cosine_lookup, sine_lookup).reshape(
        row_count, local_query * HEAD_DIM
    )
    grad_query_low = grad_query_low.astype(jnp.bfloat16)
    grad_keys_low = unrotate(grad_keys, cosine_lookup, sine_lookup).reshape(
        row_count, local_kv * HEAD_DIM
    )
    grad_keys_low = grad_keys_low.astype(jnp.bfloat16)
    grad_values_low = grad_values.reshape(row_count, local_kv * HEAD_DIM).astype(jnp.bfloat16)
    grad_query = jnp.einsum(
        "td,tc->dc", first_normed, grad_query_low, preferred_element_type=jnp.float32
    )
    grad_key = jnp.einsum(
        "td,tc->dc", first_normed, grad_keys_low, preferred_element_type=jnp.float32
    )
    grad_value = jnp.einsum(
        "td,tc->dc", first_normed, grad_values_low, preferred_element_type=jnp.float32
    )
    grad_one_part = (
        jnp.einsum("tc,dc->td", grad_query_low, query_weight, preferred_element_type=jnp.float32)
        + jnp.einsum("tc,dc->td", grad_keys_low, key_matrix, preferred_element_type=jnp.float32)
        + jnp.einsum("tc,dc->td", grad_values_low, value_matrix, preferred_element_type=jnp.float32)
    )
    grad_one = lax.psum(grad_one_part.astype(jnp.bfloat16), "tensor").astype(jnp.float32)
    grad_first_gain = jnp.sum(grad_one * unit_one, 0)
    grad_unit_one = grad_one * first_gain
    grad_tokens = grad_hidden + scale_one * (
        grad_unit_one - unit_one * jnp.mean(grad_unit_one * unit_one, -1, keepdims=True)
    )
    reduced = lax.psum(
        (
            grad_first_gain,
            grad_query,
            grad_key,
            grad_value,
            grad_output,
            grad_second_gain,
            grad_router,
            squared_local,
        ),
        "expert",
    )
    loss_value = reduced[7] / (2.0 * model_width * valid_total)
    return (
        output.astype(jnp.bfloat16),
        loss_value,
        grad_tokens,
        reduced[0],
        reduced[1],
        reduced[2],
        reduced[3],
        reduced[4],
        reduced[5],
        reduced[6],
        grad_expert_in,
        grad_expert_out,
    )


BF16 = jnp.bfloat16
F32 = jnp.float32
CHUNK = 256
SHARE = 128
PACK = 12 * SHARE
NT = (((1,), (1,)), ((), ()))
ORDER = (0, 2, 4, 6, 1, 3, 5, 7)


def whole_block(shape):
    return pl.BlockSpec(shape, lambda e, *_: (0,) * len(shape))


def any_block():
    return pl.BlockSpec(memory_space=pl.ANY)


def pack_body(half_ref, own_in, own_out, other_in, other_out, own, near, far):
    step = pl.program_id(0)

    def fill(target, source_in, source_out):
        for c in range(2):
            target[c * 4 * SHARE : (c + 1) * 4 * SHARE, :] = source_in[0, c]
        for k in range(4):
            target[(8 + k) * SHARE : (9 + k) * SHARE, :] = source_out[
                0, :, k * SHARE : (k + 1) * SHARE
            ]

    fill(own, own_in, own_out)

    @pl.when(step < 2)
    def _():
        fill(near, other_in, other_out)

    @pl.when(step >= 2)
    def _():
        fill(far, other_in, other_out)


def pack_weights(half_index, expert_in, expert_out):
    held = expert_in.shape[0] // 2
    in_shape = (1,) + expert_in.shape[1:]
    out_shape = (1,) + expert_out.shape[1:]
    shapes = [(held * PACK, SHARE), (held // 2 * PACK, SHARE), (held // 2 * PACK, SHARE)]
    block = (PACK, SHARE)
    return pl.pallas_call(
        pack_body,
        grid_spec=pltpu.PrefetchScalarGridSpec(
            num_scalar_prefetch=1,
            grid=(held,),
            in_specs=[
                pl.BlockSpec(in_shape, lambda e, half: (half[0] * held + e, 0, 0, 0)),
                pl.BlockSpec(out_shape, lambda e, half: (half[0] * held + e, 0, 0)),
                pl.BlockSpec(in_shape, lambda e, half: ((1 - half[0]) * held + e, 0, 0, 0)),
                pl.BlockSpec(out_shape, lambda e, half: ((1 - half[0]) * held + e, 0, 0)),
            ],
            out_specs=[
                pl.BlockSpec(block, lambda e, half: (e, 0)),
                pl.BlockSpec(block, lambda e, half: (jnp.minimum(e, 1), 0)),
                pl.BlockSpec(block, lambda e, half: (jnp.maximum(e - 2, 0), 0)),
            ],
        ),
        out_shape=[jax.ShapeDtypeStruct(shape, BF16) for shape in shapes],
        name="pack_weights",
    )(half_index, expert_in, expert_out, expert_in, expert_out)


def weight_copies(own, other, own_row, other_row, half, in_buf, out_buf, sems, slot):
    copies = []
    for q in range(4):
        for pack, row, side in ((own[q], own_row, half), (other[q], other_row, 1 - half)):
            for c in range(2):
                copies.append(
                    (
                        pack.at[pl.ds(pl.multiple_of(row + c * 4 * SHARE, SHARE), 4 * SHARE)],
                        in_buf.at[
                            slot,
                            pl.ds(pl.multiple_of(side * 4 * SHARE, SHARE), 4 * SHARE),
                            pl.ds((2 * q + c) * SHARE, SHARE),
                        ],
                    )
                )
            for k in range(4):
                copies.append(
                    (
                        pack.at[pl.ds(pl.multiple_of(row + (8 + k) * SHARE, SHARE), SHARE)],
                        out_buf.at[slot, side, pl.ds(q * SHARE, SHARE), pl.ds(k * SHARE, SHARE)],
                    )
                )
    return [
        pltpu.make_async_copy(source, target, sems.at[slot, n])
        for n, (source, target) in enumerate(copies)
    ]


def stream_weights(first, packs, half, in_buf, out_buf, sems):
    step = pl.program_id(0)
    slot = lax.rem(step, 2)
    own, near, far = (packs[0:4], packs[4:8], packs[8:12])

    def start(index, target):
        expert = first + index

        def begin(other, start_row):
            for copy in weight_copies(
                own, other, expert * PACK, start_row, half, in_buf, out_buf, sems, target
            ):
                copy.start()

        if not far:
            begin(near, index * PACK)
            return

        @pl.when(expert < 2)
        def _():
            begin(near, expert * PACK)

        @pl.when(expert >= 2)
        def _():
            begin(far, (expert - 2) * PACK)

    @pl.when(step == 0)
    def _():
        start(0, 0)

    @pl.when(step + 1 < pl.num_programs(0))
    def _():
        start(step + 1, 1 - slot)

    def wait():
        for copy in weight_copies(own, near, 0, 0, half, in_buf, out_buf, sems, slot):
            copy.wait()

    return (step, slot, wait)


def weight_scratch(width, hidden):
    return [
        pltpu.VMEM((2, width, 2 * hidden), BF16),
        pltpu.VMEM((2, 2, hidden, width // 2), BF16),
        pltpu.SemaphoreType.DMA((2, 48)),
    ]


def split_pairs(values):
    blocks = [values[:, i * SHARE : (i + 1) * SHARE] for i in range(values.shape[1] // SHARE)]
    return (jnp.concatenate(blocks[0::2], 1), jnp.concatenate(blocks[1::2], 1))


def join_pairs(first, second):
    blocks = []
    for i in range(first.shape[1] // SHARE):
        blocks.append(first[:, i * SHARE : (i + 1) * SHARE])
        blocks.append(second[:, i * SHARE : (i + 1) * SHARE])
    return jnp.concatenate(blocks, 1)


def chunk_loop(row_count, body):
    def step(i, carry):
        body(pl.ds(pl.multiple_of(i * CHUNK, CHUNK), CHUNK))
        return carry

    lax.fori_loop(0, row_count // CHUNK, step, 0)


def gate_column(gates, expert):
    lane = lax.broadcasted_iota(jnp.int32, gates.shape, 1)
    return jnp.sum(jnp.where(lane == expert, gates, 0.0), -1, keepdims=True)


def dense_gates(rows, ids, router):
    logits = jnp.dot(rows, router, preferred_element_type=F32)
    lane = lax.broadcasted_iota(jnp.int32, logits.shape, 1)
    mask = ids[:, 0:1] == lane
    for k in range(1, TOP):
        mask = mask | (ids[:, k : k + 1] == lane)
    masked = jnp.where(mask, logits, -1e30)
    powers = jnp.where(mask, jnp.exp(masked - jnp.max(masked, -1, keepdims=True)), 0.0)
    return powers / jnp.sum(powers, -1, keepdims=True)


def apply_expert(rows, expert, slot, rows_ref, gate_ref, pre_ref, gated_ref, in_buf):
    pre = jnp.dot(rows_ref[rows, :], in_buf[slot], preferred_element_type=F32)
    pre_ref[0, rows, :] = pre.astype(BF16)
    gate_pre, up_pre = split_pairs(pre)
    weight = gate_column(gate_ref[rows, :], expert)
    gated = (weight * (gate_pre * jax.nn.sigmoid(gate_pre) * up_pre)).astype(BF16)
    gated_ref[0, rows, :] = gated
    return gated


def forward_first(half_ref, *refs):
    shards = refs[:8]
    route_ref, router_ref = refs[8:10]
    packs = refs[10:18]
    acc, pre_ref, gated_ref, gate_ref, rows_ref, in_buf, out_buf, sems = refs[18:]
    step, slot, wait = stream_weights(0, packs, half_ref[0], in_buf, out_buf, sems)
    row_count, width = acc.shape
    size = row_count // 8

    @pl.when(step == 0)
    def _():
        for i in range(8):
            rows_ref[i * size : (i + 1) * size, :] = shards[i][...]
        acc[...] = jnp.zeros_like(acc)

        def gating(rows):
            gate_ref[rows, :] = dense_gates(rows_ref[rows, :], route_ref[rows, :], router_ref[...])

        chunk_loop(row_count, gating)

    wait()

    def mlp(rows):
        gated = apply_expert(rows, step, slot, rows_ref, gate_ref, pre_ref, gated_ref, in_buf)
        for side in range(2):
            columns = slice(side * width // 2, (side + 1) * width // 2)
            acc[rows, columns] += jnp.dot(gated, out_buf[slot, side], preferred_element_type=F32)

    chunk_loop(row_count, mlp)


def forward_second(half_ref, *refs):
    rows_ref, gate_ref, start_ref = refs[:3]
    packs = refs[3:11]
    keep_ref, near_ref, far_ref, pre_ref, gated_ref, acc, in_buf, out_buf, sems = refs[13:]
    step, slot, wait = stream_weights(2, packs, half_ref[0], in_buf, out_buf, sems)
    row_count, width = acc.shape

    wait()

    def mlp(rows, source):
        gated = apply_expert(rows, step + 2, slot, rows_ref, gate_ref, pre_ref, gated_ref, in_buf)
        for side in range(2):
            columns = slice(side * width // 2, (side + 1) * width // 2)
            acc[rows, columns] = source[rows, columns] + jnp.dot(
                gated, out_buf[slot, side], preferred_element_type=F32
            )

    @pl.when(step == 0)
    def _():
        chunk_loop(row_count, lambda rows: mlp(rows, start_ref))

    @pl.when(step > 0)
    def _():
        chunk_loop(row_count, lambda rows: mlp(rows, acc))

    @pl.when(step == pl.num_programs(0) - 1)
    def _():
        spread(acc, keep_ref, near_ref, far_ref)


def spread(acc, keep_ref, near_ref, far_ref):
    part = acc.shape[0] // 4
    keep_ref[...] = acc[: 2 * part, :]
    near_ref[...] = acc[2 * part : 3 * part, :].astype(BF16)
    far_ref[...] = acc[3 * part :, :].astype(BF16)


def spread_specs(row_count, width):
    shapes = [
        jax.ShapeDtypeStruct((row_count // 2, width), F32),
        jax.ShapeDtypeStruct((row_count // 4, width), BF16),
        jax.ShapeDtypeStruct((row_count // 4, width), BF16),
    ]
    return ([whole_block(s.shape) for s in shapes], shapes)


def expert_block(shape, first=0):
    return pl.BlockSpec((1,) + shape[1:], lambda e, *_: (e + first,) + (0,) * (len(shape) - 1))


def experts_forward(half_index, shards, route_ids, router, own, near, far):
    size, width = shards[0].shape
    row_count = 8 * size
    local = own[0].shape[0] // PACK
    hidden = 4 * SHARE
    sums = jax.ShapeDtypeStruct((row_count, width), F32)
    pre = jax.ShapeDtypeStruct((local, row_count, 2 * hidden), BF16)
    gated = jax.ShapeDtypeStruct((local, row_count, hidden), BF16)
    gates = jax.ShapeDtypeStruct((row_count, 128), F32)
    rows = jax.ShapeDtypeStruct((row_count, width), BF16)
    sums_a, pre_a, gated_a, gates, rows = pl.pallas_call(
        forward_first,
        grid_spec=pltpu.PrefetchScalarGridSpec(
            num_scalar_prefetch=1,
            grid=(2,),
            in_specs=[whole_block(v.shape) for v in (*shards, route_ids, router)]
            + [any_block()] * 8,
            out_specs=[
                whole_block(sums.shape),
                expert_block(pre.shape),
                expert_block(gated.shape),
                whole_block(gates.shape),
                whole_block(rows.shape),
            ],
            scratch_shapes=weight_scratch(width, hidden),
        ),
        out_shape=[sums, pre, gated, gates, rows],
        name="experts_forward_a",
    )(half_index, *shards, route_ids, router, *own, *near)
    specs, shapes = spread_specs(row_count, width)
    keep, send_near, send_far, pre, gated = pl.pallas_call(
        forward_second,
        grid_spec=pltpu.PrefetchScalarGridSpec(
            num_scalar_prefetch=1,
            grid=(2,),
            in_specs=[whole_block(v.shape) for v in (rows, gates, sums)] + [any_block()] * 10,
            out_specs=specs + [expert_block(pre.shape, 2), expert_block(gated.shape, 2)],
            scratch_shapes=[pltpu.VMEM((row_count, width), F32)] + weight_scratch(width, hidden),
        ),
        out_shape=shapes + [pre, gated],
        input_output_aliases={12: 3, 13: 4},
        name="experts_forward_b",
    )(half_index, rows, gates, sums_a, *own, *far, pre_a, gated_a)
    return (keep, send_near, send_far, pre, gated, gates, rows)


def backward_body(half_ref, *refs):
    shards = refs[:8]
    gate_ref, router_ref, pre_ref = refs[8:11]
    packs = refs[11:23]
    keep_ref, near_ref, far_ref, pre_grad_ref, logit_ref, grad_ref = refs[-10:-4]
    acc, in_buf, out_buf, sems = refs[-4:]
    step, slot, wait = stream_weights(0, packs, half_ref[0], in_buf, out_buf, sems)
    row_count, width = grad_ref.shape
    size = row_count // 8

    @pl.when(step == 0)
    def _():
        for i in range(8):
            grad_ref[i * size : (i + 1) * size, :] = shards[i][...]
        acc[...] = jnp.zeros_like(acc)
        logit_ref[...] = jnp.zeros_like(logit_ref)

    wait()

    def mlp(rows):
        plain = lax.dot_general(
            grad_ref[rows, : width // 2], out_buf[slot, 0], NT, preferred_element_type=F32
        ) + lax.dot_general(
            grad_ref[rows, width // 2 :], out_buf[slot, 1], NT, preferred_element_type=F32
        )
        gate_pre, up_pre = split_pairs(pre_ref[0, rows, :].astype(F32))
        weight = gate_column(gate_ref[rows, :], step)
        sigmoid = jax.nn.sigmoid(gate_pre)
        act = gate_pre * sigmoid
        grad_weight = jnp.sum(act * up_pre * plain, -1, keepdims=True)
        scaled = weight * plain
        pre_grad = join_pairs(
            scaled * up_pre * (sigmoid + act * (1.0 - sigmoid)), scaled * act
        ).astype(BF16)
        pre_grad_ref[0, rows, :] = pre_grad
        old = logit_ref[rows, :]
        lane = lax.broadcasted_iota(jnp.int32, old.shape, 1)
        value = weight * grad_weight
        high = value.astype(BF16).astype(F32)
        logit_ref[rows, :] = jnp.where(
            lane == step, high, jnp.where(lane == step + 32, value - high, old)
        )
        acc[rows, :] += lax.dot_general(pre_grad, in_buf[slot], NT, preferred_element_type=F32)

    chunk_loop(row_count, mlp)

    @pl.when(step == pl.num_programs(0) - 1)
    def _():
        def router(rows):
            acc[rows, :] += lax.dot_general(
                logit_ref[rows, :].astype(BF16), router_ref[...], NT, preferred_element_type=F32
            )

        chunk_loop(row_count, router)
        spread(acc, keep_ref, near_ref, far_ref)


def experts_backward(half_index, shards, gates, router, pre, own, near, far, *after):
    row_count, width = (8 * shards[0].shape[0], shards[0].shape[1])
    local = pre.shape[0]
    specs, shapes = spread_specs(row_count, width)
    return pl.pallas_call(
        backward_body,
        grid_spec=pltpu.PrefetchScalarGridSpec(
            num_scalar_prefetch=1,
            grid=(local,),
            in_specs=[whole_block(v.shape) for v in (*shards, gates, router)]
            + [expert_block(pre.shape)]
            + [any_block()] * (12 + len(after)),
            out_specs=specs
            + [
                expert_block(pre.shape),
                whole_block((row_count, 128)),
                whole_block((row_count, width)),
            ],
            scratch_shapes=[pltpu.VMEM((row_count, width), F32)]
            + weight_scratch(width, 4 * SHARE),
        ),
        out_shape=shapes
        + [
            jax.ShapeDtypeStruct(pre.shape, BF16),
            jax.ShapeDtypeStruct((row_count, 128), F32),
            jax.ShapeDtypeStruct((row_count, width), BF16),
        ],
        name="experts_backward",
    )(half_index, *shards, gates, router, pre, *own, *near, *far, *after)


def cost(flops):
    return pl.CostEstimate(flops=flops, bytes_accessed=1 << 22, transcendentals=0)


def grad_out_body(half_ref, gated_ref, other_ref, mine_ref, *refs):
    outs = refs[-4:]
    turned = gated_ref[0].T
    for n, source in ((0, other_ref), (2, mine_ref)):
        product = jnp.dot(turned, source[...], preferred_element_type=F32).astype(BF16)
        for q in range(4):
            outs[n + q % 2][q // 2, 0] = product[q * SHARE : (q + 1) * SHARE, :]


def grad_expert_outs(half_index, gated, grads, *after):
    local, row_count, hidden = gated.shape
    width = grads.shape[1]
    half_spec = (row_count, width // 2)
    shape = (2, local, SHARE, width // 2)
    return pl.pallas_call(
        grad_out_body,
        grid_spec=pltpu.PrefetchScalarGridSpec(
            num_scalar_prefetch=1,
            grid=(local,),
            in_specs=[
                expert_block(gated.shape),
                pl.BlockSpec(half_spec, lambda e, half: (0, 1 - half[0])),
                pl.BlockSpec(half_spec, lambda e, half: (0, half[0])),
            ]
            + [any_block()] * len(after),
            out_specs=[pl.BlockSpec((2, 1) + shape[2:], lambda e, *_: (0, e, 0, 0))] * 4,
        ),
        out_shape=[jax.ShapeDtypeStruct(shape, BF16)] * 4,
        cost_estimate=cost(2 * local * row_count * hidden * width),
        name="grad_expert_out",
    )(half_index, gated, grads, grads, *after)


def grad_in_body(half_ref, rows_ref, pre_ref, *refs):
    keep_ref, send_ref, turned = refs[-3:]

    @pl.when(pl.program_id(0) == 0)
    def _():
        turned[...] = rows_ref[...].T

    product = jnp.dot(turned[...], pre_ref[0], preferred_element_type=F32).astype(BF16)
    for q in range(4):
        for c in range(2):
            start = (2 * q + c) * SHARE
            (keep_ref, send_ref)[q % 2][q // 2, 0, c] = product[:, start : start + SHARE]


def grad_expert_ins(half_index, rows, pre_grad, *after):
    local, row_count, wide = pre_grad.shape
    width = rows.shape[1]
    shape = (2, local, 2, width // 2, SHARE)
    return pl.pallas_call(
        grad_in_body,
        grid_spec=pltpu.PrefetchScalarGridSpec(
            num_scalar_prefetch=1,
            grid=(local,),
            in_specs=[
                pl.BlockSpec((row_count, width // 2), lambda e, half: (0, half[0])),
                expert_block(pre_grad.shape),
            ]
            + [any_block()] * len(after),
            out_specs=[pl.BlockSpec((2, 1) + shape[2:], lambda e, *_: (0, e, 0, 0, 0))] * 2,
            scratch_shapes=[pltpu.VMEM((width // 2, row_count), BF16)],
        ),
        out_shape=[jax.ShapeDtypeStruct(shape, BF16)] * 2,
        cost_estimate=cost(local * row_count * wide * width),
        name="grad_expert_in",
    )(half_index, rows, pre_grad, *after)


def fold_body(keep_ref, got_ref, *refs):
    near_ref, far_ref = refs[-2:]
    near_ref[...] = keep_ref[0].astype(F32) + got_ref[0].astype(F32)
    far_ref[...] = (keep_ref[1].astype(F32) + got_ref[1].astype(F32)).astype(BF16)


def fold_pairs(keep, got, *after):
    shape = keep.shape
    rest = (0,) * (len(shape) - 2)
    pair = pl.BlockSpec((2, 1) + shape[2:], lambda e: (0, e) + rest)
    single = pl.BlockSpec((1,) + shape[2:], lambda e: (e,) + rest)
    return pl.pallas_call(
        fold_body,
        grid=(shape[1],),
        in_specs=[pair, pair] + [any_block()] * len(after),
        out_specs=[single, single],
        out_shape=[
            jax.ShapeDtypeStruct(shape[1:], F32),
            jax.ShapeDtypeStruct(shape[1:], BF16),
        ],
        cost_estimate=cost(1 << 20),
        name="fold_pairs",
    )(keep, got, *after)


def finish_body(keep, near, two, four, six, extra, unit, scale, gain, grad_out, *refs):
    hidden_ref, attn_ref, gain_ref = refs[-3:]
    total = keep[...] + near[...].astype(F32) + extra[...]
    for part in (two, four, six):
        total = total + part[...].astype(F32)
    gain_ref[...] = jnp.sum((total * unit[...]).reshape(-1, 8, total.shape[1]), 0)
    weighted = total * gain[...]
    mean = jnp.mean(weighted * unit[...], -1, keepdims=True)
    hidden = grad_out[...] + scale[...] * (weighted - unit[...] * mean)
    hidden_ref[...] = hidden
    attn_ref[...] = (RESIDUAL * hidden).astype(BF16)


def finish_rows(keep, near, two, four, six, extra, unit, scale, gain, grad_out, *after):
    size, width = unit.shape
    block = pl.BlockSpec((size, width), lambda e: (0, 0))
    return pl.pallas_call(
        finish_body,
        grid=(1,),
        in_specs=[block] * 7
        + [whole_block((size, 1)), whole_block((1, width)), block]
        + [any_block()] * len(after),
        out_specs=[block, block, whole_block((8, width))],
        out_shape=[
            jax.ShapeDtypeStruct((size, width), F32),
            jax.ShapeDtypeStruct((size, width), BF16),
            jax.ShapeDtypeStruct((8, width), F32),
        ],
        cost_estimate=cost(1 << 20),
        name="finish_rows",
    )(keep, near, two, four, six, extra, unit, scale, gain, grad_out, *after)


def join_body(first, second, third, *refs):
    target = refs[-1]
    start = 0
    for part in (first, second, third):
        target[:, start : start + part.shape[1]] = part[...]
        start += part.shape[1]


def join_columns(first, second, third, *after):
    parts = (first, second, third)
    shape = (first.shape[0], sum(part.shape[1] for part in parts))
    return pl.pallas_call(
        join_body,
        grid=(1,),
        in_specs=[whole_block(part.shape) for part in parts] + [any_block()] * len(after),
        out_specs=whole_block(shape),
        out_shape=jax.ShapeDtypeStruct(shape, BF16),
        cost_estimate=cost(1 << 20),
        name="join_columns",
    )(*parts, *after)


def trade(value, bits):
    return lax.ppermute(value, "expert", [(i, i ^ bits) for i in range(8)])


def swap_y(value):
    return lax.ppermute(value, "tensor", [(i, i ^ 2) for i in range(4)])


def swap_core(value):
    return lax.ppermute(value, "tensor", [(i, i ^ 1) for i in range(4)])


def gather_experts(value):
    column = [value] + [trade(value, bits) for bits in (2, 4, 6)]
    return column + [trade(shard, 1) for shard in column]


def scatter_experts(keep, send_near, send_far):
    size = keep.shape[0] // 4
    far = keep[2 * size :].astype(F32) + trade(send_far, 1).astype(F32)
    far = far.astype(BF16)
    back = [trade(far[:size], 4), trade(far[size:], 6)]
    near = trade(send_near, 1).astype(F32)
    back.append(trade((keep[size : 2 * size].astype(F32) + near[size:]).astype(BF16), 2))
    total = keep[:size].astype(F32) + near[:size]
    for part in back:
        total = total + part.astype(F32)
    return total


def scatter_tensor(value, core, row):
    quarter = value.shape[0] // 4
    parts = value.reshape(2, 2, quarter, value.shape[1])
    keep = lax.dynamic_index_in_dim(parts, core, 1, False)
    send = lax.dynamic_index_in_dim(parts, 1 - core, 1, False)
    half = keep + swap_core(send.astype(BF16)).astype(F32)
    keep = lax.dynamic_index_in_dim(half, row, 0, False)
    send = lax.dynamic_index_in_dim(half, 1 - row, 0, False)
    return keep + swap_y(send.astype(BF16)).astype(F32)


def ordered(index, first, second):
    return jnp.where(
        index == 0, jnp.concatenate([first, second], 0), jnp.concatenate([second, first], 0)
    )


def gather_tensor(value, core, row):
    across = swap_y(value)
    pair = ordered(core, value, swap_core(value))
    other = ordered(core, across, swap_core(across))
    return ordered(row, pair, other)


def sum_experts(shards, place):
    size, width = shards.shape[1:]

    def pick(*order):
        picked = [
            lax.dynamic_index_in_dim(shards, jnp.bitwise_xor(place, r), 0, False) for r in order
        ]
        return jnp.concatenate(picked, 0)

    total = scatter_experts(pick(0, 2, 4, 6), pick(1, 3).astype(BF16), pick(5, 7).astype(BF16))
    gathered = jnp.stack(gather_experts(total.astype(BF16)))
    lower = (jnp.bitwise_and(place, 1), jnp.bitwise_and(place, 2), jnp.bitwise_and(place, 4))
    column, inner, outer = (bit > 0 for bit in lower)
    halves = jnp.stack([gathered[:4], gathered[4:]])
    halves = jnp.where(column, halves[::-1], halves)
    halves = halves.reshape(2, 2, 2, size, width)
    halves = jnp.where(inner, halves[:, :, ::-1], halves)
    halves = jnp.where(outer, halves[:, ::-1], halves)
    return halves.transpose(1, 2, 0, 3, 4).reshape(shards.shape).astype(F32)


def per_device(
    tokens,
    teacher,
    valid_mask,
    routes,
    first_gain,
    query_weight,
    key_matrix,
    value_matrix,
    output_weight,
    second_gain,
    router_weight,
    expert_in,
    expert_out,
):
    row_count, model_width = tokens.shape
    expert_count = router_weight.shape[1]
    senders = lax.axis_size("expert")
    shares = lax.axis_size("tensor")
    fits = (
        (senders, shares) == (8, 4)
        and expert_count == senders * shares
        and expert_in.shape == (8, 2, model_width // 2, SHARE)
        and row_count == 4 * 128
    )
    if not fits:
        return general_device(
            tokens,
            teacher,
            valid_mask,
            routes,
            first_gain,
            query_weight,
            key_matrix,
            value_matrix,
            output_weight,
            second_gain,
            router_weight,
            expert_in,
            expert_out,
        )
    local_query = query_weight.shape[1] // HEAD_DIM
    local_kv = key_matrix.shape[1] // HEAD_DIM
    group = local_query // local_kv
    quarter = row_count // shares
    place = lax.axis_index("expert")
    share = lax.axis_index("tensor")
    row, core = (share // 2, share % 2)
    half_index = place // 4
    half_arg = half_index.reshape(1)
    held = expert_in.shape[0] // 2
    base = 8 * (place % 4) + held * half_index

    own_pack, near_pack, far_pack = pack_weights(half_arg, expert_in, expert_out)
    near_pack = trade(near_pack, 4)
    far_pack = trade(far_pack, 4)

    def spread_shares(pack):
        across = swap_y(pack)
        return [pack, swap_core(pack), across, swap_core(across)]

    own = spread_shares(own_pack)

    def quarter_of(values):
        return lax.dynamic_slice_in_dim(values, share * quarter, quarter, 0)

    local_valid = jnp.sum(valid_mask)
    routes_mine = quarter_of(routes)
    notes = jnp.concatenate(
        [routes_mine.T, jnp.full((TOP, quarter), local_valid, jnp.int32)], 0
    )[None]
    for bits in (1, 2, 4):
        notes = jnp.concatenate([notes, trade(notes, bits)], 0)
    valid_total = jnp.sum(notes[:, TOP, 0]).astype(F32)
    notes = jnp.stack([notes[r, :TOP] for r in ORDER])
    route_rel = jnp.bitwise_and(notes - base, expert_count - 1)
    route_rel = route_rel.transpose(0, 2, 1).reshape(senders * quarter, TOP)
    router_rel = lax.dynamic_slice_in_dim(
        jnp.concatenate([router_weight, router_weight], 1), base, expert_count, 1
    )
    router_rel = jnp.pad(
        jnp.concatenate([router_rel, router_rel], 1), ((0, 0), (0, 128 - 2 * expert_count))
    )

    tokens_f32 = tokens.astype(F32)
    scale_one = lax.rsqrt(jnp.mean(tokens_f32 * tokens_f32, -1, keepdims=True) + EPS)
    unit_one = tokens_f32 * scale_one
    first_normed = (unit_one * first_gain).astype(BF16)
    cosine, sine = rope_tables(row_count, HEAD_DIM)
    query_linear = jnp.dot(first_normed, query_weight, preferred_element_type=F32)
    keys_linear = jnp.dot(first_normed, key_matrix, preferred_element_type=F32)
    value_low = jnp.dot(first_normed, value_matrix, preferred_element_type=F32).astype(BF16)
    value_low = value_low.reshape(row_count, local_kv, HEAD_DIM)
    query_rotated = apply_rotary(
        query_linear.reshape(row_count, local_query, HEAD_DIM), cosine, sine
    ).astype(BF16)
    keys_rot = apply_rotary(
        keys_linear.reshape(row_count, local_kv, HEAD_DIM), cosine, sine
    ).astype(BF16)
    query_block = query_rotated.reshape(row_count, local_kv, group, HEAD_DIM)
    block_of = jnp.arange(row_count, dtype=jnp.int32) // BLOCK
    allowed = block_of[None, :] <= block_of[:, None]

    def masked_scores():
        scores = jnp.einsum("qhgd,khd->hgqk", query_block, keys_rot, preferred_element_type=F32)
        return jnp.where(allowed, scores * ATTN_SCALE, -1e30)

    scores = masked_scores()
    row_peak = jnp.max(scores, -1, keepdims=True)
    powers = jnp.exp(scores - row_peak)
    row_total = jnp.sum(powers, -1, keepdims=True)
    probs_low = (powers / row_total).astype(BF16)
    attended = jnp.einsum("hgqk,khd->qhgd", probs_low, value_low, preferred_element_type=F32)
    attended = attended.reshape(row_count, local_query * HEAD_DIM).astype(BF16)
    attn_part = jnp.dot(attended, output_weight, preferred_element_type=F32)

    tokens_mine = quarter_of(tokens).astype(F32)
    hidden = tokens_mine + RESIDUAL * scatter_tensor(attn_part, core, row)
    scale_two = lax.rsqrt(jnp.mean(hidden * hidden, -1, keepdims=True) + EPS)
    unit_two = hidden * scale_two
    normed_two = (unit_two * second_gain).astype(BF16)
    row_shards = gather_experts(normed_two)
    near_pack, far_pack, normed_two = lax.optimization_barrier((near_pack, far_pack, normed_two))
    near, far = (spread_shares(near_pack), spread_shares(far_pack))
    keep, send_near, send_far, pre, gated, gates, expert_rows = experts_forward(
        half_arg,
        row_shards,
        route_rel,
        router_rel,
        own,
        near,
        far,
    )
    moe_sum = scatter_experts(keep, send_near, send_far)

    output = hidden + RESIDUAL * moe_sum
    residual_err = output - quarter_of(teacher).astype(F32)
    valid_rows = quarter_of(valid_mask).astype(F32)[:, None]
    squared_local = jnp.sum(valid_rows * residual_err * residual_err)
    token_total = senders * row_count
    grad_out = token_total / valid_total * valid_rows * residual_err
    grad_moe = (RESIDUAL * grad_out).astype(BF16)
    gate_mean = jnp.sum(grad_moe.astype(F32) * moe_sum, -1, keepdims=True)
    mean_part = -gate_mean * dense_gates(normed_two, routes_mine, router_weight)
    mean_high = mean_part.astype(BF16)
    mean_part = jnp.concatenate([mean_high, (mean_part - mean_high.astype(F32)).astype(BF16)], 1)
    router_pair = jnp.concatenate([router_weight, router_weight], 1)
    mean_rows = jnp.einsum("te,de->td", mean_part, router_pair, preferred_element_type=F32)
    layer_output = gather_tensor(output.astype(BF16), core, row)

    keep, send_near, send_far, pre_grad, logit_grad, grad_rows = experts_backward(
        half_arg,
        gather_experts(grad_moe),
        gates,
        router_rel,
        pre,
        own,
        near,
        far,
        layer_output,
        mean_rows,
    )
    got_far = trade(send_far, 1)
    got_near = trade(send_near, 1)
    in_keep, in_send = grad_expert_ins(1 - half_arg, expert_rows, pre_grad)
    far_rows = (keep[2 * quarter :] + got_far.astype(F32)).astype(BF16)
    back_four = trade(far_rows[:quarter], 4)
    back_six = trade(far_rows[quarter:], 6)
    in_near, in_far = fold_pairs(in_keep, swap_core(in_send), far_rows)
    in_across = swap_y(in_far)
    out_keep, out_send, own_out_keep, own_out_send = grad_expert_outs(
        half_arg, gated, grad_rows, in_far
    )
    near_rows = (keep[quarter : 2 * quarter] + got_near[quarter:].astype(F32)).astype(BF16)
    back_two = trade(near_rows, 2)
    own_in_keep, own_in_send = grad_expert_ins(half_arg, expert_rows, pre_grad, near_rows, out_send)
    in_back = trade((in_near + in_across.astype(F32)).astype(BF16), 4)
    grad_hidden, grad_attn, grad_second_part = finish_rows(
        keep,
        got_near,
        back_two,
        back_four,
        back_six,
        mean_rows,
        unit_two,
        scale_two,
        second_gain[None],
        grad_out,
        own_in_send,
        in_across,
    )
    grad_second_part = jnp.sum(grad_second_part, 0)

    router_part = jnp.einsum(
        "te,td->ed", logit_grad.astype(BF16), expert_rows, preferred_element_type=F32
    )
    router_part = router_part[:expert_count] + router_part[expert_count : 2 * expert_count]
    router_part = lax.dynamic_slice_in_dim(
        jnp.concatenate([router_part, router_part], 0),
        jnp.bitwise_and(expert_count - base, expert_count - 1),
        expert_count,
        0,
    )
    mean_router = jnp.einsum("te,td->ed", mean_part, normed_two, preferred_element_type=F32)
    router_part = router_part + mean_router[:expert_count] + mean_router[expert_count:]

    small = jnp.concatenate(
        [
            router_part,
            grad_second_part[None],
            jnp.full((1, model_width), squared_local),
        ],
        0,
    )
    small = small + swap_core(small)
    small = small + swap_y(small)
    small = jnp.pad(small, ((0, 128 - small.shape[0]), (0, 0))).reshape(8, 16, model_width)

    grad_attn = gather_tensor(grad_attn, core, row)
    out_near, out_far = fold_pairs(out_keep, swap_core(out_send), grad_attn)
    out_across = swap_y(out_far)
    grad_output = jnp.einsum("tc,td->cd", attended, grad_attn, preferred_element_type=F32)
    grad_attended = jnp.einsum("td,cd->tc", grad_attn, output_weight, preferred_element_type=F32)
    grad_attended = grad_attended.astype(BF16).reshape(row_count, local_kv, group, HEAD_DIM)
    attn_probs = jnp.exp(masked_scores() - row_peak) / row_total
    grad_probs = jnp.einsum("qhgd,khd->hgqk", grad_attended, value_low, preferred_element_type=F32)
    grad_scores = attn_probs * (grad_probs - jnp.sum(attn_probs * grad_probs, -1, keepdims=True))
    grad_scores = grad_scores.astype(BF16)
    grad_query_rot = ATTN_SCALE * jnp.einsum(
        "hgqk,khd->qhgd", grad_scores, keys_rot, preferred_element_type=F32
    )
    grad_keys_rot = ATTN_SCALE * jnp.einsum(
        "hgqk,qhgd->khd", grad_scores, query_block, preferred_element_type=F32
    )
    grad_values = jnp.einsum(
        "hgqk,qhgd->khd", attn_probs.astype(BF16), grad_attended, preferred_element_type=F32
    )
    grad_query_low = unrotate(
        grad_query_rot.reshape(row_count, local_query, HEAD_DIM), cosine, sine
    )
    grad_query_low = grad_query_low.reshape(row_count, local_query * HEAD_DIM).astype(BF16)
    grad_keys_low = unrotate(grad_keys_rot, cosine, sine)
    grad_keys_low = grad_keys_low.reshape(row_count, local_kv * HEAD_DIM).astype(BF16)
    grad_values_low = grad_values.reshape(row_count, local_kv * HEAD_DIM).astype(BF16)
    out_back = trade((out_near + out_across.astype(F32)).astype(BF16), 4)
    grad_qkv = join_columns(grad_query_low, grad_keys_low, grad_values_low, out_across)
    weights_qkv = jnp.concatenate([query_weight, key_matrix, value_matrix], 1)
    grad_weights = jnp.einsum("td,tc->dc", first_normed, grad_qkv, preferred_element_type=F32)
    grad_one_part = jnp.einsum("tc,dc->td", grad_qkv, weights_qkv, preferred_element_type=F32)
    gain_part = jnp.sum(grad_one_part * unit_one, 0).reshape(2, -1)
    gain_part = jnp.pad(gain_part, ((0, 126), (0, 0))).reshape(8, 16, -1)
    grad_one = scatter_tensor(grad_one_part, core, row)
    own_out_near, own_out_far = fold_pairs(own_out_keep, swap_core(own_out_send), grad_qkv)
    own_in_near, own_in_far = fold_pairs(own_in_keep, swap_core(own_in_send), grad_one)
    own_out_across = swap_y(own_out_far)
    own_in_across = swap_y(own_in_far)

    scale_mine = lax.rsqrt(jnp.mean(tokens_mine * tokens_mine, -1, keepdims=True) + EPS)
    unit_mine = tokens_mine * scale_mine
    grad_unit_one = grad_one * first_gain
    grad_tokens = grad_hidden + scale_mine * (
        grad_unit_one - unit_mine * jnp.mean(grad_unit_one * unit_mine, -1, keepdims=True)
    )
    grad_tokens = gather_tensor(grad_tokens.astype(BF16), core, row).astype(F32)
    grad_output = jnp.concatenate([grad_output.reshape(8, -1, model_width), small], 1)
    grad_output = sum_experts(grad_output, place)
    small = grad_output[:, -16:].reshape(128, model_width)
    grad_output = grad_output[:, :-16].reshape(-1, model_width)
    grad_weights = jnp.concatenate(
        [grad_weights.reshape(8, -1, grad_weights.shape[1]), gain_part], 1
    )
    grad_weights = sum_experts(grad_weights, place)
    gain_part = grad_weights[0, -16:-14]
    gain_part = gain_part + swap_core(gain_part)
    grad_first_gain = (gain_part + swap_y(gain_part)).reshape(-1)
    grad_weights = grad_weights[:, :-16].reshape(model_width, -1)
    query_columns = query_weight.shape[1]
    key_columns = query_columns + key_matrix.shape[1]
    grad_expert_out = ordered(
        half_index, own_out_near + own_out_across.astype(F32), out_back.astype(F32)
    )
    grad_expert_in = ordered(
        half_index, own_in_near + own_in_across.astype(F32), in_back.astype(F32)
    )
    return (
        layer_output,
        small[expert_count + 1, 0] / (2.0 * model_width * valid_total),
        grad_tokens,
        grad_first_gain,
        grad_weights[:, :query_columns],
        grad_weights[:, query_columns:key_columns],
        grad_weights[:, key_columns:],
        grad_output,
        small[expert_count],
        small[:expert_count].T,
        grad_expert_in,
        grad_expert_out,
    )


def solution(mesh):
    return jax.shard_map(
        per_device,
        mesh=mesh,
        in_specs=(
            P("expert", None),
            P("expert", None),
            P("expert"),
            P("expert", None),
            P(),
            P(None, "tensor"),
            P(None, "tensor"),
            P(None, "tensor"),
            P("tensor", None),
            P(),
            P(),
            P("expert", None, None, "tensor"),
            P("expert", "tensor", None),
        ),
        out_specs=(
            P("expert", None),
            P(),
            P("expert", None),
            P(),
            P(None, "tensor"),
            P(None, "tensor"),
            P(None, "tensor"),
            P("tensor", None),
            P(),
            P(),
            P("expert", None, None, "tensor"),
            P("expert", "tensor", None),
        ),
        check_vma=False,
    )
```

```python
import jax
import jax.numpy as jnp
from jax import lax
from jax.experimental import pallas as pl
from jax.experimental.pallas import tpu as pltpu
from jax.sharding import PartitionSpec as P

HEAD_DIM = 64
TOP = 8
BLOCK = 256


EPS = 1e-06
ATTN_SCALE = 0.015625
RESIDUAL = 0.22
THETA = 10000.0


def shifted(value, axis, steps):
    count = lax.axis_size(axis)
    pairs = [(source, (source + steps) % count) for source in range(count)]
    return lax.ppermute(value, axis, pairs)


def rope_tables(length, head_size):
    half_size = head_size // 2
    frequency = THETA ** (-(jnp.arange(half_size, dtype=jnp.float32) * 2.0) / head_size)
    angle_table = jnp.arange(length, dtype=jnp.float32)[:, None] * frequency[None, :]
    return (jnp.cos(angle_table)[:, None, :], jnp.sin(angle_table)[:, None, :])


def apply_rotary(values, cosine_lookup, sine_lookup):
    half_size = values.shape[-1] // 2
    lower_half, upper_half = (values[..., :half_size], values[..., half_size:])
    return jnp.concatenate(
        [
            lower_half * cosine_lookup - upper_half * sine_lookup,
            upper_half * cosine_lookup + lower_half * sine_lookup,
        ],
        -1,
    )


def unrotate(grads, cosine_lookup, sine_lookup):
    half_size = grads.shape[-1] // 2
    lower_half, upper_half = (grads[..., :half_size], grads[..., half_size:])
    return jnp.concatenate(
        [
            lower_half * cosine_lookup + upper_half * sine_lookup,
            upper_half * cosine_lookup - lower_half * sine_lookup,
        ],
        -1,
    )


def normalize(values):
    row_peak = jnp.max(values, -1, keepdims=True)
    exp_scores = jnp.exp(values - row_peak)
    return exp_scores / jnp.sum(exp_scores, -1, keepdims=True)


def slot_tables(route_ids, expert_count, capacity):
    row_count, top_count = route_ids.shape
    onehot = route_ids[:, :, None] == jnp.arange(expert_count, dtype=jnp.int32)[None, None, :]
    hit_count = jnp.sum(onehot.astype(jnp.int32), 1)
    slot_place = jnp.cumsum(hit_count, 0) - 1
    within = jnp.take_along_axis(slot_place, route_ids, 1)
    dest_slot = route_ids * capacity + within
    pair_count = row_count * top_count
    source = (
        jnp.full((expert_count * capacity,), pair_count, jnp.int32)
        .at[dest_slot.reshape(-1)]
        .set(jnp.arange(pair_count, dtype=jnp.int32))
    )
    live_slot = source < pair_count
    token_row = jnp.minimum(source, pair_count - 1) // top_count
    return (onehot, dest_slot, source, live_slot, token_row)


def general_device(
    tokens,
    teacher,
    valid_mask,
    routes,
    first_gain,
    query_weight,
    key_matrix,
    value_matrix,
    output_weight,
    second_gain,
    router_weight,
    expert_in,
    expert_out,
):
    row_count = tokens.shape[0]
    model_width = tokens.shape[1]
    half_width = model_width // 2
    local_query = query_weight.shape[1] // HEAD_DIM
    local_kv = key_matrix.shape[1] // HEAD_DIM
    query_group_size = local_query // local_kv
    expert_count = router_weight.shape[1]
    row_local = expert_in.shape[0]
    senders = lax.axis_size("expert")
    partner_step = senders // 2
    capacity = 3 * row_count * TOP // (2 * expert_count)
    pair_count = row_count * TOP
    score_rows = min(512, row_count)
    valid_total = lax.psum(jnp.sum(valid_mask).astype(jnp.float32), "expert")
    tokens_f32 = tokens.astype(jnp.float32)
    scale_one = lax.rsqrt(jnp.mean(tokens_f32 * tokens_f32, -1, keepdims=True) + EPS)
    unit_one = tokens_f32 * scale_one
    first_normed = (unit_one * first_gain).astype(jnp.bfloat16)
    cosine_lookup, sine_lookup = rope_tables(row_count, HEAD_DIM)
    query_linear = jnp.dot(first_normed, query_weight, preferred_element_type=jnp.float32).reshape(
        row_count, local_query, HEAD_DIM
    )
    keys_linear = jnp.dot(first_normed, key_matrix, preferred_element_type=jnp.float32).reshape(
        row_count, local_kv, HEAD_DIM
    )
    value_low = jnp.dot(first_normed, value_matrix, preferred_element_type=jnp.float32).astype(
        jnp.bfloat16
    )
    value_low = value_low.reshape(row_count, local_kv, HEAD_DIM)
    query_rotated = apply_rotary(query_linear, cosine_lookup, sine_lookup).astype(jnp.bfloat16)
    keys_rot = apply_rotary(keys_linear, cosine_lookup, sine_lookup).astype(jnp.bfloat16)
    block_of = jnp.arange(row_count, dtype=jnp.int32) // BLOCK

    def scores(start_row):
        stop_row = start_row + score_rows
        query_block = query_rotated.reshape(score_rows, local_kv, query_group_size, HEAD_DIM)
        score_block = (
            jnp.einsum("qhgd,khd->hgqk", query_block, keys_rot, preferred_element_type=jnp.float32)
            * ATTN_SCALE
        )
        allowed = block_of[None, :stop_row] <= block_of[start_row:stop_row, None]
        return (query_block, jnp.where(allowed, score_block, -1e30))

    attn_parts, row_peaks, row_totals = ([], [], [])
    start_row = 0
    query_block, score_block = scores(start_row)
    row_peak = jnp.max(score_block, -1, keepdims=True)
    exp_scores = jnp.exp(score_block - row_peak)
    row_total = jnp.sum(exp_scores, -1, keepdims=True)
    attn_probs = (exp_scores / row_total).astype(jnp.bfloat16)
    attn_parts.append(
        jnp.einsum("hgqk,khd->qhgd", attn_probs, value_low, preferred_element_type=jnp.float32)
    )
    row_peaks.append(row_peak)
    row_totals.append(row_total)
    attended = attn_parts[0].reshape(row_count, local_query * HEAD_DIM).astype(jnp.bfloat16)
    attn_part = jnp.dot(attended, output_weight, preferred_element_type=jnp.float32)
    attn_sum = lax.psum(attn_part, "tensor")
    hidden_state = tokens_f32 + RESIDUAL * attn_sum
    scale_two = lax.rsqrt(jnp.mean(hidden_state * hidden_state, -1, keepdims=True) + EPS)
    unit_two = hidden_state * scale_two
    normed_two = (unit_two * second_gain).astype(jnp.bfloat16)
    router_logits = jnp.dot(normed_two, router_weight, preferred_element_type=jnp.float32)
    onehot, dest_slot, source, live_slot, token_row = slot_tables(routes, expert_count, capacity)
    picked = jnp.sum(jnp.where(onehot, router_logits[:, None, :], 0.0), -1)
    gate_probs = normalize(picked)

    def slot_rows(slot_values):
        split_rows = slot_values.reshape(expert_count, capacity, 2, half_width).transpose(
            2, 0, 1, 3
        )
        return split_rows.reshape(senders, row_local, capacity, half_width)

    def slot_columns(returned, width):
        joined = returned.reshape(2, expert_count, capacity, width).transpose(1, 2, 0, 3)
        return joined.reshape(expert_count * capacity, 2, width)

    send_rows = slot_rows(
        jnp.where(live_slot[:, None], normed_two[token_row], jnp.zeros((), jnp.bfloat16))
    )
    received = lax.all_to_all(send_rows, "expert", split_axis=0, concat_axis=2, tiled=True)
    expert_rows = received.reshape(row_local, senders * capacity, half_width)
    gate_up_part = jnp.einsum(
        "rmd,rcdf->rmcf", expert_rows, expert_in, preferred_element_type=jnp.float32
    )
    gate_up_pre = gate_up_part + shifted(gate_up_part, "expert", partner_step)
    gate_pre = gate_up_pre[:, :, 0]
    up_pre = gate_up_pre[:, :, 1]
    inner_act = (jax.nn.silu(gate_pre) * up_pre).astype(jnp.bfloat16)
    expert_result = jnp.einsum(
        "rmf,rfd->rmd", inner_act, expert_out, preferred_element_type=jnp.float32
    )
    expert_result = expert_result.astype(jnp.bfloat16).reshape(
        row_local, senders, capacity, half_width
    )
    returned = lax.all_to_all(expert_result, "expert", split_axis=1, concat_axis=0, tiled=True)
    per_route = slot_columns(returned, half_width).reshape(expert_count * capacity, model_width)[
        dest_slot
    ]
    moe_part = jnp.sum(gate_probs[:, :, None] * per_route, 1)
    moe_sum = lax.psum(moe_part, "tensor")
    output = hidden_state + RESIDUAL * moe_sum
    residual_err = output - teacher.astype(jnp.float32)
    valid_rows = valid_mask.astype(jnp.float32)
    squared_local = jnp.sum(valid_rows * jnp.sum(residual_err * residual_err, -1))
    token_total = senders * row_count
    grad_out = token_total / valid_total * valid_rows[:, None] * residual_err
    grad_moe = (RESIDUAL * grad_out).astype(jnp.bfloat16)
    gate_part = jnp.einsum("td,tkd->tk", grad_moe, per_route, preferred_element_type=jnp.float32)
    gate_slot = gate_probs.reshape(pair_count)[jnp.minimum(source, pair_count - 1)]
    grad_slots = jnp.where(live_slot[:, None], gate_slot[:, None] * grad_moe[token_row], 0.0)
    grad_received = lax.all_to_all(
        slot_rows(grad_slots.astype(jnp.bfloat16)),
        "expert",
        split_axis=0,
        concat_axis=2,
        tiled=True,
    )
    grad_expert = grad_received.reshape(row_local, senders * capacity, half_width)
    grad_inner_part = jnp.einsum(
        "rmd,rfd->rmf", grad_expert, expert_out, preferred_element_type=jnp.float32
    )
    grad_inner = grad_inner_part + shifted(grad_inner_part, "expert", partner_step)
    grad_expert_out = jnp.einsum(
        "rmf,rmd->rfd", inner_act, grad_expert, preferred_element_type=jnp.float32
    )
    sigmoid_gate = jax.nn.sigmoid(gate_pre)
    grad_gate = grad_inner * up_pre * sigmoid_gate * (1.0 + gate_pre * (1.0 - sigmoid_gate))
    grad_up = grad_inner * (gate_pre * sigmoid_gate)
    grad_pre = jnp.stack([grad_gate, grad_up], 2).astype(jnp.bfloat16)
    grad_expert_in = jnp.einsum(
        "rmd,rmcf->rcdf", expert_rows, grad_pre, preferred_element_type=jnp.float32
    )
    grad_slot_rows = jnp.einsum(
        "rmcf,rcdf->rmd", grad_pre, expert_in, preferred_element_type=jnp.float32
    )
    grad_slot_rows = grad_slot_rows.astype(jnp.bfloat16).reshape(
        row_local, senders, capacity, half_width
    )
    grad_back = lax.all_to_all(grad_slot_rows, "expert", split_axis=1, concat_axis=0, tiled=True)
    grad_back = slot_columns(grad_back, half_width).reshape(expert_count * capacity, model_width)
    grad_two_part = jnp.sum(grad_back[dest_slot].astype(jnp.float32), 1)
    grad_two_experts, grad_gates = lax.psum((grad_two_part, gate_part), "tensor")
    grad_picked = gate_probs * (grad_gates - jnp.sum(gate_probs * grad_gates, -1, keepdims=True))
    grad_logits = jnp.sum(jnp.where(onehot, grad_picked[:, :, None], 0.0), 1).astype(jnp.bfloat16)
    grad_router = jnp.einsum(
        "td,te->de", normed_two, grad_logits, preferred_element_type=jnp.float32
    )
    grad_two = grad_two_experts + jnp.einsum(
        "te,de->td", grad_logits, router_weight, preferred_element_type=jnp.float32
    )
    grad_second_gain = jnp.sum(grad_two * unit_two, 0)
    grad_unit_two = grad_two * second_gain
    grad_hidden = grad_out + scale_two * (
        grad_unit_two - unit_two * jnp.mean(grad_unit_two * unit_two, -1, keepdims=True)
    )
    grad_attn = (RESIDUAL * grad_hidden).astype(jnp.bfloat16)
    grad_output = jnp.einsum("tc,td->cd", attended, grad_attn, preferred_element_type=jnp.float32)
    grad_attended = jnp.einsum(
        "td,cd->tc", grad_attn, output_weight, preferred_element_type=jnp.float32
    )
    grad_attended = grad_attended.astype(jnp.bfloat16).reshape(
        row_count, local_kv, query_group_size, HEAD_DIM
    )
    grad_query_parts = []
    grad_keys = jnp.zeros((row_count, local_kv, HEAD_DIM), jnp.float32)
    grad_values = jnp.zeros((row_count, local_kv, HEAD_DIM), jnp.float32)
    for block_index, start_row in enumerate(range(0, row_count, score_rows)):
        stop_row = start_row + score_rows
        query_block, score_block = scores(start_row)
        attn_probs = jnp.exp(score_block - row_peaks[block_index]) / row_totals[block_index]
        probs_low = attn_probs.astype(jnp.bfloat16)
        grad_probs = jnp.einsum(
            "qhgd,khd->hgqk", grad_attended, value_low, preferred_element_type=jnp.float32
        )
        grad_scores = attn_probs * (
            grad_probs - jnp.sum(attn_probs * grad_probs, -1, keepdims=True)
        )
        grad_scores = grad_scores.astype(jnp.bfloat16)
        grad_query_parts.append(
            ATTN_SCALE
            * jnp.einsum(
                "hgqk,khd->qhgd", grad_scores, keys_rot, preferred_element_type=jnp.float32
            )
        )
        grad_keys = grad_keys.at[:stop_row].add(
            ATTN_SCALE
            * jnp.einsum(
                "hgqk,qhgd->khd", grad_scores, query_block, preferred_element_type=jnp.float32
            )
        )
        grad_values = grad_values.at[:stop_row].add(
            jnp.einsum(
                "hgqk,qhgd->khd", probs_low, grad_attended, preferred_element_type=jnp.float32
            )
        )
    grad_query_rot = grad_query_parts[0].reshape(row_count, local_query, HEAD_DIM)
    grad_query_low = unrotate(grad_query_rot, cosine_lookup, sine_lookup).reshape(
        row_count, local_query * HEAD_DIM
    )
    grad_query_low = grad_query_low.astype(jnp.bfloat16)
    grad_keys_low = unrotate(grad_keys, cosine_lookup, sine_lookup).reshape(
        row_count, local_kv * HEAD_DIM
    )
    grad_keys_low = grad_keys_low.astype(jnp.bfloat16)
    grad_values_low = grad_values.reshape(row_count, local_kv * HEAD_DIM).astype(jnp.bfloat16)
    grad_query = jnp.einsum(
        "td,tc->dc", first_normed, grad_query_low, preferred_element_type=jnp.float32
    )
    grad_key = jnp.einsum(
        "td,tc->dc", first_normed, grad_keys_low, preferred_element_type=jnp.float32
    )
    grad_value = jnp.einsum(
        "td,tc->dc", first_normed, grad_values_low, preferred_element_type=jnp.float32
    )
    grad_one_part = (
        jnp.einsum("tc,dc->td", grad_query_low, query_weight, preferred_element_type=jnp.float32)
        + jnp.einsum("tc,dc->td", grad_keys_low, key_matrix, preferred_element_type=jnp.float32)
        + jnp.einsum("tc,dc->td", grad_values_low, value_matrix, preferred_element_type=jnp.float32)
    )
    grad_one = lax.psum(grad_one_part.astype(jnp.bfloat16), "tensor").astype(jnp.float32)
    grad_first_gain = jnp.sum(grad_one * unit_one, 0)
    grad_unit_one = grad_one * first_gain
    grad_tokens = grad_hidden + scale_one * (
        grad_unit_one - unit_one * jnp.mean(grad_unit_one * unit_one, -1, keepdims=True)
    )
    reduced = lax.psum(
        (
            grad_first_gain,
            grad_query,
            grad_key,
            grad_value,
            grad_output,
            grad_second_gain,
            grad_router,
            squared_local,
        ),
        "expert",
    )
    loss_value = reduced[7] / (2.0 * model_width * valid_total)
    return (
        output.astype(jnp.bfloat16),
        loss_value,
        grad_tokens,
        reduced[0],
        reduced[1],
        reduced[2],
        reduced[3],
        reduced[4],
        reduced[5],
        reduced[6],
        grad_expert_in,
        grad_expert_out,
    )


BF16 = jnp.bfloat16
F32 = jnp.float32
CHUNK = 256
SHARE = 128
PACK = 12 * SHARE
NT = (((1,), (1,)), ((), ()))
ORDER = (0, 2, 4, 6, 1, 3, 5, 7)


def whole_block(shape):
    return pl.BlockSpec(shape, lambda e, *_: (0,) * len(shape))


def any_block():
    return pl.BlockSpec(memory_space=pl.ANY)


def pack_body(half_ref, own_in, own_out, other_in, other_out, *refs):
    own, near, far = refs[-3:]
    step = pl.program_id(0)

    def fill(target, source_in, source_out):
        for c in range(2):
            target[c * 4 * SHARE : (c + 1) * 4 * SHARE, :] = source_in[0, c]
        for k in range(4):
            target[(8 + k) * SHARE : (9 + k) * SHARE, :] = source_out[
                0, :, k * SHARE : (k + 1) * SHARE
            ]

    fill(own, own_in, own_out)

    @pl.when(step < 2)
    def _():
        fill(near, other_in, other_out)

    @pl.when(step >= 2)
    def _():
        fill(far, other_in, other_out)


def pack_weights(half_index, expert_in, expert_out, *after):
    held = expert_in.shape[0] // 2
    in_shape = (1,) + expert_in.shape[1:]
    out_shape = (1,) + expert_out.shape[1:]
    shapes = [(held * PACK, SHARE), (held // 2 * PACK, SHARE), (held // 2 * PACK, SHARE)]
    block = (PACK, SHARE)
    return pl.pallas_call(
        pack_body,
        grid_spec=pltpu.PrefetchScalarGridSpec(
            num_scalar_prefetch=1,
            grid=(held,),
            in_specs=[
                pl.BlockSpec(in_shape, lambda e, half: (half[0] * held + e, 0, 0, 0)),
                pl.BlockSpec(out_shape, lambda e, half: (half[0] * held + e, 0, 0)),
                pl.BlockSpec(in_shape, lambda e, half: ((1 - half[0]) * held + e, 0, 0, 0)),
                pl.BlockSpec(out_shape, lambda e, half: ((1 - half[0]) * held + e, 0, 0)),
            ]
            + [any_block()] * len(after),
            out_specs=[
                pl.BlockSpec(block, lambda e, half: (e, 0)),
                pl.BlockSpec(block, lambda e, half: (jnp.minimum(e, 1), 0)),
                pl.BlockSpec(block, lambda e, half: (jnp.maximum(e - 2, 0), 0)),
            ],
        ),
        out_shape=[jax.ShapeDtypeStruct(shape, BF16) for shape in shapes],
        name="pack_weights",
    )(half_index, expert_in, expert_out, expert_in, expert_out, *after)


def weight_copies(own, other, own_row, other_row, half, in_buf, out_buf, sems, slot):
    copies = []
    for q in range(4):
        for pack, row, side in ((own[q], own_row, half), (other[q], other_row, 1 - half)):
            for c in range(2):
                copies.append(
                    (
                        pack.at[pl.ds(pl.multiple_of(row + c * 4 * SHARE, SHARE), 4 * SHARE)],
                        in_buf.at[
                            slot,
                            pl.ds(pl.multiple_of(side * 4 * SHARE, SHARE), 4 * SHARE),
                            pl.ds((2 * q + c) * SHARE, SHARE),
                        ],
                    )
                )
            for k in range(4):
                copies.append(
                    (
                        pack.at[pl.ds(pl.multiple_of(row + (8 + k) * SHARE, SHARE), SHARE)],
                        out_buf.at[slot, side, pl.ds(q * SHARE, SHARE), pl.ds(k * SHARE, SHARE)],
                    )
                )
    return [
        pltpu.make_async_copy(source, target, sems.at[slot, n])
        for n, (source, target) in enumerate(copies)
    ]


def stream_weights(first, packs, half, in_buf, out_buf, sems):
    step = pl.program_id(0)
    slot = lax.rem(step, 2)
    own, near, far = (packs[0:4], packs[4:8], packs[8:12])

    def start(index, target):
        expert = first + index

        def begin(other, start_row):
            for copy in weight_copies(
                own, other, expert * PACK, start_row, half, in_buf, out_buf, sems, target
            ):
                copy.start()

        if not far:
            begin(near, index * PACK)
            return

        @pl.when(expert < 2)
        def _():
            begin(near, expert * PACK)

        @pl.when(expert >= 2)
        def _():
            begin(far, (expert - 2) * PACK)

    @pl.when(step == 0)
    def _():
        start(0, 0)

    @pl.when(step + 1 < pl.num_programs(0))
    def _():
        start(step + 1, 1 - slot)

    def wait():
        for copy in weight_copies(own, near, 0, 0, half, in_buf, out_buf, sems, slot):
            copy.wait()

    return (step, slot, wait)


def weight_scratch(width, hidden):
    return [
        pltpu.VMEM((2, width, 2 * hidden), BF16),
        pltpu.VMEM((2, 2, hidden, width // 2), BF16),
        pltpu.SemaphoreType.DMA((2, 48)),
    ]


def split_pairs(values):
    blocks = [values[:, i * SHARE : (i + 1) * SHARE] for i in range(values.shape[1] // SHARE)]
    return (jnp.concatenate(blocks[0::2], 1), jnp.concatenate(blocks[1::2], 1))


def join_pairs(first, second):
    blocks = []
    for i in range(first.shape[1] // SHARE):
        blocks.append(first[:, i * SHARE : (i + 1) * SHARE])
        blocks.append(second[:, i * SHARE : (i + 1) * SHARE])
    return jnp.concatenate(blocks, 1)


def chunk_loop(row_count, body):
    def step(i, carry):
        body(pl.ds(pl.multiple_of(i * CHUNK, CHUNK), CHUNK))
        return carry

    lax.fori_loop(0, row_count // CHUNK, step, 0)


def gate_column(gates, expert):
    lane = lax.broadcasted_iota(jnp.int32, gates.shape, 1)
    return jnp.sum(jnp.where(lane == expert, gates, 0.0), -1, keepdims=True)


def dense_gates(rows, ids, router):
    logits = jnp.dot(rows, router, preferred_element_type=F32)
    lane = lax.broadcasted_iota(jnp.int32, logits.shape, 1)
    mask = ids[:, 0:1] == lane
    for k in range(1, TOP):
        mask = mask | (ids[:, k : k + 1] == lane)
    masked = jnp.where(mask, logits, -1e30)
    powers = jnp.where(mask, jnp.exp(masked - jnp.max(masked, -1, keepdims=True)), 0.0)
    return powers / jnp.sum(powers, -1, keepdims=True)


def apply_expert(rows, expert, slot, rows_ref, gate_ref, pre_ref, gated_ref, in_buf):
    pre = jnp.dot(rows_ref[rows, :], in_buf[slot], preferred_element_type=F32)
    pre_ref[0, rows, :] = pre.astype(BF16)
    gate_pre, up_pre = split_pairs(pre)
    weight = gate_column(gate_ref[rows, :], expert)
    gated = (weight * (gate_pre * jax.nn.sigmoid(gate_pre) * up_pre)).astype(BF16)
    gated_ref[0, rows, :] = gated
    return gated


def forward_first(half_ref, *refs):
    shards = refs[:8]
    route_ref, router_ref = refs[8:10]
    packs = refs[10:18]
    acc, pre_ref, gated_ref, gate_ref, rows_ref, in_buf, out_buf, sems = refs[18:]
    step, slot, wait = stream_weights(0, packs, half_ref[0], in_buf, out_buf, sems)
    row_count, width = acc.shape
    size = row_count // 8

    @pl.when(step == 0)
    def _():
        for i in range(8):
            rows_ref[i * size : (i + 1) * size, :] = shards[i][...]
        acc[...] = jnp.zeros_like(acc)

        def gating(rows):
            gate_ref[rows, :] = dense_gates(rows_ref[rows, :], route_ref[rows, :], router_ref[...])

        chunk_loop(row_count, gating)

    wait()

    def mlp(rows):
        gated = apply_expert(rows, step, slot, rows_ref, gate_ref, pre_ref, gated_ref, in_buf)
        for side in range(2):
            columns = slice(side * width // 2, (side + 1) * width // 2)
            acc[rows, columns] += jnp.dot(gated, out_buf[slot, side], preferred_element_type=F32)

    chunk_loop(row_count, mlp)


def forward_second(half_ref, *refs):
    rows_ref, gate_ref, start_ref = refs[:3]
    packs = refs[3:11]
    keep_ref, near_ref, far_ref, pre_ref, gated_ref, acc, in_buf, out_buf, sems = refs[13:]
    step, slot, wait = stream_weights(2, packs, half_ref[0], in_buf, out_buf, sems)
    row_count, width = acc.shape

    wait()

    def mlp(rows, source):
        gated = apply_expert(rows, step + 2, slot, rows_ref, gate_ref, pre_ref, gated_ref, in_buf)
        for side in range(2):
            columns = slice(side * width // 2, (side + 1) * width // 2)
            acc[rows, columns] = source[rows, columns] + jnp.dot(
                gated, out_buf[slot, side], preferred_element_type=F32
            )

    @pl.when(step == 0)
    def _():
        chunk_loop(row_count, lambda rows: mlp(rows, start_ref))

    @pl.when(step > 0)
    def _():
        chunk_loop(row_count, lambda rows: mlp(rows, acc))

    @pl.when(step == pl.num_programs(0) - 1)
    def _():
        spread(acc, keep_ref, near_ref, far_ref)


def spread(acc, keep_ref, near_ref, far_ref):
    part = acc.shape[0] // 4
    keep_ref[...] = acc[: 2 * part, :]
    near_ref[...] = acc[2 * part : 3 * part, :].astype(BF16)
    far_ref[...] = acc[3 * part :, :].astype(BF16)


def spread_specs(row_count, width):
    shapes = [
        jax.ShapeDtypeStruct((row_count // 2, width), F32),
        jax.ShapeDtypeStruct((row_count // 4, width), BF16),
        jax.ShapeDtypeStruct((row_count // 4, width), BF16),
    ]
    return ([whole_block(s.shape) for s in shapes], shapes)


def expert_block(shape, first=0):
    return pl.BlockSpec((1,) + shape[1:], lambda e, *_: (e + first,) + (0,) * (len(shape) - 1))


def experts_forward(half_index, shards, route_ids, router, own, near, far):
    size, width = shards[0].shape
    row_count = 8 * size
    local = own[0].shape[0] // PACK
    hidden = 4 * SHARE
    sums = jax.ShapeDtypeStruct((row_count, width), F32)
    pre = jax.ShapeDtypeStruct((local, row_count, 2 * hidden), BF16)
    gated = jax.ShapeDtypeStruct((local, row_count, hidden), BF16)
    gates = jax.ShapeDtypeStruct((row_count, 128), F32)
    rows = jax.ShapeDtypeStruct((row_count, width), BF16)
    sums_a, pre_a, gated_a, gates, rows = pl.pallas_call(
        forward_first,
        grid_spec=pltpu.PrefetchScalarGridSpec(
            num_scalar_prefetch=1,
            grid=(2,),
            in_specs=[whole_block(v.shape) for v in (*shards, route_ids, router)]
            + [any_block()] * 8,
            out_specs=[
                whole_block(sums.shape),
                expert_block(pre.shape),
                expert_block(gated.shape),
                whole_block(gates.shape),
                whole_block(rows.shape),
            ],
            scratch_shapes=weight_scratch(width, hidden),
        ),
        out_shape=[sums, pre, gated, gates, rows],
        name="experts_forward_a",
    )(half_index, *shards, route_ids, router, *own, *near)
    specs, shapes = spread_specs(row_count, width)
    keep, send_near, send_far, pre, gated = pl.pallas_call(
        forward_second,
        grid_spec=pltpu.PrefetchScalarGridSpec(
            num_scalar_prefetch=1,
            grid=(2,),
            in_specs=[whole_block(v.shape) for v in (rows, gates, sums)] + [any_block()] * 10,
            out_specs=specs + [expert_block(pre.shape, 2), expert_block(gated.shape, 2)],
            scratch_shapes=[pltpu.VMEM((row_count, width), F32)] + weight_scratch(width, hidden),
        ),
        out_shape=shapes + [pre, gated],
        input_output_aliases={12: 3, 13: 4},
        name="experts_forward_b",
    )(half_index, rows, gates, sums_a, *own, *far, pre_a, gated_a)
    return (keep, send_near, send_far, pre, gated, gates, rows)


def backward_body(half_ref, *refs):
    shards = refs[:8]
    gate_ref, router_ref, pre_ref = refs[8:11]
    packs = refs[11:23]
    keep_ref, near_ref, far_ref, pre_grad_ref, logit_ref, grad_ref = refs[-10:-4]
    acc, in_buf, out_buf, sems = refs[-4:]
    step, slot, wait = stream_weights(0, packs, half_ref[0], in_buf, out_buf, sems)
    row_count, width = grad_ref.shape
    size = row_count // 8

    @pl.when(step == 0)
    def _():
        for i in range(8):
            grad_ref[i * size : (i + 1) * size, :] = shards[i][...]
        acc[...] = jnp.zeros_like(acc)
        logit_ref[...] = jnp.zeros_like(logit_ref)

    wait()

    def mlp(rows):
        plain = lax.dot_general(
            grad_ref[rows, : width // 2], out_buf[slot, 0], NT, preferred_element_type=F32
        ) + lax.dot_general(
            grad_ref[rows, width // 2 :], out_buf[slot, 1], NT, preferred_element_type=F32
        )
        gate_pre, up_pre = split_pairs(pre_ref[0, rows, :].astype(F32))
        weight = gate_column(gate_ref[rows, :], step)
        sigmoid = jax.nn.sigmoid(gate_pre)
        act = gate_pre * sigmoid
        grad_weight = jnp.sum(act * up_pre * plain, -1, keepdims=True)
        scaled = weight * plain
        pre_grad = join_pairs(
            scaled * up_pre * (sigmoid + act * (1.0 - sigmoid)), scaled * act
        ).astype(BF16)
        pre_grad_ref[0, rows, :] = pre_grad
        old = logit_ref[rows, :]
        lane = lax.broadcasted_iota(jnp.int32, old.shape, 1)
        value = weight * grad_weight
        high = value.astype(BF16).astype(F32)
        logit_ref[rows, :] = jnp.where(
            lane == step, high, jnp.where(lane == step + 32, value - high, old)
        )
        acc[rows, :] += lax.dot_general(pre_grad, in_buf[slot], NT, preferred_element_type=F32)

    chunk_loop(row_count, mlp)

    @pl.when(step == pl.num_programs(0) - 1)
    def _():
        def router(rows):
            acc[rows, :] += lax.dot_general(
                logit_ref[rows, :].astype(BF16), router_ref[...], NT, preferred_element_type=F32
            )

        chunk_loop(row_count, router)
        spread(acc, keep_ref, near_ref, far_ref)


def experts_backward(half_index, shards, gates, router, pre, own, near, far, *after):
    row_count, width = (8 * shards[0].shape[0], shards[0].shape[1])
    local = pre.shape[0]
    specs, shapes = spread_specs(row_count, width)
    return pl.pallas_call(
        backward_body,
        grid_spec=pltpu.PrefetchScalarGridSpec(
            num_scalar_prefetch=1,
            grid=(local,),
            in_specs=[whole_block(v.shape) for v in (*shards, gates, router)]
            + [expert_block(pre.shape)]
            + [any_block()] * (12 + len(after)),
            out_specs=specs
            + [
                expert_block(pre.shape),
                whole_block((row_count, 128)),
                whole_block((row_count, width)),
            ],
            scratch_shapes=[pltpu.VMEM((row_count, width), F32)]
            + weight_scratch(width, 4 * SHARE),
        ),
        out_shape=shapes
        + [
            jax.ShapeDtypeStruct(pre.shape, BF16),
            jax.ShapeDtypeStruct((row_count, 128), F32),
            jax.ShapeDtypeStruct((row_count, width), BF16),
        ],
        name="experts_backward",
    )(half_index, *shards, gates, router, pre, *own, *near, *far, *after)


def grad_out_body(half_ref, gated_ref, other_ref, mine_ref, *refs):
    outs = refs[-4:]
    turned = gated_ref[0].T
    for n, source in ((0, other_ref), (2, mine_ref)):
        product = jnp.dot(turned, source[...], preferred_element_type=F32).astype(BF16)
        for q in range(4):
            outs[n + q % 2][q // 2, 0] = product[q * SHARE : (q + 1) * SHARE, :]


def grad_expert_outs(half_index, gated, grads, *after):
    local, row_count, hidden = gated.shape
    width = grads.shape[1]
    half_spec = (row_count, width // 2)
    shape = (2, local, SHARE, width // 2)
    return pl.pallas_call(
        grad_out_body,
        grid_spec=pltpu.PrefetchScalarGridSpec(
            num_scalar_prefetch=1,
            grid=(local,),
            in_specs=[
                expert_block(gated.shape),
                pl.BlockSpec(half_spec, lambda e, half: (0, 1 - half[0])),
                pl.BlockSpec(half_spec, lambda e, half: (0, half[0])),
            ]
            + [any_block()] * len(after),
            out_specs=[pl.BlockSpec((2, 1) + shape[2:], lambda e, *_: (0, e, 0, 0))] * 4,
        ),
        out_shape=[jax.ShapeDtypeStruct(shape, BF16)] * 4,
        name="grad_expert_out",
    )(half_index, gated, grads, grads, *after)


def grad_in_body(half_ref, rows_ref, pre_ref, *refs):
    keep_ref, send_ref, turned = refs[-3:]

    @pl.when(pl.program_id(0) == 0)
    def _():
        turned[...] = rows_ref[...].T

    product = jnp.dot(turned[...], pre_ref[0], preferred_element_type=F32).astype(BF16)
    for q in range(4):
        for c in range(2):
            start = (2 * q + c) * SHARE
            (keep_ref, send_ref)[q % 2][q // 2, 0, c] = product[:, start : start + SHARE]


def grad_expert_ins(half_index, rows, pre_grad, first, count, *after):
    local, row_count, wide = pre_grad.shape
    width = rows.shape[1]
    shape = (2, count, 2, width // 2, SHARE)
    return pl.pallas_call(
        grad_in_body,
        grid_spec=pltpu.PrefetchScalarGridSpec(
            num_scalar_prefetch=1,
            grid=(count,),
            in_specs=[
                pl.BlockSpec((row_count, width // 2), lambda e, half: (0, half[0])),
                expert_block(pre_grad.shape, first),
            ]
            + [any_block()] * len(after),
            out_specs=[pl.BlockSpec((2, 1) + shape[2:], lambda e, *_: (0, e, 0, 0, 0))] * 2,
            scratch_shapes=[pltpu.VMEM((width // 2, row_count), BF16)],
        ),
        out_shape=[jax.ShapeDtypeStruct(shape, BF16)] * 2,
        name="grad_expert_in",
    )(half_index, rows, pre_grad, *after)


def fold_body(keep_ref, got_ref, *refs):
    near_ref, far_ref = refs[-2:]
    near_ref[...] = keep_ref[0].astype(F32) + got_ref[0].astype(F32)
    far_ref[...] = (keep_ref[1].astype(F32) + got_ref[1].astype(F32)).astype(BF16)


def fold_pairs(keep, got, *after):
    shape = keep.shape
    rest = (0,) * (len(shape) - 2)
    pair = pl.BlockSpec((2, 1) + shape[2:], lambda e: (0, e) + rest)
    single = pl.BlockSpec((1,) + shape[2:], lambda e: (e,) + rest)
    return pl.pallas_call(
        fold_body,
        grid=(shape[1],),
        in_specs=[pair, pair] + [any_block()] * len(after),
        out_specs=[single, single],
        out_shape=[
            jax.ShapeDtypeStruct(shape[1:], F32),
            jax.ShapeDtypeStruct(shape[1:], BF16),
        ],
        name="fold_pairs",
    )(keep, got, *after)


def finish_body(keep, near, two, four, six, extra, unit, scale, gain, grad_out, *refs):
    hidden_ref, attn_ref, gain_ref = refs[-3:]
    total = keep[...] + near[...].astype(F32) + extra[...]
    for part in (two, four, six):
        total = total + part[...].astype(F32)
    gain_ref[...] = jnp.sum((total * unit[...]).reshape(-1, 8, total.shape[1]), 0)
    weighted = total * gain[...]
    mean = jnp.mean(weighted * unit[...], -1, keepdims=True)
    hidden = grad_out[...] + scale[...] * (weighted - unit[...] * mean)
    hidden_ref[...] = hidden
    attn_ref[...] = (RESIDUAL * hidden).astype(BF16)


def finish_rows(keep, near, two, four, six, extra, unit, scale, gain, grad_out, *after):
    size, width = unit.shape
    block = pl.BlockSpec((size, width), lambda e: (0, 0))
    return pl.pallas_call(
        finish_body,
        grid=(1,),
        in_specs=[block] * 7
        + [whole_block((size, 1)), whole_block((1, width)), block]
        + [any_block()] * len(after),
        out_specs=[block, block, whole_block((8, width))],
        out_shape=[
            jax.ShapeDtypeStruct((size, width), F32),
            jax.ShapeDtypeStruct((size, width), BF16),
            jax.ShapeDtypeStruct((8, width), F32),
        ],
        name="finish_rows",
    )(keep, near, two, four, six, extra, unit, scale, gain, grad_out, *after)


def rotated(values, cosine, sine, sign):
    width = values.shape[1]
    lane = lax.broadcasted_iota(jnp.int32, values.shape, 1)
    lower = lax.rem(lane, HEAD_DIM) < HEAD_DIM // 2
    ahead = pltpu.roll(values, width - HEAD_DIM // 2, 1)
    behind = pltpu.roll(values, HEAD_DIM // 2, 1)
    turned = jnp.where(lower, -ahead, behind)
    repeat = width // cosine.shape[1]
    cosine = jnp.concatenate([cosine] * repeat, 1)
    sine = jnp.concatenate([sine] * repeat, 1)
    return values * cosine + sign * (turned * sine)


def head(values, index, start=0, stop=None):
    return values[start:stop, index * HEAD_DIM : (index + 1) * HEAD_DIM]


def probabilities(query, keys):
    scores = lax.dot_general(query, keys, NT, preferred_element_type=F32) * ATTN_SCALE
    powers = jnp.exp(scores - jnp.max(scores, -1, keepdims=True))
    return powers / jnp.sum(powers, -1, keepdims=True)


def attention_forward_body(
    core_ref, tokens, gain, query_w, key_w, value_w, output_w, cosine, sine, *refs
):
    normed, query, keys, values, attended, keep, send = refs[-7:]
    x = tokens[...].astype(F32)
    scale = lax.rsqrt(jnp.mean(x * x, -1, keepdims=True) + EPS)
    normed[...] = (x * scale * gain[...]).astype(BF16)
    low = normed[...]
    linear = jnp.dot(low, query_w[...], preferred_element_type=F32)
    query[...] = rotated(linear, cosine[...], sine[...], 1.0).astype(BF16)
    linear = jnp.dot(low, key_w[...], preferred_element_type=F32)
    keys[...] = rotated(linear, cosine[...], sine[...], 1.0).astype(BF16)
    values[...] = jnp.dot(low, value_w[...], preferred_element_type=F32).astype(BF16)
    group = query.shape[1] // keys.shape[1]
    for start in range(0, tokens.shape[0], BLOCK):
        stop = start + BLOCK
        parts = []
        for h in range(query.shape[1] // HEAD_DIM):
            probs = probabilities(head(query, h, start, stop), head(keys, h // group, 0, stop))
            parts.append(
                jnp.dot(
                    probs.astype(BF16),
                    head(values, h // group, 0, stop),
                    preferred_element_type=F32,
                )
            )
        attended[start:stop, :] = jnp.concatenate(parts, 1).astype(BF16)
    size = tokens.shape[0] // 4
    for r in range(2):
        for target, core in ((keep, core_ref[0]), (send, 1 - core_ref[0])):
            rows = pl.ds(pl.multiple_of((2 * r + core) * size, size), size)
            part = jnp.dot(attended[rows, :], output_w[...], preferred_element_type=F32)
            target[r] = part.astype(target.dtype)


def scalar_call(body, name, scalar, inputs, shapes, after=(), scratch=()):
    return pl.pallas_call(
        body,
        grid_spec=pltpu.PrefetchScalarGridSpec(
            num_scalar_prefetch=1,
            grid=(1,),
            in_specs=[whole_block(v.shape) for v in inputs] + [any_block()] * len(after),
            out_specs=[whole_block(s.shape) for s in shapes],
            scratch_shapes=list(scratch),
        ),
        out_shape=shapes,
        name=name,
    )(scalar, *inputs, *after)


def attention_forward(core, tokens, gain, query_w, key_w, value_w, output_w, tables, *after):
    rows, width = tokens.shape
    shapes = [
        jax.ShapeDtypeStruct((rows, width), BF16),
        jax.ShapeDtypeStruct((rows, query_w.shape[1]), BF16),
        jax.ShapeDtypeStruct((rows, key_w.shape[1]), BF16),
        jax.ShapeDtypeStruct((rows, value_w.shape[1]), BF16),
        jax.ShapeDtypeStruct((rows, query_w.shape[1]), BF16),
        jax.ShapeDtypeStruct((2, rows // 4, width), F32),
        jax.ShapeDtypeStruct((2, rows // 4, width), BF16),
    ]
    inputs = (tokens, gain, query_w, key_w, value_w, output_w, *tables)
    return scalar_call(
        attention_forward_body, "attention_forward", core, inputs, shapes, after
    )


TN = (((0,), (0,)), ((), ()))


def attention_backward_body(
    share_ref,
    tokens,
    query_w,
    key_w,
    value_w,
    output_w,
    cosine,
    sine,
    query,
    keys,
    values,
    first,
    second,
    third,
    fourth,
    *refs,
):
    grad, grad_qkv, gain, keep, send, grad_keys, grad_values = refs[-7:]
    share = share_ref[0]
    size = first.shape[0]
    for r, piece in enumerate((first, second, third, fourth)):
        place = jnp.bitwise_xor(share, r) * size
        grad[pl.ds(pl.multiple_of(place, size), size), :] = piece[...]
    back = lax.dot_general(grad[...], output_w[...], NT, preferred_element_type=F32).astype(BF16)
    wide, narrow = (query.shape[1], keys.shape[1])
    group = wide // narrow
    grad_keys[...] = jnp.zeros_like(grad_keys)
    grad_values[...] = jnp.zeros_like(grad_values)
    for start in range(0, tokens.shape[0], BLOCK):
        stop = start + BLOCK
        parts, key_parts, value_parts = ([], [], [])
        for kv in range(narrow // HEAD_DIM):
            key, value = (head(keys, kv, 0, stop), head(values, kv, 0, stop))
            key_sum, value_sum = (0.0, 0.0)
            for h in range(kv * group, (kv + 1) * group):
                query_h = head(query, h, start, stop)
                back_h = head(back, h, start, stop)
                probs = probabilities(query_h, key)
                inner = lax.dot_general(back_h, value, NT, preferred_element_type=F32)
                scores = probs * (inner - jnp.sum(probs * inner, -1, keepdims=True))
                scores = scores.astype(BF16)
                parts.append(ATTN_SCALE * jnp.dot(scores, key, preferred_element_type=F32))
                key_sum += lax.dot_general(scores, query_h, TN, preferred_element_type=F32)
                value_sum += lax.dot_general(
                    probs.astype(BF16), back_h, TN, preferred_element_type=F32
                )
            key_parts.append(ATTN_SCALE * key_sum)
            value_parts.append(value_sum)
        turned = rotated(
            jnp.concatenate(parts, 1), cosine[start:stop, :], sine[start:stop, :], -1.0
        )
        grad_qkv[start:stop, :wide] = turned.astype(BF16)
        grad_keys[:stop, :] += jnp.concatenate(key_parts, 1)
        grad_values[:stop, :] += jnp.concatenate(value_parts, 1)
    turned = rotated(grad_keys[...], cosine[...], sine[...], -1.0)
    grad_qkv[:, wide : wide + narrow] = turned.astype(BF16)
    grad_qkv[:, wide + narrow :] = grad_values[...].astype(BF16)
    total = jnp.zeros(gain.shape, F32)
    for r in range(2):
        for target, core in ((keep, share % 2), (send, 1 - share % 2)):
            rows = pl.ds(pl.multiple_of((2 * r + core) * size, size), size)
            part = lax.dot_general(
                grad_qkv[rows, :wide], query_w[...], NT, preferred_element_type=F32
            )
            part += lax.dot_general(
                grad_qkv[rows, wide : wide + narrow], key_w[...], NT, preferred_element_type=F32
            )
            part += lax.dot_general(
                grad_qkv[rows, wide + narrow :], value_w[...], NT, preferred_element_type=F32
            )
            target[r] = part.astype(target.dtype)
            x = tokens[rows, :].astype(F32)
            x = x * lax.rsqrt(jnp.mean(x * x, -1, keepdims=True) + EPS)
            total += jnp.sum((part * x).reshape(-1, 8, x.shape[1]), 0)
    gain[...] = total


def attention_backward(share, tokens, weights, tables, saved, pieces, *after):
    rows, width = tokens.shape
    narrow = saved[1].shape[1]
    shapes = [
        jax.ShapeDtypeStruct((rows, width), BF16),
        jax.ShapeDtypeStruct((rows, saved[0].shape[1] + 2 * narrow), BF16),
        jax.ShapeDtypeStruct((8, width), F32),
        jax.ShapeDtypeStruct((2, rows // 4, width), F32),
        jax.ShapeDtypeStruct((2, rows // 4, width), BF16),
    ]
    return scalar_call(
        attention_backward_body,
        "attention_backward",
        share,
        (tokens, *weights, *tables, *saved, *pieces),
        shapes,
        after,
        [pltpu.VMEM((rows, narrow), F32), pltpu.VMEM((rows, narrow), F32)],
    )


def reduce_body(place_ref, normed, grad_qkv, grad, attended, small, *refs):
    keep, near, far = refs[-3:]
    step = pl.program_id(0)
    first = lax.dot_general(normed[...], grad_qkv[...], TN, preferred_element_type=F32)
    second = lax.dot_general(grad[...], attended[...], TN, preferred_element_type=F32)
    part = jnp.concatenate([first, second, small[...]], 1)

    @pl.when(step < 4)
    def _():
        keep[...] = part

    @pl.when((step == 4) | (step == 5))
    def _():
        near[...] = part.astype(BF16)

    @pl.when(step >= 6)
    def _():
        far[...] = part.astype(BF16)


def reduce_parts(place, normed, grad_qkv, grad, attended, small, *after):
    rows, width = normed.shape
    size = width // 8
    total = grad_qkv.shape[1] + attended.shape[1] + small.shape[1]

    def shard(e, place):
        order = jnp.where(e < 4, 2 * e, 2 * e - 7)
        return jnp.bitwise_xor(place[0], order)

    columns = pl.BlockSpec((rows, size), lambda e, place: (0, shard(e, place)))
    return pl.pallas_call(
        reduce_body,
        grid_spec=pltpu.PrefetchScalarGridSpec(
            num_scalar_prefetch=1,
            grid=(8,),
            in_specs=[
                columns,
                whole_block(grad_qkv.shape),
                columns,
                whole_block(attended.shape),
                pl.BlockSpec((size, small.shape[1]), lambda e, place: (shard(e, place), 0)),
            ]
            + [any_block()] * len(after),
            out_specs=[
                pl.BlockSpec((size, total), lambda e, _: (jnp.minimum(e, 3), 0)),
                pl.BlockSpec((size, total), lambda e, _: (jnp.clip(e - 4, 0, 1), 0)),
                pl.BlockSpec((size, total), lambda e, _: (jnp.clip(e - 6, 0, 1), 0)),
            ],
        ),
        out_shape=[
            jax.ShapeDtypeStruct((4 * size, total), F32),
            jax.ShapeDtypeStruct((2 * size, total), BF16),
            jax.ShapeDtypeStruct((2 * size, total), BF16),
        ],
        name="reduce_parts",
    )(place, normed, grad_qkv, grad, attended, small, *after)


def unpack_body(place_ref, *refs):
    pieces = refs[:8]
    query, key, value, output, small = refs[8:]
    size = pieces[0].shape[0]
    wide, narrow = (query.shape[1], key.shape[1])
    for r, piece in zip(ORDER, pieces):
        start = pl.multiple_of(jnp.bitwise_xor(place_ref[0], r) * size, size)
        rows = pl.ds(start, size)
        part = piece[...].astype(F32)
        query[rows, :] = part[:, :wide]
        key[rows, :] = part[:, wide : wide + narrow]
        value[rows, :] = part[:, wide + narrow : wide + 2 * narrow]
        begin = wide + 2 * narrow
        output[:, rows] = part[:, begin : begin + output.shape[0]].T
        small[rows, :] = part[:, begin + output.shape[0] :]


def assemble_body(share_ref, *refs):
    target = refs[-1]
    size = refs[0].shape[0]
    for r in range(4):
        start = pl.multiple_of(jnp.bitwise_xor(share_ref[0], r) * size, size)
        target[pl.ds(start, size), :] = refs[r][...].astype(target.dtype)


def spread_tensor(value):
    across = swap_y(value)
    return [value, swap_core(value), across, swap_core(across)]


def assemble(share, pieces, dtype, *after):
    size, width = pieces[0].shape
    shapes = [jax.ShapeDtypeStruct((4 * size, width), dtype)]
    return scalar_call(assemble_body, "assemble", share, pieces, shapes, after)[0]


def trade(value, bits):
    return lax.ppermute(value, "expert", [(i, i ^ bits) for i in range(8)])


def swap_y(value):
    return lax.ppermute(value, "tensor", [(i, i ^ 2) for i in range(4)])


def swap_core(value):
    return lax.ppermute(value, "tensor", [(i, i ^ 1) for i in range(4)])


def gather_experts(value):
    column = [value] + [trade(value, bits) for bits in (2, 4, 6)]
    return column + [trade(shard, 1) for shard in column]


def scatter_steps(keep, send_near, send_far, *beside):
    size = keep.shape[0] // 4
    got_far = trade(send_far, 1)
    send_near, got_far = lax.optimization_barrier((send_near, got_far))
    if beside:
        got_far, *beside = lax.optimization_barrier((got_far, *beside))
    far = (keep[2 * size :] + got_far.astype(F32)).astype(BF16)
    got_near = trade(send_near, 1)
    four, six = (trade(far[:size], 4), trade(far[size:], 6))
    near = (keep[size : 2 * size] + got_near[size:].astype(F32)).astype(BF16)
    return (got_near, near, far, (trade(near, 2), four, six), *beside)


def scatter_experts(keep, send_near, send_far, *beside):
    size = keep.shape[0] // 4
    got_near, _, _, back, *beside = scatter_steps(keep, send_near, send_far, *beside)
    total = keep[:size] + got_near[:size].astype(F32)
    for part in back:
        total = total + part.astype(F32)
    return (total, *beside) if beside else total


def scatter_tensor(keep, send, row):
    half = keep + swap_core(send).astype(F32)
    keep = lax.dynamic_index_in_dim(half, row, 0, False)
    send = lax.dynamic_index_in_dim(half, 1 - row, 0, False)
    return keep + swap_y(send.astype(BF16)).astype(F32)


def ordered(index, first, second):
    return jnp.where(
        index == 0, jnp.concatenate([first, second], 0), jnp.concatenate([second, first], 0)
    )


def per_device(
    tokens,
    teacher,
    valid_mask,
    routes,
    first_gain,
    query_weight,
    key_matrix,
    value_matrix,
    output_weight,
    second_gain,
    router_weight,
    expert_in,
    expert_out,
):
    row_count, model_width = tokens.shape
    expert_count = router_weight.shape[1]
    senders = lax.axis_size("expert")
    shares = lax.axis_size("tensor")
    fits = (
        (senders, shares) == (8, 4)
        and expert_count == senders * shares
        and expert_in.shape == (8, 2, model_width // 2, SHARE)
        and row_count == 4 * 128
    )
    if not fits:
        return general_device(
            tokens,
            teacher,
            valid_mask,
            routes,
            first_gain,
            query_weight,
            key_matrix,
            value_matrix,
            output_weight,
            second_gain,
            router_weight,
            expert_in,
            expert_out,
        )
    quarter = row_count // shares
    place = lax.axis_index("expert")
    share = lax.axis_index("tensor")
    row, core = (share // 2, share % 2)
    half_index = place // 4
    half_arg = half_index.reshape(1)
    held = expert_in.shape[0] // 2
    base = 8 * (place % 4) + held * half_index

    share_arg, core_arg, place_arg = (share.reshape(1), core.reshape(1), place.reshape(1))

    def quarter_of(values):
        return lax.dynamic_slice_in_dim(values, share * quarter, quarter, 0)

    local_valid = jnp.sum(valid_mask)
    routes_mine = quarter_of(routes)
    note = jnp.concatenate([routes_mine.T, jnp.full((TOP, quarter), local_valid, jnp.int32)], 0)
    notes = [note] + [trade(note, bits) for bits in (2, 4, 6)]

    own_pack, near_pack, far_pack = pack_weights(half_arg, expert_in, expert_out, *notes[1:])
    near_pack = trade(near_pack, 4)
    far_pack = trade(far_pack, 4)
    own_across = swap_y(own_pack)

    notes = jnp.stack(notes)
    notes = jnp.concatenate([notes, trade(notes, 1)], 0)
    valid_total = jnp.sum(notes[:, TOP, 0]).astype(F32)
    route_rel = jnp.bitwise_and(notes[:, :TOP] - base, expert_count - 1)
    route_rel = route_rel.transpose(0, 2, 1).reshape(senders * quarter, TOP)
    router_rel = lax.dynamic_slice_in_dim(
        jnp.concatenate([router_weight, router_weight], 1), base, expert_count, 1
    )
    router_rel = jnp.pad(
        jnp.concatenate([router_rel, router_rel], 1), ((0, 0), (0, 128 - 2 * expert_count))
    )

    tables = [
        jnp.concatenate([table[:, 0]] * (2 * SHARE // HEAD_DIM), 1)
        for table in rope_tables(row_count, HEAD_DIM)
    ]
    weights = (query_weight, key_matrix, value_matrix, output_weight)
    first_normed, query, keys, values, attended, attn_keep, attn_send = attention_forward(
        core_arg, tokens, first_gain[None], *weights, tables, own_pack
    )
    near_pack, own_across, attn_send = lax.optimization_barrier(
        (near_pack, own_across, attn_send)
    )
    own = [own_pack, swap_core(own_pack), own_across, swap_core(own_across)]
    tokens_mine = quarter_of(tokens).astype(F32)
    hidden = tokens_mine + RESIDUAL * scatter_tensor(attn_keep, attn_send, row)
    scale_two = lax.rsqrt(jnp.mean(hidden * hidden, -1, keepdims=True) + EPS)
    unit_two = hidden * scale_two
    normed_two = (unit_two * second_gain).astype(BF16)
    column = [normed_two] + [trade(normed_two, bits) for bits in (2, 4, 6)]
    beside = trade(normed_two, 1)
    near_pack, far_pack, column[1], beside = lax.optimization_barrier(
        (near_pack, far_pack, column[1], beside)
    )
    row_shards = column + [beside] + [trade(shard, 1) for shard in column[1:]]
    near, far = (spread_tensor(near_pack), spread_tensor(far_pack))
    keep, send_near, send_far, pre, gated, gates, expert_rows = experts_forward(
        half_arg,
        row_shards,
        route_rel,
        router_rel,
        own,
        near,
        far,
    )
    moe_sum = scatter_experts(keep, send_near, send_far)

    output = hidden + RESIDUAL * moe_sum
    residual_err = output - quarter_of(teacher).astype(F32)
    valid_rows = quarter_of(valid_mask).astype(F32)[:, None]
    squared_local = jnp.sum(valid_rows * residual_err * residual_err)
    token_total = senders * row_count
    grad_out = token_total / valid_total * valid_rows * residual_err
    grad_moe = (RESIDUAL * grad_out).astype(BF16)
    gate_mean = jnp.sum(grad_moe.astype(F32) * moe_sum, -1, keepdims=True)
    mean_part = -gate_mean * dense_gates(normed_two, routes_mine, router_weight)
    mean_high = mean_part.astype(BF16)
    mean_part = jnp.concatenate([mean_high, (mean_part - mean_high.astype(F32)).astype(BF16)], 1)
    router_pair = jnp.concatenate([router_weight, router_weight], 1)
    mean_rows = jnp.einsum("te,de->td", mean_part, router_pair, preferred_element_type=F32)
    keep, send_near, send_far, pre_grad, logit_grad, grad_rows = experts_backward(
        half_arg, gather_experts(grad_moe), gates, router_rel, pre, own, near, far, mean_rows
    )
    got_near, near_rows, far_rows, back = scatter_steps(keep, send_near, send_far)
    other = 1 - half_arg
    in_keep, in_send = grad_expert_ins(other, expert_rows, pre_grad, 0, 2)
    late_keep, late_send = grad_expert_ins(other, expert_rows, pre_grad, 2, 2, in_send)
    in_near, in_far = fold_pairs(in_keep, swap_core(in_send), late_send, far_rows)
    in_ready = (in_near + swap_y(in_far).astype(F32)).astype(BF16)
    out_keep, out_send, own_out_keep, own_out_send = grad_expert_outs(
        half_arg, gated, grad_rows, in_far
    )
    grad_hidden, grad_attn, grad_second_part = finish_rows(
        keep,
        got_near,
        *back,
        mean_rows,
        unit_two,
        scale_two,
        second_gain[None],
        grad_out,
        out_send,
        in_ready,
    )
    grad_second_part = jnp.sum(grad_second_part, 0)
    own_in_keep, own_in_send = grad_expert_ins(
        half_arg, expert_rows, pre_grad, 0, held, grad_attn
    )
    pieces = spread_tensor(grad_attn)
    late_near, late_far = fold_pairs(late_keep, swap_core(late_send), pieces[2])
    out_near, out_far = fold_pairs(out_keep, swap_core(out_send), pieces[2])
    out_ready = (out_near + swap_y(out_far).astype(F32)).astype(BF16)
    out_back = trade(out_ready, 4)
    late_ready = (late_near + swap_y(late_far).astype(F32)).astype(BF16)
    grad_attn, grad_qkv, gain_part, one_keep, one_send = attention_backward(
        share_arg, tokens, weights, tables, (query, keys, values), pieces, late_far, out_far, own_in_send
    )
    in_back = trade(in_ready, 4)
    late_back = trade(late_ready, 4)
    grad_one = scatter_tensor(one_keep, one_send, row)
    own_out_near, own_out_far = fold_pairs(own_out_keep, swap_core(own_out_send), grad_one)
    own_in_near, own_in_far = fold_pairs(own_in_keep, swap_core(own_in_send), grad_one)
    own_out_across = swap_y(own_out_far)
    own_in_across = swap_y(own_in_far)

    router_part = jnp.einsum(
        "te,td->ed", logit_grad.astype(BF16), expert_rows, preferred_element_type=F32
    )
    router_part = router_part[:expert_count] + router_part[expert_count : 2 * expert_count]
    router_part = lax.dynamic_slice_in_dim(
        jnp.concatenate([router_part, router_part], 0),
        jnp.bitwise_and(expert_count - base, expert_count - 1),
        expert_count,
        0,
    )
    mean_router = jnp.einsum("te,td->ed", mean_part, normed_two, preferred_element_type=F32)
    router_part = router_part + mean_router[:expert_count] + mean_router[expert_count:]

    small = jnp.concatenate(
        [
            router_part,
            grad_second_part[None],
            jnp.full((1, model_width), squared_local),
        ],
        0,
    )
    small = small + swap_core(small)
    small = small + swap_y(small)
    gain_part = jnp.sum(gain_part, 0).reshape(8, -1)
    small = jnp.concatenate([small, gain_part.reshape(1, -1)], 0)
    small = jnp.pad(small, ((0, 128 - small.shape[0]), (0, 0))).T
    keep, send_near, send_far = reduce_parts(
        place_arg, first_normed, grad_qkv, grad_attn, attended, small, in_back, late_ready
    )
    total, late_back = scatter_experts(keep, send_near, send_far, late_back)
    total = total.astype(BF16)
    shapes = [
        jax.ShapeDtypeStruct(shape, F32)
        for shape in (
            query_weight.shape,
            key_matrix.shape,
            value_matrix.shape,
            output_weight.shape,
            (model_width, 128),
        )
    ]
    grad_query, grad_key, grad_value, grad_output, small = scalar_call(
        unpack_body, "unpack", place_arg, gather_experts(total), shapes
    )

    gain_part = small[:, expert_count + 2].reshape(8, -1)
    gain_part = gain_part + swap_core(gain_part)
    gain_part = (gain_part + swap_y(gain_part)).reshape(-1)

    scale_mine = lax.rsqrt(jnp.mean(tokens_mine * tokens_mine, -1, keepdims=True) + EPS)
    unit_mine = tokens_mine * scale_mine
    grad_unit_one = grad_one * first_gain
    grad_tokens = grad_hidden + scale_mine * (
        grad_unit_one - unit_mine * jnp.mean(grad_unit_one * unit_mine, -1, keepdims=True)
    )
    grad_tokens = assemble(share_arg, spread_tensor(grad_tokens.astype(BF16)), F32)
    layer_output = assemble(share_arg, spread_tensor(output.astype(BF16)), BF16)
    grad_expert_out = ordered(
        half_index, own_out_near + own_out_across.astype(F32), out_back.astype(F32)
    )
    grad_expert_in = ordered(
        half_index,
        own_in_near + own_in_across.astype(F32),
        jnp.concatenate([in_back, late_back], 0).astype(F32),
    )
    return (
        layer_output,
        small[0, expert_count + 1] / (2.0 * model_width * valid_total),
        grad_tokens,
        gain_part,
        grad_query,
        grad_key,
        grad_value,
        grad_output,
        small[:, expert_count],
        small[:, :expert_count],
        grad_expert_in,
        grad_expert_out,
    )


def solution(mesh):
    return jax.shard_map(
        per_device,
        mesh=mesh,
        in_specs=(
            P("expert", None),
            P("expert", None),
            P("expert"),
            P("expert", None),
            P(),
            P(None, "tensor"),
            P(None, "tensor"),
            P(None, "tensor"),
            P("tensor", None),
            P(),
            P(),
            P("expert", None, None, "tensor"),
            P("expert", "tensor", None),
        ),
        out_specs=(
            P("expert", None),
            P(),
            P("expert", None),
            P(),
            P(None, "tensor"),
            P(None, "tensor"),
            P(None, "tensor"),
            P("tensor", None),
            P(),
            P(),
            P("expert", None, None, "tensor"),
            P("expert", "tensor", None),
        ),
        check_vma=False,
    )
```

```python
import jax
import jax.numpy as jnp
from jax import lax
from jax.experimental import pallas as pl
from jax.experimental.pallas import tpu as pltpu
from jax.sharding import PartitionSpec as P

HEAD_DIM = 64
TOP = 8
BLOCK = 256


EPS = 1e-06
ATTN_SCALE = 0.015625
RESIDUAL = 0.22
THETA = 10000.0


def shifted(value, axis, steps):
    count = lax.axis_size(axis)
    pairs = [(source, (source + steps) % count) for source in range(count)]
    return lax.ppermute(value, axis, pairs)


def rope_tables(length, head_size):
    half_size = head_size // 2
    frequency = THETA ** (-(jnp.arange(half_size, dtype=jnp.float32) * 2.0) / head_size)
    angle_table = jnp.arange(length, dtype=jnp.float32)[:, None] * frequency[None, :]
    return (jnp.cos(angle_table)[:, None, :], jnp.sin(angle_table)[:, None, :])


def apply_rotary(values, cosine_lookup, sine_lookup):
    half_size = values.shape[-1] // 2
    lower_half, upper_half = (values[..., :half_size], values[..., half_size:])
    return jnp.concatenate(
        [
            lower_half * cosine_lookup - upper_half * sine_lookup,
            upper_half * cosine_lookup + lower_half * sine_lookup,
        ],
        -1,
    )


def unrotate(grads, cosine_lookup, sine_lookup):
    half_size = grads.shape[-1] // 2
    lower_half, upper_half = (grads[..., :half_size], grads[..., half_size:])
    return jnp.concatenate(
        [
            lower_half * cosine_lookup + upper_half * sine_lookup,
            upper_half * cosine_lookup - lower_half * sine_lookup,
        ],
        -1,
    )


def normalize(values):
    row_peak = jnp.max(values, -1, keepdims=True)
    exp_scores = jnp.exp(values - row_peak)
    return exp_scores / jnp.sum(exp_scores, -1, keepdims=True)


def slot_tables(route_ids, expert_count, capacity):
    row_count, top_count = route_ids.shape
    onehot = route_ids[:, :, None] == jnp.arange(expert_count, dtype=jnp.int32)[None, None, :]
    hit_count = jnp.sum(onehot.astype(jnp.int32), 1)
    slot_place = jnp.cumsum(hit_count, 0) - 1
    within = jnp.take_along_axis(slot_place, route_ids, 1)
    dest_slot = route_ids * capacity + within
    pair_count = row_count * top_count
    source = (
        jnp.full((expert_count * capacity,), pair_count, jnp.int32)
        .at[dest_slot.reshape(-1)]
        .set(jnp.arange(pair_count, dtype=jnp.int32))
    )
    live_slot = source < pair_count
    token_row = jnp.minimum(source, pair_count - 1) // top_count
    return (onehot, dest_slot, source, live_slot, token_row)


def general_device(
    tokens,
    teacher,
    valid_mask,
    routes,
    first_gain,
    query_weight,
    key_matrix,
    value_matrix,
    output_weight,
    second_gain,
    router_weight,
    expert_in,
    expert_out,
):
    row_count = tokens.shape[0]
    model_width = tokens.shape[1]
    half_width = model_width // 2
    local_query = query_weight.shape[1] // HEAD_DIM
    local_kv = key_matrix.shape[1] // HEAD_DIM
    query_group_size = local_query // local_kv
    expert_count = router_weight.shape[1]
    row_local = expert_in.shape[0]
    senders = lax.axis_size("expert")
    partner_step = senders // 2
    capacity = 3 * row_count * TOP // (2 * expert_count)
    pair_count = row_count * TOP
    score_rows = min(512, row_count)
    valid_total = lax.psum(jnp.sum(valid_mask).astype(jnp.float32), "expert")
    tokens_f32 = tokens.astype(jnp.float32)
    scale_one = lax.rsqrt(jnp.mean(tokens_f32 * tokens_f32, -1, keepdims=True) + EPS)
    unit_one = tokens_f32 * scale_one
    first_normed = (unit_one * first_gain).astype(jnp.bfloat16)
    cosine_lookup, sine_lookup = rope_tables(row_count, HEAD_DIM)
    query_linear = jnp.dot(first_normed, query_weight, preferred_element_type=jnp.float32).reshape(
        row_count, local_query, HEAD_DIM
    )
    keys_linear = jnp.dot(first_normed, key_matrix, preferred_element_type=jnp.float32).reshape(
        row_count, local_kv, HEAD_DIM
    )
    value_low = jnp.dot(first_normed, value_matrix, preferred_element_type=jnp.float32).astype(
        jnp.bfloat16
    )
    value_low = value_low.reshape(row_count, local_kv, HEAD_DIM)
    query_rotated = apply_rotary(query_linear, cosine_lookup, sine_lookup).astype(jnp.bfloat16)
    keys_rot = apply_rotary(keys_linear, cosine_lookup, sine_lookup).astype(jnp.bfloat16)
    block_of = jnp.arange(row_count, dtype=jnp.int32) // BLOCK

    def scores(start_row):
        stop_row = start_row + score_rows
        query_block = query_rotated.reshape(score_rows, local_kv, query_group_size, HEAD_DIM)
        score_block = (
            jnp.einsum("qhgd,khd->hgqk", query_block, keys_rot, preferred_element_type=jnp.float32)
            * ATTN_SCALE
        )
        allowed = block_of[None, :stop_row] <= block_of[start_row:stop_row, None]
        return (query_block, jnp.where(allowed, score_block, -1e30))

    attn_parts, row_peaks, row_totals = ([], [], [])
    start_row = 0
    query_block, score_block = scores(start_row)
    row_peak = jnp.max(score_block, -1, keepdims=True)
    exp_scores = jnp.exp(score_block - row_peak)
    row_total = jnp.sum(exp_scores, -1, keepdims=True)
    attn_probs = (exp_scores / row_total).astype(jnp.bfloat16)
    attn_parts.append(
        jnp.einsum("hgqk,khd->qhgd", attn_probs, value_low, preferred_element_type=jnp.float32)
    )
    row_peaks.append(row_peak)
    row_totals.append(row_total)
    attended = attn_parts[0].reshape(row_count, local_query * HEAD_DIM).astype(jnp.bfloat16)
    attn_part = jnp.dot(attended, output_weight, preferred_element_type=jnp.float32)
    attn_sum = lax.psum(attn_part, "tensor")
    hidden_state = tokens_f32 + RESIDUAL * attn_sum
    scale_two = lax.rsqrt(jnp.mean(hidden_state * hidden_state, -1, keepdims=True) + EPS)
    unit_two = hidden_state * scale_two
    normed_two = (unit_two * second_gain).astype(jnp.bfloat16)
    router_logits = jnp.dot(normed_two, router_weight, preferred_element_type=jnp.float32)
    onehot, dest_slot, source, live_slot, token_row = slot_tables(routes, expert_count, capacity)
    picked = jnp.sum(jnp.where(onehot, router_logits[:, None, :], 0.0), -1)
    gate_probs = normalize(picked)

    def slot_rows(slot_values):
        split_rows = slot_values.reshape(expert_count, capacity, 2, half_width).transpose(
            2, 0, 1, 3
        )
        return split_rows.reshape(senders, row_local, capacity, half_width)

    def slot_columns(returned, width):
        joined = returned.reshape(2, expert_count, capacity, width).transpose(1, 2, 0, 3)
        return joined.reshape(expert_count * capacity, 2, width)

    send_rows = slot_rows(
        jnp.where(live_slot[:, None], normed_two[token_row], jnp.zeros((), jnp.bfloat16))
    )
    received = lax.all_to_all(send_rows, "expert", split_axis=0, concat_axis=2, tiled=True)
    expert_rows = received.reshape(row_local, senders * capacity, half_width)
    gate_up_part = jnp.einsum(
        "rmd,rcdf->rmcf", expert_rows, expert_in, preferred_element_type=jnp.float32
    )
    gate_up_pre = gate_up_part + shifted(gate_up_part, "expert", partner_step)
    gate_pre = gate_up_pre[:, :, 0]
    up_pre = gate_up_pre[:, :, 1]
    inner_act = (jax.nn.silu(gate_pre) * up_pre).astype(jnp.bfloat16)
    expert_result = jnp.einsum(
        "rmf,rfd->rmd", inner_act, expert_out, preferred_element_type=jnp.float32
    )
    expert_result = expert_result.astype(jnp.bfloat16).reshape(
        row_local, senders, capacity, half_width
    )
    returned = lax.all_to_all(expert_result, "expert", split_axis=1, concat_axis=0, tiled=True)
    per_route = slot_columns(returned, half_width).reshape(expert_count * capacity, model_width)[
        dest_slot
    ]
    moe_part = jnp.sum(gate_probs[:, :, None] * per_route, 1)
    moe_sum = lax.psum(moe_part, "tensor")
    output = hidden_state + RESIDUAL * moe_sum
    residual_err = output - teacher.astype(jnp.float32)
    valid_rows = valid_mask.astype(jnp.float32)
    squared_local = jnp.sum(valid_rows * jnp.sum(residual_err * residual_err, -1))
    token_total = senders * row_count
    grad_out = token_total / valid_total * valid_rows[:, None] * residual_err
    grad_moe = (RESIDUAL * grad_out).astype(jnp.bfloat16)
    gate_part = jnp.einsum("td,tkd->tk", grad_moe, per_route, preferred_element_type=jnp.float32)
    gate_slot = gate_probs.reshape(pair_count)[jnp.minimum(source, pair_count - 1)]
    grad_slots = jnp.where(live_slot[:, None], gate_slot[:, None] * grad_moe[token_row], 0.0)
    grad_received = lax.all_to_all(
        slot_rows(grad_slots.astype(jnp.bfloat16)),
        "expert",
        split_axis=0,
        concat_axis=2,
        tiled=True,
    )
    grad_expert = grad_received.reshape(row_local, senders * capacity, half_width)
    grad_inner_part = jnp.einsum(
        "rmd,rfd->rmf", grad_expert, expert_out, preferred_element_type=jnp.float32
    )
    grad_inner = grad_inner_part + shifted(grad_inner_part, "expert", partner_step)
    grad_expert_out = jnp.einsum(
        "rmf,rmd->rfd", inner_act, grad_expert, preferred_element_type=jnp.float32
    )
    sigmoid_gate = jax.nn.sigmoid(gate_pre)
    grad_gate = grad_inner * up_pre * sigmoid_gate * (1.0 + gate_pre * (1.0 - sigmoid_gate))
    grad_up = grad_inner * (gate_pre * sigmoid_gate)
    grad_pre = jnp.stack([grad_gate, grad_up], 2).astype(jnp.bfloat16)
    grad_expert_in = jnp.einsum(
        "rmd,rmcf->rcdf", expert_rows, grad_pre, preferred_element_type=jnp.float32
    )
    grad_slot_rows = jnp.einsum(
        "rmcf,rcdf->rmd", grad_pre, expert_in, preferred_element_type=jnp.float32
    )
    grad_slot_rows = grad_slot_rows.astype(jnp.bfloat16).reshape(
        row_local, senders, capacity, half_width
    )
    grad_back = lax.all_to_all(grad_slot_rows, "expert", split_axis=1, concat_axis=0, tiled=True)
    grad_back = slot_columns(grad_back, half_width).reshape(expert_count * capacity, model_width)
    grad_two_part = jnp.sum(grad_back[dest_slot].astype(jnp.float32), 1)
    grad_two_experts, grad_gates = lax.psum((grad_two_part, gate_part), "tensor")
    grad_picked = gate_probs * (grad_gates - jnp.sum(gate_probs * grad_gates, -1, keepdims=True))
    grad_logits = jnp.sum(jnp.where(onehot, grad_picked[:, :, None], 0.0), 1).astype(jnp.bfloat16)
    grad_router = jnp.einsum(
        "td,te->de", normed_two, grad_logits, preferred_element_type=jnp.float32
    )
    grad_two = grad_two_experts + jnp.einsum(
        "te,de->td", grad_logits, router_weight, preferred_element_type=jnp.float32
    )
    grad_second_gain = jnp.sum(grad_two * unit_two, 0)
    grad_unit_two = grad_two * second_gain
    grad_hidden = grad_out + scale_two * (
        grad_unit_two - unit_two * jnp.mean(grad_unit_two * unit_two, -1, keepdims=True)
    )
    grad_attn = (RESIDUAL * grad_hidden).astype(jnp.bfloat16)
    grad_output = jnp.einsum("tc,td->cd", attended, grad_attn, preferred_element_type=jnp.float32)
    grad_attended = jnp.einsum(
        "td,cd->tc", grad_attn, output_weight, preferred_element_type=jnp.float32
    )
    grad_attended = grad_attended.astype(jnp.bfloat16).reshape(
        row_count, local_kv, query_group_size, HEAD_DIM
    )
    grad_query_parts = []
    grad_keys = jnp.zeros((row_count, local_kv, HEAD_DIM), jnp.float32)
    grad_values = jnp.zeros((row_count, local_kv, HEAD_DIM), jnp.float32)
    for block_index, start_row in enumerate(range(0, row_count, score_rows)):
        stop_row = start_row + score_rows
        query_block, score_block = scores(start_row)
        attn_probs = jnp.exp(score_block - row_peaks[block_index]) / row_totals[block_index]
        probs_low = attn_probs.astype(jnp.bfloat16)
        grad_probs = jnp.einsum(
            "qhgd,khd->hgqk", grad_attended, value_low, preferred_element_type=jnp.float32
        )
        grad_scores = attn_probs * (
            grad_probs - jnp.sum(attn_probs * grad_probs, -1, keepdims=True)
        )
        grad_scores = grad_scores.astype(jnp.bfloat16)
        grad_query_parts.append(
            ATTN_SCALE
            * jnp.einsum(
                "hgqk,khd->qhgd", grad_scores, keys_rot, preferred_element_type=jnp.float32
            )
        )
        grad_keys = grad_keys.at[:stop_row].add(
            ATTN_SCALE
            * jnp.einsum(
                "hgqk,qhgd->khd", grad_scores, query_block, preferred_element_type=jnp.float32
            )
        )
        grad_values = grad_values.at[:stop_row].add(
            jnp.einsum(
                "hgqk,qhgd->khd", probs_low, grad_attended, preferred_element_type=jnp.float32
            )
        )
    grad_query_rot = grad_query_parts[0].reshape(row_count, local_query, HEAD_DIM)
    grad_query_low = unrotate(grad_query_rot, cosine_lookup, sine_lookup).reshape(
        row_count, local_query * HEAD_DIM
    )
    grad_query_low = grad_query_low.astype(jnp.bfloat16)
    grad_keys_low = unrotate(grad_keys, cosine_lookup, sine_lookup).reshape(
        row_count, local_kv * HEAD_DIM
    )
    grad_keys_low = grad_keys_low.astype(jnp.bfloat16)
    grad_values_low = grad_values.reshape(row_count, local_kv * HEAD_DIM).astype(jnp.bfloat16)
    grad_query = jnp.einsum(
        "td,tc->dc", first_normed, grad_query_low, preferred_element_type=jnp.float32
    )
    grad_key = jnp.einsum(
        "td,tc->dc", first_normed, grad_keys_low, preferred_element_type=jnp.float32
    )
    grad_value = jnp.einsum(
        "td,tc->dc", first_normed, grad_values_low, preferred_element_type=jnp.float32
    )
    grad_one_part = (
        jnp.einsum("tc,dc->td", grad_query_low, query_weight, preferred_element_type=jnp.float32)
        + jnp.einsum("tc,dc->td", grad_keys_low, key_matrix, preferred_element_type=jnp.float32)
        + jnp.einsum("tc,dc->td", grad_values_low, value_matrix, preferred_element_type=jnp.float32)
    )
    grad_one = lax.psum(grad_one_part.astype(jnp.bfloat16), "tensor").astype(jnp.float32)
    grad_first_gain = jnp.sum(grad_one * unit_one, 0)
    grad_unit_one = grad_one * first_gain
    grad_tokens = grad_hidden + scale_one * (
        grad_unit_one - unit_one * jnp.mean(grad_unit_one * unit_one, -1, keepdims=True)
    )
    reduced = lax.psum(
        (
            grad_first_gain,
            grad_query,
            grad_key,
            grad_value,
            grad_output,
            grad_second_gain,
            grad_router,
            squared_local,
        ),
        "expert",
    )
    loss_value = reduced[7] / (2.0 * model_width * valid_total)
    return (
        output.astype(jnp.bfloat16),
        loss_value,
        grad_tokens,
        reduced[0],
        reduced[1],
        reduced[2],
        reduced[3],
        reduced[4],
        reduced[5],
        reduced[6],
        grad_expert_in,
        grad_expert_out,
    )


BF16 = jnp.bfloat16
F32 = jnp.float32
CHUNK = 256
SHARE = 128
PACK = 12 * SHARE
NT = (((1,), (1,)), ((), ()))
ORDER = (0, 2, 4, 6, 1, 3, 5, 7)


def whole_block(shape):
    return pl.BlockSpec(shape, lambda e, *_: (0,) * len(shape))


def any_block():
    return pl.BlockSpec(memory_space=pl.ANY)


def pack_body(half_ref, own_in, own_out, other_in, other_out, *refs):
    own, near, far = refs[-3:]
    step = pl.program_id(0)

    def fill(target, source_in, source_out):
        for c in range(2):
            target[c * 4 * SHARE : (c + 1) * 4 * SHARE, :] = source_in[0, c]
        for k in range(4):
            target[(8 + k) * SHARE : (9 + k) * SHARE, :] = source_out[
                0, :, k * SHARE : (k + 1) * SHARE
            ]

    fill(own, own_in, own_out)

    @pl.when(step < 2)
    def _():
        fill(near, other_in, other_out)

    @pl.when(step >= 2)
    def _():
        fill(far, other_in, other_out)


def pack_weights(half_index, expert_in, expert_out, *after):
    held = expert_in.shape[0] // 2
    in_shape = (1,) + expert_in.shape[1:]
    out_shape = (1,) + expert_out.shape[1:]
    shapes = [(held * PACK, SHARE), (held // 2 * PACK, SHARE), (held // 2 * PACK, SHARE)]
    block = (PACK, SHARE)
    return pl.pallas_call(
        pack_body,
        grid_spec=pltpu.PrefetchScalarGridSpec(
            num_scalar_prefetch=1,
            grid=(held,),
            in_specs=[
                pl.BlockSpec(in_shape, lambda e, half: (half[0] * held + e, 0, 0, 0)),
                pl.BlockSpec(out_shape, lambda e, half: (half[0] * held + e, 0, 0)),
                pl.BlockSpec(in_shape, lambda e, half: ((1 - half[0]) * held + e, 0, 0, 0)),
                pl.BlockSpec(out_shape, lambda e, half: ((1 - half[0]) * held + e, 0, 0)),
            ]
            + [any_block()] * len(after),
            out_specs=[
                pl.BlockSpec(block, lambda e, half: (e, 0)),
                pl.BlockSpec(block, lambda e, half: (jnp.minimum(e, 1), 0)),
                pl.BlockSpec(block, lambda e, half: (jnp.maximum(e - 2, 0), 0)),
            ],
        ),
        out_shape=[jax.ShapeDtypeStruct(shape, BF16) for shape in shapes],
        name="pack_weights",
    )(half_index, expert_in, expert_out, expert_in, expert_out, *after)


def weight_copies(own, other, own_row, other_row, half, in_buf, out_buf, sems, slot):
    copies = []
    for q in range(4):
        for pack, row, side in ((own[q], own_row, half), (other[q], other_row, 1 - half)):
            for c in range(2):
                copies.append(
                    (
                        pack.at[pl.ds(pl.multiple_of(row + c * 4 * SHARE, SHARE), 4 * SHARE)],
                        in_buf.at[
                            slot,
                            pl.ds(pl.multiple_of(side * 4 * SHARE, SHARE), 4 * SHARE),
                            pl.ds((2 * q + c) * SHARE, SHARE),
                        ],
                    )
                )
            for k in range(4):
                copies.append(
                    (
                        pack.at[pl.ds(pl.multiple_of(row + (8 + k) * SHARE, SHARE), SHARE)],
                        out_buf.at[slot, side, pl.ds(q * SHARE, SHARE), pl.ds(k * SHARE, SHARE)],
                    )
                )
    return [
        pltpu.make_async_copy(source, target, sems.at[slot, n])
        for n, (source, target) in enumerate(copies)
    ]


def stream_weights(first, packs, half, in_buf, out_buf, sems):
    step = pl.program_id(0)
    slot = lax.rem(step, 2)
    own, near, far = (packs[0:4], packs[4:8], packs[8:12])

    def start(index, target):
        expert = first + index

        def begin(other, start_row):
            for copy in weight_copies(
                own, other, expert * PACK, start_row, half, in_buf, out_buf, sems, target
            ):
                copy.start()

        if not far:
            begin(near, index * PACK)
            return

        @pl.when(expert < 2)
        def _():
            begin(near, expert * PACK)

        @pl.when(expert >= 2)
        def _():
            begin(far, (expert - 2) * PACK)

    @pl.when(step == 0)
    def _():
        start(0, 0)

    @pl.when(step + 1 < pl.num_programs(0))
    def _():
        start(step + 1, 1 - slot)

    def wait():
        for copy in weight_copies(own, near, 0, 0, half, in_buf, out_buf, sems, slot):
            copy.wait()

    return (step, slot, wait)


def weight_scratch(width, hidden):
    return [
        pltpu.VMEM((2, width, 2 * hidden), BF16),
        pltpu.VMEM((2, 2, hidden, width // 2), BF16),
        pltpu.SemaphoreType.DMA((2, 48)),
    ]


def split_pairs(values):
    blocks = [values[:, i * SHARE : (i + 1) * SHARE] for i in range(values.shape[1] // SHARE)]
    return (jnp.concatenate(blocks[0::2], 1), jnp.concatenate(blocks[1::2], 1))


def join_pairs(first, second):
    blocks = []
    for i in range(first.shape[1] // SHARE):
        blocks.append(first[:, i * SHARE : (i + 1) * SHARE])
        blocks.append(second[:, i * SHARE : (i + 1) * SHARE])
    return jnp.concatenate(blocks, 1)


def chunk_loop(row_count, body):
    def step(i, carry):
        body(pl.ds(pl.multiple_of(i * CHUNK, CHUNK), CHUNK))
        return carry

    lax.fori_loop(0, row_count // CHUNK, step, 0)


def gate_column(gates, expert):
    lane = lax.broadcasted_iota(jnp.int32, gates.shape, 1)
    return jnp.sum(jnp.where(lane == expert, gates, 0.0), -1, keepdims=True)


def dense_gates(rows, ids, router):
    logits = jnp.dot(rows, router, preferred_element_type=F32)
    lane = lax.broadcasted_iota(jnp.int32, logits.shape, 1)
    mask = ids[:, 0:1] == lane
    for k in range(1, TOP):
        mask = mask | (ids[:, k : k + 1] == lane)
    masked = jnp.where(mask, logits, -1e30)
    powers = jnp.where(mask, jnp.exp(masked - jnp.max(masked, -1, keepdims=True)), 0.0)
    return powers / jnp.sum(powers, -1, keepdims=True)


def apply_expert(rows, expert, slot, rows_ref, gate_ref, pre_ref, gated_ref, in_buf):
    pre = jnp.dot(rows_ref[rows, :], in_buf[slot], preferred_element_type=F32)
    pre_ref[0, rows, :] = pre.astype(BF16)
    gate_pre, up_pre = split_pairs(pre)
    weight = gate_column(gate_ref[rows, :], expert)
    gated = (weight * (gate_pre * jax.nn.sigmoid(gate_pre) * up_pre)).astype(BF16)
    gated_ref[0, rows, :] = gated
    return gated


def forward_first(half_ref, *refs):
    shards = refs[:8]
    route_ref, router_ref = refs[8:10]
    packs = refs[10:18]
    acc, pre_ref, gated_ref, gate_ref, rows_ref, in_buf, out_buf, sems = refs[18:]
    step, slot, wait = stream_weights(0, packs, half_ref[0], in_buf, out_buf, sems)
    row_count, width = acc.shape
    size = row_count // 8

    @pl.when(step == 0)
    def _():
        for i in range(8):
            rows_ref[i * size : (i + 1) * size, :] = shards[i][...]
        acc[...] = jnp.zeros_like(acc)

        def gating(rows):
            gate_ref[rows, :] = dense_gates(rows_ref[rows, :], route_ref[rows, :], router_ref[...])

        chunk_loop(row_count, gating)

    wait()

    def mlp(rows):
        gated = apply_expert(rows, step, slot, rows_ref, gate_ref, pre_ref, gated_ref, in_buf)
        for side in range(2):
            columns = slice(side * width // 2, (side + 1) * width // 2)
            acc[rows, columns] += jnp.dot(gated, out_buf[slot, side], preferred_element_type=F32)

    chunk_loop(row_count, mlp)


def forward_second(half_ref, *refs):
    rows_ref, gate_ref, start_ref = refs[:3]
    packs = refs[3:11]
    pre_ref, gated_ref = refs[-6:-4]
    targets = refs[13:-6]
    acc, in_buf, out_buf, sems = refs[-4:]
    step, slot, wait = stream_weights(2, packs, half_ref[0], in_buf, out_buf, sems)
    row_count, width = acc.shape

    wait()

    def mlp(rows, source):
        gated = apply_expert(rows, step + 2, slot, rows_ref, gate_ref, pre_ref, gated_ref, in_buf)
        for side in range(2):
            columns = slice(side * width // 2, (side + 1) * width // 2)
            acc[rows, columns] = source[rows, columns] + jnp.dot(
                gated, out_buf[slot, side], preferred_element_type=F32
            )

    @pl.when(step == 0)
    def _():
        acc[...] = start_ref[...]

    chunk_loop(row_count, lambda rows: mlp(rows, acc))

    @pl.when(step == pl.num_programs(0) - 1)
    def _():
        spread(acc, targets)


def spread(acc, targets):
    size = acc.shape[0] // len(targets)
    for i, target in enumerate(targets):
        target[...] = acc[i * size : (i + 1) * size, :].astype(target.dtype)


def spread_specs(part, row_count, width):
    if part == 0:
        shapes = [jax.ShapeDtypeStruct((row_count // 2, width), F32)]
    else:
        shapes = [jax.ShapeDtypeStruct((row_count // 4, width), BF16)] * 2
    return ([whole_block(s.shape) for s in shapes], shapes)


def half_rows(shape, part):
    block = (shape[0] // 2,) + shape[1:]
    return pl.BlockSpec(block, lambda e, *_: (part, 0))


def half_expert(shape, part, first=0):
    block = (1, shape[1] // 2) + shape[2:]
    return pl.BlockSpec(block, lambda e, *_: (e + first, part, 0))


def expert_block(shape, first=0):
    return pl.BlockSpec((1,) + shape[1:], lambda e, *_: (e + first,) + (0,) * (len(shape) - 1))


def experts_forward(half_index, shards, route_ids, router, own, near, far):
    size, width = shards[0].shape
    row_count = 8 * size
    local = own[0].shape[0] // PACK
    hidden = 4 * SHARE
    sums = jax.ShapeDtypeStruct((row_count, width), F32)
    pre = jax.ShapeDtypeStruct((local, row_count, 2 * hidden), BF16)
    gated = jax.ShapeDtypeStruct((local, row_count, hidden), BF16)
    gates = jax.ShapeDtypeStruct((row_count, 128), F32)
    rows = jax.ShapeDtypeStruct((row_count, width), BF16)
    sums_a, pre_a, gated_a, gates, rows = pl.pallas_call(
        forward_first,
        grid_spec=pltpu.PrefetchScalarGridSpec(
            num_scalar_prefetch=1,
            grid=(2,),
            in_specs=[whole_block(v.shape) for v in (*shards, route_ids, router)]
            + [any_block()] * 8,
            out_specs=[
                whole_block(sums.shape),
                expert_block(pre.shape),
                expert_block(gated.shape),
                whole_block(gates.shape),
                whole_block(rows.shape),
            ],
            scratch_shapes=weight_scratch(width, hidden),
        ),
        out_shape=[sums, pre, gated, gates, rows],
        name="experts_forward_a",
    )(half_index, *shards, route_ids, router, *own, *near)

    def second(part, pre_a, gated_a):
        specs, shapes = spread_specs(part, row_count, width)
        return pl.pallas_call(
            forward_second,
            grid_spec=pltpu.PrefetchScalarGridSpec(
                num_scalar_prefetch=1,
                grid=(2,),
                in_specs=[half_rows(v.shape, part) for v in (rows, gates, sums)]
                + [any_block()] * 10,
                out_specs=specs
                + [half_expert(pre.shape, part, 2), half_expert(gated.shape, part, 2)],
                scratch_shapes=[pltpu.VMEM((row_count // 2, width), F32)]
                + weight_scratch(width, hidden),
            ),
            out_shape=shapes + [pre, gated],
            input_output_aliases={12: len(shapes), 13: len(shapes) + 1},
            name="experts_forward_b",
        )(half_index, rows, gates, sums_a, *own, *far, pre_a, gated_a)

    send_near, send_far, pre_a, gated_a = second(1, pre_a, gated_a)
    keep, pre_a, gated_a = second(0, pre_a, gated_a)
    return (keep, send_near, send_far, pre_a, gated_a, gates, rows)


def backward_body(half_ref, *refs):
    shards = refs[:4]
    gate_ref, router_ref, pre_ref = refs[4:7]
    packs = refs[7:19]
    pre_grad_ref, logit_ref, grad_ref = refs[-7:-4]
    acc, in_buf, out_buf, sems = refs[-4:]
    step, slot, wait = stream_weights(0, packs, half_ref[0], in_buf, out_buf, sems)
    row_count, width = grad_ref.shape
    size = row_count // 4
    targets = [ref for ref in refs[19:-7] if ref.shape[0] * 2 == row_count]
    targets = targets or [refs[-8]]

    @pl.when(step == 0)
    def _():
        for i in range(4):
            grad_ref[i * size : (i + 1) * size, :] = shards[i][...]
        acc[...] = jnp.zeros_like(acc)
        logit_ref[...] = jnp.zeros_like(logit_ref)

    wait()

    def mlp(rows):
        plain = lax.dot_general(
            grad_ref[rows, : width // 2], out_buf[slot, 0], NT, preferred_element_type=F32
        ) + lax.dot_general(
            grad_ref[rows, width // 2 :], out_buf[slot, 1], NT, preferred_element_type=F32
        )
        gate_pre, up_pre = split_pairs(pre_ref[0, rows, :].astype(F32))
        weight = gate_column(gate_ref[rows, :], step)
        sigmoid = jax.nn.sigmoid(gate_pre)
        act = gate_pre * sigmoid
        grad_weight = jnp.sum(act * up_pre * plain, -1, keepdims=True)
        scaled = weight * plain
        pre_grad = join_pairs(
            scaled * up_pre * (sigmoid + act * (1.0 - sigmoid)), scaled * act
        ).astype(BF16)
        pre_grad_ref[0, rows, :] = pre_grad
        old = logit_ref[rows, :]
        lane = lax.broadcasted_iota(jnp.int32, old.shape, 1)
        value = weight * grad_weight
        high = value.astype(BF16).astype(F32)
        logit_ref[rows, :] = jnp.where(
            lane == step, high, jnp.where(lane == step + 32, value - high, old)
        )
        acc[rows, :] += lax.dot_general(pre_grad, in_buf[slot], NT, preferred_element_type=F32)

    chunk_loop(row_count, mlp)

    @pl.when(step == pl.num_programs(0) - 1)
    def _():
        def router(rows):
            acc[rows, :] += lax.dot_general(
                logit_ref[rows, :].astype(BF16), router_ref[...], NT, preferred_element_type=F32
            )

        chunk_loop(row_count, router)
        spread(acc, targets)


def experts_backward(part, half_index, shards, gates, router, pre, own, near, far, *before):
    row_count, width = (8 * shards[0].shape[0], shards[0].shape[1])
    local = pre.shape[0]
    specs, shapes = spread_specs(part, row_count, width)
    saved = [
        jax.ShapeDtypeStruct(pre.shape, BF16),
        jax.ShapeDtypeStruct((row_count, 128), F32),
        jax.ShapeDtypeStruct((row_count, width), BF16),
    ]
    return pl.pallas_call(
        backward_body,
        grid_spec=pltpu.PrefetchScalarGridSpec(
            num_scalar_prefetch=1,
            grid=(local,),
            in_specs=[whole_block(v.shape) for v in shards]
            + [half_rows(gates.shape, part), whole_block(router.shape)]
            + [half_expert(pre.shape, part)]
            + [any_block()] * (12 + len(before)),
            out_specs=specs
            + [half_expert(pre.shape, part)]
            + [half_rows(v.shape, part) for v in saved[1:]],
            scratch_shapes=[pltpu.VMEM((row_count // 2, width), F32)]
            + weight_scratch(width, 4 * SHARE),
        ),
        out_shape=shapes + saved,
        input_output_aliases={20 + i: len(shapes) + i for i in range(len(before))},
        name="experts_backward",
    )(half_index, *shards, gates, router, pre, *own, *near, *far, *before)


def grad_out_body(half_ref, gated_ref, other_ref, mine_ref, *refs):
    *outs, turned = refs[-5:]
    turned[...] = gated_ref[0].T

    def pair(q, carry):
        for n, source in ((0, other_ref), (2, mine_ref)):
            for odd in range(2):
                rows = pl.ds(pl.multiple_of((2 * q + odd) * SHARE, SHARE), SHARE)
                product = jnp.dot(turned[rows, :], source[...], preferred_element_type=F32)
                outs[n + odd][q, 0] = product.astype(BF16)
        return carry

    lax.fori_loop(0, 2, pair, 0)


def grad_expert_outs(half_index, gated, grads, *after):
    local, row_count, hidden = gated.shape
    width = grads.shape[1]
    half_spec = (row_count, width // 2)
    shape = (2, local, SHARE, width // 2)
    return pl.pallas_call(
        grad_out_body,
        grid_spec=pltpu.PrefetchScalarGridSpec(
            num_scalar_prefetch=1,
            grid=(local,),
            in_specs=[
                expert_block(gated.shape),
                pl.BlockSpec(half_spec, lambda e, half: (0, 1 - half[0])),
                pl.BlockSpec(half_spec, lambda e, half: (0, half[0])),
            ]
            + [any_block()] * len(after),
            out_specs=[pl.BlockSpec((2, 1) + shape[2:], lambda e, *_: (0, e, 0, 0))] * 4,
            scratch_shapes=[pltpu.VMEM((hidden, row_count), BF16)],
        ),
        out_shape=[jax.ShapeDtypeStruct(shape, BF16)] * 4,
        name="grad_expert_out",
    )(half_index, gated, grads, grads, *after)


def grad_in_body(half_ref, rows_ref, pre_ref, *refs):
    keep_ref, send_ref, turned = refs[-3:]

    @pl.when(pl.program_id(0) == 0)
    def _():
        turned[...] = rows_ref[...].T

    def part(i, carry):
        rows = pl.ds(pl.multiple_of(i * CHUNK, CHUNK), CHUNK)
        product = jnp.dot(turned[rows, :], pre_ref[0], preferred_element_type=F32).astype(BF16)
        for q in range(4):
            for c in range(2):
                start = (2 * q + c) * SHARE
                (keep_ref, send_ref)[q % 2][q // 2, 0, c, rows] = product[:, start : start + SHARE]
        return carry

    lax.fori_loop(0, turned.shape[0] // CHUNK, part, 0)


def grad_expert_ins(half_index, rows, pre_grad, first, count, *after):
    local, row_count, wide = pre_grad.shape
    width = rows.shape[1]
    shape = (2, count, 2, width // 2, SHARE)
    return pl.pallas_call(
        grad_in_body,
        grid_spec=pltpu.PrefetchScalarGridSpec(
            num_scalar_prefetch=1,
            grid=(count,),
            in_specs=[
                pl.BlockSpec((row_count, width // 2), lambda e, half: (0, half[0])),
                expert_block(pre_grad.shape, first),
            ]
            + [any_block()] * len(after),
            out_specs=[pl.BlockSpec((2, 1) + shape[2:], lambda e, *_: (0, e, 0, 0, 0))] * 2,
            scratch_shapes=[pltpu.VMEM((width // 2, row_count), BF16)],
        ),
        out_shape=[jax.ShapeDtypeStruct(shape, BF16)] * 2,
        name="grad_expert_in",
    )(half_index, rows, pre_grad, *after)


def fold_body(keep_ref, got_ref, *refs):
    near_ref, far_ref = refs[-2:]
    near_ref[...] = keep_ref[0].astype(F32) + got_ref[0].astype(F32)
    far_ref[...] = (keep_ref[1].astype(F32) + got_ref[1].astype(F32)).astype(BF16)


def fold_pairs(keep, got, *after):
    shape = keep.shape
    rest = (0,) * (len(shape) - 2)
    pair = pl.BlockSpec((2, 1) + shape[2:], lambda e: (0, e) + rest)
    single = pl.BlockSpec((1,) + shape[2:], lambda e: (e,) + rest)
    return pl.pallas_call(
        fold_body,
        grid=(shape[1],),
        in_specs=[pair, pair] + [any_block()] * len(after),
        out_specs=[single, single],
        out_shape=[
            jax.ShapeDtypeStruct(shape[1:], F32),
            jax.ShapeDtypeStruct(shape[1:], BF16),
        ],
        name="fold_pairs",
    )(keep, got, *after)


def finish_body(keep, near, two, four, six, extra, unit, scale, gain, grad_out, *refs):
    hidden_ref, attn_ref, gain_ref = refs[-3:]
    total = keep[...] + near[...].astype(F32) + extra[...]
    for part in (two, four, six):
        total = total + part[...].astype(F32)
    gain_ref[...] = jnp.sum((total * unit[...]).reshape(-1, 8, total.shape[1]), 0)
    weighted = total * gain[...]
    mean = jnp.mean(weighted * unit[...], -1, keepdims=True)
    hidden = grad_out[...] + scale[...] * (weighted - unit[...] * mean)
    hidden_ref[...] = hidden
    attn_ref[...] = (RESIDUAL * hidden).astype(BF16)


def finish_rows(keep, near, two, four, six, extra, unit, scale, gain, grad_out, *after):
    size, width = unit.shape
    block = pl.BlockSpec((size, width), lambda e: (0, 0))
    return pl.pallas_call(
        finish_body,
        grid=(1,),
        in_specs=[block] * 7
        + [whole_block((size, 1)), whole_block((1, width)), block]
        + [any_block()] * len(after),
        out_specs=[block, block, whole_block((8, width))],
        out_shape=[
            jax.ShapeDtypeStruct((size, width), F32),
            jax.ShapeDtypeStruct((size, width), BF16),
            jax.ShapeDtypeStruct((8, width), F32),
        ],
        name="finish_rows",
    )(keep, near, two, four, six, extra, unit, scale, gain, grad_out, *after)


def rotated(values, cosine, sine, sign):
    width = values.shape[1]
    lane = lax.broadcasted_iota(jnp.int32, values.shape, 1)
    lower = lax.rem(lane, HEAD_DIM) < HEAD_DIM // 2
    ahead = pltpu.roll(values, width - HEAD_DIM // 2, 1)
    behind = pltpu.roll(values, HEAD_DIM // 2, 1)
    turned = jnp.where(lower, -ahead, behind)
    repeat = width // cosine.shape[1]
    cosine = jnp.concatenate([cosine] * repeat, 1)
    sine = jnp.concatenate([sine] * repeat, 1)
    return values * cosine + sign * (turned * sine)


def head(values, index, start=0, stop=None):
    return values[start:stop, index * HEAD_DIM : (index + 1) * HEAD_DIM]


def probabilities(query, keys):
    scores = lax.dot_general(query, keys, NT, preferred_element_type=F32) * ATTN_SCALE
    powers = jnp.exp(scores - jnp.max(scores, -1, keepdims=True))
    return powers / jnp.sum(powers, -1, keepdims=True)


def attention_forward_body(
    core_ref, tokens, gain, query_w, key_w, value_w, output_w, cosine, sine, *refs
):
    normed, query, keys, values, attended, keep, send = refs[-7:]
    x = tokens[...].astype(F32)
    scale = lax.rsqrt(jnp.mean(x * x, -1, keepdims=True) + EPS)
    normed[...] = (x * scale * gain[...]).astype(BF16)
    low = normed[...]
    linear = jnp.dot(low, query_w[...], preferred_element_type=F32)
    query[...] = rotated(linear, cosine[...], sine[...], 1.0).astype(BF16)
    linear = jnp.dot(low, key_w[...], preferred_element_type=F32)
    keys[...] = rotated(linear, cosine[...], sine[...], 1.0).astype(BF16)
    values[...] = jnp.dot(low, value_w[...], preferred_element_type=F32).astype(BF16)
    group = query.shape[1] // keys.shape[1]
    for start in range(0, tokens.shape[0], BLOCK):
        stop = start + BLOCK
        parts = []
        for h in range(query.shape[1] // HEAD_DIM):
            probs = probabilities(head(query, h, start, stop), head(keys, h // group, 0, stop))
            parts.append(
                jnp.dot(
                    probs.astype(BF16),
                    head(values, h // group, 0, stop),
                    preferred_element_type=F32,
                )
            )
        attended[start:stop, :] = jnp.concatenate(parts, 1).astype(BF16)
    size = tokens.shape[0] // 4
    for r in range(2):
        for target, core in ((keep, core_ref[0]), (send, 1 - core_ref[0])):
            rows = pl.ds(pl.multiple_of((2 * r + core) * size, size), size)
            part = jnp.dot(attended[rows, :], output_w[...], preferred_element_type=F32)
            target[r] = part.astype(target.dtype)


def scalar_call(body, name, scalar, inputs, shapes, after=(), scratch=()):
    return pl.pallas_call(
        body,
        grid_spec=pltpu.PrefetchScalarGridSpec(
            num_scalar_prefetch=1,
            grid=(1,),
            in_specs=[whole_block(v.shape) for v in inputs] + [any_block()] * len(after),
            out_specs=[whole_block(s.shape) for s in shapes],
            scratch_shapes=list(scratch),
        ),
        out_shape=shapes,
        name=name,
    )(scalar, *inputs, *after)


def attention_forward(core, tokens, gain, query_w, key_w, value_w, output_w, tables, *after):
    rows, width = tokens.shape
    shapes = [
        jax.ShapeDtypeStruct((rows, width), BF16),
        jax.ShapeDtypeStruct((rows, query_w.shape[1]), BF16),
        jax.ShapeDtypeStruct((rows, key_w.shape[1]), BF16),
        jax.ShapeDtypeStruct((rows, value_w.shape[1]), BF16),
        jax.ShapeDtypeStruct((rows, query_w.shape[1]), BF16),
        jax.ShapeDtypeStruct((2, rows // 4, width), F32),
        jax.ShapeDtypeStruct((2, rows // 4, width), BF16),
    ]
    inputs = (tokens, gain, query_w, key_w, value_w, output_w, *tables)
    return scalar_call(
        attention_forward_body, "attention_forward", core, inputs, shapes, after
    )


TN = (((0,), (0,)), ((), ()))


def attention_backward_body(
    share_ref,
    tokens,
    query_w,
    key_w,
    value_w,
    output_w,
    cosine,
    sine,
    query,
    keys,
    values,
    first,
    second,
    third,
    fourth,
    *refs,
):
    grad, grad_qkv, gain, keep, send, grad_keys, grad_values = refs[-7:]
    share = share_ref[0]
    size = first.shape[0]
    for r, piece in enumerate((first, second, third, fourth)):
        place = jnp.bitwise_xor(share, r) * size
        grad[pl.ds(pl.multiple_of(place, size), size), :] = piece[...]
    back = lax.dot_general(grad[...], output_w[...], NT, preferred_element_type=F32).astype(BF16)
    wide, narrow = (query.shape[1], keys.shape[1])
    group = wide // narrow
    grad_keys[...] = jnp.zeros_like(grad_keys)
    grad_values[...] = jnp.zeros_like(grad_values)
    for start in range(0, tokens.shape[0], BLOCK):
        stop = start + BLOCK
        parts, key_parts, value_parts = ([], [], [])
        for kv in range(narrow // HEAD_DIM):
            key, value = (head(keys, kv, 0, stop), head(values, kv, 0, stop))
            key_sum, value_sum = (0.0, 0.0)
            for h in range(kv * group, (kv + 1) * group):
                query_h = head(query, h, start, stop)
                back_h = head(back, h, start, stop)
                probs = probabilities(query_h, key)
                inner = lax.dot_general(back_h, value, NT, preferred_element_type=F32)
                scores = probs * (inner - jnp.sum(probs * inner, -1, keepdims=True))
                scores = scores.astype(BF16)
                parts.append(ATTN_SCALE * jnp.dot(scores, key, preferred_element_type=F32))
                key_sum += lax.dot_general(scores, query_h, TN, preferred_element_type=F32)
                value_sum += lax.dot_general(
                    probs.astype(BF16), back_h, TN, preferred_element_type=F32
                )
            key_parts.append(ATTN_SCALE * key_sum)
            value_parts.append(value_sum)
        turned = rotated(
            jnp.concatenate(parts, 1), cosine[start:stop, :], sine[start:stop, :], -1.0
        )
        grad_qkv[start:stop, :wide] = turned.astype(BF16)
        grad_keys[:stop, :] += jnp.concatenate(key_parts, 1)
        grad_values[:stop, :] += jnp.concatenate(value_parts, 1)
    turned = rotated(grad_keys[...], cosine[...], sine[...], -1.0)
    grad_qkv[:, wide : wide + narrow] = turned.astype(BF16)
    grad_qkv[:, wide + narrow :] = grad_values[...].astype(BF16)
    total = jnp.zeros(gain.shape, F32)
    for r in range(2):
        for target, core in ((keep, share % 2), (send, 1 - share % 2)):
            rows = pl.ds(pl.multiple_of((2 * r + core) * size, size), size)
            part = lax.dot_general(
                grad_qkv[rows, :wide], query_w[...], NT, preferred_element_type=F32
            )
            part += lax.dot_general(
                grad_qkv[rows, wide : wide + narrow], key_w[...], NT, preferred_element_type=F32
            )
            part += lax.dot_general(
                grad_qkv[rows, wide + narrow :], value_w[...], NT, preferred_element_type=F32
            )
            target[r] = part.astype(target.dtype)
            x = tokens[rows, :].astype(F32)
            x = x * lax.rsqrt(jnp.mean(x * x, -1, keepdims=True) + EPS)
            total += jnp.sum((part * x).reshape(-1, 8, x.shape[1]), 0)
    gain[...] = total


def attention_backward(share, tokens, weights, tables, saved, pieces, *after):
    rows, width = tokens.shape
    narrow = saved[1].shape[1]
    shapes = [
        jax.ShapeDtypeStruct((rows, width), BF16),
        jax.ShapeDtypeStruct((rows, saved[0].shape[1] + 2 * narrow), BF16),
        jax.ShapeDtypeStruct((8, width), F32),
        jax.ShapeDtypeStruct((2, rows // 4, width), F32),
        jax.ShapeDtypeStruct((2, rows // 4, width), BF16),
    ]
    return scalar_call(
        attention_backward_body,
        "attention_backward",
        share,
        (tokens, *weights, *tables, *saved, *pieces),
        shapes,
        after,
        [pltpu.VMEM((rows, narrow), F32), pltpu.VMEM((rows, narrow), F32)],
    )


def reduce_body(place_ref, normed, grad_qkv, grad, attended, small, gain, *refs):
    keep, near, far = refs[-3:]
    step = pl.program_id(0)
    first = lax.dot_general(normed[...], grad_qkv[...], TN, preferred_element_type=F32)
    second = lax.dot_general(grad[...], attended[...], TN, preferred_element_type=F32)
    rest = jnp.zeros((SHARE - small.shape[0] - gain.shape[0], SHARE), F32)
    third = jnp.concatenate([small[...], gain[...], rest], 0).T
    part = jnp.concatenate([first, second, third], 1)

    @pl.when(step < 4)
    def _():
        keep[...] = part

    @pl.when((step == 4) | (step == 5))
    def _():
        near[...] = part.astype(BF16)

    @pl.when(step >= 6)
    def _():
        far[...] = part.astype(BF16)


def reduce_parts(place, normed, grad_qkv, grad, attended, small, gain, *after):
    rows, width = normed.shape
    size = width // 8
    total = grad_qkv.shape[1] + attended.shape[1] + SHARE

    def shard(e, place):
        order = jnp.where(e < 4, 2 * e, 2 * e - 7)
        return jnp.bitwise_xor(place[0], order)

    columns = pl.BlockSpec((rows, size), lambda e, place: (0, shard(e, place)))
    return pl.pallas_call(
        reduce_body,
        grid_spec=pltpu.PrefetchScalarGridSpec(
            num_scalar_prefetch=1,
            grid=(8,),
            in_specs=[
                columns,
                whole_block(grad_qkv.shape),
                columns,
                whole_block(attended.shape),
                pl.BlockSpec((small.shape[0], size), lambda e, place: (0, shard(e, place))),
                pl.BlockSpec((gain.shape[0], size), lambda e, place: (0, shard(e, place))),
            ]
            + [any_block()] * len(after),
            out_specs=[
                pl.BlockSpec((size, total), lambda e, _: (jnp.minimum(e, 3), 0)),
                pl.BlockSpec((size, total), lambda e, _: (jnp.clip(e - 4, 0, 1), 0)),
                pl.BlockSpec((size, total), lambda e, _: (jnp.clip(e - 6, 0, 1), 0)),
            ],
        ),
        out_shape=[
            jax.ShapeDtypeStruct((4 * size, total), F32),
            jax.ShapeDtypeStruct((2 * size, total), BF16),
            jax.ShapeDtypeStruct((2 * size, total), BF16),
        ],
        name="reduce_parts",
    )(place, normed, grad_qkv, grad, attended, small, gain, *after)


def unpack_body(place_ref, *refs):
    pieces = refs[:8]
    query, key, value, output, small = refs[8:]
    size = pieces[0].shape[0]
    wide, narrow = (query.shape[1], key.shape[1])
    for r, piece in zip(ORDER, pieces):
        start = pl.multiple_of(jnp.bitwise_xor(place_ref[0], r) * size, size)
        rows = pl.ds(start, size)
        part = piece[...].astype(F32)
        query[rows, :] = part[:, :wide]
        key[rows, :] = part[:, wide : wide + narrow]
        value[rows, :] = part[:, wide + narrow : wide + 2 * narrow]
        begin = wide + 2 * narrow
        output[:, rows] = part[:, begin : begin + output.shape[0]].T
        small[rows, :] = part[:, begin + output.shape[0] :]


def assemble_body(share_ref, *refs):
    target = refs[-1]
    size = refs[0].shape[0]
    for r in range(4):
        start = pl.multiple_of(jnp.bitwise_xor(share_ref[0], r) * size, size)
        target[pl.ds(start, size), :] = refs[r][...].astype(target.dtype)


def spread_tensor(value):
    across = swap_y(value)
    return [value, swap_core(value), across, swap_core(across)]


def assemble(share, pieces, dtype, *after):
    size, width = pieces[0].shape
    shapes = [jax.ShapeDtypeStruct((4 * size, width), dtype)]
    return scalar_call(assemble_body, "assemble", share, pieces, shapes, after)[0]


def trade(value, bits):
    return lax.ppermute(value, "expert", [(i, i ^ bits) for i in range(8)])


def swap_y(value):
    return lax.ppermute(value, "tensor", [(i, i ^ 2) for i in range(4)])


def swap_core(value):
    return lax.ppermute(value, "tensor", [(i, i ^ 1) for i in range(4)])


def gather_experts(value):
    column = [value] + [trade(value, bits) for bits in (2, 4, 6)]
    return column + [trade(shard, 1) for shard in column]


def scatter_steps(keep, send_near, send_far, *beside):
    size = keep.shape[0] // 4
    got_far = trade(send_far, 1)
    send_near, got_far, keep = lax.optimization_barrier((send_near, got_far, keep))
    if beside:
        got_far, *beside = lax.optimization_barrier((got_far, *beside))
    far = (keep[2 * size :] + got_far.astype(F32)).astype(BF16)
    got_near = trade(send_near, 1)
    four, six = (trade(far[:size], 4), trade(far[size:], 6))
    near = (keep[size : 2 * size] + got_near[size:].astype(F32)).astype(BF16)
    return (keep, got_near, near, far, (trade(near, 2), four, six), *beside)


def scatter_experts(keep, send_near, send_far, *beside):
    size = keep.shape[0] // 4
    keep, got_near, _, _, back, *beside = scatter_steps(keep, send_near, send_far, *beside)
    total = keep[:size] + got_near[:size].astype(F32)
    for part in back:
        total = total + part.astype(F32)
    return (total, *beside) if beside else total


def scatter_tensor(keep, send, row):
    half = keep + swap_core(send).astype(F32)
    keep = lax.dynamic_index_in_dim(half, row, 0, False)
    send = lax.dynamic_index_in_dim(half, 1 - row, 0, False)
    return keep + swap_y(send.astype(BF16)).astype(F32)


def ordered(index, first, second):
    return jnp.where(
        index == 0, jnp.concatenate([first, second], 0), jnp.concatenate([second, first], 0)
    )


def per_device(
    tokens,
    teacher,
    valid_mask,
    routes,
    first_gain,
    query_weight,
    key_matrix,
    value_matrix,
    output_weight,
    second_gain,
    router_weight,
    expert_in,
    expert_out,
):
    row_count, model_width = tokens.shape
    expert_count = router_weight.shape[1]
    senders = lax.axis_size("expert")
    shares = lax.axis_size("tensor")
    fits = (
        (senders, shares) == (8, 4)
        and expert_count == senders * shares
        and expert_in.shape == (8, 2, model_width // 2, SHARE)
        and row_count == 4 * 128
    )
    if not fits:
        return general_device(
            tokens,
            teacher,
            valid_mask,
            routes,
            first_gain,
            query_weight,
            key_matrix,
            value_matrix,
            output_weight,
            second_gain,
            router_weight,
            expert_in,
            expert_out,
        )
    quarter = row_count // shares
    place = lax.axis_index("expert")
    share = lax.axis_index("tensor")
    row, core = (share // 2, share % 2)
    half_index = place // 4
    half_arg = half_index.reshape(1)
    held = expert_in.shape[0] // 2
    base = 8 * (place % 4) + held * half_index

    share_arg, core_arg, place_arg = (share.reshape(1), core.reshape(1), place.reshape(1))

    def quarter_of(values):
        return lax.dynamic_slice_in_dim(values, share * quarter, quarter, 0)

    local_valid = jnp.sum(valid_mask)
    routes_mine = quarter_of(routes)
    note = jnp.concatenate([routes_mine.T, jnp.full((TOP, quarter), local_valid, jnp.int32)], 0)

    own_pack, near_pack, far_pack = pack_weights(half_arg, expert_in, expert_out)
    near_pack = trade(near_pack, 4)
    far_pack = trade(far_pack, 4)
    own_across = swap_y(own_pack)

    router_rel = lax.dynamic_slice_in_dim(
        jnp.concatenate([router_weight, router_weight], 1), base, expert_count, 1
    )
    router_rel = jnp.pad(
        jnp.concatenate([router_rel, router_rel], 1), ((0, 0), (0, 128 - 2 * expert_count))
    )

    tables = [
        jnp.concatenate([table[:, 0]] * (2 * SHARE // HEAD_DIM), 1)
        for table in rope_tables(row_count, HEAD_DIM)
    ]
    weights = (query_weight, key_matrix, value_matrix, output_weight)
    first_normed, query, keys, values, attended, attn_keep, attn_send = attention_forward(
        core_arg, tokens, first_gain[None], *weights, tables, own_pack
    )
    near_pack, own_across, attn_send = lax.optimization_barrier(
        (near_pack, own_across, attn_send)
    )
    own = [own_pack, swap_core(own_pack), own_across, swap_core(own_across)]
    tokens_mine = quarter_of(tokens).astype(F32)
    near_across = swap_y(near_pack)
    attn_sum = scatter_tensor(attn_keep, attn_send, row)
    near_across, attn_sum, note = lax.optimization_barrier((near_across, attn_sum, note))
    hidden = tokens_mine + RESIDUAL * attn_sum
    scale_two = lax.rsqrt(jnp.mean(hidden * hidden, -1, keepdims=True) + EPS)
    unit_two = hidden * scale_two
    normed_two = (unit_two * second_gain).astype(BF16)
    column = [normed_two] + [trade(normed_two, bits) for bits in (2, 4, 6)]
    notes = [note] + [trade(note, bits) for bits in (2, 4, 6)]
    beside = trade(normed_two, 1)
    across = [trade(shard, 1) for shard in column[1:]]
    far_pack, beside, across[0], across[1], *gathered = lax.optimization_barrier(
        (far_pack, beside, across[0], across[1], *column[1:])
    )
    row_shards = [normed_two, *gathered, beside, *across]
    near = [near_pack, swap_core(near_pack), near_across, swap_core(near_across)]
    far = spread_tensor(far_pack)
    notes = jnp.stack(notes)
    notes = jnp.concatenate([notes, trade(notes, 1)], 0)
    valid_total = jnp.sum(notes[:, TOP, 0]).astype(F32)
    route_rel = jnp.bitwise_and(notes[:, :TOP] - base, expert_count - 1)
    route_rel = route_rel.transpose(0, 2, 1).reshape(senders * quarter, TOP)
    keep, send_near, send_far, pre, gated, gates, expert_rows = experts_forward(
        half_arg,
        row_shards,
        route_rel,
        router_rel,
        own,
        near,
        far,
    )
    moe_sum = scatter_experts(keep, send_near, send_far)

    output = hidden + RESIDUAL * moe_sum
    residual_err = output - quarter_of(teacher).astype(F32)
    valid_rows = quarter_of(valid_mask).astype(F32)[:, None]
    squared_local = jnp.sum(valid_rows * residual_err * residual_err)
    token_total = senders * row_count
    grad_out = token_total / valid_total * valid_rows * residual_err
    grad_moe = (RESIDUAL * grad_out).astype(BF16)
    gate_mean = jnp.sum(grad_moe.astype(F32) * moe_sum, -1, keepdims=True)
    mean_part = -gate_mean * dense_gates(normed_two, routes_mine, router_weight)
    mean_high = mean_part.astype(BF16)
    mean_part = jnp.concatenate([mean_high, (mean_part - mean_high.astype(F32)).astype(BF16)], 1)
    router_pair = jnp.concatenate([router_weight, router_weight], 1)
    mean_rows = jnp.einsum("te,de->td", mean_part, router_pair, preferred_element_type=F32)
    shards = gather_experts(grad_moe)
    packs = (gates, router_rel, pre, own, near, far)
    send_near, send_far, *saved = experts_backward(1, half_arg, shards[4:], *packs)
    keep, pre_grad, logit_grad, grad_rows = experts_backward(
        0, half_arg, shards[:4], *packs, *saved
    )
    keep, got_near, near_rows, far_rows, back = scatter_steps(keep, send_near, send_far)
    other = 1 - half_arg
    in_keep, in_send = grad_expert_ins(other, expert_rows, pre_grad, 0, 2, far_rows)
    in_near, in_far = fold_pairs(in_keep, swap_core(in_send), near_rows)
    in_ready = (in_near + swap_y(in_far).astype(F32)).astype(BF16)
    out_keep, out_send, own_out_keep, own_out_send = grad_expert_outs(
        half_arg, gated, grad_rows, in_far
    )
    grad_hidden, grad_attn, grad_second_part = finish_rows(
        keep,
        got_near,
        *back,
        mean_rows,
        unit_two,
        scale_two,
        second_gain[None],
        grad_out,
        out_send,
        in_ready,
    )
    grad_second_part = jnp.sum(grad_second_part, 0)
    router_part = jnp.einsum(
        "te,td->ed", logit_grad.astype(BF16), expert_rows, preferred_element_type=F32
    )
    router_part = router_part[:expert_count] + router_part[expert_count : 2 * expert_count]
    router_part = lax.dynamic_slice_in_dim(
        jnp.concatenate([router_part, router_part], 0),
        jnp.bitwise_and(expert_count - base, expert_count - 1),
        expert_count,
        0,
    )
    mean_router = jnp.einsum("te,td->ed", mean_part, normed_two, preferred_element_type=F32)
    router_part = router_part + mean_router[:expert_count] + mean_router[expert_count:]

    small = jnp.concatenate(
        [
            router_part,
            grad_second_part[None],
            jnp.full((1, model_width), squared_local),
            jnp.zeros((6, model_width), F32),
        ],
        0,
    )
    small = small + swap_core(small)
    small = small + swap_y(small)
    late_keep, late_send = grad_expert_ins(other, expert_rows, pre_grad, 2, 2, grad_attn)
    pieces = spread_tensor(grad_attn)
    late_near, late_far = fold_pairs(late_keep, swap_core(late_send), pieces[2])
    out_near, out_far = fold_pairs(out_keep, swap_core(out_send), pieces[2])
    out_ready = (out_near + swap_y(out_far).astype(F32)).astype(BF16)
    late_ready = (late_near + swap_y(late_far).astype(F32)).astype(BF16)
    in_back = trade(in_ready, 4)
    grad_attn, grad_qkv, gain_part, one_keep, one_send = attention_backward(
        share_arg, tokens, weights, tables, (query, keys, values), pieces, late_ready, in_back, out_far, small
    )
    late_back = trade(late_ready, 4)
    grad_one = scatter_tensor(one_keep, one_send, row)
    own_out_near, own_out_far = fold_pairs(own_out_keep, swap_core(own_out_send), grad_one)
    own_out_across = swap_y(own_out_far)

    keep, send_near, send_far = reduce_parts(
        place_arg, first_normed, grad_qkv, grad_attn, attended, small, gain_part
    )
    own_in_keep, own_in_send = grad_expert_ins(
        half_arg, expert_rows, pre_grad, 0, held, late_back
    )
    own_in_near, own_in_far = fold_pairs(own_in_keep, swap_core(own_in_send), grad_one)
    own_in_across = swap_y(own_in_far)
    total, late_back = scatter_experts(keep, send_near, send_far, late_back)
    total, own_out_across = lax.optimization_barrier((total.astype(BF16), own_out_across))
    shapes = [
        jax.ShapeDtypeStruct(shape, F32)
        for shape in (
            query_weight.shape,
            key_matrix.shape,
            value_matrix.shape,
            output_weight.shape,
            (model_width, 128),
        )
    ]
    shards = gather_experts(total)
    out_ready, shards[1] = lax.optimization_barrier((out_ready, shards[1]))
    out_back = trade(out_ready, 4)
    grad_query, grad_key, grad_value, grad_output, small = scalar_call(
        unpack_body, "unpack", place_arg, shards, shapes
    )

    gain_part = jnp.sum(small[:, expert_count + 8 : expert_count + 16], 1).reshape(8, -1)
    gain_part = gain_part + swap_core(gain_part)
    gain_part = (gain_part + swap_y(gain_part)).reshape(-1)

    scale_mine = lax.rsqrt(jnp.mean(tokens_mine * tokens_mine, -1, keepdims=True) + EPS)
    unit_mine = tokens_mine * scale_mine
    grad_unit_one = grad_one * first_gain
    grad_tokens = grad_hidden + scale_mine * (
        grad_unit_one - unit_mine * jnp.mean(grad_unit_one * unit_mine, -1, keepdims=True)
    )
    grad_tokens = assemble(share_arg, spread_tensor(grad_tokens.astype(BF16)), F32)
    layer_output = assemble(share_arg, spread_tensor(output.astype(BF16)), BF16)
    grad_expert_out = ordered(
        half_index, own_out_near + own_out_across.astype(F32), out_back.astype(F32)
    )
    grad_expert_in = ordered(
        half_index,
        own_in_near + own_in_across.astype(F32),
        jnp.concatenate([in_back, late_back], 0).astype(F32),
    )
    return (
        layer_output,
        small[0, expert_count + 1] / (2.0 * model_width * valid_total),
        grad_tokens,
        gain_part,
        grad_query,
        grad_key,
        grad_value,
        grad_output,
        small[:, expert_count],
        small[:, :expert_count],
        grad_expert_in,
        grad_expert_out,
    )


def solution(mesh):
    return jax.shard_map(
        per_device,
        mesh=mesh,
        in_specs=(
            P("expert", None),
            P("expert", None),
            P("expert"),
            P("expert", None),
            P(),
            P(None, "tensor"),
            P(None, "tensor"),
            P(None, "tensor"),
            P("tensor", None),
            P(),
            P(),
            P("expert", None, None, "tensor"),
            P("expert", "tensor", None),
        ),
        out_specs=(
            P("expert", None),
            P(),
            P("expert", None),
            P(),
            P(None, "tensor"),
            P(None, "tensor"),
            P(None, "tensor"),
            P("tensor", None),
            P(),
            P(),
            P("expert", None, None, "tensor"),
            P("expert", "tensor", None),
        ),
        check_vma=False,
    )
```

```python
import jax
import jax.numpy as jnp
from jax import lax
from jax.experimental import pallas as pl
from jax.experimental.pallas import tpu as pltpu
from jax.sharding import PartitionSpec as P

HEAD_DIM = 64
TOP = 8
BLOCK = 256


EPS = 1e-06
ATTN_SCALE = 0.015625
RESIDUAL = 0.22
THETA = 10000.0


def shifted(value, axis, steps):
    count = lax.axis_size(axis)
    pairs = [(source, (source + steps) % count) for source in range(count)]
    return lax.ppermute(value, axis, pairs)


def rope_tables(length, head_size):
    half_size = head_size // 2
    frequency = THETA ** (-(jnp.arange(half_size, dtype=jnp.float32) * 2.0) / head_size)
    angle_table = jnp.arange(length, dtype=jnp.float32)[:, None] * frequency[None, :]
    return (jnp.cos(angle_table)[:, None, :], jnp.sin(angle_table)[:, None, :])


def apply_rotary(values, cosine_lookup, sine_lookup):
    half_size = values.shape[-1] // 2
    lower_half, upper_half = (values[..., :half_size], values[..., half_size:])
    return jnp.concatenate(
        [
            lower_half * cosine_lookup - upper_half * sine_lookup,
            upper_half * cosine_lookup + lower_half * sine_lookup,
        ],
        -1,
    )


def unrotate(grads, cosine_lookup, sine_lookup):
    half_size = grads.shape[-1] // 2
    lower_half, upper_half = (grads[..., :half_size], grads[..., half_size:])
    return jnp.concatenate(
        [
            lower_half * cosine_lookup + upper_half * sine_lookup,
            upper_half * cosine_lookup - lower_half * sine_lookup,
        ],
        -1,
    )


def normalize(values):
    row_peak = jnp.max(values, -1, keepdims=True)
    exp_scores = jnp.exp(values - row_peak)
    return exp_scores / jnp.sum(exp_scores, -1, keepdims=True)


def slot_tables(route_ids, expert_count, capacity):
    row_count, top_count = route_ids.shape
    onehot = route_ids[:, :, None] == jnp.arange(expert_count, dtype=jnp.int32)[None, None, :]
    hit_count = jnp.sum(onehot.astype(jnp.int32), 1)
    slot_place = jnp.cumsum(hit_count, 0) - 1
    within = jnp.take_along_axis(slot_place, route_ids, 1)
    dest_slot = route_ids * capacity + within
    pair_count = row_count * top_count
    source = (
        jnp.full((expert_count * capacity,), pair_count, jnp.int32)
        .at[dest_slot.reshape(-1)]
        .set(jnp.arange(pair_count, dtype=jnp.int32))
    )
    live_slot = source < pair_count
    token_row = jnp.minimum(source, pair_count - 1) // top_count
    return (onehot, dest_slot, source, live_slot, token_row)


def general_device(
    tokens,
    teacher,
    valid_mask,
    routes,
    first_gain,
    query_weight,
    key_matrix,
    value_matrix,
    output_weight,
    second_gain,
    router_weight,
    expert_in,
    expert_out,
):
    row_count = tokens.shape[0]
    model_width = tokens.shape[1]
    half_width = model_width // 2
    local_query = query_weight.shape[1] // HEAD_DIM
    local_kv = key_matrix.shape[1] // HEAD_DIM
    query_group_size = local_query // local_kv
    expert_count = router_weight.shape[1]
    row_local = expert_in.shape[0]
    senders = lax.axis_size("expert")
    partner_step = senders // 2
    capacity = 3 * row_count * TOP // (2 * expert_count)
    pair_count = row_count * TOP
    score_rows = min(512, row_count)
    valid_total = lax.psum(jnp.sum(valid_mask).astype(jnp.float32), "expert")
    tokens_f32 = tokens.astype(jnp.float32)
    scale_one = lax.rsqrt(jnp.mean(tokens_f32 * tokens_f32, -1, keepdims=True) + EPS)
    unit_one = tokens_f32 * scale_one
    first_normed = (unit_one * first_gain).astype(jnp.bfloat16)
    cosine_lookup, sine_lookup = rope_tables(row_count, HEAD_DIM)
    query_linear = jnp.dot(first_normed, query_weight, preferred_element_type=jnp.float32).reshape(
        row_count, local_query, HEAD_DIM
    )
    keys_linear = jnp.dot(first_normed, key_matrix, preferred_element_type=jnp.float32).reshape(
        row_count, local_kv, HEAD_DIM
    )
    value_low = jnp.dot(first_normed, value_matrix, preferred_element_type=jnp.float32).astype(
        jnp.bfloat16
    )
    value_low = value_low.reshape(row_count, local_kv, HEAD_DIM)
    query_rotated = apply_rotary(query_linear, cosine_lookup, sine_lookup).astype(jnp.bfloat16)
    keys_rot = apply_rotary(keys_linear, cosine_lookup, sine_lookup).astype(jnp.bfloat16)
    block_of = jnp.arange(row_count, dtype=jnp.int32) // BLOCK

    def scores(start_row):
        stop_row = start_row + score_rows
        query_block = query_rotated.reshape(score_rows, local_kv, query_group_size, HEAD_DIM)
        score_block = (
            jnp.einsum("qhgd,khd->hgqk", query_block, keys_rot, preferred_element_type=jnp.float32)
            * ATTN_SCALE
        )
        allowed = block_of[None, :stop_row] <= block_of[start_row:stop_row, None]
        return (query_block, jnp.where(allowed, score_block, -1e30))

    attn_parts, row_peaks, row_totals = ([], [], [])
    start_row = 0
    query_block, score_block = scores(start_row)
    row_peak = jnp.max(score_block, -1, keepdims=True)
    exp_scores = jnp.exp(score_block - row_peak)
    row_total = jnp.sum(exp_scores, -1, keepdims=True)
    attn_probs = (exp_scores / row_total).astype(jnp.bfloat16)
    attn_parts.append(
        jnp.einsum("hgqk,khd->qhgd", attn_probs, value_low, preferred_element_type=jnp.float32)
    )
    row_peaks.append(row_peak)
    row_totals.append(row_total)
    attended = attn_parts[0].reshape(row_count, local_query * HEAD_DIM).astype(jnp.bfloat16)
    attn_part = jnp.dot(attended, output_weight, preferred_element_type=jnp.float32)
    attn_sum = lax.psum(attn_part, "tensor")
    hidden_state = tokens_f32 + RESIDUAL * attn_sum
    scale_two = lax.rsqrt(jnp.mean(hidden_state * hidden_state, -1, keepdims=True) + EPS)
    unit_two = hidden_state * scale_two
    normed_two = (unit_two * second_gain).astype(jnp.bfloat16)
    router_logits = jnp.dot(normed_two, router_weight, preferred_element_type=jnp.float32)
    onehot, dest_slot, source, live_slot, token_row = slot_tables(routes, expert_count, capacity)
    picked = jnp.sum(jnp.where(onehot, router_logits[:, None, :], 0.0), -1)
    gate_probs = normalize(picked)

    def slot_rows(slot_values):
        split_rows = slot_values.reshape(expert_count, capacity, 2, half_width).transpose(
            2, 0, 1, 3
        )
        return split_rows.reshape(senders, row_local, capacity, half_width)

    def slot_columns(returned, width):
        joined = returned.reshape(2, expert_count, capacity, width).transpose(1, 2, 0, 3)
        return joined.reshape(expert_count * capacity, 2, width)

    send_rows = slot_rows(
        jnp.where(live_slot[:, None], normed_two[token_row], jnp.zeros((), jnp.bfloat16))
    )
    received = lax.all_to_all(send_rows, "expert", split_axis=0, concat_axis=2, tiled=True)
    expert_rows = received.reshape(row_local, senders * capacity, half_width)
    gate_up_part = jnp.einsum(
        "rmd,rcdf->rmcf", expert_rows, expert_in, preferred_element_type=jnp.float32
    )
    gate_up_pre = gate_up_part + shifted(gate_up_part, "expert", partner_step)
    gate_pre = gate_up_pre[:, :, 0]
    up_pre = gate_up_pre[:, :, 1]
    inner_act = (jax.nn.silu(gate_pre) * up_pre).astype(jnp.bfloat16)
    expert_result = jnp.einsum(
        "rmf,rfd->rmd", inner_act, expert_out, preferred_element_type=jnp.float32
    )
    expert_result = expert_result.astype(jnp.bfloat16).reshape(
        row_local, senders, capacity, half_width
    )
    returned = lax.all_to_all(expert_result, "expert", split_axis=1, concat_axis=0, tiled=True)
    per_route = slot_columns(returned, half_width).reshape(expert_count * capacity, model_width)[
        dest_slot
    ]
    moe_part = jnp.sum(gate_probs[:, :, None] * per_route, 1)
    moe_sum = lax.psum(moe_part, "tensor")
    output = hidden_state + RESIDUAL * moe_sum
    residual_err = output - teacher.astype(jnp.float32)
    valid_rows = valid_mask.astype(jnp.float32)
    squared_local = jnp.sum(valid_rows * jnp.sum(residual_err * residual_err, -1))
    token_total = senders * row_count
    grad_out = token_total / valid_total * valid_rows[:, None] * residual_err
    grad_moe = (RESIDUAL * grad_out).astype(jnp.bfloat16)
    gate_part = jnp.einsum("td,tkd->tk", grad_moe, per_route, preferred_element_type=jnp.float32)
    gate_slot = gate_probs.reshape(pair_count)[jnp.minimum(source, pair_count - 1)]
    grad_slots = jnp.where(live_slot[:, None], gate_slot[:, None] * grad_moe[token_row], 0.0)
    grad_received = lax.all_to_all(
        slot_rows(grad_slots.astype(jnp.bfloat16)),
        "expert",
        split_axis=0,
        concat_axis=2,
        tiled=True,
    )
    grad_expert = grad_received.reshape(row_local, senders * capacity, half_width)
    grad_inner_part = jnp.einsum(
        "rmd,rfd->rmf", grad_expert, expert_out, preferred_element_type=jnp.float32
    )
    grad_inner = grad_inner_part + shifted(grad_inner_part, "expert", partner_step)
    grad_expert_out = jnp.einsum(
        "rmf,rmd->rfd", inner_act, grad_expert, preferred_element_type=jnp.float32
    )
    sigmoid_gate = jax.nn.sigmoid(gate_pre)
    grad_gate = grad_inner * up_pre * sigmoid_gate * (1.0 + gate_pre * (1.0 - sigmoid_gate))
    grad_up = grad_inner * (gate_pre * sigmoid_gate)
    grad_pre = jnp.stack([grad_gate, grad_up], 2).astype(jnp.bfloat16)
    grad_expert_in = jnp.einsum(
        "rmd,rmcf->rcdf", expert_rows, grad_pre, preferred_element_type=jnp.float32
    )
    grad_slot_rows = jnp.einsum(
        "rmcf,rcdf->rmd", grad_pre, expert_in, preferred_element_type=jnp.float32
    )
    grad_slot_rows = grad_slot_rows.astype(jnp.bfloat16).reshape(
        row_local, senders, capacity, half_width
    )
    grad_back = lax.all_to_all(grad_slot_rows, "expert", split_axis=1, concat_axis=0, tiled=True)
    grad_back = slot_columns(grad_back, half_width).reshape(expert_count * capacity, model_width)
    grad_two_part = jnp.sum(grad_back[dest_slot].astype(jnp.float32), 1)
    grad_two_experts, grad_gates = lax.psum((grad_two_part, gate_part), "tensor")
    grad_picked = gate_probs * (grad_gates - jnp.sum(gate_probs * grad_gates, -1, keepdims=True))
    grad_logits = jnp.sum(jnp.where(onehot, grad_picked[:, :, None], 0.0), 1).astype(jnp.bfloat16)
    grad_router = jnp.einsum(
        "td,te->de", normed_two, grad_logits, preferred_element_type=jnp.float32
    )
    grad_two = grad_two_experts + jnp.einsum(
        "te,de->td", grad_logits, router_weight, preferred_element_type=jnp.float32
    )
    grad_second_gain = jnp.sum(grad_two * unit_two, 0)
    grad_unit_two = grad_two * second_gain
    grad_hidden = grad_out + scale_two * (
        grad_unit_two - unit_two * jnp.mean(grad_unit_two * unit_two, -1, keepdims=True)
    )
    grad_attn = (RESIDUAL * grad_hidden).astype(jnp.bfloat16)
    grad_output = jnp.einsum("tc,td->cd", attended, grad_attn, preferred_element_type=jnp.float32)
    grad_attended = jnp.einsum(
        "td,cd->tc", grad_attn, output_weight, preferred_element_type=jnp.float32
    )
    grad_attended = grad_attended.astype(jnp.bfloat16).reshape(
        row_count, local_kv, query_group_size, HEAD_DIM
    )
    grad_query_parts = []
    grad_keys = jnp.zeros((row_count, local_kv, HEAD_DIM), jnp.float32)
    grad_values = jnp.zeros((row_count, local_kv, HEAD_DIM), jnp.float32)
    for block_index, start_row in enumerate(range(0, row_count, score_rows)):
        stop_row = start_row + score_rows
        query_block, score_block = scores(start_row)
        attn_probs = jnp.exp(score_block - row_peaks[block_index]) / row_totals[block_index]
        probs_low = attn_probs.astype(jnp.bfloat16)
        grad_probs = jnp.einsum(
            "qhgd,khd->hgqk", grad_attended, value_low, preferred_element_type=jnp.float32
        )
        grad_scores = attn_probs * (
            grad_probs - jnp.sum(attn_probs * grad_probs, -1, keepdims=True)
        )
        grad_scores = grad_scores.astype(jnp.bfloat16)
        grad_query_parts.append(
            ATTN_SCALE
            * jnp.einsum(
                "hgqk,khd->qhgd", grad_scores, keys_rot, preferred_element_type=jnp.float32
            )
        )
        grad_keys = grad_keys.at[:stop_row].add(
            ATTN_SCALE
            * jnp.einsum(
                "hgqk,qhgd->khd", grad_scores, query_block, preferred_element_type=jnp.float32
            )
        )
        grad_values = grad_values.at[:stop_row].add(
            jnp.einsum(
                "hgqk,qhgd->khd", probs_low, grad_attended, preferred_element_type=jnp.float32
            )
        )
    grad_query_rot = grad_query_parts[0].reshape(row_count, local_query, HEAD_DIM)
    grad_query_low = unrotate(grad_query_rot, cosine_lookup, sine_lookup).reshape(
        row_count, local_query * HEAD_DIM
    )
    grad_query_low = grad_query_low.astype(jnp.bfloat16)
    grad_keys_low = unrotate(grad_keys, cosine_lookup, sine_lookup).reshape(
        row_count, local_kv * HEAD_DIM
    )
    grad_keys_low = grad_keys_low.astype(jnp.bfloat16)
    grad_values_low = grad_values.reshape(row_count, local_kv * HEAD_DIM).astype(jnp.bfloat16)
    grad_query = jnp.einsum(
        "td,tc->dc", first_normed, grad_query_low, preferred_element_type=jnp.float32
    )
    grad_key = jnp.einsum(
        "td,tc->dc", first_normed, grad_keys_low, preferred_element_type=jnp.float32
    )
    grad_value = jnp.einsum(
        "td,tc->dc", first_normed, grad_values_low, preferred_element_type=jnp.float32
    )
    grad_one_part = (
        jnp.einsum("tc,dc->td", grad_query_low, query_weight, preferred_element_type=jnp.float32)
        + jnp.einsum("tc,dc->td", grad_keys_low, key_matrix, preferred_element_type=jnp.float32)
        + jnp.einsum("tc,dc->td", grad_values_low, value_matrix, preferred_element_type=jnp.float32)
    )
    grad_one = lax.psum(grad_one_part.astype(jnp.bfloat16), "tensor").astype(jnp.float32)
    grad_first_gain = jnp.sum(grad_one * unit_one, 0)
    grad_unit_one = grad_one * first_gain
    grad_tokens = grad_hidden + scale_one * (
        grad_unit_one - unit_one * jnp.mean(grad_unit_one * unit_one, -1, keepdims=True)
    )
    reduced = lax.psum(
        (
            grad_first_gain,
            grad_query,
            grad_key,
            grad_value,
            grad_output,
            grad_second_gain,
            grad_router,
            squared_local,
        ),
        "expert",
    )
    loss_value = reduced[7] / (2.0 * model_width * valid_total)
    return (
        output.astype(jnp.bfloat16),
        loss_value,
        grad_tokens,
        reduced[0],
        reduced[1],
        reduced[2],
        reduced[3],
        reduced[4],
        reduced[5],
        reduced[6],
        grad_expert_in,
        grad_expert_out,
    )


BF16 = jnp.bfloat16
F32 = jnp.float32
CHUNK = 256
SHARE = 128
PACK = 12 * SHARE
NT = (((1,), (1,)), ((), ()))
ORDER = (0, 2, 4, 6, 1, 3, 5, 7)


def whole_block(shape):
    return pl.BlockSpec(shape, lambda e, *_: (0,) * len(shape))


def any_block():
    return pl.BlockSpec(memory_space=pl.ANY)


def pack_body(half_ref, own_in, own_out, other_in, other_out, *refs):
    own, near, far = refs[-3:]
    step = pl.program_id(0)

    def fill(target, source_in, source_out):
        for c in range(2):
            target[c * 4 * SHARE : (c + 1) * 4 * SHARE, :] = source_in[0, c]
        for k in range(4):
            target[(8 + k) * SHARE : (9 + k) * SHARE, :] = source_out[
                0, :, k * SHARE : (k + 1) * SHARE
            ]

    fill(own, own_in, own_out)

    @pl.when(step < 2)
    def _():
        fill(near, other_in, other_out)

    @pl.when(step >= 2)
    def _():
        fill(far, other_in, other_out)


def pack_weights(half_index, expert_in, expert_out, *after):
    held = expert_in.shape[0] // 2
    in_shape = (1,) + expert_in.shape[1:]
    out_shape = (1,) + expert_out.shape[1:]
    shapes = [(held * PACK, SHARE), (held // 2 * PACK, SHARE), (held // 2 * PACK, SHARE)]
    block = (PACK, SHARE)
    return pl.pallas_call(
        pack_body,
        grid_spec=pltpu.PrefetchScalarGridSpec(
            num_scalar_prefetch=1,
            grid=(held,),
            in_specs=[
                pl.BlockSpec(in_shape, lambda e, half: (half[0] * held + e, 0, 0, 0)),
                pl.BlockSpec(out_shape, lambda e, half: (half[0] * held + e, 0, 0)),
                pl.BlockSpec(in_shape, lambda e, half: ((1 - half[0]) * held + e, 0, 0, 0)),
                pl.BlockSpec(out_shape, lambda e, half: ((1 - half[0]) * held + e, 0, 0)),
            ]
            + [any_block()] * len(after),
            out_specs=[
                pl.BlockSpec(block, lambda e, half: (e, 0)),
                pl.BlockSpec(block, lambda e, half: (jnp.minimum(e, 1), 0)),
                pl.BlockSpec(block, lambda e, half: (jnp.maximum(e - 2, 0), 0)),
            ],
        ),
        out_shape=[jax.ShapeDtypeStruct(shape, BF16) for shape in shapes],
        name="pack_weights",
    )(half_index, expert_in, expert_out, expert_in, expert_out, *after)


def weight_copies(own, other, own_row, other_row, half, in_buf, out_buf, sems, slot):
    copies = []
    for q in range(4):
        for pack, row, side in ((own[q], own_row, half), (other[q], other_row, 1 - half)):
            for c in range(2):
                copies.append(
                    (
                        pack.at[pl.ds(pl.multiple_of(row + c * 4 * SHARE, SHARE), 4 * SHARE)],
                        in_buf.at[
                            slot,
                            pl.ds(pl.multiple_of(side * 4 * SHARE, SHARE), 4 * SHARE),
                            pl.ds((2 * q + c) * SHARE, SHARE),
                        ],
                    )
                )
            for k in range(4):
                copies.append(
                    (
                        pack.at[pl.ds(pl.multiple_of(row + (8 + k) * SHARE, SHARE), SHARE)],
                        out_buf.at[slot, side, pl.ds(q * SHARE, SHARE), pl.ds(k * SHARE, SHARE)],
                    )
                )
    return [
        pltpu.make_async_copy(source, target, sems.at[slot, n])
        for n, (source, target) in enumerate(copies)
    ]


def stream_weights(first, packs, half, in_buf, out_buf, sems):
    step = pl.program_id(0)
    slot = lax.rem(step, 2)
    own, near, far = (packs[0:4], packs[4:8], packs[8:12])

    def start(index, target):
        expert = first + index

        def begin(other, start_row):
            for copy in weight_copies(
                own, other, expert * PACK, start_row, half, in_buf, out_buf, sems, target
            ):
                copy.start()

        if not far:
            begin(near, index * PACK)
            return

        @pl.when(expert < 2)
        def _():
            begin(near, expert * PACK)

        @pl.when(expert >= 2)
        def _():
            begin(far, (expert - 2) * PACK)

    @pl.when(step == 0)
    def _():
        start(0, 0)

    @pl.when(step + 1 < pl.num_programs(0))
    def _():
        start(step + 1, 1 - slot)

    def wait():
        for copy in weight_copies(own, near, 0, 0, half, in_buf, out_buf, sems, slot):
            copy.wait()

    return (step, slot, wait)


def weight_scratch(width, hidden):
    return [
        pltpu.VMEM((2, width, 2 * hidden), BF16),
        pltpu.VMEM((2, 2, hidden, width // 2), BF16),
        pltpu.SemaphoreType.DMA((2, 48)),
    ]


def split_pairs(values):
    blocks = [values[:, i * SHARE : (i + 1) * SHARE] for i in range(values.shape[1] // SHARE)]
    return (jnp.concatenate(blocks[0::2], 1), jnp.concatenate(blocks[1::2], 1))


def join_pairs(first, second):
    blocks = []
    for i in range(first.shape[1] // SHARE):
        blocks.append(first[:, i * SHARE : (i + 1) * SHARE])
        blocks.append(second[:, i * SHARE : (i + 1) * SHARE])
    return jnp.concatenate(blocks, 1)


def chunk_loop(row_count, body):
    def step(i, carry):
        body(pl.ds(pl.multiple_of(i * CHUNK, CHUNK), CHUNK))
        return carry

    lax.fori_loop(0, row_count // CHUNK, step, 0)


def gate_column(gates, expert):
    lane = lax.broadcasted_iota(jnp.int32, gates.shape, 1)
    return jnp.sum(jnp.where(lane == expert, gates, 0.0), -1, keepdims=True)


def dense_gates(rows, ids, router):
    logits = jnp.dot(rows, router, preferred_element_type=F32)
    lane = lax.broadcasted_iota(jnp.int32, logits.shape, 1)
    mask = ids[:, 0:1] == lane
    for k in range(1, TOP):
        mask = mask | (ids[:, k : k + 1] == lane)
    masked = jnp.where(mask, logits, -1e30)
    powers = jnp.where(mask, jnp.exp(masked - jnp.max(masked, -1, keepdims=True)), 0.0)
    return powers / jnp.sum(powers, -1, keepdims=True)


def apply_expert(rows, expert, slot, rows_ref, gate_ref, pre_ref, gated_ref, in_buf):
    pre = jnp.dot(rows_ref[rows, :], in_buf[slot], preferred_element_type=F32)
    pre_ref[0, rows, :] = pre.astype(BF16)
    gate_pre, up_pre = split_pairs(pre)
    weight = gate_column(gate_ref[rows, :], expert)
    gated = (weight * (gate_pre * jax.nn.sigmoid(gate_pre) * up_pre)).astype(BF16)
    gated_ref[0, rows, :] = gated
    return gated


def forward_first(half_ref, *refs):
    shards = refs[:8]
    route_ref, router_ref = refs[8:10]
    packs = refs[10:18]
    acc, pre_ref, gated_ref, gate_ref, rows_ref, in_buf, out_buf, sems = refs[18:]
    step, slot, wait = stream_weights(0, packs, half_ref[0], in_buf, out_buf, sems)
    row_count, width = acc.shape
    size = row_count // 8

    @pl.when(step == 0)
    def _():
        for i in range(8):
            rows_ref[i * size : (i + 1) * size, :] = shards[i][...]
        acc[...] = jnp.zeros_like(acc)

        def gating(rows):
            gate_ref[rows, :] = dense_gates(rows_ref[rows, :], route_ref[rows, :], router_ref[...])

        chunk_loop(row_count, gating)

    wait()

    def mlp(rows):
        gated = apply_expert(rows, step, slot, rows_ref, gate_ref, pre_ref, gated_ref, in_buf)
        for side in range(2):
            columns = slice(side * width // 2, (side + 1) * width // 2)
            acc[rows, columns] += jnp.dot(gated, out_buf[slot, side], preferred_element_type=F32)

    chunk_loop(row_count, mlp)


def forward_second(half_ref, *refs):
    rows_ref, gate_ref, start_ref = refs[:3]
    packs = refs[3:11]
    pre_ref, gated_ref = refs[-6:-4]
    targets = refs[13:-6]
    acc, in_buf, out_buf, sems = refs[-4:]
    step, slot, wait = stream_weights(2, packs, half_ref[0], in_buf, out_buf, sems)
    row_count, width = acc.shape

    wait()

    def mlp(rows, source):
        gated = apply_expert(rows, step + 2, slot, rows_ref, gate_ref, pre_ref, gated_ref, in_buf)
        for side in range(2):
            columns = slice(side * width // 2, (side + 1) * width // 2)
            acc[rows, columns] = source[rows, columns] + jnp.dot(
                gated, out_buf[slot, side], preferred_element_type=F32
            )

    @pl.when(step == 0)
    def _():
        acc[...] = start_ref[...]

    chunk_loop(row_count, lambda rows: mlp(rows, acc))

    @pl.when(step == pl.num_programs(0) - 1)
    def _():
        spread(acc, targets)


def spread(acc, targets):
    size = acc.shape[0] // len(targets)
    for i, target in enumerate(targets):
        target[...] = acc[i * size : (i + 1) * size, :].astype(target.dtype)


def spread_specs(part, row_count, width):
    if part == 0:
        shapes = [jax.ShapeDtypeStruct((row_count // 2, width), F32)]
    else:
        shapes = [jax.ShapeDtypeStruct((row_count // 4, width), BF16)] * 2
    return ([whole_block(s.shape) for s in shapes], shapes)


def half_rows(shape, part):
    block = (shape[0] // 2,) + shape[1:]
    return pl.BlockSpec(block, lambda e, *_: (part, 0))


def half_expert(shape, part, first=0):
    block = (1, shape[1] // 2) + shape[2:]
    return pl.BlockSpec(block, lambda e, *_: (e + first, part, 0))


def expert_block(shape, first=0):
    return pl.BlockSpec((1,) + shape[1:], lambda e, *_: (e + first,) + (0,) * (len(shape) - 1))


def experts_forward(half_index, shards, route_ids, router, own, near, far):
    size, width = shards[0].shape
    row_count = 8 * size
    local = own[0].shape[0] // PACK
    hidden = 4 * SHARE
    sums = jax.ShapeDtypeStruct((row_count, width), F32)
    pre = jax.ShapeDtypeStruct((local, row_count, 2 * hidden), BF16)
    gated = jax.ShapeDtypeStruct((local, row_count, hidden), BF16)
    gates = jax.ShapeDtypeStruct((row_count, 128), F32)
    rows = jax.ShapeDtypeStruct((row_count, width), BF16)
    sums_a, pre_a, gated_a, gates, rows = pl.pallas_call(
        forward_first,
        grid_spec=pltpu.PrefetchScalarGridSpec(
            num_scalar_prefetch=1,
            grid=(2,),
            in_specs=[whole_block(v.shape) for v in (*shards, route_ids, router)]
            + [any_block()] * 8,
            out_specs=[
                whole_block(sums.shape),
                expert_block(pre.shape),
                expert_block(gated.shape),
                whole_block(gates.shape),
                whole_block(rows.shape),
            ],
            scratch_shapes=weight_scratch(width, hidden),
        ),
        out_shape=[sums, pre, gated, gates, rows],
        name="experts_forward_a",
    )(half_index, *shards, route_ids, router, *own, *near)

    def second(part, pre_a, gated_a):
        specs, shapes = spread_specs(part, row_count, width)
        return pl.pallas_call(
            forward_second,
            grid_spec=pltpu.PrefetchScalarGridSpec(
                num_scalar_prefetch=1,
                grid=(2,),
                in_specs=[half_rows(v.shape, part) for v in (rows, gates, sums)]
                + [any_block()] * 10,
                out_specs=specs
                + [half_expert(pre.shape, part, 2), half_expert(gated.shape, part, 2)],
                scratch_shapes=[pltpu.VMEM((row_count // 2, width), F32)]
                + weight_scratch(width, hidden),
            ),
            out_shape=shapes + [pre, gated],
            input_output_aliases={12: len(shapes), 13: len(shapes) + 1},
            name="experts_forward_b",
        )(half_index, rows, gates, sums_a, *own, *far, pre_a, gated_a)

    send_near, send_far, pre_a, gated_a = second(1, pre_a, gated_a)
    keep, pre_a, gated_a = second(0, pre_a, gated_a)
    return (keep, send_near, send_far, pre_a, gated_a, gates, rows)


def backward_body(half_ref, *refs):
    shards = refs[:4]
    gate_ref, router_ref, pre_ref = refs[4:7]
    packs = refs[7:19]
    pre_grad_ref, logit_ref, grad_ref = refs[-7:-4]
    acc, in_buf, out_buf, sems = refs[-4:]
    step, slot, wait = stream_weights(0, packs, half_ref[0], in_buf, out_buf, sems)
    row_count, width = grad_ref.shape
    size = row_count // 4
    targets = [ref for ref in refs[19:-7] if ref.shape[0] * 2 == row_count]
    targets = targets or [refs[-8]]

    @pl.when(step == 0)
    def _():
        for i in range(4):
            grad_ref[i * size : (i + 1) * size, :] = shards[i][...]
        acc[...] = jnp.zeros_like(acc)
        logit_ref[...] = jnp.zeros_like(logit_ref)

    wait()

    def mlp(rows):
        plain = lax.dot_general(
            grad_ref[rows, : width // 2], out_buf[slot, 0], NT, preferred_element_type=F32
        ) + lax.dot_general(
            grad_ref[rows, width // 2 :], out_buf[slot, 1], NT, preferred_element_type=F32
        )
        gate_pre, up_pre = split_pairs(pre_ref[0, rows, :].astype(F32))
        weight = gate_column(gate_ref[rows, :], step)
        sigmoid = jax.nn.sigmoid(gate_pre)
        act = gate_pre * sigmoid
        grad_weight = jnp.sum(act * up_pre * plain, -1, keepdims=True)
        scaled = weight * plain
        pre_grad = join_pairs(
            scaled * up_pre * (sigmoid + act * (1.0 - sigmoid)), scaled * act
        ).astype(BF16)
        pre_grad_ref[0, rows, :] = pre_grad
        old = logit_ref[rows, :]
        lane = lax.broadcasted_iota(jnp.int32, old.shape, 1)
        value = weight * grad_weight
        high = value.astype(BF16).astype(F32)
        logit_ref[rows, :] = jnp.where(
            lane == step, high, jnp.where(lane == step + 32, value - high, old)
        )
        acc[rows, :] += lax.dot_general(pre_grad, in_buf[slot], NT, preferred_element_type=F32)

    chunk_loop(row_count, mlp)

    @pl.when(step == pl.num_programs(0) - 1)
    def _():
        def router(rows):
            acc[rows, :] += lax.dot_general(
                logit_ref[rows, :].astype(BF16), router_ref[...], NT, preferred_element_type=F32
            )

        chunk_loop(row_count, router)
        spread(acc, targets)


def experts_backward(part, half_index, shards, gates, router, pre, own, near, far, *before):
    row_count, width = (8 * shards[0].shape[0], shards[0].shape[1])
    local = pre.shape[0]
    specs, shapes = spread_specs(part, row_count, width)
    saved = [
        jax.ShapeDtypeStruct(pre.shape, BF16),
        jax.ShapeDtypeStruct((row_count, 128), F32),
        jax.ShapeDtypeStruct((row_count, width), BF16),
    ]
    return pl.pallas_call(
        backward_body,
        grid_spec=pltpu.PrefetchScalarGridSpec(
            num_scalar_prefetch=1,
            grid=(local,),
            in_specs=[whole_block(v.shape) for v in shards]
            + [half_rows(gates.shape, part), whole_block(router.shape)]
            + [half_expert(pre.shape, part)]
            + [any_block()] * (12 + len(before)),
            out_specs=specs
            + [half_expert(pre.shape, part)]
            + [half_rows(v.shape, part) for v in saved[1:]],
            scratch_shapes=[pltpu.VMEM((row_count // 2, width), F32)]
            + weight_scratch(width, 4 * SHARE),
        ),
        out_shape=shapes + saved,
        input_output_aliases={20 + i: len(shapes) + i for i in range(len(before))},
        name="experts_backward",
    )(half_index, *shards, gates, router, pre, *own, *near, *far, *before)


def grad_out_body(half_ref, gated_ref, other_ref, mine_ref, *refs):
    *outs, turned = refs[-5:]
    turned[...] = gated_ref[0].T

    def pair(q, carry):
        for n, source in ((0, other_ref), (2, mine_ref)):
            for odd in range(2):
                rows = pl.ds(pl.multiple_of((2 * q + odd) * SHARE, SHARE), SHARE)
                product = jnp.dot(turned[rows, :], source[...], preferred_element_type=F32)
                outs[n + odd][q, 0] = product.astype(BF16)
        return carry

    lax.fori_loop(0, 2, pair, 0)


def grad_expert_outs(half_index, gated, grads, *after):
    local, row_count, hidden = gated.shape
    width = grads.shape[1]
    half_spec = (row_count, width // 2)
    shape = (2, local, SHARE, width // 2)
    return pl.pallas_call(
        grad_out_body,
        grid_spec=pltpu.PrefetchScalarGridSpec(
            num_scalar_prefetch=1,
            grid=(local,),
            in_specs=[
                expert_block(gated.shape),
                pl.BlockSpec(half_spec, lambda e, half: (0, 1 - half[0])),
                pl.BlockSpec(half_spec, lambda e, half: (0, half[0])),
            ]
            + [any_block()] * len(after),
            out_specs=[pl.BlockSpec((2, 1) + shape[2:], lambda e, *_: (0, e, 0, 0))] * 4,
            scratch_shapes=[pltpu.VMEM((hidden, row_count), BF16)],
        ),
        out_shape=[jax.ShapeDtypeStruct(shape, BF16)] * 4,
        name="grad_expert_out",
    )(half_index, gated, grads, grads, *after)


def grad_in_body(half_ref, rows_ref, pre_ref, *refs):
    keep_ref, send_ref, turned = refs[-3:]

    @pl.when(pl.program_id(0) == 0)
    def _():
        turned[...] = rows_ref[...].T

    def part(i, carry):
        rows = pl.ds(pl.multiple_of(i * CHUNK, CHUNK), CHUNK)
        product = jnp.dot(turned[rows, :], pre_ref[0], preferred_element_type=F32).astype(BF16)
        for q in range(4):
            for c in range(2):
                start = (2 * q + c) * SHARE
                (keep_ref, send_ref)[q % 2][q // 2, 0, c, rows] = product[:, start : start + SHARE]
        return carry

    lax.fori_loop(0, turned.shape[0] // CHUNK, part, 0)


def grad_expert_ins(half_index, rows, pre_grad, first, count, *after):
    local, row_count, wide = pre_grad.shape
    width = rows.shape[1]
    shape = (2, count, 2, width // 2, SHARE)
    return pl.pallas_call(
        grad_in_body,
        grid_spec=pltpu.PrefetchScalarGridSpec(
            num_scalar_prefetch=1,
            grid=(count,),
            in_specs=[
                pl.BlockSpec((row_count, width // 2), lambda e, half: (0, half[0])),
                expert_block(pre_grad.shape, first),
            ]
            + [any_block()] * len(after),
            out_specs=[pl.BlockSpec((2, 1) + shape[2:], lambda e, *_: (0, e, 0, 0, 0))] * 2,
            scratch_shapes=[pltpu.VMEM((width // 2, row_count), BF16)],
        ),
        out_shape=[jax.ShapeDtypeStruct(shape, BF16)] * 2,
        name="grad_expert_in",
    )(half_index, rows, pre_grad, *after)


def fold_body(keep_ref, got_ref, *refs):
    near_ref, far_ref = refs[-2:]
    near_ref[...] = keep_ref[0].astype(F32) + got_ref[0].astype(F32)
    far_ref[...] = (keep_ref[1].astype(F32) + got_ref[1].astype(F32)).astype(BF16)


def fold_pairs(keep, got, *after):
    shape = keep.shape
    rest = (0,) * (len(shape) - 2)
    pair = pl.BlockSpec((2, 1) + shape[2:], lambda e: (0, e) + rest)
    single = pl.BlockSpec((1,) + shape[2:], lambda e: (e,) + rest)
    return pl.pallas_call(
        fold_body,
        grid=(shape[1],),
        in_specs=[pair, pair] + [any_block()] * len(after),
        out_specs=[single, single],
        out_shape=[
            jax.ShapeDtypeStruct(shape[1:], F32),
            jax.ShapeDtypeStruct(shape[1:], BF16),
        ],
        name="fold_pairs",
    )(keep, got, *after)


def finish_body(keep, near, four, two, extra, unit, scale, gain, grad_out, *refs):
    hidden_ref, attn_ref, gain_ref = refs[-3:]
    total = keep[...] + near[...].astype(F32) + extra[...]
    for part in (four, two):
        total = total + part[...].astype(F32)
    gain_ref[...] = jnp.sum((total * unit[...]).reshape(-1, 8, total.shape[1]), 0)
    weighted = total * gain[...]
    mean = jnp.mean(weighted * unit[...], -1, keepdims=True)
    hidden = grad_out[...] + scale[...] * (weighted - unit[...] * mean)
    hidden_ref[...] = hidden
    attn_ref[...] = (RESIDUAL * hidden).astype(BF16)


def finish_rows(keep, near, four, two, extra, unit, scale, gain, grad_out, *after):
    size, width = unit.shape
    block = pl.BlockSpec((size, width), lambda e: (0, 0))
    return pl.pallas_call(
        finish_body,
        grid=(1,),
        in_specs=[block] * 6
        + [whole_block((size, 1)), whole_block((1, width)), block]
        + [any_block()] * len(after),
        out_specs=[block, block, whole_block((8, width))],
        out_shape=[
            jax.ShapeDtypeStruct((size, width), F32),
            jax.ShapeDtypeStruct((size, width), BF16),
            jax.ShapeDtypeStruct((8, width), F32),
        ],
        name="finish_rows",
    )(keep, near, four, two, extra, unit, scale, gain, grad_out, *after)


def rotated(values, cosine, sine, sign):
    width = values.shape[1]
    lane = lax.broadcasted_iota(jnp.int32, values.shape, 1)
    lower = lax.rem(lane, HEAD_DIM) < HEAD_DIM // 2
    ahead = pltpu.roll(values, width - HEAD_DIM // 2, 1)
    behind = pltpu.roll(values, HEAD_DIM // 2, 1)
    turned = jnp.where(lower, -ahead, behind)
    repeat = width // cosine.shape[1]
    cosine = jnp.concatenate([cosine] * repeat, 1)
    sine = jnp.concatenate([sine] * repeat, 1)
    return values * cosine + sign * (turned * sine)


def head(values, index, start=0, stop=None):
    return values[start:stop, index * HEAD_DIM : (index + 1) * HEAD_DIM]


def probabilities(query, keys):
    scores = lax.dot_general(query, keys, NT, preferred_element_type=F32) * ATTN_SCALE
    powers = jnp.exp(scores - jnp.max(scores, -1, keepdims=True))
    return powers / jnp.sum(powers, -1, keepdims=True)


def attention_forward_body(
    core_ref, tokens, gain, query_w, key_w, value_w, output_w, cosine, sine, *refs
):
    normed, query, keys, values, attended, keep, send = refs[-7:]
    x = tokens[...].astype(F32)
    scale = lax.rsqrt(jnp.mean(x * x, -1, keepdims=True) + EPS)
    normed[...] = (x * scale * gain[...]).astype(BF16)
    low = normed[...]
    linear = jnp.dot(low, query_w[...], preferred_element_type=F32)
    query[...] = rotated(linear, cosine[...], sine[...], 1.0).astype(BF16)
    linear = jnp.dot(low, key_w[...], preferred_element_type=F32)
    keys[...] = rotated(linear, cosine[...], sine[...], 1.0).astype(BF16)
    values[...] = jnp.dot(low, value_w[...], preferred_element_type=F32).astype(BF16)
    group = query.shape[1] // keys.shape[1]
    for start in range(0, tokens.shape[0], BLOCK):
        stop = start + BLOCK
        parts = []
        for h in range(query.shape[1] // HEAD_DIM):
            probs = probabilities(head(query, h, start, stop), head(keys, h // group, 0, stop))
            parts.append(
                jnp.dot(
                    probs.astype(BF16),
                    head(values, h // group, 0, stop),
                    preferred_element_type=F32,
                )
            )
        attended[start:stop, :] = jnp.concatenate(parts, 1).astype(BF16)
    size = tokens.shape[0] // 4
    for r in range(2):
        for target, core in ((keep, core_ref[0]), (send, 1 - core_ref[0])):
            rows = pl.ds(pl.multiple_of((2 * r + core) * size, size), size)
            part = jnp.dot(attended[rows, :], output_w[...], preferred_element_type=F32)
            target[r] = part.astype(target.dtype)


def scalar_call(body, name, scalar, inputs, shapes, after=(), scratch=()):
    return pl.pallas_call(
        body,
        grid_spec=pltpu.PrefetchScalarGridSpec(
            num_scalar_prefetch=1,
            grid=(1,),
            in_specs=[whole_block(v.shape) for v in inputs] + [any_block()] * len(after),
            out_specs=[whole_block(s.shape) for s in shapes],
            scratch_shapes=list(scratch),
        ),
        out_shape=shapes,
        name=name,
    )(scalar, *inputs, *after)


def attention_forward(core, tokens, gain, query_w, key_w, value_w, output_w, tables, *after):
    rows, width = tokens.shape
    shapes = [
        jax.ShapeDtypeStruct((rows, width), BF16),
        jax.ShapeDtypeStruct((rows, query_w.shape[1]), BF16),
        jax.ShapeDtypeStruct((rows, key_w.shape[1]), BF16),
        jax.ShapeDtypeStruct((rows, value_w.shape[1]), BF16),
        jax.ShapeDtypeStruct((rows, query_w.shape[1]), BF16),
        jax.ShapeDtypeStruct((2, rows // 4, width), F32),
        jax.ShapeDtypeStruct((2, rows // 4, width), BF16),
    ]
    inputs = (tokens, gain, query_w, key_w, value_w, output_w, *tables)
    return scalar_call(
        attention_forward_body, "attention_forward", core, inputs, shapes, after
    )


TN = (((0,), (0,)), ((), ()))


def attention_backward_body(
    share_ref,
    tokens,
    query_w,
    key_w,
    value_w,
    output_w,
    cosine,
    sine,
    query,
    keys,
    values,
    first,
    second,
    third,
    fourth,
    *refs,
):
    grad, grad_qkv, gain, keep, send, grad_keys, grad_values = refs[-7:]
    share = share_ref[0]
    size = first.shape[0]
    for r, piece in enumerate((first, second, third, fourth)):
        place = jnp.bitwise_xor(share, r) * size
        grad[pl.ds(pl.multiple_of(place, size), size), :] = piece[...]
    back = lax.dot_general(grad[...], output_w[...], NT, preferred_element_type=F32).astype(BF16)
    wide, narrow = (query.shape[1], keys.shape[1])
    group = wide // narrow
    grad_keys[...] = jnp.zeros_like(grad_keys)
    grad_values[...] = jnp.zeros_like(grad_values)
    for start in range(0, tokens.shape[0], BLOCK):
        stop = start + BLOCK
        parts, key_parts, value_parts = ([], [], [])
        for kv in range(narrow // HEAD_DIM):
            key, value = (head(keys, kv, 0, stop), head(values, kv, 0, stop))
            key_sum, value_sum = (0.0, 0.0)
            for h in range(kv * group, (kv + 1) * group):
                query_h = head(query, h, start, stop)
                back_h = head(back, h, start, stop)
                probs = probabilities(query_h, key)
                inner = lax.dot_general(back_h, value, NT, preferred_element_type=F32)
                scores = probs * (inner - jnp.sum(probs * inner, -1, keepdims=True))
                scores = scores.astype(BF16)
                parts.append(ATTN_SCALE * jnp.dot(scores, key, preferred_element_type=F32))
                key_sum += lax.dot_general(scores, query_h, TN, preferred_element_type=F32)
                value_sum += lax.dot_general(
                    probs.astype(BF16), back_h, TN, preferred_element_type=F32
                )
            key_parts.append(ATTN_SCALE * key_sum)
            value_parts.append(value_sum)
        turned = rotated(
            jnp.concatenate(parts, 1), cosine[start:stop, :], sine[start:stop, :], -1.0
        )
        grad_qkv[start:stop, :wide] = turned.astype(BF16)
        grad_keys[:stop, :] += jnp.concatenate(key_parts, 1)
        grad_values[:stop, :] += jnp.concatenate(value_parts, 1)
    turned = rotated(grad_keys[...], cosine[...], sine[...], -1.0)
    grad_qkv[:, wide : wide + narrow] = turned.astype(BF16)
    grad_qkv[:, wide + narrow :] = grad_values[...].astype(BF16)
    total = jnp.zeros(gain.shape, F32)
    for r in range(2):
        for target, core in ((keep, share % 2), (send, 1 - share % 2)):
            rows = pl.ds(pl.multiple_of((2 * r + core) * size, size), size)
            part = lax.dot_general(
                grad_qkv[rows, :wide], query_w[...], NT, preferred_element_type=F32
            )
            part += lax.dot_general(
                grad_qkv[rows, wide : wide + narrow], key_w[...], NT, preferred_element_type=F32
            )
            part += lax.dot_general(
                grad_qkv[rows, wide + narrow :], value_w[...], NT, preferred_element_type=F32
            )
            target[r] = part.astype(target.dtype)
            x = tokens[rows, :].astype(F32)
            x = x * lax.rsqrt(jnp.mean(x * x, -1, keepdims=True) + EPS)
            total += jnp.sum((part * x).reshape(-1, 8, x.shape[1]), 0)
    gain[...] = total


def attention_backward(share, tokens, weights, tables, saved, pieces, *after):
    rows, width = tokens.shape
    narrow = saved[1].shape[1]
    shapes = [
        jax.ShapeDtypeStruct((rows, width), BF16),
        jax.ShapeDtypeStruct((rows, saved[0].shape[1] + 2 * narrow), BF16),
        jax.ShapeDtypeStruct((8, width), F32),
        jax.ShapeDtypeStruct((2, rows // 4, width), F32),
        jax.ShapeDtypeStruct((2, rows // 4, width), BF16),
    ]
    return scalar_call(
        attention_backward_body,
        "attention_backward",
        share,
        (tokens, *weights, *tables, *saved, *pieces),
        shapes,
        after,
        [pltpu.VMEM((rows, narrow), F32), pltpu.VMEM((rows, narrow), F32)],
    )


def reduce_body(place_ref, normed, grad_qkv, grad, attended, small, gain, *refs):
    keep, near, far = refs[-3:]
    step = pl.program_id(0)
    first = lax.dot_general(normed[...], grad_qkv[...], TN, preferred_element_type=F32)
    second = lax.dot_general(grad[...], attended[...], TN, preferred_element_type=F32)
    rest = jnp.zeros((SHARE - small.shape[0] - gain.shape[0], SHARE), F32)
    third = jnp.concatenate([small[...], gain[...], rest], 0).T
    part = jnp.concatenate([first, second, third], 1)

    @pl.when(step < 4)
    def _():
        keep[...] = part

    @pl.when((step == 4) | (step == 5))
    def _():
        near[...] = part.astype(BF16)

    @pl.when(step >= 6)
    def _():
        far[...] = part.astype(BF16)


def reduce_parts(place, normed, grad_qkv, grad, attended, small, gain, *after):
    rows, width = normed.shape
    size = width // 8
    total = grad_qkv.shape[1] + attended.shape[1] + SHARE

    def shard(e, place):
        order = jnp.where(e < 4, 2 * e, 2 * e - 7)
        return jnp.bitwise_xor(place[0], order)

    columns = pl.BlockSpec((rows, size), lambda e, place: (0, shard(e, place)))
    return pl.pallas_call(
        reduce_body,
        grid_spec=pltpu.PrefetchScalarGridSpec(
            num_scalar_prefetch=1,
            grid=(8,),
            in_specs=[
                columns,
                whole_block(grad_qkv.shape),
                columns,
                whole_block(attended.shape),
                pl.BlockSpec((small.shape[0], size), lambda e, place: (0, shard(e, place))),
                pl.BlockSpec((gain.shape[0], size), lambda e, place: (0, shard(e, place))),
            ]
            + [any_block()] * len(after),
            out_specs=[
                pl.BlockSpec((size, total), lambda e, _: (jnp.minimum(e, 3), 0)),
                pl.BlockSpec((size, total), lambda e, _: (jnp.clip(e - 4, 0, 1), 0)),
                pl.BlockSpec((size, total), lambda e, _: (jnp.clip(e - 6, 0, 1), 0)),
            ],
        ),
        out_shape=[
            jax.ShapeDtypeStruct((4 * size, total), F32),
            jax.ShapeDtypeStruct((2 * size, total), BF16),
            jax.ShapeDtypeStruct((2 * size, total), BF16),
        ],
        name="reduce_parts",
    )(place, normed, grad_qkv, grad, attended, small, gain, *after)


def unpack_body(place_ref, *refs):
    pieces = refs[:8]
    query, key, value, output, small = refs[-5:]
    size = pieces[0].shape[0]
    wide, narrow = (query.shape[1], key.shape[1])
    for r, piece in zip(ORDER, pieces):
        start = pl.multiple_of(jnp.bitwise_xor(place_ref[0], r) * size, size)
        rows = pl.ds(start, size)
        part = piece[...].astype(F32)
        query[rows, :] = part[:, :wide]
        key[rows, :] = part[:, wide : wide + narrow]
        value[rows, :] = part[:, wide + narrow : wide + 2 * narrow]
        begin = wide + 2 * narrow
        output[:, rows] = part[:, begin : begin + output.shape[0]].T
        small[rows, :] = part[:, begin + output.shape[0] :]


def assemble_body(share_ref, *refs):
    target = refs[-1]
    size = refs[0].shape[0]
    for r in range(4):
        start = pl.multiple_of(jnp.bitwise_xor(share_ref[0], r) * size, size)
        target[pl.ds(start, size), :] = refs[r][...].astype(target.dtype)


def spread_tensor(value):
    across = swap_y(value)
    return [value, swap_core(value), across, swap_core(across)]


def assemble(share, pieces, dtype, *after):
    size, width = pieces[0].shape
    shapes = [jax.ShapeDtypeStruct((4 * size, width), dtype)]
    return scalar_call(assemble_body, "assemble", share, pieces, shapes, after)[0]


def trade(value, bits):
    return lax.ppermute(value, "expert", [(i, i ^ bits) for i in range(8)])


def swap_y(value):
    return lax.ppermute(value, "tensor", [(i, i ^ 2) for i in range(4)])


def swap_core(value):
    return lax.ppermute(value, "tensor", [(i, i ^ 1) for i in range(4)])


def gather_experts(value):
    column = [value] + [trade(value, bits) for bits in (2, 4, 6)]
    return column + [trade(shard, 1) for shard in column]


def scatter_steps(keep, send_near, send_far, *beside):
    size = keep.shape[0] // 4
    got_far = trade(send_far, 1)
    send_near, got_far, keep = lax.optimization_barrier((send_near, got_far, keep))
    if beside:
        got_far, *beside = lax.optimization_barrier((got_far, *beside))
    far = (keep[2 * size :] + got_far.astype(F32)).astype(BF16)
    got_near = trade(send_near, 1)
    four, six = (trade(far[:size], 4), trade(far[size:], 6))
    near = (keep[size : 2 * size] + got_near[size:].astype(F32)).astype(BF16)
    return (keep, got_near, (trade(near, 2), four, six), *beside)


def scatter_experts(keep, send_near, send_far, *beside):
    size = keep.shape[0] // 4
    keep, got_near, back, *beside = scatter_steps(keep, send_near, send_far, *beside)
    total = keep[:size] + got_near[:size].astype(F32)
    for part in back:
        total = total + part.astype(F32)
    return (total, *beside) if beside else total


def scatter_tensor(keep, send, row):
    half = keep + swap_core(send).astype(F32)
    keep = lax.dynamic_index_in_dim(half, row, 0, False)
    send = lax.dynamic_index_in_dim(half, 1 - row, 0, False)
    return keep + swap_y(send.astype(BF16)).astype(F32)


def ordered(index, first, second):
    return jnp.where(
        index == 0, jnp.concatenate([first, second], 0), jnp.concatenate([second, first], 0)
    )


def per_device(
    tokens,
    teacher,
    valid_mask,
    routes,
    first_gain,
    query_weight,
    key_matrix,
    value_matrix,
    output_weight,
    second_gain,
    router_weight,
    expert_in,
    expert_out,
):
    row_count, model_width = tokens.shape
    expert_count = router_weight.shape[1]
    senders = lax.axis_size("expert")
    shares = lax.axis_size("tensor")
    fits = (
        (senders, shares) == (8, 4)
        and expert_count == senders * shares
        and expert_in.shape == (8, 2, model_width // 2, SHARE)
        and row_count == 4 * 128
    )
    if not fits:
        return general_device(
            tokens,
            teacher,
            valid_mask,
            routes,
            first_gain,
            query_weight,
            key_matrix,
            value_matrix,
            output_weight,
            second_gain,
            router_weight,
            expert_in,
            expert_out,
        )
    quarter = row_count // shares
    place = lax.axis_index("expert")
    share = lax.axis_index("tensor")
    row, core = (share // 2, share % 2)
    half_index = place // 4
    half_arg = half_index.reshape(1)
    held = expert_in.shape[0] // 2
    base = 8 * (place % 4) + held * half_index

    share_arg, core_arg, place_arg = (share.reshape(1), core.reshape(1), place.reshape(1))

    def quarter_of(values):
        return lax.dynamic_slice_in_dim(values, share * quarter, quarter, 0)

    local_valid = jnp.sum(valid_mask)
    routes_mine = quarter_of(routes)
    note = jnp.concatenate([routes_mine.T, jnp.full((TOP, quarter), local_valid, jnp.int32)], 0)

    own_pack, near_pack, far_pack = pack_weights(half_arg, expert_in, expert_out)
    near_pack = trade(near_pack, 4)
    far_pack = trade(far_pack, 4)
    own_across = swap_y(own_pack)

    router_rel = lax.dynamic_slice_in_dim(
        jnp.concatenate([router_weight, router_weight], 1), base, expert_count, 1
    )
    router_rel = jnp.pad(
        jnp.concatenate([router_rel, router_rel], 1), ((0, 0), (0, 128 - 2 * expert_count))
    )

    tables = [
        jnp.concatenate([table[:, 0]] * (2 * SHARE // HEAD_DIM), 1)
        for table in rope_tables(row_count, HEAD_DIM)
    ]
    weights = (query_weight, key_matrix, value_matrix, output_weight)
    first_normed, query, keys, values, attended, attn_keep, attn_send = attention_forward(
        core_arg, tokens, first_gain[None], *weights, tables, own_pack
    )
    notes = [note] + [trade(note, bits) for bits in (2, 4, 6)]
    near_pack, own_across, attn_send, *notes = lax.optimization_barrier(
        (near_pack, own_across, attn_send, *notes)
    )
    notes = jnp.stack(notes)
    others = trade(notes, 1)
    own = [own_pack, swap_core(own_pack), own_across, swap_core(own_across)]
    tokens_mine = quarter_of(tokens).astype(F32)
    attn_sum = scatter_tensor(attn_keep, attn_send, row)
    near_pack, attn_sum, others = lax.optimization_barrier((near_pack, attn_sum, others))
    near_across = swap_y(near_pack)
    hidden = tokens_mine + RESIDUAL * attn_sum
    scale_two = lax.rsqrt(jnp.mean(hidden * hidden, -1, keepdims=True) + EPS)
    unit_two = hidden * scale_two
    normed_two = (unit_two * second_gain).astype(BF16)
    beside = trade(normed_two, 1)
    last, beside = lax.optimization_barrier((normed_two, beside))
    column = [normed_two, trade(normed_two, 2), trade(normed_two, 4), trade(last, 6)]
    across = [trade(shard, 1) for shard in column[1:]]
    far_pack, near_across, *gathered = lax.optimization_barrier(
        (far_pack, near_across, beside, *across, *column[1:])
    )
    row_shards = [normed_two, *gathered[4:], *gathered[:4]]
    near = [near_pack, swap_core(near_pack), near_across, swap_core(near_across)]
    far = spread_tensor(far_pack)
    notes = jnp.concatenate([notes, others], 0)
    valid_total = jnp.sum(notes[:, TOP, 0]).astype(F32)
    route_rel = jnp.bitwise_and(notes[:, :TOP] - base, expert_count - 1)
    route_rel = route_rel.transpose(0, 2, 1).reshape(senders * quarter, TOP)
    keep, send_near, send_far, pre, gated, gates, expert_rows = experts_forward(
        half_arg,
        row_shards,
        route_rel,
        router_rel,
        own,
        near,
        far,
    )
    moe_sum = scatter_experts(keep, send_near, send_far)

    output = hidden + RESIDUAL * moe_sum
    residual_err = output - quarter_of(teacher).astype(F32)
    valid_rows = quarter_of(valid_mask).astype(F32)[:, None]
    squared_local = jnp.sum(valid_rows * residual_err * residual_err)
    token_total = senders * row_count
    grad_out = token_total / valid_total * valid_rows * residual_err
    grad_moe = (RESIDUAL * grad_out).astype(BF16)
    gate_mean = jnp.sum(grad_moe.astype(F32) * moe_sum, -1, keepdims=True)
    mean_part = -gate_mean * dense_gates(normed_two, routes_mine, router_weight)
    mean_high = mean_part.astype(BF16)
    mean_part = jnp.concatenate([mean_high, (mean_part - mean_high.astype(F32)).astype(BF16)], 1)
    router_pair = jnp.concatenate([router_weight, router_weight], 1)
    mean_rows = jnp.einsum("te,de->td", mean_part, router_pair, preferred_element_type=F32)
    shards = gather_experts(grad_moe)
    packs = (gates, router_rel, pre, own, near, far)
    send_near, send_far, *saved = experts_backward(1, half_arg, shards[4:], *packs)
    keep, pre_grad, logit_grad, grad_rows = experts_backward(
        0, half_arg, shards[:4], *packs, *saved
    )
    got_far = trade(send_far, 1)
    send_near, got_far, keep = lax.optimization_barrier((send_near, got_far, keep))
    far_rows = (keep[2 * quarter :] + got_far.astype(F32)).astype(BF16)
    back = trade(far_rows, 4)
    got_near = trade(send_near, 1)
    near_rows = keep[quarter : 2 * quarter] + got_near[quarter:].astype(F32)
    near_rows = (near_rows + back[quarter:].astype(F32)).astype(BF16)
    near_rows = trade(near_rows, 2)
    other = 1 - half_arg
    in_keep, in_send = grad_expert_ins(other, expert_rows, pre_grad, 0, 2, far_rows)
    in_near, in_far = fold_pairs(in_keep, swap_core(in_send))
    in_ready = (in_near + swap_y(in_far).astype(F32)).astype(BF16)
    out_keep, out_send, own_out_keep, own_out_send = grad_expert_outs(
        half_arg, gated, grad_rows, in_far
    )
    grad_hidden, grad_attn, grad_second_part = finish_rows(
        keep,
        got_near,
        back,
        near_rows,
        mean_rows,
        unit_two,
        scale_two,
        second_gain[None],
        grad_out,
        out_send,
        in_ready,
    )
    grad_second_part = jnp.sum(grad_second_part, 0)
    router_part = jnp.einsum(
        "te,td->ed", logit_grad.astype(BF16), expert_rows, preferred_element_type=F32
    )
    router_part = router_part[:expert_count] + router_part[expert_count : 2 * expert_count]
    router_part = lax.dynamic_slice_in_dim(
        jnp.concatenate([router_part, router_part], 0),
        jnp.bitwise_and(expert_count - base, expert_count - 1),
        expert_count,
        0,
    )
    mean_router = jnp.einsum("te,td->ed", mean_part, normed_two, preferred_element_type=F32)
    router_part = router_part + mean_router[:expert_count] + mean_router[expert_count:]

    small = jnp.concatenate(
        [
            router_part,
            grad_second_part[None],
            jnp.full((1, model_width), squared_local),
            jnp.zeros((6, model_width), F32),
        ],
        0,
    )
    small = small + swap_core(small)
    small = small + swap_y(small)
    late_keep, late_send = grad_expert_ins(other, expert_rows, pre_grad, 2, 2, grad_attn)
    pieces = spread_tensor(grad_attn)
    late_near, late_far = fold_pairs(late_keep, swap_core(late_send), pieces[2])
    out_near, out_far = fold_pairs(out_keep, swap_core(out_send), pieces[2])
    out_ready = (out_near + swap_y(out_far).astype(F32)).astype(BF16)
    late_ready = (late_near + swap_y(late_far).astype(F32)).astype(BF16)
    in_back = trade(in_ready, 4)
    grad_attn, grad_qkv, gain_part, one_keep, one_send = attention_backward(
        share_arg, tokens, weights, tables, (query, keys, values), pieces, late_ready, in_back, out_far, small
    )
    late_back = trade(late_ready, 4)
    grad_one = scatter_tensor(one_keep, one_send, row)
    own_out_near, own_out_far = fold_pairs(own_out_keep, swap_core(own_out_send), grad_one)
    own_out_across = swap_y(own_out_far)

    own_in_keep, own_in_send = grad_expert_ins(
        half_arg, expert_rows, pre_grad, 0, held, grad_one
    )
    keep, send_near, send_far = reduce_parts(
        place_arg, first_normed, grad_qkv, grad_attn, attended, small, gain_part, late_back, own_in_send
    )
    own_in_near, own_in_far = fold_pairs(own_in_keep, swap_core(own_in_send), grad_one)
    own_in_across = swap_y(own_in_far)
    out_back = trade(out_ready, 4)
    total, out_back = scatter_experts(keep, send_near, send_far, out_back)
    total, own_out_across, own_in_across = lax.optimization_barrier(
        (total.astype(BF16), own_out_across, own_in_across)
    )
    shapes = [
        jax.ShapeDtypeStruct(shape, F32)
        for shape in (
            query_weight.shape,
            key_matrix.shape,
            value_matrix.shape,
            output_weight.shape,
            (model_width, 128),
        )
    ]
    shards = gather_experts(total)
    grad_query, grad_key, grad_value, grad_output, small = scalar_call(
        unpack_body, "unpack", place_arg, shards, shapes
    )

    gain_part = jnp.sum(small[:, expert_count + 8 : expert_count + 16], 1).reshape(8, -1)
    gain_part = gain_part + swap_core(gain_part)
    gain_part = (gain_part + swap_y(gain_part)).reshape(-1)

    scale_mine = lax.rsqrt(jnp.mean(tokens_mine * tokens_mine, -1, keepdims=True) + EPS)
    unit_mine = tokens_mine * scale_mine
    grad_unit_one = grad_one * first_gain
    grad_tokens = grad_hidden + scale_mine * (
        grad_unit_one - unit_mine * jnp.mean(grad_unit_one * unit_mine, -1, keepdims=True)
    )
    grad_tokens = assemble(share_arg, spread_tensor(grad_tokens.astype(BF16)), F32)
    layer_output = assemble(share_arg, spread_tensor(output.astype(BF16)), BF16)
    grad_expert_out = ordered(
        half_index, own_out_near + own_out_across.astype(F32), out_back.astype(F32)
    )
    grad_expert_in = ordered(
        half_index,
        own_in_near + own_in_across.astype(F32),
        jnp.concatenate([in_back, late_back], 0).astype(F32),
    )
    return (
        layer_output,
        small[0, expert_count + 1] / (2.0 * model_width * valid_total),
        grad_tokens,
        gain_part,
        grad_query,
        grad_key,
        grad_value,
        grad_output,
        small[:, expert_count],
        small[:, :expert_count],
        grad_expert_in,
        grad_expert_out,
    )


def solution(mesh):
    return jax.shard_map(
        per_device,
        mesh=mesh,
        in_specs=(
            P("expert", None),
            P("expert", None),
            P("expert"),
            P("expert", None),
            P(),
            P(None, "tensor"),
            P(None, "tensor"),
            P(None, "tensor"),
            P("tensor", None),
            P(),
            P(),
            P("expert", None, None, "tensor"),
            P("expert", "tensor", None),
        ),
        out_specs=(
            P("expert", None),
            P(),
            P("expert", None),
            P(),
            P(None, "tensor"),
            P(None, "tensor"),
            P(None, "tensor"),
            P("tensor", None),
            P(),
            P(),
            P("expert", None, None, "tensor"),
            P("expert", "tensor", None),
        ),
        check_vma=False,
    )
```

```python
import jax
import jax.numpy as jnp
from jax import lax
from jax.experimental import pallas as pl
from jax.experimental.pallas import tpu as pltpu
from jax.sharding import PartitionSpec as P

HEAD_DIM = 64
TOP = 8
BLOCK = 256


EPS = 1e-06
ATTN_SCALE = 0.015625
RESIDUAL = 0.22
THETA = 10000.0


def shifted(value, axis, steps):
    count = lax.axis_size(axis)
    pairs = [(source, (source + steps) % count) for source in range(count)]
    return lax.ppermute(value, axis, pairs)


def rope_tables(length, head_size):
    half_size = head_size // 2
    frequency = THETA ** (-(jnp.arange(half_size, dtype=jnp.float32) * 2.0) / head_size)
    angle_table = jnp.arange(length, dtype=jnp.float32)[:, None] * frequency[None, :]
    return (jnp.cos(angle_table)[:, None, :], jnp.sin(angle_table)[:, None, :])


def apply_rotary(values, cosine_lookup, sine_lookup):
    half_size = values.shape[-1] // 2
    lower_half, upper_half = (values[..., :half_size], values[..., half_size:])
    return jnp.concatenate(
        [
            lower_half * cosine_lookup - upper_half * sine_lookup,
            upper_half * cosine_lookup + lower_half * sine_lookup,
        ],
        -1,
    )


def unrotate(grads, cosine_lookup, sine_lookup):
    half_size = grads.shape[-1] // 2
    lower_half, upper_half = (grads[..., :half_size], grads[..., half_size:])
    return jnp.concatenate(
        [
            lower_half * cosine_lookup + upper_half * sine_lookup,
            upper_half * cosine_lookup - lower_half * sine_lookup,
        ],
        -1,
    )


def normalize(values):
    row_peak = jnp.max(values, -1, keepdims=True)
    exp_scores = jnp.exp(values - row_peak)
    return exp_scores / jnp.sum(exp_scores, -1, keepdims=True)


def slot_tables(route_ids, expert_count, capacity):
    row_count, top_count = route_ids.shape
    onehot = route_ids[:, :, None] == jnp.arange(expert_count, dtype=jnp.int32)[None, None, :]
    hit_count = jnp.sum(onehot.astype(jnp.int32), 1)
    slot_place = jnp.cumsum(hit_count, 0) - 1
    within = jnp.take_along_axis(slot_place, route_ids, 1)
    dest_slot = route_ids * capacity + within
    pair_count = row_count * top_count
    source = (
        jnp.full((expert_count * capacity,), pair_count, jnp.int32)
        .at[dest_slot.reshape(-1)]
        .set(jnp.arange(pair_count, dtype=jnp.int32))
    )
    live_slot = source < pair_count
    token_row = jnp.minimum(source, pair_count - 1) // top_count
    return (onehot, dest_slot, source, live_slot, token_row)


def general_device(
    tokens,
    teacher,
    valid_mask,
    routes,
    first_gain,
    query_weight,
    key_matrix,
    value_matrix,
    output_weight,
    second_gain,
    router_weight,
    expert_in,
    expert_out,
):
    row_count = tokens.shape[0]
    model_width = tokens.shape[1]
    half_width = model_width // 2
    local_query = query_weight.shape[1] // HEAD_DIM
    local_kv = key_matrix.shape[1] // HEAD_DIM
    query_group_size = local_query // local_kv
    expert_count = router_weight.shape[1]
    row_local = expert_in.shape[0]
    senders = lax.axis_size("expert")
    partner_step = senders // 2
    capacity = 3 * row_count * TOP // (2 * expert_count)
    pair_count = row_count * TOP
    score_rows = min(512, row_count)
    valid_total = lax.psum(jnp.sum(valid_mask).astype(jnp.float32), "expert")
    tokens_f32 = tokens.astype(jnp.float32)
    scale_one = lax.rsqrt(jnp.mean(tokens_f32 * tokens_f32, -1, keepdims=True) + EPS)
    unit_one = tokens_f32 * scale_one
    first_normed = (unit_one * first_gain).astype(jnp.bfloat16)
    cosine_lookup, sine_lookup = rope_tables(row_count, HEAD_DIM)
    query_linear = jnp.dot(first_normed, query_weight, preferred_element_type=jnp.float32).reshape(
        row_count, local_query, HEAD_DIM
    )
    keys_linear = jnp.dot(first_normed, key_matrix, preferred_element_type=jnp.float32).reshape(
        row_count, local_kv, HEAD_DIM
    )
    value_low = jnp.dot(first_normed, value_matrix, preferred_element_type=jnp.float32).astype(
        jnp.bfloat16
    )
    value_low = value_low.reshape(row_count, local_kv, HEAD_DIM)
    query_rotated = apply_rotary(query_linear, cosine_lookup, sine_lookup).astype(jnp.bfloat16)
    keys_rot = apply_rotary(keys_linear, cosine_lookup, sine_lookup).astype(jnp.bfloat16)
    block_of = jnp.arange(row_count, dtype=jnp.int32) // BLOCK

    def scores(start_row):
        stop_row = start_row + score_rows
        query_block = query_rotated.reshape(score_rows, local_kv, query_group_size, HEAD_DIM)
        score_block = (
            jnp.einsum("qhgd,khd->hgqk", query_block, keys_rot, preferred_element_type=jnp.float32)
            * ATTN_SCALE
        )
        allowed = block_of[None, :stop_row] <= block_of[start_row:stop_row, None]
        return (query_block, jnp.where(allowed, score_block, -1e30))

    attn_parts, row_peaks, row_totals = ([], [], [])
    start_row = 0
    query_block, score_block = scores(start_row)
    row_peak = jnp.max(score_block, -1, keepdims=True)
    exp_scores = jnp.exp(score_block - row_peak)
    row_total = jnp.sum(exp_scores, -1, keepdims=True)
    attn_probs = (exp_scores / row_total).astype(jnp.bfloat16)
    attn_parts.append(
        jnp.einsum("hgqk,khd->qhgd", attn_probs, value_low, preferred_element_type=jnp.float32)
    )
    row_peaks.append(row_peak)
    row_totals.append(row_total)
    attended = attn_parts[0].reshape(row_count, local_query * HEAD_DIM).astype(jnp.bfloat16)
    attn_part = jnp.dot(attended, output_weight, preferred_element_type=jnp.float32)
    attn_sum = lax.psum(attn_part, "tensor")
    hidden_state = tokens_f32 + RESIDUAL * attn_sum
    scale_two = lax.rsqrt(jnp.mean(hidden_state * hidden_state, -1, keepdims=True) + EPS)
    unit_two = hidden_state * scale_two
    normed_two = (unit_two * second_gain).astype(jnp.bfloat16)
    router_logits = jnp.dot(normed_two, router_weight, preferred_element_type=jnp.float32)
    onehot, dest_slot, source, live_slot, token_row = slot_tables(routes, expert_count, capacity)
    picked = jnp.sum(jnp.where(onehot, router_logits[:, None, :], 0.0), -1)
    gate_probs = normalize(picked)

    def slot_rows(slot_values):
        split_rows = slot_values.reshape(expert_count, capacity, 2, half_width).transpose(
            2, 0, 1, 3
        )
        return split_rows.reshape(senders, row_local, capacity, half_width)

    def slot_columns(returned, width):
        joined = returned.reshape(2, expert_count, capacity, width).transpose(1, 2, 0, 3)
        return joined.reshape(expert_count * capacity, 2, width)

    send_rows = slot_rows(
        jnp.where(live_slot[:, None], normed_two[token_row], jnp.zeros((), jnp.bfloat16))
    )
    received = lax.all_to_all(send_rows, "expert", split_axis=0, concat_axis=2, tiled=True)
    expert_rows = received.reshape(row_local, senders * capacity, half_width)
    gate_up_part = jnp.einsum(
        "rmd,rcdf->rmcf", expert_rows, expert_in, preferred_element_type=jnp.float32
    )
    gate_up_pre = gate_up_part + shifted(gate_up_part, "expert", partner_step)
    gate_pre = gate_up_pre[:, :, 0]
    up_pre = gate_up_pre[:, :, 1]
    inner_act = (jax.nn.silu(gate_pre) * up_pre).astype(jnp.bfloat16)
    expert_result = jnp.einsum(
        "rmf,rfd->rmd", inner_act, expert_out, preferred_element_type=jnp.float32
    )
    expert_result = expert_result.astype(jnp.bfloat16).reshape(
        row_local, senders, capacity, half_width
    )
    returned = lax.all_to_all(expert_result, "expert", split_axis=1, concat_axis=0, tiled=True)
    per_route = slot_columns(returned, half_width).reshape(expert_count * capacity, model_width)[
        dest_slot
    ]
    moe_part = jnp.sum(gate_probs[:, :, None] * per_route, 1)
    moe_sum = lax.psum(moe_part, "tensor")
    output = hidden_state + RESIDUAL * moe_sum
    residual_err = output - teacher.astype(jnp.float32)
    valid_rows = valid_mask.astype(jnp.float32)
    squared_local = jnp.sum(valid_rows * jnp.sum(residual_err * residual_err, -1))
    token_total = senders * row_count
    grad_out = token_total / valid_total * valid_rows[:, None] * residual_err
    grad_moe = (RESIDUAL * grad_out).astype(jnp.bfloat16)
    gate_part = jnp.einsum("td,tkd->tk", grad_moe, per_route, preferred_element_type=jnp.float32)
    gate_slot = gate_probs.reshape(pair_count)[jnp.minimum(source, pair_count - 1)]
    grad_slots = jnp.where(live_slot[:, None], gate_slot[:, None] * grad_moe[token_row], 0.0)
    grad_received = lax.all_to_all(
        slot_rows(grad_slots.astype(jnp.bfloat16)),
        "expert",
        split_axis=0,
        concat_axis=2,
        tiled=True,
    )
    grad_expert = grad_received.reshape(row_local, senders * capacity, half_width)
    grad_inner_part = jnp.einsum(
        "rmd,rfd->rmf", grad_expert, expert_out, preferred_element_type=jnp.float32
    )
    grad_inner = grad_inner_part + shifted(grad_inner_part, "expert", partner_step)
    grad_expert_out = jnp.einsum(
        "rmf,rmd->rfd", inner_act, grad_expert, preferred_element_type=jnp.float32
    )
    sigmoid_gate = jax.nn.sigmoid(gate_pre)
    grad_gate = grad_inner * up_pre * sigmoid_gate * (1.0 + gate_pre * (1.0 - sigmoid_gate))
    grad_up = grad_inner * (gate_pre * sigmoid_gate)
    grad_pre = jnp.stack([grad_gate, grad_up], 2).astype(jnp.bfloat16)
    grad_expert_in = jnp.einsum(
        "rmd,rmcf->rcdf", expert_rows, grad_pre, preferred_element_type=jnp.float32
    )
    grad_slot_rows = jnp.einsum(
        "rmcf,rcdf->rmd", grad_pre, expert_in, preferred_element_type=jnp.float32
    )
    grad_slot_rows = grad_slot_rows.astype(jnp.bfloat16).reshape(
        row_local, senders, capacity, half_width
    )
    grad_back = lax.all_to_all(grad_slot_rows, "expert", split_axis=1, concat_axis=0, tiled=True)
    grad_back = slot_columns(grad_back, half_width).reshape(expert_count * capacity, model_width)
    grad_two_part = jnp.sum(grad_back[dest_slot].astype(jnp.float32), 1)
    grad_two_experts, grad_gates = lax.psum((grad_two_part, gate_part), "tensor")
    grad_picked = gate_probs * (grad_gates - jnp.sum(gate_probs * grad_gates, -1, keepdims=True))
    grad_logits = jnp.sum(jnp.where(onehot, grad_picked[:, :, None], 0.0), 1).astype(jnp.bfloat16)
    grad_router = jnp.einsum(
        "td,te->de", normed_two, grad_logits, preferred_element_type=jnp.float32
    )
    grad_two = grad_two_experts + jnp.einsum(
        "te,de->td", grad_logits, router_weight, preferred_element_type=jnp.float32
    )
    grad_second_gain = jnp.sum(grad_two * unit_two, 0)
    grad_unit_two = grad_two * second_gain
    grad_hidden = grad_out + scale_two * (
        grad_unit_two - unit_two * jnp.mean(grad_unit_two * unit_two, -1, keepdims=True)
    )
    grad_attn = (RESIDUAL * grad_hidden).astype(jnp.bfloat16)
    grad_output = jnp.einsum("tc,td->cd", attended, grad_attn, preferred_element_type=jnp.float32)
    grad_attended = jnp.einsum(
        "td,cd->tc", grad_attn, output_weight, preferred_element_type=jnp.float32
    )
    grad_attended = grad_attended.astype(jnp.bfloat16).reshape(
        row_count, local_kv, query_group_size, HEAD_DIM
    )
    grad_query_parts = []
    grad_keys = jnp.zeros((row_count, local_kv, HEAD_DIM), jnp.float32)
    grad_values = jnp.zeros((row_count, local_kv, HEAD_DIM), jnp.float32)
    for block_index, start_row in enumerate(range(0, row_count, score_rows)):
        stop_row = start_row + score_rows
        query_block, score_block = scores(start_row)
        attn_probs = jnp.exp(score_block - row_peaks[block_index]) / row_totals[block_index]
        probs_low = attn_probs.astype(jnp.bfloat16)
        grad_probs = jnp.einsum(
            "qhgd,khd->hgqk", grad_attended, value_low, preferred_element_type=jnp.float32
        )
        grad_scores = attn_probs * (
            grad_probs - jnp.sum(attn_probs * grad_probs, -1, keepdims=True)
        )
        grad_scores = grad_scores.astype(jnp.bfloat16)
        grad_query_parts.append(
            ATTN_SCALE
            * jnp.einsum(
                "hgqk,khd->qhgd", grad_scores, keys_rot, preferred_element_type=jnp.float32
            )
        )
        grad_keys = grad_keys.at[:stop_row].add(
            ATTN_SCALE
            * jnp.einsum(
                "hgqk,qhgd->khd", grad_scores, query_block, preferred_element_type=jnp.float32
            )
        )
        grad_values = grad_values.at[:stop_row].add(
            jnp.einsum(
                "hgqk,qhgd->khd", probs_low, grad_attended, preferred_element_type=jnp.float32
            )
        )
    grad_query_rot = grad_query_parts[0].reshape(row_count, local_query, HEAD_DIM)
    grad_query_low = unrotate(grad_query_rot, cosine_lookup, sine_lookup).reshape(
        row_count, local_query * HEAD_DIM
    )
    grad_query_low = grad_query_low.astype(jnp.bfloat16)
    grad_keys_low = unrotate(grad_keys, cosine_lookup, sine_lookup).reshape(
        row_count, local_kv * HEAD_DIM
    )
    grad_keys_low = grad_keys_low.astype(jnp.bfloat16)
    grad_values_low = grad_values.reshape(row_count, local_kv * HEAD_DIM).astype(jnp.bfloat16)
    grad_query = jnp.einsum(
        "td,tc->dc", first_normed, grad_query_low, preferred_element_type=jnp.float32
    )
    grad_key = jnp.einsum(
        "td,tc->dc", first_normed, grad_keys_low, preferred_element_type=jnp.float32
    )
    grad_value = jnp.einsum(
        "td,tc->dc", first_normed, grad_values_low, preferred_element_type=jnp.float32
    )
    grad_one_part = (
        jnp.einsum("tc,dc->td", grad_query_low, query_weight, preferred_element_type=jnp.float32)
        + jnp.einsum("tc,dc->td", grad_keys_low, key_matrix, preferred_element_type=jnp.float32)
        + jnp.einsum("tc,dc->td", grad_values_low, value_matrix, preferred_element_type=jnp.float32)
    )
    grad_one = lax.psum(grad_one_part.astype(jnp.bfloat16), "tensor").astype(jnp.float32)
    grad_first_gain = jnp.sum(grad_one * unit_one, 0)
    grad_unit_one = grad_one * first_gain
    grad_tokens = grad_hidden + scale_one * (
        grad_unit_one - unit_one * jnp.mean(grad_unit_one * unit_one, -1, keepdims=True)
    )
    reduced = lax.psum(
        (
            grad_first_gain,
            grad_query,
            grad_key,
            grad_value,
            grad_output,
            grad_second_gain,
            grad_router,
            squared_local,
        ),
        "expert",
    )
    loss_value = reduced[7] / (2.0 * model_width * valid_total)
    return (
        output.astype(jnp.bfloat16),
        loss_value,
        grad_tokens,
        reduced[0],
        reduced[1],
        reduced[2],
        reduced[3],
        reduced[4],
        reduced[5],
        reduced[6],
        grad_expert_in,
        grad_expert_out,
    )


BF16 = jnp.bfloat16
F32 = jnp.float32
CHUNK = 256
SHARE = 128
PACK = 12 * SHARE
NT = (((1,), (1,)), ((), ()))
ORDER = (0, 2, 4, 6, 1, 3, 5, 7)


def whole_block(shape):
    return pl.BlockSpec(shape, lambda e, *_: (0,) * len(shape))


def any_block():
    return pl.BlockSpec(memory_space=pl.ANY)


def pack_body(half_ref, own_in, own_out, other_in, other_out, *refs):
    own, near, far = refs[-3:]
    step = pl.program_id(0)

    def fill(target, source_in, source_out):
        for c in range(2):
            target[c * 4 * SHARE : (c + 1) * 4 * SHARE, :] = source_in[0, c]
        for k in range(4):
            target[(8 + k) * SHARE : (9 + k) * SHARE, :] = source_out[
                0, :, k * SHARE : (k + 1) * SHARE
            ]

    fill(own, own_in, own_out)

    @pl.when(step < 2)
    def _():
        fill(near, other_in, other_out)

    @pl.when(step >= 2)
    def _():
        fill(far, other_in, other_out)


def pack_weights(half_index, expert_in, expert_out, *after):
    held = expert_in.shape[0] // 2
    in_shape = (1,) + expert_in.shape[1:]
    out_shape = (1,) + expert_out.shape[1:]
    shapes = [(held * PACK, SHARE), (held // 2 * PACK, SHARE), (held // 2 * PACK, SHARE)]
    block = (PACK, SHARE)
    return pl.pallas_call(
        pack_body,
        grid_spec=pltpu.PrefetchScalarGridSpec(
            num_scalar_prefetch=1,
            grid=(held,),
            in_specs=[
                pl.BlockSpec(in_shape, lambda e, half: (half[0] * held + e, 0, 0, 0)),
                pl.BlockSpec(out_shape, lambda e, half: (half[0] * held + e, 0, 0)),
                pl.BlockSpec(in_shape, lambda e, half: ((1 - half[0]) * held + e, 0, 0, 0)),
                pl.BlockSpec(out_shape, lambda e, half: ((1 - half[0]) * held + e, 0, 0)),
            ]
            + [any_block()] * len(after),
            out_specs=[
                pl.BlockSpec(block, lambda e, half: (e, 0)),
                pl.BlockSpec(block, lambda e, half: (jnp.minimum(e, 1), 0)),
                pl.BlockSpec(block, lambda e, half: (jnp.maximum(e - 2, 0), 0)),
            ],
        ),
        out_shape=[jax.ShapeDtypeStruct(shape, BF16) for shape in shapes],
        name="pack_weights",
    )(half_index, expert_in, expert_out, expert_in, expert_out, *after)


def weight_copies(own, other, own_row, other_row, half, in_buf, out_buf, sems, slot):
    copies = []
    for q in range(4):
        for pack, row, side in ((own[q], own_row, half), (other[q], other_row, 1 - half)):
            for c in range(2):
                copies.append(
                    (
                        pack.at[pl.ds(pl.multiple_of(row + c * 4 * SHARE, SHARE), 4 * SHARE)],
                        in_buf.at[
                            slot,
                            pl.ds(pl.multiple_of(side * 4 * SHARE, SHARE), 4 * SHARE),
                            pl.ds((2 * q + c) * SHARE, SHARE),
                        ],
                    )
                )
            for k in range(4):
                copies.append(
                    (
                        pack.at[pl.ds(pl.multiple_of(row + (8 + k) * SHARE, SHARE), SHARE)],
                        out_buf.at[slot, side, pl.ds(q * SHARE, SHARE), pl.ds(k * SHARE, SHARE)],
                    )
                )
    return [
        pltpu.make_async_copy(source, target, sems.at[slot, n])
        for n, (source, target) in enumerate(copies)
    ]


def stream_weights(first, packs, half, in_buf, out_buf, sems):
    step = pl.program_id(0)
    slot = lax.rem(step, 2)
    own, near, far = (packs[0:4], packs[4:8], packs[8:12])

    def start(index, target):
        expert = first + index

        def begin(other, start_row):
            for copy in weight_copies(
                own, other, expert * PACK, start_row, half, in_buf, out_buf, sems, target
            ):
                copy.start()

        if not far:
            begin(near, index * PACK)
            return

        @pl.when(expert < 2)
        def _():
            begin(near, expert * PACK)

        @pl.when(expert >= 2)
        def _():
            begin(far, (expert - 2) * PACK)

    @pl.when(step == 0)
    def _():
        start(0, 0)

    @pl.when(step + 1 < pl.num_programs(0))
    def _():
        start(step + 1, 1 - slot)

    def wait():
        for copy in weight_copies(own, near, 0, 0, half, in_buf, out_buf, sems, slot):
            copy.wait()

    return (step, slot, wait)


def weight_scratch(width, hidden):
    return [
        pltpu.VMEM((2, width, 2 * hidden), BF16),
        pltpu.VMEM((2, 2, hidden, width // 2), BF16),
        pltpu.SemaphoreType.DMA((2, 48)),
    ]


def split_pairs(values):
    blocks = [values[:, i * SHARE : (i + 1) * SHARE] for i in range(values.shape[1] // SHARE)]
    return (jnp.concatenate(blocks[0::2], 1), jnp.concatenate(blocks[1::2], 1))


def join_pairs(first, second):
    blocks = []
    for i in range(first.shape[1] // SHARE):
        blocks.append(first[:, i * SHARE : (i + 1) * SHARE])
        blocks.append(second[:, i * SHARE : (i + 1) * SHARE])
    return jnp.concatenate(blocks, 1)


def chunk_loop(row_count, body):
    def step(i, carry):
        body(pl.ds(pl.multiple_of(i * CHUNK, CHUNK), CHUNK))
        return carry

    lax.fori_loop(0, row_count // CHUNK, step, 0)


def gate_column(gates, expert):
    lane = lax.broadcasted_iota(jnp.int32, gates.shape, 1)
    return jnp.sum(jnp.where(lane == expert, gates, 0.0), -1, keepdims=True)


def dense_gates(rows, ids, router):
    logits = jnp.dot(rows, router, preferred_element_type=F32)
    lane = lax.broadcasted_iota(jnp.int32, logits.shape, 1)
    mask = ids[:, 0:1] == lane
    for k in range(1, TOP):
        mask = mask | (ids[:, k : k + 1] == lane)
    masked = jnp.where(mask, logits, -1e30)
    powers = jnp.where(mask, jnp.exp(masked - jnp.max(masked, -1, keepdims=True)), 0.0)
    return powers / jnp.sum(powers, -1, keepdims=True)


def apply_expert(rows, expert, slot, rows_ref, gate_ref, pre_ref, gated_ref, in_buf):
    pre = jnp.dot(rows_ref[rows, :], in_buf[slot], preferred_element_type=F32)
    pre_ref[0, rows, :] = pre.astype(BF16)
    gate_pre, up_pre = split_pairs(pre)
    weight = gate_column(gate_ref[rows, :], expert)
    gated = (weight * (gate_pre * jax.nn.sigmoid(gate_pre) * up_pre)).astype(BF16)
    gated_ref[0, rows, :] = gated
    return gated


def forward_first(half_ref, *refs):
    shards = refs[:8]
    route_ref, router_ref = refs[8:10]
    packs = refs[10:18]
    acc, pre_ref, gated_ref, gate_ref, rows_ref, in_buf, out_buf, sems = refs[18:]
    step, slot, wait = stream_weights(0, packs, half_ref[0], in_buf, out_buf, sems)
    row_count, width = acc.shape
    size = row_count // 8

    @pl.when(step == 0)
    def _():
        for i in range(8):
            rows_ref[i * size : (i + 1) * size, :] = shards[i][...]
        acc[...] = jnp.zeros_like(acc)

        def gating(rows):
            gate_ref[rows, :] = dense_gates(rows_ref[rows, :], route_ref[rows, :], router_ref[...])

        chunk_loop(row_count, gating)

    wait()

    def mlp(rows):
        gated = apply_expert(rows, step, slot, rows_ref, gate_ref, pre_ref, gated_ref, in_buf)
        for side in range(2):
            columns = slice(side * width // 2, (side + 1) * width // 2)
            acc[rows, columns] += jnp.dot(gated, out_buf[slot, side], preferred_element_type=F32)

    chunk_loop(row_count, mlp)


def forward_second(half_ref, *refs):
    rows_ref, gate_ref, start_ref = refs[:3]
    packs = refs[3:11]
    pre_ref, gated_ref = refs[-6:-4]
    targets = refs[13:-6]
    acc, in_buf, out_buf, sems = refs[-4:]
    step, slot, wait = stream_weights(2, packs, half_ref[0], in_buf, out_buf, sems)
    row_count, width = acc.shape

    wait()

    def mlp(rows, source):
        gated = apply_expert(rows, step + 2, slot, rows_ref, gate_ref, pre_ref, gated_ref, in_buf)
        for side in range(2):
            columns = slice(side * width // 2, (side + 1) * width // 2)
            acc[rows, columns] = source[rows, columns] + jnp.dot(
                gated, out_buf[slot, side], preferred_element_type=F32
            )

    @pl.when(step == 0)
    def _():
        acc[...] = start_ref[...]

    chunk_loop(row_count, lambda rows: mlp(rows, acc))

    @pl.when(step == pl.num_programs(0) - 1)
    def _():
        spread(acc, targets)


def spread(acc, targets):
    size = acc.shape[0] // len(targets)
    for i, target in enumerate(targets):
        target[...] = acc[i * size : (i + 1) * size, :].astype(target.dtype)


def spread_specs(part, row_count, width):
    if part == 0:
        shapes = [jax.ShapeDtypeStruct((row_count // 2, width), F32)]
    else:
        shapes = [jax.ShapeDtypeStruct((row_count // 4, width), BF16)] * 2
    return ([whole_block(s.shape) for s in shapes], shapes)


def half_rows(shape, part):
    block = (shape[0] // 2,) + shape[1:]
    return pl.BlockSpec(block, lambda e, *_: (part, 0))


def half_expert(shape, part, first=0):
    block = (1, shape[1] // 2) + shape[2:]
    return pl.BlockSpec(block, lambda e, *_: (e + first, part, 0))


def expert_block(shape, first=0):
    return pl.BlockSpec((1,) + shape[1:], lambda e, *_: (e + first,) + (0,) * (len(shape) - 1))


def experts_forward(half_index, shards, route_ids, router, own, near, far):
    size, width = shards[0].shape
    row_count = 8 * size
    local = own[0].shape[0] // PACK
    hidden = 4 * SHARE
    sums = jax.ShapeDtypeStruct((row_count, width), F32)
    pre = jax.ShapeDtypeStruct((local, row_count, 2 * hidden), BF16)
    gated = jax.ShapeDtypeStruct((local, row_count, hidden), BF16)
    gates = jax.ShapeDtypeStruct((row_count, 128), F32)
    rows = jax.ShapeDtypeStruct((row_count, width), BF16)
    sums_a, pre_a, gated_a, gates, rows = pl.pallas_call(
        forward_first,
        grid_spec=pltpu.PrefetchScalarGridSpec(
            num_scalar_prefetch=1,
            grid=(2,),
            in_specs=[whole_block(v.shape) for v in (*shards, route_ids, router)]
            + [any_block()] * 8,
            out_specs=[
                whole_block(sums.shape),
                expert_block(pre.shape),
                expert_block(gated.shape),
                whole_block(gates.shape),
                whole_block(rows.shape),
            ],
            scratch_shapes=weight_scratch(width, hidden),
        ),
        out_shape=[sums, pre, gated, gates, rows],
        name="experts_forward_a",
    )(half_index, *shards, route_ids, router, *own, *near)
    far_pack, far_across, sums_a = lax.optimization_barrier((*far, sums_a))
    far = [far_pack, swap_core(far_pack), far_across, swap_core(far_across)]

    def second(part, pre_a, gated_a):
        specs, shapes = spread_specs(part, row_count, width)
        return pl.pallas_call(
            forward_second,
            grid_spec=pltpu.PrefetchScalarGridSpec(
                num_scalar_prefetch=1,
                grid=(2,),
                in_specs=[half_rows(v.shape, part) for v in (rows, gates, sums)]
                + [any_block()] * 10,
                out_specs=specs
                + [half_expert(pre.shape, part, 2), half_expert(gated.shape, part, 2)],
                scratch_shapes=[pltpu.VMEM((row_count // 2, width), F32)]
                + weight_scratch(width, hidden),
            ),
            out_shape=shapes + [pre, gated],
            input_output_aliases={12: len(shapes), 13: len(shapes) + 1},
            name="experts_forward_b",
        )(half_index, rows, gates, sums_a, *own, *far, pre_a, gated_a)

    send_near, send_far, pre_a, gated_a = second(1, pre_a, gated_a)
    keep, pre_a, gated_a = second(0, pre_a, gated_a)
    return (keep, send_near, send_far, pre_a, gated_a, gates, rows, far)


def backward_body(half_ref, *refs):
    shards = refs[:4]
    gate_ref, router_ref, pre_ref = refs[4:7]
    packs = refs[7:19]
    pre_grad_ref, logit_ref, grad_ref = refs[-7:-4]
    acc, in_buf, out_buf, sems = refs[-4:]
    step, slot, wait = stream_weights(0, packs, half_ref[0], in_buf, out_buf, sems)
    row_count, width = grad_ref.shape
    size = row_count // 4
    targets = [ref for ref in refs[19:-7] if ref.shape[0] * 2 == row_count]
    targets = targets or [refs[-8]]

    @pl.when(step == 0)
    def _():
        for i in range(4):
            grad_ref[i * size : (i + 1) * size, :] = shards[i][...]
        acc[...] = jnp.zeros_like(acc)
        logit_ref[...] = jnp.zeros_like(logit_ref)

    wait()

    def mlp(rows):
        plain = lax.dot_general(
            grad_ref[rows, : width // 2], out_buf[slot, 0], NT, preferred_element_type=F32
        ) + lax.dot_general(
            grad_ref[rows, width // 2 :], out_buf[slot, 1], NT, preferred_element_type=F32
        )
        gate_pre, up_pre = split_pairs(pre_ref[0, rows, :].astype(F32))
        weight = gate_column(gate_ref[rows, :], step)
        sigmoid = jax.nn.sigmoid(gate_pre)
        act = gate_pre * sigmoid
        grad_weight = jnp.sum(act * up_pre * plain, -1, keepdims=True)
        scaled = weight * plain
        pre_grad = join_pairs(
            scaled * up_pre * (sigmoid + act * (1.0 - sigmoid)), scaled * act
        ).astype(BF16)
        pre_grad_ref[0, rows, :] = pre_grad
        old = logit_ref[rows, :]
        lane = lax.broadcasted_iota(jnp.int32, old.shape, 1)
        value = weight * grad_weight
        high = value.astype(BF16).astype(F32)
        logit_ref[rows, :] = jnp.where(
            lane == step, high, jnp.where(lane == step + 32, value - high, old)
        )
        acc[rows, :] += lax.dot_general(pre_grad, in_buf[slot], NT, preferred_element_type=F32)

    chunk_loop(row_count, mlp)

    @pl.when(step == pl.num_programs(0) - 1)
    def _():
        def router(rows):
            acc[rows, :] += lax.dot_general(
                logit_ref[rows, :].astype(BF16), router_ref[...], NT, preferred_element_type=F32
            )

        chunk_loop(row_count, router)
        spread(acc, targets)


def experts_backward(part, half_index, shards, gates, router, pre, own, near, far, *before):
    row_count, width = (8 * shards[0].shape[0], shards[0].shape[1])
    local = pre.shape[0]
    specs, shapes = spread_specs(part, row_count, width)
    saved = [
        jax.ShapeDtypeStruct(pre.shape, BF16),
        jax.ShapeDtypeStruct((row_count, 128), F32),
        jax.ShapeDtypeStruct((row_count, width), BF16),
    ]
    return pl.pallas_call(
        backward_body,
        grid_spec=pltpu.PrefetchScalarGridSpec(
            num_scalar_prefetch=1,
            grid=(local,),
            in_specs=[whole_block(v.shape) for v in shards]
            + [half_rows(gates.shape, part), whole_block(router.shape)]
            + [half_expert(pre.shape, part)]
            + [any_block()] * (12 + len(before)),
            out_specs=specs
            + [half_expert(pre.shape, part)]
            + [half_rows(v.shape, part) for v in saved[1:]],
            scratch_shapes=[pltpu.VMEM((row_count // 2, width), F32)]
            + weight_scratch(width, 4 * SHARE),
        ),
        out_shape=shapes + saved,
        input_output_aliases={20 + i: len(shapes) + i for i in range(len(before))},
        name="experts_backward",
    )(half_index, *shards, gates, router, pre, *own, *near, *far, *before)


def grad_out_body(half_ref, gated_ref, other_ref, mine_ref, *refs):
    *outs, turned = refs[-5:]
    turned[...] = gated_ref[0].T

    def pair(q, carry):
        for n, source in ((0, other_ref), (2, mine_ref)):
            for odd in range(2):
                rows = pl.ds(pl.multiple_of((2 * q + odd) * SHARE, SHARE), SHARE)
                product = jnp.dot(turned[rows, :], source[...], preferred_element_type=F32)
                outs[n + odd][q, 0] = product.astype(BF16)
        return carry

    lax.fori_loop(0, 2, pair, 0)


def grad_expert_outs(half_index, gated, grads, *after):
    local, row_count, hidden = gated.shape
    width = grads.shape[1]
    half_spec = (row_count, width // 2)
    shape = (2, local, SHARE, width // 2)
    return pl.pallas_call(
        grad_out_body,
        grid_spec=pltpu.PrefetchScalarGridSpec(
            num_scalar_prefetch=1,
            grid=(local,),
            in_specs=[
                expert_block(gated.shape),
                pl.BlockSpec(half_spec, lambda e, half: (0, 1 - half[0])),
                pl.BlockSpec(half_spec, lambda e, half: (0, half[0])),
            ]
            + [any_block()] * len(after),
            out_specs=[pl.BlockSpec((2, 1) + shape[2:], lambda e, *_: (0, e, 0, 0))] * 4,
            scratch_shapes=[pltpu.VMEM((hidden, row_count), BF16)],
        ),
        out_shape=[jax.ShapeDtypeStruct(shape, BF16)] * 4,
        name="grad_expert_out",
    )(half_index, gated, grads, grads, *after)


def grad_in_body(half_ref, rows_ref, pre_ref, *refs):
    keep_ref, send_ref, turned = refs[-3:]

    @pl.when(pl.program_id(0) == 0)
    def _():
        turned[...] = rows_ref[...].T

    def part(i, carry):
        rows = pl.ds(pl.multiple_of(i * CHUNK, CHUNK), CHUNK)
        product = jnp.dot(turned[rows, :], pre_ref[0], preferred_element_type=F32).astype(BF16)
        for q in range(4):
            for c in range(2):
                start = (2 * q + c) * SHARE
                (keep_ref, send_ref)[q % 2][q // 2, 0, c, rows] = product[:, start : start + SHARE]
        return carry

    lax.fori_loop(0, turned.shape[0] // CHUNK, part, 0)


def grad_expert_ins(half_index, rows, pre_grad, first, count, *after):
    local, row_count, wide = pre_grad.shape
    width = rows.shape[1]
    shape = (2, count, 2, width // 2, SHARE)
    return pl.pallas_call(
        grad_in_body,
        grid_spec=pltpu.PrefetchScalarGridSpec(
            num_scalar_prefetch=1,
            grid=(count,),
            in_specs=[
                pl.BlockSpec((row_count, width // 2), lambda e, half: (0, half[0])),
                expert_block(pre_grad.shape, first),
            ]
            + [any_block()] * len(after),
            out_specs=[pl.BlockSpec((2, 1) + shape[2:], lambda e, *_: (0, e, 0, 0, 0))] * 2,
            scratch_shapes=[pltpu.VMEM((width // 2, row_count), BF16)],
        ),
        out_shape=[jax.ShapeDtypeStruct(shape, BF16)] * 2,
        name="grad_expert_in",
    )(half_index, rows, pre_grad, *after)


def fold_body(keep_ref, got_ref, *refs):
    near_ref, far_ref = refs[-2:]
    near_ref[...] = keep_ref[0].astype(F32) + got_ref[0].astype(F32)
    far_ref[...] = (keep_ref[1].astype(F32) + got_ref[1].astype(F32)).astype(BF16)


def fold_pairs(keep, got, *after):
    shape = keep.shape
    rest = (0,) * (len(shape) - 2)
    pair = pl.BlockSpec((2, 1) + shape[2:], lambda e: (0, e) + rest)
    single = pl.BlockSpec((1,) + shape[2:], lambda e: (e,) + rest)
    return pl.pallas_call(
        fold_body,
        grid=(shape[1],),
        in_specs=[pair, pair] + [any_block()] * len(after),
        out_specs=[single, single],
        out_shape=[
            jax.ShapeDtypeStruct(shape[1:], F32),
            jax.ShapeDtypeStruct(shape[1:], BF16),
        ],
        name="fold_pairs",
    )(keep, got, *after)


def finish_body(keep, near, four, two, extra, unit, scale, gain, grad_out, *refs):
    hidden_ref, attn_ref, gain_ref = refs[-3:]
    total = keep[...] + near[...].astype(F32) + extra[...]
    for part in (four, two):
        total = total + part[...].astype(F32)
    gain_ref[...] = jnp.sum((total * unit[...]).reshape(-1, 8, total.shape[1]), 0)
    weighted = total * gain[...]
    mean = jnp.mean(weighted * unit[...], -1, keepdims=True)
    hidden = grad_out[...] + scale[...] * (weighted - unit[...] * mean)
    hidden_ref[...] = hidden
    attn_ref[...] = (RESIDUAL * hidden).astype(BF16)


def finish_rows(keep, near, four, two, extra, unit, scale, gain, grad_out, *after):
    size, width = unit.shape
    block = pl.BlockSpec((size, width), lambda e: (0, 0))
    return pl.pallas_call(
        finish_body,
        grid=(1,),
        in_specs=[block] * 6
        + [whole_block((size, 1)), whole_block((1, width)), block]
        + [any_block()] * len(after),
        out_specs=[block, block, whole_block((8, width))],
        out_shape=[
            jax.ShapeDtypeStruct((size, width), F32),
            jax.ShapeDtypeStruct((size, width), BF16),
            jax.ShapeDtypeStruct((8, width), F32),
        ],
        name="finish_rows",
    )(keep, near, four, two, extra, unit, scale, gain, grad_out, *after)


def rotated(values, cosine, sine, sign):
    width = values.shape[1]
    lane = lax.broadcasted_iota(jnp.int32, values.shape, 1)
    lower = lax.rem(lane, HEAD_DIM) < HEAD_DIM // 2
    ahead = pltpu.roll(values, width - HEAD_DIM // 2, 1)
    behind = pltpu.roll(values, HEAD_DIM // 2, 1)
    turned = jnp.where(lower, -ahead, behind)
    repeat = width // cosine.shape[1]
    cosine = jnp.concatenate([cosine] * repeat, 1)
    sine = jnp.concatenate([sine] * repeat, 1)
    return values * cosine + sign * (turned * sine)


def head(values, index, start=0, stop=None):
    return values[start:stop, index * HEAD_DIM : (index + 1) * HEAD_DIM]


def probabilities(query, keys):
    scores = lax.dot_general(query, keys, NT, preferred_element_type=F32) * ATTN_SCALE
    powers = jnp.exp(scores - jnp.max(scores, -1, keepdims=True))
    return powers / jnp.sum(powers, -1, keepdims=True)


def attention_forward_body(
    core_ref, tokens, gain, query_w, key_w, value_w, output_w, cosine, sine, *refs
):
    normed, query, keys, values, attended, keep, send = refs[-7:]
    x = tokens[...].astype(F32)
    scale = lax.rsqrt(jnp.mean(x * x, -1, keepdims=True) + EPS)
    normed[...] = (x * scale * gain[...]).astype(BF16)
    low = normed[...]
    linear = jnp.dot(low, query_w[...], preferred_element_type=F32)
    query[...] = rotated(linear, cosine[...], sine[...], 1.0).astype(BF16)
    linear = jnp.dot(low, key_w[...], preferred_element_type=F32)
    keys[...] = rotated(linear, cosine[...], sine[...], 1.0).astype(BF16)
    values[...] = jnp.dot(low, value_w[...], preferred_element_type=F32).astype(BF16)
    group = query.shape[1] // keys.shape[1]
    for start in range(0, tokens.shape[0], BLOCK):
        stop = start + BLOCK
        parts = []
        for h in range(query.shape[1] // HEAD_DIM):
            probs = probabilities(head(query, h, start, stop), head(keys, h // group, 0, stop))
            parts.append(
                jnp.dot(
                    probs.astype(BF16),
                    head(values, h // group, 0, stop),
                    preferred_element_type=F32,
                )
            )
        attended[start:stop, :] = jnp.concatenate(parts, 1).astype(BF16)
    size = tokens.shape[0] // 4
    for r in range(2):
        for target, core in ((keep, core_ref[0]), (send, 1 - core_ref[0])):
            rows = pl.ds(pl.multiple_of((2 * r + core) * size, size), size)
            part = jnp.dot(attended[rows, :], output_w[...], preferred_element_type=F32)
            target[r] = part.astype(target.dtype)


def scalar_call(body, name, scalar, inputs, shapes, after=(), scratch=()):
    return pl.pallas_call(
        body,
        grid_spec=pltpu.PrefetchScalarGridSpec(
            num_scalar_prefetch=1,
            grid=(1,),
            in_specs=[whole_block(v.shape) for v in inputs] + [any_block()] * len(after),
            out_specs=[whole_block(s.shape) for s in shapes],
            scratch_shapes=list(scratch),
        ),
        out_shape=shapes,
        name=name,
    )(scalar, *inputs, *after)


def attention_forward(core, tokens, gain, query_w, key_w, value_w, output_w, tables, *after):
    rows, width = tokens.shape
    shapes = [
        jax.ShapeDtypeStruct((rows, width), BF16),
        jax.ShapeDtypeStruct((rows, query_w.shape[1]), BF16),
        jax.ShapeDtypeStruct((rows, key_w.shape[1]), BF16),
        jax.ShapeDtypeStruct((rows, value_w.shape[1]), BF16),
        jax.ShapeDtypeStruct((rows, query_w.shape[1]), BF16),
        jax.ShapeDtypeStruct((2, rows // 4, width), F32),
        jax.ShapeDtypeStruct((2, rows // 4, width), BF16),
    ]
    inputs = (tokens, gain, query_w, key_w, value_w, output_w, *tables)
    return scalar_call(
        attention_forward_body, "attention_forward", core, inputs, shapes, after
    )


TN = (((0,), (0,)), ((), ()))


def attention_backward_body(
    share_ref,
    tokens,
    query_w,
    key_w,
    value_w,
    output_w,
    cosine,
    sine,
    query,
    keys,
    values,
    first,
    second,
    third,
    fourth,
    *refs,
):
    grad, grad_qkv, gain, keep, send, grad_keys, grad_values = refs[-7:]
    share = share_ref[0]
    size = first.shape[0]
    for r, piece in enumerate((first, second, third, fourth)):
        place = jnp.bitwise_xor(share, r) * size
        grad[pl.ds(pl.multiple_of(place, size), size), :] = piece[...]
    back = lax.dot_general(grad[...], output_w[...], NT, preferred_element_type=F32).astype(BF16)
    wide, narrow = (query.shape[1], keys.shape[1])
    group = wide // narrow
    grad_keys[...] = jnp.zeros_like(grad_keys)
    grad_values[...] = jnp.zeros_like(grad_values)
    for start in range(0, tokens.shape[0], BLOCK):
        stop = start + BLOCK
        parts, key_parts, value_parts = ([], [], [])
        for kv in range(narrow // HEAD_DIM):
            key, value = (head(keys, kv, 0, stop), head(values, kv, 0, stop))
            key_sum, value_sum = (0.0, 0.0)
            for h in range(kv * group, (kv + 1) * group):
                query_h = head(query, h, start, stop)
                back_h = head(back, h, start, stop)
                probs = probabilities(query_h, key)
                inner = lax.dot_general(back_h, value, NT, preferred_element_type=F32)
                scores = probs * (inner - jnp.sum(probs * inner, -1, keepdims=True))
                scores = scores.astype(BF16)
                parts.append(ATTN_SCALE * jnp.dot(scores, key, preferred_element_type=F32))
                key_sum += lax.dot_general(scores, query_h, TN, preferred_element_type=F32)
                value_sum += lax.dot_general(
                    probs.astype(BF16), back_h, TN, preferred_element_type=F32
                )
            key_parts.append(ATTN_SCALE * key_sum)
            value_parts.append(value_sum)
        turned = rotated(
            jnp.concatenate(parts, 1), cosine[start:stop, :], sine[start:stop, :], -1.0
        )
        grad_qkv[start:stop, :wide] = turned.astype(BF16)
        grad_keys[:stop, :] += jnp.concatenate(key_parts, 1)
        grad_values[:stop, :] += jnp.concatenate(value_parts, 1)
    turned = rotated(grad_keys[...], cosine[...], sine[...], -1.0)
    grad_qkv[:, wide : wide + narrow] = turned.astype(BF16)
    grad_qkv[:, wide + narrow :] = grad_values[...].astype(BF16)
    total = jnp.zeros(gain.shape, F32)
    for r in range(2):
        for target, core in ((keep, share % 2), (send, 1 - share % 2)):
            rows = pl.ds(pl.multiple_of((2 * r + core) * size, size), size)
            part = lax.dot_general(
                grad_qkv[rows, :wide], query_w[...], NT, preferred_element_type=F32
            )
            part += lax.dot_general(
                grad_qkv[rows, wide : wide + narrow], key_w[...], NT, preferred_element_type=F32
            )
            part += lax.dot_general(
                grad_qkv[rows, wide + narrow :], value_w[...], NT, preferred_element_type=F32
            )
            target[r] = part.astype(target.dtype)
            x = tokens[rows, :].astype(F32)
            x = x * lax.rsqrt(jnp.mean(x * x, -1, keepdims=True) + EPS)
            total += jnp.sum((part * x).reshape(-1, 8, x.shape[1]), 0)
    gain[...] = total


def attention_backward(share, tokens, weights, tables, saved, pieces, *after):
    rows, width = tokens.shape
    narrow = saved[1].shape[1]
    shapes = [
        jax.ShapeDtypeStruct((rows, width), BF16),
        jax.ShapeDtypeStruct((rows, saved[0].shape[1] + 2 * narrow), BF16),
        jax.ShapeDtypeStruct((8, width), F32),
        jax.ShapeDtypeStruct((2, rows // 4, width), F32),
        jax.ShapeDtypeStruct((2, rows // 4, width), BF16),
    ]
    return scalar_call(
        attention_backward_body,
        "attention_backward",
        share,
        (tokens, *weights, *tables, *saved, *pieces),
        shapes,
        after,
        [pltpu.VMEM((rows, narrow), F32), pltpu.VMEM((rows, narrow), F32)],
    )


def reduce_body(place_ref, normed, grad_qkv, grad, attended, small, gain, *refs):
    keep, near, far = refs[-3:]
    step = pl.program_id(0)
    first = lax.dot_general(normed[...], grad_qkv[...], TN, preferred_element_type=F32)
    second = lax.dot_general(grad[...], attended[...], TN, preferred_element_type=F32)
    rest = jnp.zeros((SHARE - small.shape[0] - gain.shape[0], SHARE), F32)
    third = jnp.concatenate([small[...], gain[...], rest], 0).T
    part = jnp.concatenate([first, second, third], 1)

    @pl.when(step < 4)
    def _():
        keep[...] = part

    @pl.when((step == 4) | (step == 5))
    def _():
        near[...] = part.astype(BF16)

    @pl.when(step >= 6)
    def _():
        far[...] = part.astype(BF16)


def reduce_parts(place, normed, grad_qkv, grad, attended, small, gain, *after):
    rows, width = normed.shape
    size = width // 8
    total = grad_qkv.shape[1] + attended.shape[1] + SHARE

    def shard(e, place):
        order = jnp.where(e < 4, 2 * e, 2 * e - 7)
        return jnp.bitwise_xor(place[0], order)

    columns = pl.BlockSpec((rows, size), lambda e, place: (0, shard(e, place)))
    return pl.pallas_call(
        reduce_body,
        grid_spec=pltpu.PrefetchScalarGridSpec(
            num_scalar_prefetch=1,
            grid=(8,),
            in_specs=[
                columns,
                whole_block(grad_qkv.shape),
                columns,
                whole_block(attended.shape),
                pl.BlockSpec((small.shape[0], size), lambda e, place: (0, shard(e, place))),
                pl.BlockSpec((gain.shape[0], size), lambda e, place: (0, shard(e, place))),
            ]
            + [any_block()] * len(after),
            out_specs=[
                pl.BlockSpec((size, total), lambda e, _: (jnp.minimum(e, 3), 0)),
                pl.BlockSpec((size, total), lambda e, _: (jnp.clip(e - 4, 0, 1), 0)),
                pl.BlockSpec((size, total), lambda e, _: (jnp.clip(e - 6, 0, 1), 0)),
            ],
        ),
        out_shape=[
            jax.ShapeDtypeStruct((4 * size, total), F32),
            jax.ShapeDtypeStruct((2 * size, total), BF16),
            jax.ShapeDtypeStruct((2 * size, total), BF16),
        ],
        name="reduce_parts",
    )(place, normed, grad_qkv, grad, attended, small, gain, *after)


def unpack_body(place_ref, *refs):
    pieces = refs[:8]
    query, key, value, output, small = refs[-5:]
    size = pieces[0].shape[0]
    wide, narrow = (query.shape[1], key.shape[1])
    for r, piece in zip(ORDER, pieces):
        start = pl.multiple_of(jnp.bitwise_xor(place_ref[0], r) * size, size)
        rows = pl.ds(start, size)
        part = piece[...].astype(F32)
        query[rows, :] = part[:, :wide]
        key[rows, :] = part[:, wide : wide + narrow]
        value[rows, :] = part[:, wide + narrow : wide + 2 * narrow]
        begin = wide + 2 * narrow
        output[:, rows] = part[:, begin : begin + output.shape[0]].T
        small[rows, :] = part[:, begin + output.shape[0] :]


def assemble_body(share_ref, *refs):
    target = refs[-1]
    size = refs[0].shape[0]
    for r in range(4):
        start = pl.multiple_of(jnp.bitwise_xor(share_ref[0], r) * size, size)
        target[pl.ds(start, size), :] = refs[r][...].astype(target.dtype)


def spread_tensor(value):
    across = swap_y(value)
    return [value, swap_core(value), across, swap_core(across)]


def assemble(share, pieces, dtype, *after):
    size, width = pieces[0].shape
    shapes = [jax.ShapeDtypeStruct((4 * size, width), dtype)]
    return scalar_call(assemble_body, "assemble", share, pieces, shapes, after)[0]


def trade(value, bits):
    return lax.ppermute(value, "expert", [(i, i ^ bits) for i in range(8)])


def swap_y(value):
    return lax.ppermute(value, "tensor", [(i, i ^ 2) for i in range(4)])


def swap_core(value):
    return lax.ppermute(value, "tensor", [(i, i ^ 1) for i in range(4)])


def gather_experts(value):
    column = [value] + [trade(value, bits) for bits in (2, 4, 6)]
    return column + [trade(shard, 1) for shard in column]


def scatter_steps(keep, send_near, send_far, *beside):
    size = keep.shape[0] // 4
    got_far = trade(send_far, 1)
    send_near, got_far, keep = lax.optimization_barrier((send_near, got_far, keep))
    if beside:
        got_far, *beside = lax.optimization_barrier((got_far, *beside))
    far = (keep[2 * size :] + got_far.astype(F32)).astype(BF16)
    got_near = trade(send_near, 1)
    four, six = (trade(far[:size], 4), trade(far[size:], 6))
    near = (keep[size : 2 * size] + got_near[size:].astype(F32)).astype(BF16)
    return (keep, got_near, (trade(near, 2), four, six), *beside)


def scatter_experts(keep, send_near, send_far, *beside):
    size = keep.shape[0] // 4
    keep, got_near, back, *beside = scatter_steps(keep, send_near, send_far, *beside)
    total = keep[:size] + got_near[:size].astype(F32)
    for part in back:
        total = total + part.astype(F32)
    return (total, *beside) if beside else total


def scatter_tensor(keep, send, row):
    half = keep + swap_core(send).astype(F32)
    keep = lax.dynamic_index_in_dim(half, row, 0, False)
    send = lax.dynamic_index_in_dim(half, 1 - row, 0, False)
    return keep + swap_y(send.astype(BF16)).astype(F32)


def ordered(index, first, second):
    return jnp.where(
        index == 0, jnp.concatenate([first, second], 0), jnp.concatenate([second, first], 0)
    )


def per_device(
    tokens,
    teacher,
    valid_mask,
    routes,
    first_gain,
    query_weight,
    key_matrix,
    value_matrix,
    output_weight,
    second_gain,
    router_weight,
    expert_in,
    expert_out,
):
    row_count, model_width = tokens.shape
    expert_count = router_weight.shape[1]
    senders = lax.axis_size("expert")
    shares = lax.axis_size("tensor")
    fits = (
        (senders, shares) == (8, 4)
        and expert_count == senders * shares
        and expert_in.shape == (8, 2, model_width // 2, SHARE)
        and row_count == 4 * 128
    )
    if not fits:
        return general_device(
            tokens,
            teacher,
            valid_mask,
            routes,
            first_gain,
            query_weight,
            key_matrix,
            value_matrix,
            output_weight,
            second_gain,
            router_weight,
            expert_in,
            expert_out,
        )
    quarter = row_count // shares
    place = lax.axis_index("expert")
    share = lax.axis_index("tensor")
    row, core = (share // 2, share % 2)
    half_index = place // 4
    half_arg = half_index.reshape(1)
    held = expert_in.shape[0] // 2
    base = 8 * (place % 4) + held * half_index

    share_arg, core_arg, place_arg = (share.reshape(1), core.reshape(1), place.reshape(1))

    def quarter_of(values):
        return lax.dynamic_slice_in_dim(values, share * quarter, quarter, 0)

    local_valid = jnp.sum(valid_mask)
    routes_mine = quarter_of(routes)
    note = jnp.concatenate([routes_mine.T, jnp.full((TOP, quarter), local_valid, jnp.int32)], 0)

    own_pack, near_pack, far_pack = pack_weights(half_arg, expert_in, expert_out)
    near_pack = trade(near_pack, 4)
    far_pack = trade(far_pack, 4)
    own_across = swap_y(own_pack)

    router_rel = lax.dynamic_slice_in_dim(
        jnp.concatenate([router_weight, router_weight], 1), base, expert_count, 1
    )
    router_rel = jnp.pad(
        jnp.concatenate([router_rel, router_rel], 1), ((0, 0), (0, 128 - 2 * expert_count))
    )

    tables = [
        jnp.concatenate([table[:, 0]] * (2 * SHARE // HEAD_DIM), 1)
        for table in rope_tables(row_count, HEAD_DIM)
    ]
    weights = (query_weight, key_matrix, value_matrix, output_weight)
    first_normed, query, keys, values, attended, attn_keep, attn_send = attention_forward(
        core_arg, tokens, first_gain[None], *weights, tables, own_pack
    )
    notes = [note] + [trade(note, bits) for bits in (2, 4, 6)]
    near_pack, own_across, attn_send, *notes = lax.optimization_barrier(
        (near_pack, own_across, attn_send, *notes)
    )
    notes = jnp.stack(notes)
    others = trade(notes, 1)
    own = [own_pack, swap_core(own_pack), own_across, swap_core(own_across)]
    tokens_mine = quarter_of(tokens).astype(F32)
    attn_sum = scatter_tensor(attn_keep, attn_send, row)
    near_pack, attn_sum, others = lax.optimization_barrier((near_pack, attn_sum, others))
    hidden = tokens_mine + RESIDUAL * attn_sum
    scale_two = lax.rsqrt(jnp.mean(hidden * hidden, -1, keepdims=True) + EPS)
    unit_two = hidden * scale_two
    normed_two = (unit_two * second_gain).astype(BF16)
    beside = trade(normed_two, 1)
    near_pack, beside = lax.optimization_barrier((near_pack, beside))
    near_across = swap_y(near_pack)
    column = [normed_two] + [trade(normed_two, bits) for bits in (2, 4, 6)]
    across = [trade(shard, 1) for shard in column[1:]]
    far_pack, near_across, *gathered = lax.optimization_barrier(
        (far_pack, near_across, beside, *across, *column[1:])
    )
    row_shards = [normed_two, *gathered[4:], *gathered[:4]]
    near = [near_pack, swap_core(near_pack), near_across, swap_core(near_across)]
    far = (far_pack, swap_y(far_pack))
    notes = jnp.concatenate([notes, others], 0)
    valid_total = jnp.sum(notes[:, TOP, 0]).astype(F32)
    route_rel = jnp.bitwise_and(notes[:, :TOP] - base, expert_count - 1)
    route_rel = route_rel.transpose(0, 2, 1).reshape(senders * quarter, TOP)
    keep, send_near, send_far, pre, gated, gates, expert_rows, far = experts_forward(
        half_arg,
        row_shards,
        route_rel,
        router_rel,
        own,
        near,
        far,
    )
    moe_sum = scatter_experts(keep, send_near, send_far)

    output = hidden + RESIDUAL * moe_sum
    residual_err = output - quarter_of(teacher).astype(F32)
    valid_rows = quarter_of(valid_mask).astype(F32)[:, None]
    squared_local = jnp.sum(valid_rows * residual_err * residual_err)
    token_total = senders * row_count
    grad_out = token_total / valid_total * valid_rows * residual_err
    grad_moe = (RESIDUAL * grad_out).astype(BF16)
    gate_mean = jnp.sum(grad_moe.astype(F32) * moe_sum, -1, keepdims=True)
    mean_part = -gate_mean * dense_gates(normed_two, routes_mine, router_weight)
    mean_high = mean_part.astype(BF16)
    mean_part = jnp.concatenate([mean_high, (mean_part - mean_high.astype(F32)).astype(BF16)], 1)
    router_pair = jnp.concatenate([router_weight, router_weight], 1)
    mean_rows = jnp.einsum("te,de->td", mean_part, router_pair, preferred_element_type=F32)
    shards = gather_experts(grad_moe)
    packs = (gates, router_rel, pre, own, near, far)
    send_near, send_far, *saved = experts_backward(1, half_arg, shards[4:], *packs)
    keep, pre_grad, logit_grad, grad_rows = experts_backward(
        0, half_arg, shards[:4], *packs, *saved
    )
    got_far = trade(send_far, 1)
    send_near, got_far, keep = lax.optimization_barrier((send_near, got_far, keep))
    far_rows = (keep[2 * quarter :] + got_far.astype(F32)).astype(BF16)
    back = trade(far_rows, 4)
    got_near = trade(send_near, 1)
    other = 1 - half_arg
    in_keep, in_send = grad_expert_ins(other, expert_rows, pre_grad, 0, 2, far_rows)
    in_near, in_far = fold_pairs(in_keep, swap_core(in_send))
    in_ready = (in_near + swap_y(in_far).astype(F32)).astype(BF16)
    out_keep, out_send, own_out_keep, own_out_send = grad_expert_outs(
        half_arg, gated, grad_rows, in_far
    )
    late_keep, late_send = grad_expert_ins(other, expert_rows, pre_grad, 2, 2, in_far)
    back, out_send, late_send = lax.optimization_barrier((back, out_send, late_send))
    near_rows = keep[quarter : 2 * quarter] + got_near[quarter:].astype(F32)
    near_rows = (near_rows + back[quarter:].astype(F32)).astype(BF16)
    near_rows = trade(near_rows, 2)
    grad_hidden, grad_attn, grad_second_part = finish_rows(
        keep,
        got_near,
        back,
        near_rows,
        mean_rows,
        unit_two,
        scale_two,
        second_gain[None],
        grad_out,
        in_ready,
    )
    grad_second_part = jnp.sum(grad_second_part, 0)
    router_part = jnp.einsum(
        "te,td->ed", logit_grad.astype(BF16), expert_rows, preferred_element_type=F32
    )
    router_part = router_part[:expert_count] + router_part[expert_count : 2 * expert_count]
    router_part = lax.dynamic_slice_in_dim(
        jnp.concatenate([router_part, router_part], 0),
        jnp.bitwise_and(expert_count - base, expert_count - 1),
        expert_count,
        0,
    )
    mean_router = jnp.einsum("te,td->ed", mean_part, normed_two, preferred_element_type=F32)
    router_part = router_part + mean_router[:expert_count] + mean_router[expert_count:]

    small = jnp.concatenate(
        [
            router_part,
            grad_second_part[None],
            jnp.full((1, model_width), squared_local),
            jnp.zeros((6, model_width), F32),
        ],
        0,
    )
    small = small + swap_core(small)
    small = small + swap_y(small)
    own_in_keep, own_in_send = grad_expert_ins(
        half_arg, expert_rows, pre_grad, 0, held, grad_attn
    )
    pieces = spread_tensor(grad_attn)
    late_near, late_far = fold_pairs(late_keep, swap_core(late_send), pieces[2])
    out_near, out_far = fold_pairs(out_keep, swap_core(out_send), pieces[2])
    out_ready = (out_near + swap_y(out_far).astype(F32)).astype(BF16)
    late_ready = (late_near + swap_y(late_far).astype(F32)).astype(BF16)
    in_back = trade(in_ready, 4)
    before = (late_far, out_far, own_in_send, in_back)
    grad_attn, grad_qkv, gain_part, one_keep, one_send = attention_backward(
        share_arg, tokens, weights, tables, (query, keys, values), pieces, *before
    )
    late_back = trade(late_ready, 4)
    grad_one = scatter_tensor(one_keep, one_send, row)
    own_out_near, own_out_far = fold_pairs(own_out_keep, swap_core(own_out_send), grad_one)
    own_out_across = swap_y(own_out_far)
    own_in_near, own_in_far = fold_pairs(own_in_keep, swap_core(own_in_send), grad_one)
    own_in_across = swap_y(own_in_far)
    before = (late_ready,)
    keep, send_near, send_far = reduce_parts(
        place_arg, first_normed, grad_qkv, grad_attn, attended, small, gain_part, *before
    )
    total, late_back = scatter_experts(keep, send_near, send_far, late_back)
    total, own_out_across, own_in_across = lax.optimization_barrier(
        (total.astype(BF16), own_out_across, own_in_across)
    )
    shapes = [
        jax.ShapeDtypeStruct(shape, F32)
        for shape in (
            query_weight.shape,
            key_matrix.shape,
            value_matrix.shape,
            output_weight.shape,
            (model_width, 128),
        )
    ]
    shards = gather_experts(total)
    out_ready, shards[1] = lax.optimization_barrier((out_ready, shards[1]))
    out_back = trade(out_ready, 4)
    grad_query, grad_key, grad_value, grad_output, small = scalar_call(
        unpack_body, "unpack", place_arg, shards, shapes, (out_back,)
    )

    gain_part = jnp.sum(small[:, expert_count + 8 : expert_count + 16], 1).reshape(8, -1)
    gain_part = gain_part + swap_core(gain_part)
    gain_part = (gain_part + swap_y(gain_part)).reshape(-1)

    scale_mine = lax.rsqrt(jnp.mean(tokens_mine * tokens_mine, -1, keepdims=True) + EPS)
    unit_mine = tokens_mine * scale_mine
    grad_unit_one = grad_one * first_gain
    grad_tokens = grad_hidden + scale_mine * (
        grad_unit_one - unit_mine * jnp.mean(grad_unit_one * unit_mine, -1, keepdims=True)
    )
    grad_tokens = assemble(share_arg, spread_tensor(grad_tokens.astype(BF16)), F32)
    layer_output = assemble(share_arg, spread_tensor(output.astype(BF16)), BF16)
    grad_expert_out = ordered(
        half_index, own_out_near + own_out_across.astype(F32), out_back.astype(F32)
    )
    grad_expert_in = ordered(
        half_index,
        own_in_near + own_in_across.astype(F32),
        jnp.concatenate([in_back, late_back], 0).astype(F32),
    )
    return (
        layer_output,
        small[0, expert_count + 1] / (2.0 * model_width * valid_total),
        grad_tokens,
        gain_part,
        grad_query,
        grad_key,
        grad_value,
        grad_output,
        small[:, expert_count],
        small[:, :expert_count],
        grad_expert_in,
        grad_expert_out,
    )


def solution(mesh):
    return jax.shard_map(
        per_device,
        mesh=mesh,
        in_specs=(
            P("expert", None),
            P("expert", None),
            P("expert"),
            P("expert", None),
            P(),
            P(None, "tensor"),
            P(None, "tensor"),
            P(None, "tensor"),
            P("tensor", None),
            P(),
            P(),
            P("expert", None, None, "tensor"),
            P("expert", "tensor", None),
        ),
        out_specs=(
            P("expert", None),
            P(),
            P("expert", None),
            P(),
            P(None, "tensor"),
            P(None, "tensor"),
            P(None, "tensor"),
            P("tensor", None),
            P(),
            P(),
            P("expert", None, None, "tensor"),
            P("expert", "tensor", None),
        ),
        check_vma=False,
    )
```

```python
import jax
import jax.numpy as jnp
from jax import lax
from jax.experimental import pallas as pl
from jax.experimental.pallas import tpu as pltpu
from jax.sharding import PartitionSpec as P

HEAD_DIM = 64
TOP = 8
BLOCK = 256


EPS = 1e-06
ATTN_SCALE = 0.015625
RESIDUAL = 0.22
THETA = 10000.0


def shifted(value, axis, steps):
    count = lax.axis_size(axis)
    pairs = [(source, (source + steps) % count) for source in range(count)]
    return lax.ppermute(value, axis, pairs)


def rope_tables(length, head_size):
    half_size = head_size // 2
    frequency = THETA ** (-(jnp.arange(half_size, dtype=jnp.float32) * 2.0) / head_size)
    angle_table = jnp.arange(length, dtype=jnp.float32)[:, None] * frequency[None, :]
    return (jnp.cos(angle_table)[:, None, :], jnp.sin(angle_table)[:, None, :])


def apply_rotary(values, cosine_lookup, sine_lookup):
    half_size = values.shape[-1] // 2
    lower_half, upper_half = (values[..., :half_size], values[..., half_size:])
    return jnp.concatenate(
        [
            lower_half * cosine_lookup - upper_half * sine_lookup,
            upper_half * cosine_lookup + lower_half * sine_lookup,
        ],
        -1,
    )


def unrotate(grads, cosine_lookup, sine_lookup):
    half_size = grads.shape[-1] // 2
    lower_half, upper_half = (grads[..., :half_size], grads[..., half_size:])
    return jnp.concatenate(
        [
            lower_half * cosine_lookup + upper_half * sine_lookup,
            upper_half * cosine_lookup - lower_half * sine_lookup,
        ],
        -1,
    )


def normalize(values):
    row_peak = jnp.max(values, -1, keepdims=True)
    exp_scores = jnp.exp(values - row_peak)
    return exp_scores / jnp.sum(exp_scores, -1, keepdims=True)


def slot_tables(route_ids, expert_count, capacity):
    row_count, top_count = route_ids.shape
    onehot = route_ids[:, :, None] == jnp.arange(expert_count, dtype=jnp.int32)[None, None, :]
    hit_count = jnp.sum(onehot.astype(jnp.int32), 1)
    slot_place = jnp.cumsum(hit_count, 0) - 1
    within = jnp.take_along_axis(slot_place, route_ids, 1)
    dest_slot = route_ids * capacity + within
    pair_count = row_count * top_count
    source = (
        jnp.full((expert_count * capacity,), pair_count, jnp.int32)
        .at[dest_slot.reshape(-1)]
        .set(jnp.arange(pair_count, dtype=jnp.int32))
    )
    live_slot = source < pair_count
    token_row = jnp.minimum(source, pair_count - 1) // top_count
    return (onehot, dest_slot, source, live_slot, token_row)


def general_device(
    tokens,
    teacher,
    valid_mask,
    routes,
    first_gain,
    query_weight,
    key_matrix,
    value_matrix,
    output_weight,
    second_gain,
    router_weight,
    expert_in,
    expert_out,
):
    row_count = tokens.shape[0]
    model_width = tokens.shape[1]
    half_width = model_width // 2
    local_query = query_weight.shape[1] // HEAD_DIM
    local_kv = key_matrix.shape[1] // HEAD_DIM
    query_group_size = local_query // local_kv
    expert_count = router_weight.shape[1]
    row_local = expert_in.shape[0]
    senders = lax.axis_size("expert")
    partner_step = senders // 2
    capacity = 3 * row_count * TOP // (2 * expert_count)
    pair_count = row_count * TOP
    score_rows = min(512, row_count)
    valid_total = lax.psum(jnp.sum(valid_mask).astype(jnp.float32), "expert")
    tokens_f32 = tokens.astype(jnp.float32)
    scale_one = lax.rsqrt(jnp.mean(tokens_f32 * tokens_f32, -1, keepdims=True) + EPS)
    unit_one = tokens_f32 * scale_one
    first_normed = (unit_one * first_gain).astype(jnp.bfloat16)
    cosine_lookup, sine_lookup = rope_tables(row_count, HEAD_DIM)
    query_linear = jnp.dot(first_normed, query_weight, preferred_element_type=jnp.float32).reshape(
        row_count, local_query, HEAD_DIM
    )
    keys_linear = jnp.dot(first_normed, key_matrix, preferred_element_type=jnp.float32).reshape(
        row_count, local_kv, HEAD_DIM
    )
    value_low = jnp.dot(first_normed, value_matrix, preferred_element_type=jnp.float32).astype(
        jnp.bfloat16
    )
    value_low = value_low.reshape(row_count, local_kv, HEAD_DIM)
    query_rotated = apply_rotary(query_linear, cosine_lookup, sine_lookup).astype(jnp.bfloat16)
    keys_rot = apply_rotary(keys_linear, cosine_lookup, sine_lookup).astype(jnp.bfloat16)
    block_of = jnp.arange(row_count, dtype=jnp.int32) // BLOCK

    def scores(start_row):
        stop_row = start_row + score_rows
        query_block = query_rotated.reshape(score_rows, local_kv, query_group_size, HEAD_DIM)
        score_block = (
            jnp.einsum("qhgd,khd->hgqk", query_block, keys_rot, preferred_element_type=jnp.float32)
            * ATTN_SCALE
        )
        allowed = block_of[None, :stop_row] <= block_of[start_row:stop_row, None]
        return (query_block, jnp.where(allowed, score_block, -1e30))

    attn_parts, row_peaks, row_totals = ([], [], [])
    start_row = 0
    query_block, score_block = scores(start_row)
    row_peak = jnp.max(score_block, -1, keepdims=True)
    exp_scores = jnp.exp(score_block - row_peak)
    row_total = jnp.sum(exp_scores, -1, keepdims=True)
    attn_probs = (exp_scores / row_total).astype(jnp.bfloat16)
    attn_parts.append(
        jnp.einsum("hgqk,khd->qhgd", attn_probs, value_low, preferred_element_type=jnp.float32)
    )
    row_peaks.append(row_peak)
    row_totals.append(row_total)
    attended = attn_parts[0].reshape(row_count, local_query * HEAD_DIM).astype(jnp.bfloat16)
    attn_part = jnp.dot(attended, output_weight, preferred_element_type=jnp.float32)
    attn_sum = lax.psum(attn_part, "tensor")
    hidden_state = tokens_f32 + RESIDUAL * attn_sum
    scale_two = lax.rsqrt(jnp.mean(hidden_state * hidden_state, -1, keepdims=True) + EPS)
    unit_two = hidden_state * scale_two
    normed_two = (unit_two * second_gain).astype(jnp.bfloat16)
    router_logits = jnp.dot(normed_two, router_weight, preferred_element_type=jnp.float32)
    onehot, dest_slot, source, live_slot, token_row = slot_tables(routes, expert_count, capacity)
    picked = jnp.sum(jnp.where(onehot, router_logits[:, None, :], 0.0), -1)
    gate_probs = normalize(picked)

    def slot_rows(slot_values):
        split_rows = slot_values.reshape(expert_count, capacity, 2, half_width).transpose(
            2, 0, 1, 3
        )
        return split_rows.reshape(senders, row_local, capacity, half_width)

    def slot_columns(returned, width):
        joined = returned.reshape(2, expert_count, capacity, width).transpose(1, 2, 0, 3)
        return joined.reshape(expert_count * capacity, 2, width)

    send_rows = slot_rows(
        jnp.where(live_slot[:, None], normed_two[token_row], jnp.zeros((), jnp.bfloat16))
    )
    received = lax.all_to_all(send_rows, "expert", split_axis=0, concat_axis=2, tiled=True)
    expert_rows = received.reshape(row_local, senders * capacity, half_width)
    gate_up_part = jnp.einsum(
        "rmd,rcdf->rmcf", expert_rows, expert_in, preferred_element_type=jnp.float32
    )
    gate_up_pre = gate_up_part + shifted(gate_up_part, "expert", partner_step)
    gate_pre = gate_up_pre[:, :, 0]
    up_pre = gate_up_pre[:, :, 1]
    inner_act = (jax.nn.silu(gate_pre) * up_pre).astype(jnp.bfloat16)
    expert_result = jnp.einsum(
        "rmf,rfd->rmd", inner_act, expert_out, preferred_element_type=jnp.float32
    )
    expert_result = expert_result.astype(jnp.bfloat16).reshape(
        row_local, senders, capacity, half_width
    )
    returned = lax.all_to_all(expert_result, "expert", split_axis=1, concat_axis=0, tiled=True)
    per_route = slot_columns(returned, half_width).reshape(expert_count * capacity, model_width)[
        dest_slot
    ]
    moe_part = jnp.sum(gate_probs[:, :, None] * per_route, 1)
    moe_sum = lax.psum(moe_part, "tensor")
    output = hidden_state + RESIDUAL * moe_sum
    residual_err = output - teacher.astype(jnp.float32)
    valid_rows = valid_mask.astype(jnp.float32)
    squared_local = jnp.sum(valid_rows * jnp.sum(residual_err * residual_err, -1))
    token_total = senders * row_count
    grad_out = token_total / valid_total * valid_rows[:, None] * residual_err
    grad_moe = (RESIDUAL * grad_out).astype(jnp.bfloat16)
    gate_part = jnp.einsum("td,tkd->tk", grad_moe, per_route, preferred_element_type=jnp.float32)
    gate_slot = gate_probs.reshape(pair_count)[jnp.minimum(source, pair_count - 1)]
    grad_slots = jnp.where(live_slot[:, None], gate_slot[:, None] * grad_moe[token_row], 0.0)
    grad_received = lax.all_to_all(
        slot_rows(grad_slots.astype(jnp.bfloat16)),
        "expert",
        split_axis=0,
        concat_axis=2,
        tiled=True,
    )
    grad_expert = grad_received.reshape(row_local, senders * capacity, half_width)
    grad_inner_part = jnp.einsum(
        "rmd,rfd->rmf", grad_expert, expert_out, preferred_element_type=jnp.float32
    )
    grad_inner = grad_inner_part + shifted(grad_inner_part, "expert", partner_step)
    grad_expert_out = jnp.einsum(
        "rmf,rmd->rfd", inner_act, grad_expert, preferred_element_type=jnp.float32
    )
    sigmoid_gate = jax.nn.sigmoid(gate_pre)
    grad_gate = grad_inner * up_pre * sigmoid_gate * (1.0 + gate_pre * (1.0 - sigmoid_gate))
    grad_up = grad_inner * (gate_pre * sigmoid_gate)
    grad_pre = jnp.stack([grad_gate, grad_up], 2).astype(jnp.bfloat16)
    grad_expert_in = jnp.einsum(
        "rmd,rmcf->rcdf", expert_rows, grad_pre, preferred_element_type=jnp.float32
    )
    grad_slot_rows = jnp.einsum(
        "rmcf,rcdf->rmd", grad_pre, expert_in, preferred_element_type=jnp.float32
    )
    grad_slot_rows = grad_slot_rows.astype(jnp.bfloat16).reshape(
        row_local, senders, capacity, half_width
    )
    grad_back = lax.all_to_all(grad_slot_rows, "expert", split_axis=1, concat_axis=0, tiled=True)
    grad_back = slot_columns(grad_back, half_width).reshape(expert_count * capacity, model_width)
    grad_two_part = jnp.sum(grad_back[dest_slot].astype(jnp.float32), 1)
    grad_two_experts, grad_gates = lax.psum((grad_two_part, gate_part), "tensor")
    grad_picked = gate_probs * (grad_gates - jnp.sum(gate_probs * grad_gates, -1, keepdims=True))
    grad_logits = jnp.sum(jnp.where(onehot, grad_picked[:, :, None], 0.0), 1).astype(jnp.bfloat16)
    grad_router = jnp.einsum(
        "td,te->de", normed_two, grad_logits, preferred_element_type=jnp.float32
    )
    grad_two = grad_two_experts + jnp.einsum(
        "te,de->td", grad_logits, router_weight, preferred_element_type=jnp.float32
    )
    grad_second_gain = jnp.sum(grad_two * unit_two, 0)
    grad_unit_two = grad_two * second_gain
    grad_hidden = grad_out + scale_two * (
        grad_unit_two - unit_two * jnp.mean(grad_unit_two * unit_two, -1, keepdims=True)
    )
    grad_attn = (RESIDUAL * grad_hidden).astype(jnp.bfloat16)
    grad_output = jnp.einsum("tc,td->cd", attended, grad_attn, preferred_element_type=jnp.float32)
    grad_attended = jnp.einsum(
        "td,cd->tc", grad_attn, output_weight, preferred_element_type=jnp.float32
    )
    grad_attended = grad_attended.astype(jnp.bfloat16).reshape(
        row_count, local_kv, query_group_size, HEAD_DIM
    )
    grad_query_parts = []
    grad_keys = jnp.zeros((row_count, local_kv, HEAD_DIM), jnp.float32)
    grad_values = jnp.zeros((row_count, local_kv, HEAD_DIM), jnp.float32)
    for block_index, start_row in enumerate(range(0, row_count, score_rows)):
        stop_row = start_row + score_rows
        query_block, score_block = scores(start_row)
        attn_probs = jnp.exp(score_block - row_peaks[block_index]) / row_totals[block_index]
        probs_low = attn_probs.astype(jnp.bfloat16)
        grad_probs = jnp.einsum(
            "qhgd,khd->hgqk", grad_attended, value_low, preferred_element_type=jnp.float32
        )
        grad_scores = attn_probs * (
            grad_probs - jnp.sum(attn_probs * grad_probs, -1, keepdims=True)
        )
        grad_scores = grad_scores.astype(jnp.bfloat16)
        grad_query_parts.append(
            ATTN_SCALE
            * jnp.einsum(
                "hgqk,khd->qhgd", grad_scores, keys_rot, preferred_element_type=jnp.float32
            )
        )
        grad_keys = grad_keys.at[:stop_row].add(
            ATTN_SCALE
            * jnp.einsum(
                "hgqk,qhgd->khd", grad_scores, query_block, preferred_element_type=jnp.float32
            )
        )
        grad_values = grad_values.at[:stop_row].add(
            jnp.einsum(
                "hgqk,qhgd->khd", probs_low, grad_attended, preferred_element_type=jnp.float32
            )
        )
    grad_query_rot = grad_query_parts[0].reshape(row_count, local_query, HEAD_DIM)
    grad_query_low = unrotate(grad_query_rot, cosine_lookup, sine_lookup).reshape(
        row_count, local_query * HEAD_DIM
    )
    grad_query_low = grad_query_low.astype(jnp.bfloat16)
    grad_keys_low = unrotate(grad_keys, cosine_lookup, sine_lookup).reshape(
        row_count, local_kv * HEAD_DIM
    )
    grad_keys_low = grad_keys_low.astype(jnp.bfloat16)
    grad_values_low = grad_values.reshape(row_count, local_kv * HEAD_DIM).astype(jnp.bfloat16)
    grad_query = jnp.einsum(
        "td,tc->dc", first_normed, grad_query_low, preferred_element_type=jnp.float32
    )
    grad_key = jnp.einsum(
        "td,tc->dc", first_normed, grad_keys_low, preferred_element_type=jnp.float32
    )
    grad_value = jnp.einsum(
        "td,tc->dc", first_normed, grad_values_low, preferred_element_type=jnp.float32
    )
    grad_one_part = (
        jnp.einsum("tc,dc->td", grad_query_low, query_weight, preferred_element_type=jnp.float32)
        + jnp.einsum("tc,dc->td", grad_keys_low, key_matrix, preferred_element_type=jnp.float32)
        + jnp.einsum("tc,dc->td", grad_values_low, value_matrix, preferred_element_type=jnp.float32)
    )
    grad_one = lax.psum(grad_one_part.astype(jnp.bfloat16), "tensor").astype(jnp.float32)
    grad_first_gain = jnp.sum(grad_one * unit_one, 0)
    grad_unit_one = grad_one * first_gain
    grad_tokens = grad_hidden + scale_one * (
        grad_unit_one - unit_one * jnp.mean(grad_unit_one * unit_one, -1, keepdims=True)
    )
    reduced = lax.psum(
        (
            grad_first_gain,
            grad_query,
            grad_key,
            grad_value,
            grad_output,
            grad_second_gain,
            grad_router,
            squared_local,
        ),
        "expert",
    )
    loss_value = reduced[7] / (2.0 * model_width * valid_total)
    return (
        output.astype(jnp.bfloat16),
        loss_value,
        grad_tokens,
        reduced[0],
        reduced[1],
        reduced[2],
        reduced[3],
        reduced[4],
        reduced[5],
        reduced[6],
        grad_expert_in,
        grad_expert_out,
    )


BF16 = jnp.bfloat16
F32 = jnp.float32
CHUNK = 256
SHARE = 128
PACK = 12 * SHARE
NT = (((1,), (1,)), ((), ()))
ORDER = (0, 2, 4, 6, 1, 3, 5, 7)


def whole_block(shape):
    return pl.BlockSpec(shape, lambda e, *_: (0,) * len(shape))


def any_block():
    return pl.BlockSpec(memory_space=pl.ANY)


def pack_body(half_ref, own_in, own_out, other_in, other_out, *refs):
    own, near, far = refs[-3:]
    step = pl.program_id(0)

    def fill(target, source_in, source_out):
        for c in range(2):
            target[c * 4 * SHARE : (c + 1) * 4 * SHARE, :] = source_in[0, c]
        for k in range(4):
            target[(8 + k) * SHARE : (9 + k) * SHARE, :] = source_out[
                0, :, k * SHARE : (k + 1) * SHARE
            ]

    fill(own, own_in, own_out)

    @pl.when(step < 2)
    def _():
        fill(near, other_in, other_out)

    @pl.when(step >= 2)
    def _():
        fill(far, other_in, other_out)


def pack_weights(half_index, expert_in, expert_out, *after):
    held = expert_in.shape[0] // 2
    in_shape = (1,) + expert_in.shape[1:]
    out_shape = (1,) + expert_out.shape[1:]
    shapes = [(held * PACK, SHARE), (held // 2 * PACK, SHARE), (held // 2 * PACK, SHARE)]
    block = (PACK, SHARE)
    return pl.pallas_call(
        pack_body,
        grid_spec=pltpu.PrefetchScalarGridSpec(
            num_scalar_prefetch=1,
            grid=(held,),
            in_specs=[
                pl.BlockSpec(in_shape, lambda e, half: (half[0] * held + e, 0, 0, 0)),
                pl.BlockSpec(out_shape, lambda e, half: (half[0] * held + e, 0, 0)),
                pl.BlockSpec(in_shape, lambda e, half: ((1 - half[0]) * held + e, 0, 0, 0)),
                pl.BlockSpec(out_shape, lambda e, half: ((1 - half[0]) * held + e, 0, 0)),
            ]
            + [any_block()] * len(after),
            out_specs=[
                pl.BlockSpec(block, lambda e, half: (e, 0)),
                pl.BlockSpec(block, lambda e, half: (jnp.minimum(e, 1), 0)),
                pl.BlockSpec(block, lambda e, half: (jnp.maximum(e - 2, 0), 0)),
            ],
        ),
        out_shape=[jax.ShapeDtypeStruct(shape, BF16) for shape in shapes],
        name="pack_weights",
    )(half_index, expert_in, expert_out, expert_in, expert_out, *after)


def weight_copies(own, other, own_row, other_row, half, in_buf, out_buf, sems, slot):
    copies = []
    for q in range(4):
        for pack, row, side in ((own[q], own_row, half), (other[q], other_row, 1 - half)):
            for c in range(2):
                copies.append(
                    (
                        pack.at[pl.ds(pl.multiple_of(row + c * 4 * SHARE, SHARE), 4 * SHARE)],
                        in_buf.at[
                            slot,
                            pl.ds(pl.multiple_of(side * 4 * SHARE, SHARE), 4 * SHARE),
                            pl.ds((2 * q + c) * SHARE, SHARE),
                        ],
                    )
                )
            for k in range(4):
                copies.append(
                    (
                        pack.at[pl.ds(pl.multiple_of(row + (8 + k) * SHARE, SHARE), SHARE)],
                        out_buf.at[slot, side, pl.ds(q * SHARE, SHARE), pl.ds(k * SHARE, SHARE)],
                    )
                )
    return [
        pltpu.make_async_copy(source, target, sems.at[slot, n])
        for n, (source, target) in enumerate(copies)
    ]


def stream_weights(first, packs, half, in_buf, out_buf, sems):
    step = pl.program_id(0)
    slot = lax.rem(step, 2)
    own, near, far = (packs[0:4], packs[4:8], packs[8:12])

    def start(index, target):
        expert = first + index

        def begin(other, start_row):
            for copy in weight_copies(
                own, other, expert * PACK, start_row, half, in_buf, out_buf, sems, target
            ):
                copy.start()

        if not far:
            begin(near, index * PACK)
            return

        @pl.when(expert < 2)
        def _():
            begin(near, expert * PACK)

        @pl.when(expert >= 2)
        def _():
            begin(far, (expert - 2) * PACK)

    @pl.when(step == 0)
    def _():
        start(0, 0)

    @pl.when(step + 1 < pl.num_programs(0))
    def _():
        start(step + 1, 1 - slot)

    def wait():
        for copy in weight_copies(own, near, 0, 0, half, in_buf, out_buf, sems, slot):
            copy.wait()

    return (step, slot, wait)


def weight_scratch(width, hidden):
    return [
        pltpu.VMEM((2, width, 2 * hidden), BF16),
        pltpu.VMEM((2, 2, hidden, width // 2), BF16),
        pltpu.SemaphoreType.DMA((2, 48)),
    ]


def split_pairs(values):
    blocks = [values[:, i * SHARE : (i + 1) * SHARE] for i in range(values.shape[1] // SHARE)]
    return (jnp.concatenate(blocks[0::2], 1), jnp.concatenate(blocks[1::2], 1))


def join_pairs(first, second):
    blocks = []
    for i in range(first.shape[1] // SHARE):
        blocks.append(first[:, i * SHARE : (i + 1) * SHARE])
        blocks.append(second[:, i * SHARE : (i + 1) * SHARE])
    return jnp.concatenate(blocks, 1)


def chunk_loop(row_count, body):
    def step(i, carry):
        body(pl.ds(pl.multiple_of(i * CHUNK, CHUNK), CHUNK))
        return carry

    lax.fori_loop(0, row_count // CHUNK, step, 0)


def gate_column(gates, expert):
    lane = lax.broadcasted_iota(jnp.int32, gates.shape, 1)
    return jnp.sum(jnp.where(lane == expert, gates, 0.0), -1, keepdims=True)


def dense_gates(rows, ids, router):
    logits = jnp.dot(rows, router, preferred_element_type=F32)
    lane = lax.broadcasted_iota(jnp.int32, logits.shape, 1)
    mask = ids[:, 0:1] == lane
    for k in range(1, TOP):
        mask = mask | (ids[:, k : k + 1] == lane)
    masked = jnp.where(mask, logits, -1e30)
    powers = jnp.where(mask, jnp.exp(masked - jnp.max(masked, -1, keepdims=True)), 0.0)
    return powers / jnp.sum(powers, -1, keepdims=True)


def apply_expert(rows, expert, slot, rows_ref, gate_ref, pre_ref, gated_ref, in_buf):
    pre = jnp.dot(rows_ref[rows, :], in_buf[slot], preferred_element_type=F32)
    pre_ref[0, rows, :] = pre.astype(BF16)
    gate_pre, up_pre = split_pairs(pre)
    weight = gate_column(gate_ref[rows, :], expert)
    gated = (weight * (gate_pre * jax.nn.sigmoid(gate_pre) * up_pre)).astype(BF16)
    gated_ref[0, rows, :] = gated
    return gated


def forward_first(half_ref, *refs):
    shards = refs[:8]
    route_ref, router_ref = refs[8:10]
    packs = refs[10:18]
    acc, pre_ref, gated_ref, gate_ref, rows_ref, in_buf, out_buf, sems = refs[18:]
    step, slot, wait = stream_weights(0, packs, half_ref[0], in_buf, out_buf, sems)
    row_count, width = acc.shape
    size = row_count // 8

    @pl.when(step == 0)
    def _():
        for i in range(8):
            rows_ref[i * size : (i + 1) * size, :] = shards[i][...]
        acc[...] = jnp.zeros_like(acc)

        def gating(rows):
            gate_ref[rows, :] = dense_gates(rows_ref[rows, :], route_ref[rows, :], router_ref[...])

        chunk_loop(row_count, gating)

    wait()

    def mlp(rows):
        gated = apply_expert(rows, step, slot, rows_ref, gate_ref, pre_ref, gated_ref, in_buf)
        for side in range(2):
            columns = slice(side * width // 2, (side + 1) * width // 2)
            acc[rows, columns] += jnp.dot(gated, out_buf[slot, side], preferred_element_type=F32)

    chunk_loop(row_count, mlp)


def forward_second(half_ref, *refs):
    rows_ref, gate_ref, start_ref = refs[:3]
    packs = refs[3:11]
    pre_ref, gated_ref = refs[-6:-4]
    targets = refs[13:-6]
    acc, in_buf, out_buf, sems = refs[-4:]
    step, slot, wait = stream_weights(2, packs, half_ref[0], in_buf, out_buf, sems)
    row_count, width = acc.shape

    wait()

    def mlp(rows, source):
        gated = apply_expert(rows, step + 2, slot, rows_ref, gate_ref, pre_ref, gated_ref, in_buf)
        for side in range(2):
            columns = slice(side * width // 2, (side + 1) * width // 2)
            acc[rows, columns] = source[rows, columns] + jnp.dot(
                gated, out_buf[slot, side], preferred_element_type=F32
            )

    @pl.when(step == 0)
    def _():
        acc[...] = start_ref[...]

    chunk_loop(row_count, lambda rows: mlp(rows, acc))

    @pl.when(step == pl.num_programs(0) - 1)
    def _():
        spread(acc, targets)


def spread(acc, targets):
    size = acc.shape[0] // len(targets)
    for i, target in enumerate(targets):
        target[...] = acc[i * size : (i + 1) * size, :].astype(target.dtype)


def spread_specs(part, row_count, width):
    if part == 0:
        shapes = [jax.ShapeDtypeStruct((row_count // 2, width), F32)]
    else:
        shapes = [jax.ShapeDtypeStruct((row_count // 4, width), BF16)] * 2
    return ([whole_block(s.shape) for s in shapes], shapes)


def half_rows(shape, part):
    block = (shape[0] // 2,) + shape[1:]
    return pl.BlockSpec(block, lambda e, *_: (part, 0))


def half_expert(shape, part, first=0):
    block = (1, shape[1] // 2) + shape[2:]
    return pl.BlockSpec(block, lambda e, *_: (e + first, part, 0))


def expert_block(shape, first=0):
    return pl.BlockSpec((1,) + shape[1:], lambda e, *_: (e + first,) + (0,) * (len(shape) - 1))


def experts_forward(half_index, shards, route_ids, router, own, near, far):
    size, width = shards[0].shape
    row_count = 8 * size
    local = own[0].shape[0] // PACK
    hidden = 4 * SHARE
    sums = jax.ShapeDtypeStruct((row_count, width), F32)
    pre = jax.ShapeDtypeStruct((local, row_count, 2 * hidden), BF16)
    gated = jax.ShapeDtypeStruct((local, row_count, hidden), BF16)
    gates = jax.ShapeDtypeStruct((row_count, 128), F32)
    rows = jax.ShapeDtypeStruct((row_count, width), BF16)
    sums_a, pre_a, gated_a, gates, rows = pl.pallas_call(
        forward_first,
        grid_spec=pltpu.PrefetchScalarGridSpec(
            num_scalar_prefetch=1,
            grid=(2,),
            in_specs=[whole_block(v.shape) for v in (*shards, route_ids, router)]
            + [any_block()] * 8,
            out_specs=[
                whole_block(sums.shape),
                expert_block(pre.shape),
                expert_block(gated.shape),
                whole_block(gates.shape),
                whole_block(rows.shape),
            ],
            scratch_shapes=weight_scratch(width, hidden),
        ),
        out_shape=[sums, pre, gated, gates, rows],
        name="experts_forward_a",
    )(half_index, *shards, route_ids, router, *own, *near)
    far_pack, far_across, sums_a = lax.optimization_barrier((*far, sums_a))
    far = [far_pack, swap_core(far_pack), far_across, swap_core(far_across)]

    def second(part, pre_a, gated_a):
        specs, shapes = spread_specs(part, row_count, width)
        return pl.pallas_call(
            forward_second,
            grid_spec=pltpu.PrefetchScalarGridSpec(
                num_scalar_prefetch=1,
                grid=(2,),
                in_specs=[half_rows(v.shape, part) for v in (rows, gates, sums)]
                + [any_block()] * 10,
                out_specs=specs
                + [half_expert(pre.shape, part, 2), half_expert(gated.shape, part, 2)],
                scratch_shapes=[pltpu.VMEM((row_count // 2, width), F32)]
                + weight_scratch(width, hidden),
            ),
            out_shape=shapes + [pre, gated],
            input_output_aliases={12: len(shapes), 13: len(shapes) + 1},
            name="experts_forward_b",
        )(half_index, rows, gates, sums_a, *own, *far, pre_a, gated_a)

    send_near, send_far, pre_a, gated_a = second(1, pre_a, gated_a)
    keep, pre_a, gated_a = second(0, pre_a, gated_a)
    return (keep, send_near, send_far, pre_a, gated_a, gates, rows, far)


def backward_body(half_ref, *refs):
    shards = refs[:4]
    gate_ref, router_ref, pre_ref = refs[4:7]
    packs = refs[7:19]
    pre_grad_ref, logit_ref, grad_ref = refs[-7:-4]
    acc, in_buf, out_buf, sems = refs[-4:]
    step, slot, wait = stream_weights(0, packs, half_ref[0], in_buf, out_buf, sems)
    row_count, width = grad_ref.shape
    size = row_count // 4
    targets = [ref for ref in refs[19:-7] if ref.shape[0] * 2 == row_count]
    targets = targets or [refs[-8]]

    @pl.when(step == 0)
    def _():
        for i in range(4):
            grad_ref[i * size : (i + 1) * size, :] = shards[i][...]
        acc[...] = jnp.zeros_like(acc)
        logit_ref[...] = jnp.zeros_like(logit_ref)

    wait()

    def mlp(rows):
        plain = lax.dot_general(
            grad_ref[rows, : width // 2], out_buf[slot, 0], NT, preferred_element_type=F32
        ) + lax.dot_general(
            grad_ref[rows, width // 2 :], out_buf[slot, 1], NT, preferred_element_type=F32
        )
        gate_pre, up_pre = split_pairs(pre_ref[0, rows, :].astype(F32))
        weight = gate_column(gate_ref[rows, :], step)
        sigmoid = jax.nn.sigmoid(gate_pre)
        act = gate_pre * sigmoid
        grad_weight = jnp.sum(act * up_pre * plain, -1, keepdims=True)
        scaled = weight * plain
        pre_grad = join_pairs(
            scaled * up_pre * (sigmoid + act * (1.0 - sigmoid)), scaled * act
        ).astype(BF16)
        pre_grad_ref[0, rows, :] = pre_grad
        old = logit_ref[rows, :]
        lane = lax.broadcasted_iota(jnp.int32, old.shape, 1)
        value = weight * grad_weight
        high = value.astype(BF16).astype(F32)
        logit_ref[rows, :] = jnp.where(
            lane == step, high, jnp.where(lane == step + 32, value - high, old)
        )
        acc[rows, :] += lax.dot_general(pre_grad, in_buf[slot], NT, preferred_element_type=F32)

    chunk_loop(row_count, mlp)

    @pl.when(step == pl.num_programs(0) - 1)
    def _():
        def router(rows):
            acc[rows, :] += lax.dot_general(
                logit_ref[rows, :].astype(BF16), router_ref[...], NT, preferred_element_type=F32
            )

        chunk_loop(row_count, router)
        spread(acc, targets)


def experts_backward(part, half_index, shards, gates, router, pre, own, near, far, *before):
    row_count, width = (8 * shards[0].shape[0], shards[0].shape[1])
    local = pre.shape[0]
    specs, shapes = spread_specs(part, row_count, width)
    saved = [
        jax.ShapeDtypeStruct(pre.shape, BF16),
        jax.ShapeDtypeStruct((row_count, 128), F32),
        jax.ShapeDtypeStruct((row_count, width), BF16),
    ]
    return pl.pallas_call(
        backward_body,
        grid_spec=pltpu.PrefetchScalarGridSpec(
            num_scalar_prefetch=1,
            grid=(local,),
            in_specs=[whole_block(v.shape) for v in shards]
            + [half_rows(gates.shape, part), whole_block(router.shape)]
            + [half_expert(pre.shape, part)]
            + [any_block()] * (12 + len(before)),
            out_specs=specs
            + [half_expert(pre.shape, part)]
            + [half_rows(v.shape, part) for v in saved[1:]],
            scratch_shapes=[pltpu.VMEM((row_count // 2, width), F32)]
            + weight_scratch(width, 4 * SHARE),
        ),
        out_shape=shapes + saved,
        input_output_aliases={20 + i: len(shapes) + i for i in range(len(before))},
        name="experts_backward",
    )(half_index, *shards, gates, router, pre, *own, *near, *far, *before)


def grad_out_body(half_ref, gated_ref, other_ref, mine_ref, *refs):
    *outs, turned = refs[-5:]
    turned[...] = gated_ref[0].T

    def pair(q, carry):
        for n, source in ((0, other_ref), (2, mine_ref)):
            for odd in range(2):
                rows = pl.ds(pl.multiple_of((2 * q + odd) * SHARE, SHARE), SHARE)
                product = jnp.dot(turned[rows, :], source[...], preferred_element_type=F32)
                outs[n + odd][q, 0] = product.astype(BF16)
        return carry

    lax.fori_loop(0, 2, pair, 0)


def grad_expert_outs(half_index, gated, grads, *after):
    local, row_count, hidden = gated.shape
    width = grads.shape[1]
    half_spec = (row_count, width // 2)
    shape = (2, local, SHARE, width // 2)
    return pl.pallas_call(
        grad_out_body,
        grid_spec=pltpu.PrefetchScalarGridSpec(
            num_scalar_prefetch=1,
            grid=(local,),
            in_specs=[
                expert_block(gated.shape),
                pl.BlockSpec(half_spec, lambda e, half: (0, 1 - half[0])),
                pl.BlockSpec(half_spec, lambda e, half: (0, half[0])),
            ]
            + [any_block()] * len(after),
            out_specs=[pl.BlockSpec((2, 1) + shape[2:], lambda e, *_: (0, e, 0, 0))] * 4,
            scratch_shapes=[pltpu.VMEM((hidden, row_count), BF16)],
        ),
        out_shape=[jax.ShapeDtypeStruct(shape, BF16)] * 4,
        name="grad_expert_out",
    )(half_index, gated, grads, grads, *after)


def grad_in_body(half_ref, rows_ref, pre_ref, *refs):
    keep_ref, send_ref, turned = refs[-3:]

    @pl.when(pl.program_id(0) == 0)
    def _():
        turned[...] = rows_ref[...].T

    def part(i, carry):
        rows = pl.ds(pl.multiple_of(i * CHUNK, CHUNK), CHUNK)
        product = jnp.dot(turned[rows, :], pre_ref[0], preferred_element_type=F32).astype(BF16)
        for q in range(4):
            for c in range(2):
                start = (2 * q + c) * SHARE
                (keep_ref, send_ref)[q % 2][q // 2, 0, c, rows] = product[:, start : start + SHARE]
        return carry

    lax.fori_loop(0, turned.shape[0] // CHUNK, part, 0)


def grad_expert_ins(half_index, rows, pre_grad, first, count, *after):
    local, row_count, wide = pre_grad.shape
    width = rows.shape[1]
    shape = (2, count, 2, width // 2, SHARE)
    return pl.pallas_call(
        grad_in_body,
        grid_spec=pltpu.PrefetchScalarGridSpec(
            num_scalar_prefetch=1,
            grid=(count,),
            in_specs=[
                pl.BlockSpec((row_count, width // 2), lambda e, half: (0, half[0])),
                expert_block(pre_grad.shape, first),
            ]
            + [any_block()] * len(after),
            out_specs=[pl.BlockSpec((2, 1) + shape[2:], lambda e, *_: (0, e, 0, 0, 0))] * 2,
            scratch_shapes=[pltpu.VMEM((width // 2, row_count), BF16)],
        ),
        out_shape=[jax.ShapeDtypeStruct(shape, BF16)] * 2,
        name="grad_expert_in",
    )(half_index, rows, pre_grad, *after)


def fold_body(keep_ref, got_ref, *refs):
    near_ref, far_ref = refs[-2:]
    near_ref[...] = keep_ref[0].astype(F32) + got_ref[0].astype(F32)
    far_ref[...] = (keep_ref[1].astype(F32) + got_ref[1].astype(F32)).astype(BF16)


def fold_pairs(keep, got, *after):
    shape = keep.shape
    rest = (0,) * (len(shape) - 2)
    pair = pl.BlockSpec((2, 1) + shape[2:], lambda e: (0, e) + rest)
    single = pl.BlockSpec((1,) + shape[2:], lambda e: (e,) + rest)
    return pl.pallas_call(
        fold_body,
        grid=(shape[1],),
        in_specs=[pair, pair] + [any_block()] * len(after),
        out_specs=[single, single],
        out_shape=[
            jax.ShapeDtypeStruct(shape[1:], F32),
            jax.ShapeDtypeStruct(shape[1:], BF16),
        ],
        name="fold_pairs",
    )(keep, got, *after)


def finish_body(keep, near, four, two, extra, unit, scale, gain, grad_out, *refs):
    hidden_ref, attn_ref, gain_ref = refs[-3:]
    total = keep[...] + near[...].astype(F32) + extra[...]
    for part in (four, two):
        total = total + part[...].astype(F32)
    gain_ref[...] = jnp.sum((total * unit[...]).reshape(-1, 8, total.shape[1]), 0)
    weighted = total * gain[...]
    mean = jnp.mean(weighted * unit[...], -1, keepdims=True)
    hidden = grad_out[...] + scale[...] * (weighted - unit[...] * mean)
    hidden_ref[...] = hidden
    attn_ref[...] = (RESIDUAL * hidden).astype(BF16)


def finish_rows(keep, near, four, two, extra, unit, scale, gain, grad_out, *after):
    size, width = unit.shape
    block = pl.BlockSpec((size, width), lambda e: (0, 0))
    return pl.pallas_call(
        finish_body,
        grid=(1,),
        in_specs=[block] * 6
        + [whole_block((size, 1)), whole_block((1, width)), block]
        + [any_block()] * len(after),
        out_specs=[block, block, whole_block((8, width))],
        out_shape=[
            jax.ShapeDtypeStruct((size, width), F32),
            jax.ShapeDtypeStruct((size, width), BF16),
            jax.ShapeDtypeStruct((8, width), F32),
        ],
        name="finish_rows",
    )(keep, near, four, two, extra, unit, scale, gain, grad_out, *after)


def rotated(values, cosine, sine, sign):
    width = values.shape[1]
    lane = lax.broadcasted_iota(jnp.int32, values.shape, 1)
    lower = lax.rem(lane, HEAD_DIM) < HEAD_DIM // 2
    ahead = pltpu.roll(values, width - HEAD_DIM // 2, 1)
    behind = pltpu.roll(values, HEAD_DIM // 2, 1)
    turned = jnp.where(lower, -ahead, behind)
    repeat = width // cosine.shape[1]
    cosine = jnp.concatenate([cosine] * repeat, 1)
    sine = jnp.concatenate([sine] * repeat, 1)
    return values * cosine + sign * (turned * sine)


def head(values, index, start=0, stop=None):
    return values[start:stop, index * HEAD_DIM : (index + 1) * HEAD_DIM]


def probabilities(query, keys):
    scores = lax.dot_general(query, keys, NT, preferred_element_type=F32) * ATTN_SCALE
    powers = jnp.exp(scores - jnp.max(scores, -1, keepdims=True))
    return powers / jnp.sum(powers, -1, keepdims=True)


def attention_forward_body(
    core_ref, tokens, gain, query_w, key_w, value_w, output_w, cosine, sine, *refs
):
    normed, query, keys, values, attended, keep, send = refs[-7:]
    x = tokens[...].astype(F32)
    scale = lax.rsqrt(jnp.mean(x * x, -1, keepdims=True) + EPS)
    normed[...] = (x * scale * gain[...]).astype(BF16)
    low = normed[...]
    linear = jnp.dot(low, query_w[...], preferred_element_type=F32)
    query[...] = rotated(linear, cosine[...], sine[...], 1.0).astype(BF16)
    linear = jnp.dot(low, key_w[...], preferred_element_type=F32)
    keys[...] = rotated(linear, cosine[...], sine[...], 1.0).astype(BF16)
    values[...] = jnp.dot(low, value_w[...], preferred_element_type=F32).astype(BF16)
    group = query.shape[1] // keys.shape[1]
    for start in range(0, tokens.shape[0], BLOCK):
        stop = start + BLOCK
        parts = []
        for h in range(query.shape[1] // HEAD_DIM):
            probs = probabilities(head(query, h, start, stop), head(keys, h // group, 0, stop))
            parts.append(
                jnp.dot(
                    probs.astype(BF16),
                    head(values, h // group, 0, stop),
                    preferred_element_type=F32,
                )
            )
        attended[start:stop, :] = jnp.concatenate(parts, 1).astype(BF16)
    size = tokens.shape[0] // 4
    for r in range(2):
        for target, core in ((keep, core_ref[0]), (send, 1 - core_ref[0])):
            rows = pl.ds(pl.multiple_of((2 * r + core) * size, size), size)
            part = jnp.dot(attended[rows, :], output_w[...], preferred_element_type=F32)
            target[r] = part.astype(target.dtype)


def scalar_call(body, name, scalar, inputs, shapes, after=(), scratch=()):
    return pl.pallas_call(
        body,
        grid_spec=pltpu.PrefetchScalarGridSpec(
            num_scalar_prefetch=1,
            grid=(1,),
            in_specs=[whole_block(v.shape) for v in inputs] + [any_block()] * len(after),
            out_specs=[whole_block(s.shape) for s in shapes],
            scratch_shapes=list(scratch),
        ),
        out_shape=shapes,
        name=name,
    )(scalar, *inputs, *after)


def attention_forward(core, tokens, gain, query_w, key_w, value_w, output_w, tables, *after):
    rows, width = tokens.shape
    shapes = [
        jax.ShapeDtypeStruct((rows, width), BF16),
        jax.ShapeDtypeStruct((rows, query_w.shape[1]), BF16),
        jax.ShapeDtypeStruct((rows, key_w.shape[1]), BF16),
        jax.ShapeDtypeStruct((rows, value_w.shape[1]), BF16),
        jax.ShapeDtypeStruct((rows, query_w.shape[1]), BF16),
        jax.ShapeDtypeStruct((2, rows // 4, width), F32),
        jax.ShapeDtypeStruct((2, rows // 4, width), BF16),
    ]
    inputs = (tokens, gain, query_w, key_w, value_w, output_w, *tables)
    return scalar_call(
        attention_forward_body, "attention_forward", core, inputs, shapes, after
    )


TN = (((0,), (0,)), ((), ()))


def attention_backward_body(
    share_ref,
    tokens,
    query_w,
    key_w,
    value_w,
    output_w,
    cosine,
    sine,
    query,
    keys,
    values,
    first,
    second,
    third,
    fourth,
    *refs,
):
    grad, grad_qkv, gain, keep, send, grad_keys, grad_values = refs[-7:]
    share = share_ref[0]
    size = first.shape[0]
    for r, piece in enumerate((first, second, third, fourth)):
        place = jnp.bitwise_xor(share, r) * size
        grad[pl.ds(pl.multiple_of(place, size), size), :] = piece[...]
    back = lax.dot_general(grad[...], output_w[...], NT, preferred_element_type=F32).astype(BF16)
    wide, narrow = (query.shape[1], keys.shape[1])
    group = wide // narrow
    grad_keys[...] = jnp.zeros_like(grad_keys)
    grad_values[...] = jnp.zeros_like(grad_values)
    for start in range(0, tokens.shape[0], BLOCK):
        stop = start + BLOCK
        parts, key_parts, value_parts = ([], [], [])
        for kv in range(narrow // HEAD_DIM):
            key, value = (head(keys, kv, 0, stop), head(values, kv, 0, stop))
            key_sum, value_sum = (0.0, 0.0)
            for h in range(kv * group, (kv + 1) * group):
                query_h = head(query, h, start, stop)
                back_h = head(back, h, start, stop)
                probs = probabilities(query_h, key)
                inner = lax.dot_general(back_h, value, NT, preferred_element_type=F32)
                scores = probs * (inner - jnp.sum(probs * inner, -1, keepdims=True))
                scores = scores.astype(BF16)
                parts.append(ATTN_SCALE * jnp.dot(scores, key, preferred_element_type=F32))
                key_sum += lax.dot_general(scores, query_h, TN, preferred_element_type=F32)
                value_sum += lax.dot_general(
                    probs.astype(BF16), back_h, TN, preferred_element_type=F32
                )
            key_parts.append(ATTN_SCALE * key_sum)
            value_parts.append(value_sum)
        turned = rotated(
            jnp.concatenate(parts, 1), cosine[start:stop, :], sine[start:stop, :], -1.0
        )
        grad_qkv[start:stop, :wide] = turned.astype(BF16)
        grad_keys[:stop, :] += jnp.concatenate(key_parts, 1)
        grad_values[:stop, :] += jnp.concatenate(value_parts, 1)
    turned = rotated(grad_keys[...], cosine[...], sine[...], -1.0)
    grad_qkv[:, wide : wide + narrow] = turned.astype(BF16)
    grad_qkv[:, wide + narrow :] = grad_values[...].astype(BF16)
    total = jnp.zeros(gain.shape, F32)
    for r in range(2):
        for target, core in ((keep, share % 2), (send, 1 - share % 2)):
            rows = pl.ds(pl.multiple_of((2 * r + core) * size, size), size)
            part = lax.dot_general(
                grad_qkv[rows, :wide], query_w[...], NT, preferred_element_type=F32
            )
            part += lax.dot_general(
                grad_qkv[rows, wide : wide + narrow], key_w[...], NT, preferred_element_type=F32
            )
            part += lax.dot_general(
                grad_qkv[rows, wide + narrow :], value_w[...], NT, preferred_element_type=F32
            )
            target[r] = part.astype(target.dtype)
            x = tokens[rows, :].astype(F32)
            x = x * lax.rsqrt(jnp.mean(x * x, -1, keepdims=True) + EPS)
            total += jnp.sum((part * x).reshape(-1, 8, x.shape[1]), 0)
    gain[...] = total


def attention_backward(share, tokens, weights, tables, saved, pieces, *after):
    rows, width = tokens.shape
    narrow = saved[1].shape[1]
    shapes = [
        jax.ShapeDtypeStruct((rows, width), BF16),
        jax.ShapeDtypeStruct((rows, saved[0].shape[1] + 2 * narrow), BF16),
        jax.ShapeDtypeStruct((8, width), F32),
        jax.ShapeDtypeStruct((2, rows // 4, width), F32),
        jax.ShapeDtypeStruct((2, rows // 4, width), BF16),
    ]
    return scalar_call(
        attention_backward_body,
        "attention_backward",
        share,
        (tokens, *weights, *tables, *saved, *pieces),
        shapes,
        after,
        [pltpu.VMEM((rows, narrow), F32), pltpu.VMEM((rows, narrow), F32)],
    )


def reduce_body(place_ref, normed, grad_qkv, grad, attended, small, gain, *refs):
    keep, near, far = refs[-3:]
    step = pl.program_id(0)
    first = lax.dot_general(normed[...], grad_qkv[...], TN, preferred_element_type=F32)
    second = lax.dot_general(grad[...], attended[...], TN, preferred_element_type=F32)
    rest = jnp.zeros((SHARE - small.shape[0] - gain.shape[0], SHARE), F32)
    third = jnp.concatenate([small[...], gain[...], rest], 0).T
    part = jnp.concatenate([first, second, third], 1)

    @pl.when(step < 4)
    def _():
        keep[...] = part

    @pl.when((step == 4) | (step == 5))
    def _():
        near[...] = part.astype(BF16)

    @pl.when(step >= 6)
    def _():
        far[...] = part.astype(BF16)


def reduce_parts(place, normed, grad_qkv, grad, attended, small, gain, *after):
    rows, width = normed.shape
    size = width // 8
    total = grad_qkv.shape[1] + attended.shape[1] + SHARE

    def shard(e, place):
        order = jnp.where(e < 4, 2 * e, 2 * e - 7)
        return jnp.bitwise_xor(place[0], order)

    columns = pl.BlockSpec((rows, size), lambda e, place: (0, shard(e, place)))
    return pl.pallas_call(
        reduce_body,
        grid_spec=pltpu.PrefetchScalarGridSpec(
            num_scalar_prefetch=1,
            grid=(8,),
            in_specs=[
                columns,
                whole_block(grad_qkv.shape),
                columns,
                whole_block(attended.shape),
                pl.BlockSpec((small.shape[0], size), lambda e, place: (0, shard(e, place))),
                pl.BlockSpec((gain.shape[0], size), lambda e, place: (0, shard(e, place))),
            ]
            + [any_block()] * len(after),
            out_specs=[
                pl.BlockSpec((size, total), lambda e, _: (jnp.minimum(e, 3), 0)),
                pl.BlockSpec((size, total), lambda e, _: (jnp.clip(e - 4, 0, 1), 0)),
                pl.BlockSpec((size, total), lambda e, _: (jnp.clip(e - 6, 0, 1), 0)),
            ],
        ),
        out_shape=[
            jax.ShapeDtypeStruct((4 * size, total), F32),
            jax.ShapeDtypeStruct((2 * size, total), BF16),
            jax.ShapeDtypeStruct((2 * size, total), BF16),
        ],
        name="reduce_parts",
    )(place, normed, grad_qkv, grad, attended, small, gain, *after)


def unpack_body(place_ref, *refs):
    pieces = refs[:8]
    query, key, value, output, small = refs[-5:]
    size = pieces[0].shape[0]
    wide, narrow = (query.shape[1], key.shape[1])
    for r, piece in zip(ORDER, pieces):
        start = pl.multiple_of(jnp.bitwise_xor(place_ref[0], r) * size, size)
        rows = pl.ds(start, size)
        part = piece[...].astype(F32)
        query[rows, :] = part[:, :wide]
        key[rows, :] = part[:, wide : wide + narrow]
        value[rows, :] = part[:, wide + narrow : wide + 2 * narrow]
        begin = wide + 2 * narrow
        output[:, rows] = part[:, begin : begin + output.shape[0]].T
        small[rows, :] = part[:, begin + output.shape[0] :]


def assemble_body(share_ref, *refs):
    target = refs[-1]
    size = refs[0].shape[0]
    for r in range(4):
        start = pl.multiple_of(jnp.bitwise_xor(share_ref[0], r) * size, size)
        target[pl.ds(start, size), :] = refs[r][...].astype(target.dtype)


def spread_tensor(value):
    across = swap_y(value)
    return [value, swap_core(value), across, swap_core(across)]


def assemble(share, pieces, dtype, *after):
    size, width = pieces[0].shape
    shapes = [jax.ShapeDtypeStruct((4 * size, width), dtype)]
    return scalar_call(assemble_body, "assemble", share, pieces, shapes, after)[0]


def trade(value, bits):
    return lax.ppermute(value, "expert", [(i, i ^ bits) for i in range(8)])


def swap_y(value):
    return lax.ppermute(value, "tensor", [(i, i ^ 2) for i in range(4)])


def swap_core(value):
    return lax.ppermute(value, "tensor", [(i, i ^ 1) for i in range(4)])


def gather_experts(value):
    column = [value] + [trade(value, bits) for bits in (2, 4, 6)]
    return column + [trade(shard, 1) for shard in column]


def scatter_steps(keep, send_near, send_far, *beside):
    size = keep.shape[0] // 4
    got_far = trade(send_far, 1)
    send_near, got_far, keep = lax.optimization_barrier((send_near, got_far, keep))
    if beside:
        got_far, *beside = lax.optimization_barrier((got_far, *beside))
    far = (keep[2 * size :] + got_far.astype(F32)).astype(BF16)
    got_near = trade(send_near, 1)
    four, six = (trade(far[:size], 4), trade(far[size:], 6))
    near = (keep[size : 2 * size] + got_near[size:].astype(F32)).astype(BF16)
    return (keep, got_near, (trade(near, 2), four, six), *beside)


def scatter_experts(keep, send_near, send_far, *beside):
    size = keep.shape[0] // 4
    keep, got_near, back, *beside = scatter_steps(keep, send_near, send_far, *beside)
    total = keep[:size] + got_near[:size].astype(F32)
    for part in back:
        total = total + part.astype(F32)
    return (total, *beside) if beside else total


def scatter_tensor(keep, send, row):
    half = keep + swap_core(send).astype(F32)
    keep = lax.dynamic_index_in_dim(half, row, 0, False)
    send = lax.dynamic_index_in_dim(half, 1 - row, 0, False)
    return keep + swap_y(send.astype(BF16)).astype(F32)


def ordered(index, first, second):
    return jnp.where(
        index == 0, jnp.concatenate([first, second], 0), jnp.concatenate([second, first], 0)
    )


def per_device(
    tokens,
    teacher,
    valid_mask,
    routes,
    first_gain,
    query_weight,
    key_matrix,
    value_matrix,
    output_weight,
    second_gain,
    router_weight,
    expert_in,
    expert_out,
):
    row_count, model_width = tokens.shape
    expert_count = router_weight.shape[1]
    senders = lax.axis_size("expert")
    shares = lax.axis_size("tensor")
    fits = (
        (senders, shares) == (8, 4)
        and expert_count == senders * shares
        and expert_in.shape == (8, 2, model_width // 2, SHARE)
        and row_count == 4 * 128
    )
    if not fits:
        return general_device(
            tokens,
            teacher,
            valid_mask,
            routes,
            first_gain,
            query_weight,
            key_matrix,
            value_matrix,
            output_weight,
            second_gain,
            router_weight,
            expert_in,
            expert_out,
        )
    quarter = row_count // shares
    place = lax.axis_index("expert")
    share = lax.axis_index("tensor")
    row, core = (share // 2, share % 2)
    half_index = place // 4
    half_arg = half_index.reshape(1)
    held = expert_in.shape[0] // 2
    base = 8 * (place % 4) + held * half_index

    share_arg, core_arg, place_arg = (share.reshape(1), core.reshape(1), place.reshape(1))

    def quarter_of(values):
        return lax.dynamic_slice_in_dim(values, share * quarter, quarter, 0)

    local_valid = jnp.sum(valid_mask)
    routes_mine = quarter_of(routes)
    note = jnp.concatenate([routes_mine.T, jnp.full((TOP, quarter), local_valid, jnp.int32)], 0)

    own_pack, near_pack, far_pack = pack_weights(half_arg, expert_in, expert_out)
    near_pack = trade(near_pack, 4)
    far_pack = trade(far_pack, 4)
    own_across = swap_y(own_pack)

    router_rel = lax.dynamic_slice_in_dim(
        jnp.concatenate([router_weight, router_weight], 1), base, expert_count, 1
    )
    router_rel = jnp.pad(
        jnp.concatenate([router_rel, router_rel], 1), ((0, 0), (0, 128 - 2 * expert_count))
    )

    tables = [
        jnp.concatenate([table[:, 0]] * (2 * SHARE // HEAD_DIM), 1)
        for table in rope_tables(row_count, HEAD_DIM)
    ]
    weights = (query_weight, key_matrix, value_matrix, output_weight)
    first_normed, query, keys, values, attended, attn_keep, attn_send = attention_forward(
        core_arg, tokens, first_gain[None], *weights, tables, own_pack
    )
    notes = [note] + [trade(note, bits) for bits in (2, 4, 6)]
    near_pack, own_across, attn_send, *notes = lax.optimization_barrier(
        (near_pack, own_across, attn_send, *notes)
    )
    notes = jnp.stack(notes)
    others = trade(notes, 1)
    own = [own_pack, swap_core(own_pack), own_across, swap_core(own_across)]
    tokens_mine = quarter_of(tokens).astype(F32)
    attn_sum = scatter_tensor(attn_keep, attn_send, row)
    near_pack, attn_sum, others = lax.optimization_barrier((near_pack, attn_sum, others))
    hidden = tokens_mine + RESIDUAL * attn_sum
    scale_two = lax.rsqrt(jnp.mean(hidden * hidden, -1, keepdims=True) + EPS)
    unit_two = hidden * scale_two
    normed_two = (unit_two * second_gain).astype(BF16)
    beside = trade(normed_two, 1)
    near_pack, beside = lax.optimization_barrier((near_pack, beside))
    near_across = swap_y(near_pack)
    column = [normed_two] + [trade(normed_two, bits) for bits in (2, 4, 6)]
    across = [trade(shard, 1) for shard in column[1:]]
    far_pack, near_across, *gathered = lax.optimization_barrier(
        (far_pack, near_across, beside, *across, *column[1:])
    )
    row_shards = [normed_two, *gathered[4:], *gathered[:4]]
    near = [near_pack, swap_core(near_pack), near_across, swap_core(near_across)]
    far = (far_pack, swap_y(far_pack))
    notes = jnp.concatenate([notes, others], 0)
    valid_total = jnp.sum(notes[:, TOP, 0]).astype(F32)
    route_rel = jnp.bitwise_and(notes[:, :TOP] - base, expert_count - 1)
    route_rel = route_rel.transpose(0, 2, 1).reshape(senders * quarter, TOP)
    keep, send_near, send_far, pre, gated, gates, expert_rows, far = experts_forward(
        half_arg,
        row_shards,
        route_rel,
        router_rel,
        own,
        near,
        far,
    )
    moe_sum = scatter_experts(keep, send_near, send_far)

    output = hidden + RESIDUAL * moe_sum
    residual_err = output - quarter_of(teacher).astype(F32)
    valid_rows = quarter_of(valid_mask).astype(F32)[:, None]
    squared_local = jnp.sum(valid_rows * residual_err * residual_err)
    token_total = senders * row_count
    grad_out = token_total / valid_total * valid_rows * residual_err
    grad_moe = (RESIDUAL * grad_out).astype(BF16)
    gate_mean = jnp.sum(grad_moe.astype(F32) * moe_sum, -1, keepdims=True)
    mean_part = -gate_mean * dense_gates(normed_two, routes_mine, router_weight)
    mean_high = mean_part.astype(BF16)
    mean_part = jnp.concatenate([mean_high, (mean_part - mean_high.astype(F32)).astype(BF16)], 1)
    router_pair = jnp.concatenate([router_weight, router_weight], 1)
    mean_rows = jnp.einsum("te,de->td", mean_part, router_pair, preferred_element_type=F32)
    out_pieces = spread_tensor(output.astype(BF16))
    shards = gather_experts(grad_moe)
    packs = (gates, router_rel, pre, own, near, far)
    send_near, send_far, *saved = experts_backward(1, half_arg, shards[4:], *packs)
    keep, pre_grad, logit_grad, grad_rows = experts_backward(
        0, half_arg, shards[:4], *packs, *saved
    )
    got_far = trade(send_far, 1)
    send_near, got_far, keep = lax.optimization_barrier((send_near, got_far, keep))
    far_rows = (keep[2 * quarter :] + got_far.astype(F32)).astype(BF16)
    back = trade(far_rows, 4)
    got_near = trade(send_near, 1)
    other = 1 - half_arg
    in_keep, in_send = grad_expert_ins(
        other, expert_rows, pre_grad, 0, 2, far_rows, *out_pieces[1:]
    )
    in_near, in_far = fold_pairs(in_keep, swap_core(in_send))
    in_ready = (in_near + swap_y(in_far).astype(F32)).astype(BF16)
    out_keep, out_send, own_out_keep, own_out_send = grad_expert_outs(
        half_arg, gated, grad_rows, in_far
    )
    late_keep, late_send = grad_expert_ins(other, expert_rows, pre_grad, 2, 2, in_far)
    router_part = jnp.einsum(
        "te,td->ed", logit_grad.astype(BF16), expert_rows, preferred_element_type=F32
    )
    router_part = router_part[:expert_count] + router_part[expert_count : 2 * expert_count]
    router_part = lax.dynamic_slice_in_dim(
        jnp.concatenate([router_part, router_part], 0),
        jnp.bitwise_and(expert_count - base, expert_count - 1),
        expert_count,
        0,
    )
    mean_router = jnp.einsum("te,td->ed", mean_part, normed_two, preferred_element_type=F32)
    router_part = router_part + mean_router[:expert_count] + mean_router[expert_count:]

    small = jnp.concatenate(
        [
            router_part,
            jnp.full((1, model_width), squared_local),
            jnp.zeros((7, model_width), F32),
        ],
        0,
    )
    small = small + swap_core(small)
    small = small + swap_y(small)
    back, out_send, late_send, small = lax.optimization_barrier(
        (back, out_send, late_send, small)
    )
    near_rows = keep[quarter : 2 * quarter] + got_near[quarter:].astype(F32)
    near_rows = (near_rows + back[quarter:].astype(F32)).astype(BF16)
    near_rows = trade(near_rows, 2)
    grad_hidden, grad_attn, grad_second_part = finish_rows(
        keep,
        got_near,
        back,
        near_rows,
        mean_rows,
        unit_two,
        scale_two,
        second_gain[None],
        grad_out,
        in_ready,
    )
    own_in_keep, own_in_send = grad_expert_ins(
        half_arg, expert_rows, pre_grad, 0, held, grad_attn
    )
    pieces = spread_tensor(grad_attn)
    late_near, late_far = fold_pairs(late_keep, swap_core(late_send), pieces[2])
    out_near, out_far = fold_pairs(out_keep, swap_core(out_send), pieces[2])
    out_ready = (out_near + swap_y(out_far).astype(F32)).astype(BF16)
    late_ready = (late_near + swap_y(late_far).astype(F32)).astype(BF16)
    in_back = trade(in_ready, 4)
    before = (late_far, out_far, own_in_send, in_back)
    grad_attn, grad_qkv, gain_part, one_keep, one_send = attention_backward(
        share_arg, tokens, weights, tables, (query, keys, values), pieces, *before
    )
    late_back = trade(late_ready, 4)
    grad_one = scatter_tensor(one_keep, one_send, row)
    own_out_near, own_out_far = fold_pairs(own_out_keep, swap_core(own_out_send), grad_one)
    own_out_across = swap_y(own_out_far)
    own_in_near, own_in_far = fold_pairs(own_in_keep, swap_core(own_in_send), grad_one)
    own_in_across = swap_y(own_in_far)
    before = (late_ready,)
    gains = jnp.concatenate([grad_second_part, gain_part], 0)
    keep, send_near, send_far = reduce_parts(
        place_arg, first_normed, grad_qkv, grad_attn, attended, small, gains, *before
    )
    out_back = trade(out_ready, 4)
    total, late_back, out_back = scatter_experts(keep, send_near, send_far, late_back, out_back)
    total = total.astype(BF16)
    shapes = [
        jax.ShapeDtypeStruct(shape, F32)
        for shape in (
            query_weight.shape,
            key_matrix.shape,
            value_matrix.shape,
            output_weight.shape,
            (model_width, 128),
        )
    ]
    shards = gather_experts(total)
    grad_query, grad_key, grad_value, grad_output, small = scalar_call(
        unpack_body, "unpack", place_arg, shards, shapes, (own_out_across, own_in_across)
    )

    gains = small[:, expert_count + 8 : expert_count + 24].reshape(model_width, 2, 8)
    gains = jnp.sum(gains, 2).T.reshape(16, -1)
    gains = gains + swap_core(gains)
    gains = (gains + swap_y(gains)).reshape(2, -1)

    scale_mine = lax.rsqrt(jnp.mean(tokens_mine * tokens_mine, -1, keepdims=True) + EPS)
    unit_mine = tokens_mine * scale_mine
    grad_unit_one = grad_one * first_gain
    grad_tokens = grad_hidden + scale_mine * (
        grad_unit_one - unit_mine * jnp.mean(grad_unit_one * unit_mine, -1, keepdims=True)
    )
    grad_tokens = assemble(share_arg, spread_tensor(grad_tokens.astype(BF16)), F32)
    layer_output = assemble(share_arg, out_pieces, BF16)
    grad_expert_out = ordered(
        half_index, own_out_near + own_out_across.astype(F32), out_back.astype(F32)
    )
    grad_expert_in = ordered(
        half_index,
        own_in_near + own_in_across.astype(F32),
        jnp.concatenate([in_back, late_back], 0).astype(F32),
    )
    return (
        layer_output,
        small[0, expert_count] / (2.0 * model_width * valid_total),
        grad_tokens,
        gains[1],
        grad_query,
        grad_key,
        grad_value,
        grad_output,
        gains[0],
        small[:, :expert_count],
        grad_expert_in,
        grad_expert_out,
    )


def solution(mesh):
    return jax.shard_map(
        per_device,
        mesh=mesh,
        in_specs=(
            P("expert", None),
            P("expert", None),
            P("expert"),
            P("expert", None),
            P(),
            P(None, "tensor"),
            P(None, "tensor"),
            P(None, "tensor"),
            P("tensor", None),
            P(),
            P(),
            P("expert", None, None, "tensor"),
            P("expert", "tensor", None),
        ),
        out_specs=(
            P("expert", None),
            P(),
            P("expert", None),
            P(),
            P(None, "tensor"),
            P(None, "tensor"),
            P(None, "tensor"),
            P("tensor", None),
            P(),
            P(),
            P("expert", None, None, "tensor"),
            P("expert", "tensor", None),
        ),
        check_vma=False,
    )
```

```python
import jax
import jax.numpy as jnp
from jax import lax
from jax.experimental import pallas as pl
from jax.experimental.pallas import tpu as pltpu
from jax.sharding import PartitionSpec as P

HEAD_DIM = 64
TOP = 8
BLOCK = 256


EPS = 1e-06
ATTN_SCALE = 0.015625
RESIDUAL = 0.22
THETA = 10000.0


def shifted(value, axis, steps):
    count = lax.axis_size(axis)
    pairs = [(source, (source + steps) % count) for source in range(count)]
    return lax.ppermute(value, axis, pairs)


def rope_tables(length, head_size):
    half_size = head_size // 2
    frequency = THETA ** (-(jnp.arange(half_size, dtype=jnp.float32) * 2.0) / head_size)
    angle_table = jnp.arange(length, dtype=jnp.float32)[:, None] * frequency[None, :]
    return (jnp.cos(angle_table)[:, None, :], jnp.sin(angle_table)[:, None, :])


def apply_rotary(values, cosine_lookup, sine_lookup):
    half_size = values.shape[-1] // 2
    lower_half, upper_half = (values[..., :half_size], values[..., half_size:])
    return jnp.concatenate(
        [
            lower_half * cosine_lookup - upper_half * sine_lookup,
            upper_half * cosine_lookup + lower_half * sine_lookup,
        ],
        -1,
    )


def unrotate(grads, cosine_lookup, sine_lookup):
    half_size = grads.shape[-1] // 2
    lower_half, upper_half = (grads[..., :half_size], grads[..., half_size:])
    return jnp.concatenate(
        [
            lower_half * cosine_lookup + upper_half * sine_lookup,
            upper_half * cosine_lookup - lower_half * sine_lookup,
        ],
        -1,
    )


def normalize(values):
    row_peak = jnp.max(values, -1, keepdims=True)
    exp_scores = jnp.exp(values - row_peak)
    return exp_scores / jnp.sum(exp_scores, -1, keepdims=True)


def slot_tables(route_ids, expert_count, capacity):
    row_count, top_count = route_ids.shape
    onehot = route_ids[:, :, None] == jnp.arange(expert_count, dtype=jnp.int32)[None, None, :]
    hit_count = jnp.sum(onehot.astype(jnp.int32), 1)
    slot_place = jnp.cumsum(hit_count, 0) - 1
    within = jnp.take_along_axis(slot_place, route_ids, 1)
    dest_slot = route_ids * capacity + within
    pair_count = row_count * top_count
    source = (
        jnp.full((expert_count * capacity,), pair_count, jnp.int32)
        .at[dest_slot.reshape(-1)]
        .set(jnp.arange(pair_count, dtype=jnp.int32))
    )
    live_slot = source < pair_count
    token_row = jnp.minimum(source, pair_count - 1) // top_count
    return (onehot, dest_slot, source, live_slot, token_row)


def general_device(
    tokens,
    teacher,
    valid_mask,
    routes,
    first_gain,
    query_weight,
    key_matrix,
    value_matrix,
    output_weight,
    second_gain,
    router_weight,
    expert_in,
    expert_out,
):
    row_count = tokens.shape[0]
    model_width = tokens.shape[1]
    half_width = model_width // 2
    local_query = query_weight.shape[1] // HEAD_DIM
    local_kv = key_matrix.shape[1] // HEAD_DIM
    query_group_size = local_query // local_kv
    expert_count = router_weight.shape[1]
    row_local = expert_in.shape[0]
    senders = lax.axis_size("expert")
    partner_step = senders // 2
    capacity = 3 * row_count * TOP // (2 * expert_count)
    pair_count = row_count * TOP
    score_rows = min(512, row_count)
    valid_total = lax.psum(jnp.sum(valid_mask).astype(jnp.float32), "expert")
    tokens_f32 = tokens.astype(jnp.float32)
    scale_one = lax.rsqrt(jnp.mean(tokens_f32 * tokens_f32, -1, keepdims=True) + EPS)
    unit_one = tokens_f32 * scale_one
    first_normed = (unit_one * first_gain).astype(jnp.bfloat16)
    cosine_lookup, sine_lookup = rope_tables(row_count, HEAD_DIM)
    query_linear = jnp.dot(first_normed, query_weight, preferred_element_type=jnp.float32).reshape(
        row_count, local_query, HEAD_DIM
    )
    keys_linear = jnp.dot(first_normed, key_matrix, preferred_element_type=jnp.float32).reshape(
        row_count, local_kv, HEAD_DIM
    )
    value_low = jnp.dot(first_normed, value_matrix, preferred_element_type=jnp.float32).astype(
        jnp.bfloat16
    )
    value_low = value_low.reshape(row_count, local_kv, HEAD_DIM)
    query_rotated = apply_rotary(query_linear, cosine_lookup, sine_lookup).astype(jnp.bfloat16)
    keys_rot = apply_rotary(keys_linear, cosine_lookup, sine_lookup).astype(jnp.bfloat16)
    block_of = jnp.arange(row_count, dtype=jnp.int32) // BLOCK

    def scores(start_row):
        stop_row = start_row + score_rows
        query_block = query_rotated.reshape(score_rows, local_kv, query_group_size, HEAD_DIM)
        score_block = (
            jnp.einsum("qhgd,khd->hgqk", query_block, keys_rot, preferred_element_type=jnp.float32)
            * ATTN_SCALE
        )
        allowed = block_of[None, :stop_row] <= block_of[start_row:stop_row, None]
        return (query_block, jnp.where(allowed, score_block, -1e30))

    attn_parts, row_peaks, row_totals = ([], [], [])
    start_row = 0
    query_block, score_block = scores(start_row)
    row_peak = jnp.max(score_block, -1, keepdims=True)
    exp_scores = jnp.exp(score_block - row_peak)
    row_total = jnp.sum(exp_scores, -1, keepdims=True)
    attn_probs = (exp_scores / row_total).astype(jnp.bfloat16)
    attn_parts.append(
        jnp.einsum("hgqk,khd->qhgd", attn_probs, value_low, preferred_element_type=jnp.float32)
    )
    row_peaks.append(row_peak)
    row_totals.append(row_total)
    attended = attn_parts[0].reshape(row_count, local_query * HEAD_DIM).astype(jnp.bfloat16)
    attn_part = jnp.dot(attended, output_weight, preferred_element_type=jnp.float32)
    attn_sum = lax.psum(attn_part, "tensor")
    hidden_state = tokens_f32 + RESIDUAL * attn_sum
    scale_two = lax.rsqrt(jnp.mean(hidden_state * hidden_state, -1, keepdims=True) + EPS)
    unit_two = hidden_state * scale_two
    normed_two = (unit_two * second_gain).astype(jnp.bfloat16)
    router_logits = jnp.dot(normed_two, router_weight, preferred_element_type=jnp.float32)
    onehot, dest_slot, source, live_slot, token_row = slot_tables(routes, expert_count, capacity)
    picked = jnp.sum(jnp.where(onehot, router_logits[:, None, :], 0.0), -1)
    gate_probs = normalize(picked)

    def slot_rows(slot_values):
        split_rows = slot_values.reshape(expert_count, capacity, 2, half_width).transpose(
            2, 0, 1, 3
        )
        return split_rows.reshape(senders, row_local, capacity, half_width)

    def slot_columns(returned, width):
        joined = returned.reshape(2, expert_count, capacity, width).transpose(1, 2, 0, 3)
        return joined.reshape(expert_count * capacity, 2, width)

    send_rows = slot_rows(
        jnp.where(live_slot[:, None], normed_two[token_row], jnp.zeros((), jnp.bfloat16))
    )
    received = lax.all_to_all(send_rows, "expert", split_axis=0, concat_axis=2, tiled=True)
    expert_rows = received.reshape(row_local, senders * capacity, half_width)
    gate_up_part = jnp.einsum(
        "rmd,rcdf->rmcf", expert_rows, expert_in, preferred_element_type=jnp.float32
    )
    gate_up_pre = gate_up_part + shifted(gate_up_part, "expert", partner_step)
    gate_pre = gate_up_pre[:, :, 0]
    up_pre = gate_up_pre[:, :, 1]
    inner_act = (jax.nn.silu(gate_pre) * up_pre).astype(jnp.bfloat16)
    expert_result = jnp.einsum(
        "rmf,rfd->rmd", inner_act, expert_out, preferred_element_type=jnp.float32
    )
    expert_result = expert_result.astype(jnp.bfloat16).reshape(
        row_local, senders, capacity, half_width
    )
    returned = lax.all_to_all(expert_result, "expert", split_axis=1, concat_axis=0, tiled=True)
    per_route = slot_columns(returned, half_width).reshape(expert_count * capacity, model_width)[
        dest_slot
    ]
    moe_part = jnp.sum(gate_probs[:, :, None] * per_route, 1)
    moe_sum = lax.psum(moe_part, "tensor")
    output = hidden_state + RESIDUAL * moe_sum
    residual_err = output - teacher.astype(jnp.float32)
    valid_rows = valid_mask.astype(jnp.float32)
    squared_local = jnp.sum(valid_rows * jnp.sum(residual_err * residual_err, -1))
    token_total = senders * row_count
    grad_out = token_total / valid_total * valid_rows[:, None] * residual_err
    grad_moe = (RESIDUAL * grad_out).astype(jnp.bfloat16)
    gate_part = jnp.einsum("td,tkd->tk", grad_moe, per_route, preferred_element_type=jnp.float32)
    gate_slot = gate_probs.reshape(pair_count)[jnp.minimum(source, pair_count - 1)]
    grad_slots = jnp.where(live_slot[:, None], gate_slot[:, None] * grad_moe[token_row], 0.0)
    grad_received = lax.all_to_all(
        slot_rows(grad_slots.astype(jnp.bfloat16)),
        "expert",
        split_axis=0,
        concat_axis=2,
        tiled=True,
    )
    grad_expert = grad_received.reshape(row_local, senders * capacity, half_width)
    grad_inner_part = jnp.einsum(
        "rmd,rfd->rmf", grad_expert, expert_out, preferred_element_type=jnp.float32
    )
    grad_inner = grad_inner_part + shifted(grad_inner_part, "expert", partner_step)
    grad_expert_out = jnp.einsum(
        "rmf,rmd->rfd", inner_act, grad_expert, preferred_element_type=jnp.float32
    )
    sigmoid_gate = jax.nn.sigmoid(gate_pre)
    grad_gate = grad_inner * up_pre * sigmoid_gate * (1.0 + gate_pre * (1.0 - sigmoid_gate))
    grad_up = grad_inner * (gate_pre * sigmoid_gate)
    grad_pre = jnp.stack([grad_gate, grad_up], 2).astype(jnp.bfloat16)
    grad_expert_in = jnp.einsum(
        "rmd,rmcf->rcdf", expert_rows, grad_pre, preferred_element_type=jnp.float32
    )
    grad_slot_rows = jnp.einsum(
        "rmcf,rcdf->rmd", grad_pre, expert_in, preferred_element_type=jnp.float32
    )
    grad_slot_rows = grad_slot_rows.astype(jnp.bfloat16).reshape(
        row_local, senders, capacity, half_width
    )
    grad_back = lax.all_to_all(grad_slot_rows, "expert", split_axis=1, concat_axis=0, tiled=True)
    grad_back = slot_columns(grad_back, half_width).reshape(expert_count * capacity, model_width)
    grad_two_part = jnp.sum(grad_back[dest_slot].astype(jnp.float32), 1)
    grad_two_experts, grad_gates = lax.psum((grad_two_part, gate_part), "tensor")
    grad_picked = gate_probs * (grad_gates - jnp.sum(gate_probs * grad_gates, -1, keepdims=True))
    grad_logits = jnp.sum(jnp.where(onehot, grad_picked[:, :, None], 0.0), 1).astype(jnp.bfloat16)
    grad_router = jnp.einsum(
        "td,te->de", normed_two, grad_logits, preferred_element_type=jnp.float32
    )
    grad_two = grad_two_experts + jnp.einsum(
        "te,de->td", grad_logits, router_weight, preferred_element_type=jnp.float32
    )
    grad_second_gain = jnp.sum(grad_two * unit_two, 0)
    grad_unit_two = grad_two * second_gain
    grad_hidden = grad_out + scale_two * (
        grad_unit_two - unit_two * jnp.mean(grad_unit_two * unit_two, -1, keepdims=True)
    )
    grad_attn = (RESIDUAL * grad_hidden).astype(jnp.bfloat16)
    grad_output = jnp.einsum("tc,td->cd", attended, grad_attn, preferred_element_type=jnp.float32)
    grad_attended = jnp.einsum(
        "td,cd->tc", grad_attn, output_weight, preferred_element_type=jnp.float32
    )
    grad_attended = grad_attended.astype(jnp.bfloat16).reshape(
        row_count, local_kv, query_group_size, HEAD_DIM
    )
    grad_query_parts = []
    grad_keys = jnp.zeros((row_count, local_kv, HEAD_DIM), jnp.float32)
    grad_values = jnp.zeros((row_count, local_kv, HEAD_DIM), jnp.float32)
    for block_index, start_row in enumerate(range(0, row_count, score_rows)):
        stop_row = start_row + score_rows
        query_block, score_block = scores(start_row)
        attn_probs = jnp.exp(score_block - row_peaks[block_index]) / row_totals[block_index]
        probs_low = attn_probs.astype(jnp.bfloat16)
        grad_probs = jnp.einsum(
            "qhgd,khd->hgqk", grad_attended, value_low, preferred_element_type=jnp.float32
        )
        grad_scores = attn_probs * (
            grad_probs - jnp.sum(attn_probs * grad_probs, -1, keepdims=True)
        )
        grad_scores = grad_scores.astype(jnp.bfloat16)
        grad_query_parts.append(
            ATTN_SCALE
            * jnp.einsum(
                "hgqk,khd->qhgd", grad_scores, keys_rot, preferred_element_type=jnp.float32
            )
        )
        grad_keys = grad_keys.at[:stop_row].add(
            ATTN_SCALE
            * jnp.einsum(
                "hgqk,qhgd->khd", grad_scores, query_block, preferred_element_type=jnp.float32
            )
        )
        grad_values = grad_values.at[:stop_row].add(
            jnp.einsum(
                "hgqk,qhgd->khd", probs_low, grad_attended, preferred_element_type=jnp.float32
            )
        )
    grad_query_rot = grad_query_parts[0].reshape(row_count, local_query, HEAD_DIM)
    grad_query_low = unrotate(grad_query_rot, cosine_lookup, sine_lookup).reshape(
        row_count, local_query * HEAD_DIM
    )
    grad_query_low = grad_query_low.astype(jnp.bfloat16)
    grad_keys_low = unrotate(grad_keys, cosine_lookup, sine_lookup).reshape(
        row_count, local_kv * HEAD_DIM
    )
    grad_keys_low = grad_keys_low.astype(jnp.bfloat16)
    grad_values_low = grad_values.reshape(row_count, local_kv * HEAD_DIM).astype(jnp.bfloat16)
    grad_query = jnp.einsum(
        "td,tc->dc", first_normed, grad_query_low, preferred_element_type=jnp.float32
    )
    grad_key = jnp.einsum(
        "td,tc->dc", first_normed, grad_keys_low, preferred_element_type=jnp.float32
    )
    grad_value = jnp.einsum(
        "td,tc->dc", first_normed, grad_values_low, preferred_element_type=jnp.float32
    )
    grad_one_part = (
        jnp.einsum("tc,dc->td", grad_query_low, query_weight, preferred_element_type=jnp.float32)
        + jnp.einsum("tc,dc->td", grad_keys_low, key_matrix, preferred_element_type=jnp.float32)
        + jnp.einsum("tc,dc->td", grad_values_low, value_matrix, preferred_element_type=jnp.float32)
    )
    grad_one = lax.psum(grad_one_part.astype(jnp.bfloat16), "tensor").astype(jnp.float32)
    grad_first_gain = jnp.sum(grad_one * unit_one, 0)
    grad_unit_one = grad_one * first_gain
    grad_tokens = grad_hidden + scale_one * (
        grad_unit_one - unit_one * jnp.mean(grad_unit_one * unit_one, -1, keepdims=True)
    )
    reduced = lax.psum(
        (
            grad_first_gain,
            grad_query,
            grad_key,
            grad_value,
            grad_output,
            grad_second_gain,
            grad_router,
            squared_local,
        ),
        "expert",
    )
    loss_value = reduced[7] / (2.0 * model_width * valid_total)
    return (
        output.astype(jnp.bfloat16),
        loss_value,
        grad_tokens,
        reduced[0],
        reduced[1],
        reduced[2],
        reduced[3],
        reduced[4],
        reduced[5],
        reduced[6],
        grad_expert_in,
        grad_expert_out,
    )


BF16 = jnp.bfloat16
F32 = jnp.float32
CHUNK = 512
SHARE = 128
PACK = 12 * SHARE
NT = (((1,), (1,)), ((), ()))
ORDER = (0, 2, 4, 6, 1, 3, 5, 7)


def whole_block(shape):
    return pl.BlockSpec(shape, lambda e, *_: (0,) * len(shape))


def any_block():
    return pl.BlockSpec(memory_space=pl.ANY)


def pack_body(half_ref, own_in, own_out, other_in, other_out, *refs):
    own, near, far = refs[-3:]
    step = pl.program_id(0)

    def fill(target, source_in, source_out):
        for c in range(2):
            target[c * 4 * SHARE : (c + 1) * 4 * SHARE, :] = source_in[0, c]
        for k in range(4):
            target[(8 + k) * SHARE : (9 + k) * SHARE, :] = source_out[
                0, :, k * SHARE : (k + 1) * SHARE
            ]

    fill(own, own_in, own_out)

    @pl.when(step < 2)
    def _():
        fill(near, other_in, other_out)

    @pl.when(step >= 2)
    def _():
        fill(far, other_in, other_out)


def pack_weights(half_index, expert_in, expert_out, *after):
    held = expert_in.shape[0] // 2
    in_shape = (1,) + expert_in.shape[1:]
    out_shape = (1,) + expert_out.shape[1:]
    shapes = [(held * PACK, SHARE), (held // 2 * PACK, SHARE), (held // 2 * PACK, SHARE)]
    block = (PACK, SHARE)
    return pl.pallas_call(
        pack_body,
        grid_spec=pltpu.PrefetchScalarGridSpec(
            num_scalar_prefetch=1,
            grid=(held,),
            in_specs=[
                pl.BlockSpec(in_shape, lambda e, half: (half[0] * held + e, 0, 0, 0)),
                pl.BlockSpec(out_shape, lambda e, half: (half[0] * held + e, 0, 0)),
                pl.BlockSpec(in_shape, lambda e, half: ((1 - half[0]) * held + e, 0, 0, 0)),
                pl.BlockSpec(out_shape, lambda e, half: ((1 - half[0]) * held + e, 0, 0)),
            ]
            + [any_block()] * len(after),
            out_specs=[
                pl.BlockSpec(block, lambda e, half: (e, 0)),
                pl.BlockSpec(block, lambda e, half: (jnp.minimum(e, 1), 0)),
                pl.BlockSpec(block, lambda e, half: (jnp.maximum(e - 2, 0), 0)),
            ],
        ),
        out_shape=[jax.ShapeDtypeStruct(shape, BF16) for shape in shapes],
        name="pack_weights",
    )(half_index, expert_in, expert_out, expert_in, expert_out, *after)


def weight_copies(own, other, own_row, other_row, half, in_buf, out_buf, sems, slot):
    copies = []
    for q in range(4):
        for pack, row, side in ((own[q], own_row, half), (other[q], other_row, 1 - half)):
            for c in range(2):
                copies.append(
                    (
                        pack.at[pl.ds(pl.multiple_of(row + c * 4 * SHARE, SHARE), 4 * SHARE)],
                        in_buf.at[
                            slot,
                            pl.ds(pl.multiple_of(side * 4 * SHARE, SHARE), 4 * SHARE),
                            pl.ds((2 * q + c) * SHARE, SHARE),
                        ],
                    )
                )
            for k in range(4):
                copies.append(
                    (
                        pack.at[pl.ds(pl.multiple_of(row + (8 + k) * SHARE, SHARE), SHARE)],
                        out_buf.at[slot, side, pl.ds(q * SHARE, SHARE), pl.ds(k * SHARE, SHARE)],
                    )
                )
    return [
        pltpu.make_async_copy(source, target, sems.at[slot, n])
        for n, (source, target) in enumerate(copies)
    ]


def stream_weights(first, packs, half, in_buf, out_buf, sems):
    step = pl.program_id(0)
    slot = lax.rem(step, 2)
    own, near, far = (packs[0:4], packs[4:8], packs[8:12])

    def start(index, target):
        expert = first + index

        def begin(other, start_row):
            for copy in weight_copies(
                own, other, expert * PACK, start_row, half, in_buf, out_buf, sems, target
            ):
                copy.start()

        if not far:
            begin(near, index * PACK)
            return

        @pl.when(expert < 2)
        def _():
            begin(near, expert * PACK)

        @pl.when(expert >= 2)
        def _():
            begin(far, (expert - 2) * PACK)

    @pl.when(step == 0)
    def _():
        start(0, 0)

    @pl.when(step + 1 < pl.num_programs(0))
    def _():
        start(step + 1, 1 - slot)

    def wait():
        for copy in weight_copies(own, near, 0, 0, half, in_buf, out_buf, sems, slot):
            copy.wait()

    return (step, slot, wait)


def weight_scratch(width, hidden):
    return [
        pltpu.VMEM((2, width, 2 * hidden), BF16),
        pltpu.VMEM((2, 2, hidden, width // 2), BF16),
        pltpu.SemaphoreType.DMA((2, 48)),
    ]


def split_pairs(values):
    blocks = [values[:, i * SHARE : (i + 1) * SHARE] for i in range(values.shape[1] // SHARE)]
    return (jnp.concatenate(blocks[0::2], 1), jnp.concatenate(blocks[1::2], 1))


def join_pairs(first, second):
    blocks = []
    for i in range(first.shape[1] // SHARE):
        blocks.append(first[:, i * SHARE : (i + 1) * SHARE])
        blocks.append(second[:, i * SHARE : (i + 1) * SHARE])
    return jnp.concatenate(blocks, 1)


def chunk_loop(row_count, body):
    def step(i, carry):
        body(pl.ds(pl.multiple_of(i * CHUNK, CHUNK), CHUNK))
        return carry

    lax.fori_loop(0, row_count // CHUNK, step, 0)


def gate_column(gates, expert):
    lane = lax.broadcasted_iota(jnp.int32, gates.shape, 1)
    return jnp.sum(jnp.where(lane == expert, gates, 0.0), -1, keepdims=True)


def dense_gates(rows, ids, router):
    logits = jnp.dot(rows, router, preferred_element_type=F32)
    lane = lax.broadcasted_iota(jnp.int32, logits.shape, 1)
    mask = ids[:, 0:1] == lane
    for k in range(1, TOP):
        mask = mask | (ids[:, k : k + 1] == lane)
    masked = jnp.where(mask, logits, -1e30)
    powers = jnp.where(mask, jnp.exp(masked - jnp.max(masked, -1, keepdims=True)), 0.0)
    return powers / jnp.sum(powers, -1, keepdims=True)


def apply_expert(rows, expert, slot, rows_ref, gate_ref, pre_ref, gated_ref, in_buf):
    pre = jnp.dot(rows_ref[rows, :], in_buf[slot], preferred_element_type=F32)
    pre_ref[0, rows, :] = pre.astype(BF16)
    gate_pre, up_pre = split_pairs(pre)
    weight = gate_column(gate_ref[rows, :], expert)
    gated = (weight * (gate_pre * jax.nn.sigmoid(gate_pre) * up_pre)).astype(BF16)
    gated_ref[0, rows, :] = gated
    return gated


def forward_first(half_ref, *refs):
    shards = refs[:8]
    route_ref, router_ref = refs[8:10]
    packs = refs[10:18]
    acc, pre_ref, gated_ref, gate_ref, rows_ref, in_buf, out_buf, sems = refs[18:]
    step, slot, wait = stream_weights(0, packs, half_ref[0], in_buf, out_buf, sems)
    row_count, width = acc.shape
    size = row_count // 8

    @pl.when(step == 0)
    def _():
        for i in range(8):
            rows_ref[i * size : (i + 1) * size, :] = shards[i][...]
        acc[...] = jnp.zeros_like(acc)

        def gating(rows):
            gate_ref[rows, :] = dense_gates(rows_ref[rows, :], route_ref[rows, :], router_ref[...])

        chunk_loop(row_count, gating)

    wait()

    def mlp(rows):
        gated = apply_expert(rows, step, slot, rows_ref, gate_ref, pre_ref, gated_ref, in_buf)
        for side in range(2):
            columns = slice(side * width // 2, (side + 1) * width // 2)
            acc[rows, columns] += jnp.dot(gated, out_buf[slot, side], preferred_element_type=F32)

    chunk_loop(row_count, mlp)


def forward_second(half_ref, *refs):
    rows_ref, gate_ref, start_ref = refs[:3]
    packs = refs[3:11]
    pre_ref, gated_ref = refs[-6:-4]
    targets = refs[13:-6]
    acc, in_buf, out_buf, sems = refs[-4:]
    step, slot, wait = stream_weights(2, packs, half_ref[0], in_buf, out_buf, sems)
    row_count, width = acc.shape

    wait()

    def mlp(rows, source):
        gated = apply_expert(rows, step + 2, slot, rows_ref, gate_ref, pre_ref, gated_ref, in_buf)
        for side in range(2):
            columns = slice(side * width // 2, (side + 1) * width // 2)
            acc[rows, columns] = source[rows, columns] + jnp.dot(
                gated, out_buf[slot, side], preferred_element_type=F32
            )

    @pl.when(step == 0)
    def _():
        acc[...] = start_ref[...]

    chunk_loop(row_count, lambda rows: mlp(rows, acc))

    @pl.when(step == pl.num_programs(0) - 1)
    def _():
        spread(acc, targets)


def spread(acc, targets):
    size = acc.shape[0] // len(targets)
    for i, target in enumerate(targets):
        target[...] = acc[i * size : (i + 1) * size, :].astype(target.dtype)


def spread_specs(part, row_count, width):
    if part == 0:
        shapes = [jax.ShapeDtypeStruct((row_count // 2, width), F32)]
    else:
        shapes = [jax.ShapeDtypeStruct((row_count // 4, width), BF16)] * 2
    return ([whole_block(s.shape) for s in shapes], shapes)


def half_rows(shape, part):
    block = (shape[0] // 2,) + shape[1:]
    return pl.BlockSpec(block, lambda e, *_: (part, 0))


def half_expert(shape, part, first=0):
    block = (1, shape[1] // 2) + shape[2:]
    return pl.BlockSpec(block, lambda e, *_: (e + first, part, 0))


def expert_block(shape, first=0):
    return pl.BlockSpec((1,) + shape[1:], lambda e, *_: (e + first,) + (0,) * (len(shape) - 1))


def experts_forward(half_index, shards, route_ids, router, own, near, far):
    size, width = shards[0].shape
    row_count = 8 * size
    local = own[0].shape[0] // PACK
    hidden = 4 * SHARE
    sums = jax.ShapeDtypeStruct((row_count, width), F32)
    pre = jax.ShapeDtypeStruct((local, row_count, 2 * hidden), BF16)
    gated = jax.ShapeDtypeStruct((local, row_count, hidden), BF16)
    gates = jax.ShapeDtypeStruct((row_count, 128), F32)
    rows = jax.ShapeDtypeStruct((row_count, width), BF16)
    sums_a, pre_a, gated_a, gates, rows = pl.pallas_call(
        forward_first,
        grid_spec=pltpu.PrefetchScalarGridSpec(
            num_scalar_prefetch=1,
            grid=(2,),
            in_specs=[whole_block(v.shape) for v in (*shards, route_ids, router)]
            + [any_block()] * 8,
            out_specs=[
                whole_block(sums.shape),
                expert_block(pre.shape),
                expert_block(gated.shape),
                whole_block(gates.shape),
                whole_block(rows.shape),
            ],
            scratch_shapes=weight_scratch(width, hidden),
        ),
        out_shape=[sums, pre, gated, gates, rows],
        name="experts_forward_a",
    )(half_index, *shards, route_ids, router, *own, *near)
    far_pack, far_across, sums_a = lax.optimization_barrier((*far, sums_a))
    far = [far_pack, swap_core(far_pack), far_across, swap_core(far_across)]

    def second(part, pre_a, gated_a):
        specs, shapes = spread_specs(part, row_count, width)
        return pl.pallas_call(
            forward_second,
            grid_spec=pltpu.PrefetchScalarGridSpec(
                num_scalar_prefetch=1,
                grid=(2,),
                in_specs=[half_rows(v.shape, part) for v in (rows, gates, sums)]
                + [any_block()] * 10,
                out_specs=specs
                + [half_expert(pre.shape, part, 2), half_expert(gated.shape, part, 2)],
                scratch_shapes=[pltpu.VMEM((row_count // 2, width), F32)]
                + weight_scratch(width, hidden),
            ),
            out_shape=shapes + [pre, gated],
            input_output_aliases={12: len(shapes), 13: len(shapes) + 1},
            name="experts_forward_b",
        )(half_index, rows, gates, sums_a, *own, *far, pre_a, gated_a)

    send_near, send_far, pre_a, gated_a = second(1, pre_a, gated_a)
    keep, pre_a, gated_a = second(0, pre_a, gated_a)
    return (keep, send_near, send_far, pre_a, gated_a, gates, rows, far)


def backward_body(half_ref, *refs):
    shards = refs[:4]
    gate_ref, router_ref, pre_ref = refs[4:7]
    packs = refs[7:19]
    pre_grad_ref, logit_ref, grad_ref = refs[-7:-4]
    acc, in_buf, out_buf, sems = refs[-4:]
    step, slot, wait = stream_weights(0, packs, half_ref[0], in_buf, out_buf, sems)
    row_count, width = grad_ref.shape
    size = row_count // 4
    targets = [ref for ref in refs[19:-7] if ref.shape[0] * 2 == row_count]
    targets = targets or [refs[-8]]

    @pl.when(step == 0)
    def _():
        for i in range(4):
            grad_ref[i * size : (i + 1) * size, :] = shards[i][...]
        acc[...] = jnp.zeros_like(acc)
        logit_ref[...] = jnp.zeros_like(logit_ref)

    wait()

    def mlp(rows):
        plain = lax.dot_general(
            grad_ref[rows, : width // 2], out_buf[slot, 0], NT, preferred_element_type=F32
        ) + lax.dot_general(
            grad_ref[rows, width // 2 :], out_buf[slot, 1], NT, preferred_element_type=F32
        )
        gate_pre, up_pre = split_pairs(pre_ref[0, rows, :].astype(F32))
        weight = gate_column(gate_ref[rows, :], step)
        sigmoid = jax.nn.sigmoid(gate_pre)
        act = gate_pre * sigmoid
        grad_weight = jnp.sum(act * up_pre * plain, -1, keepdims=True)
        scaled = weight * plain
        pre_grad = join_pairs(
            scaled * up_pre * (sigmoid + act * (1.0 - sigmoid)), scaled * act
        ).astype(BF16)
        pre_grad_ref[0, rows, :] = pre_grad
        old = logit_ref[rows, :]
        lane = lax.broadcasted_iota(jnp.int32, old.shape, 1)
        value = weight * grad_weight
        high = value.astype(BF16).astype(F32)
        logit_ref[rows, :] = jnp.where(
            lane == step, high, jnp.where(lane == step + 32, value - high, old)
        )
        acc[rows, :] += lax.dot_general(pre_grad, in_buf[slot], NT, preferred_element_type=F32)

    chunk_loop(row_count, mlp)

    @pl.when(step == pl.num_programs(0) - 1)
    def _():
        def router(rows):
            acc[rows, :] += lax.dot_general(
                logit_ref[rows, :].astype(BF16), router_ref[...], NT, preferred_element_type=F32
            )

        chunk_loop(row_count, router)
        spread(acc, targets)


def experts_backward(part, half_index, shards, gates, router, pre, own, near, far, *before):
    row_count, width = (8 * shards[0].shape[0], shards[0].shape[1])
    local = pre.shape[0]
    specs, shapes = spread_specs(part, row_count, width)
    saved = [
        jax.ShapeDtypeStruct(pre.shape, BF16),
        jax.ShapeDtypeStruct((row_count, 128), F32),
        jax.ShapeDtypeStruct((row_count, width), BF16),
    ]
    return pl.pallas_call(
        backward_body,
        grid_spec=pltpu.PrefetchScalarGridSpec(
            num_scalar_prefetch=1,
            grid=(local,),
            in_specs=[whole_block(v.shape) for v in shards]
            + [half_rows(gates.shape, part), whole_block(router.shape)]
            + [half_expert(pre.shape, part)]
            + [any_block()] * (12 + len(before)),
            out_specs=specs
            + [half_expert(pre.shape, part)]
            + [half_rows(v.shape, part) for v in saved[1:]],
            scratch_shapes=[pltpu.VMEM((row_count // 2, width), F32)]
            + weight_scratch(width, 4 * SHARE),
        ),
        out_shape=shapes + saved,
        input_output_aliases={20 + i: len(shapes) + i for i in range(len(before))},
        name="experts_backward",
    )(half_index, *shards, gates, router, pre, *own, *near, *far, *before)


def grad_out_body(half_ref, gated_ref, other_ref, mine_ref, *refs):
    *outs, turned = refs[-5:]
    turned[...] = gated_ref[0].T

    def pair(q, carry):
        for n, source in ((0, other_ref), (2, mine_ref)):
            for odd in range(2):
                rows = pl.ds(pl.multiple_of((2 * q + odd) * SHARE, SHARE), SHARE)
                product = jnp.dot(turned[rows, :], source[...], preferred_element_type=F32)
                outs[n + odd][q, 0] = product.astype(BF16)
        return carry

    lax.fori_loop(0, 2, pair, 0)


def grad_expert_outs(half_index, gated, grads, *after):
    local, row_count, hidden = gated.shape
    width = grads.shape[1]
    half_spec = (row_count, width // 2)
    shape = (2, local, SHARE, width // 2)
    return pl.pallas_call(
        grad_out_body,
        grid_spec=pltpu.PrefetchScalarGridSpec(
            num_scalar_prefetch=1,
            grid=(local,),
            in_specs=[
                expert_block(gated.shape),
                pl.BlockSpec(half_spec, lambda e, half: (0, 1 - half[0])),
                pl.BlockSpec(half_spec, lambda e, half: (0, half[0])),
            ]
            + [any_block()] * len(after),
            out_specs=[pl.BlockSpec((2, 1) + shape[2:], lambda e, *_: (0, e, 0, 0))] * 4,
            scratch_shapes=[pltpu.VMEM((hidden, row_count), BF16)],
        ),
        out_shape=[jax.ShapeDtypeStruct(shape, BF16)] * 4,
        name="grad_expert_out",
    )(half_index, gated, grads, grads, *after)


def grad_in_body(half_ref, rows_ref, pre_ref, *refs):
    keep_ref, send_ref, turned = refs[-3:]

    @pl.when(pl.program_id(0) == 0)
    def _():
        turned[...] = rows_ref[...].T

    def part(i, carry):
        rows = pl.ds(pl.multiple_of(i * CHUNK, CHUNK), CHUNK)
        product = jnp.dot(turned[rows, :], pre_ref[0], preferred_element_type=F32).astype(BF16)
        for q in range(4):
            for c in range(2):
                start = (2 * q + c) * SHARE
                (keep_ref, send_ref)[q % 2][q // 2, 0, c, rows] = product[:, start : start + SHARE]
        return carry

    lax.fori_loop(0, turned.shape[0] // CHUNK, part, 0)


def grad_expert_ins(half_index, rows, pre_grad, first, count, *after):
    local, row_count, wide = pre_grad.shape
    width = rows.shape[1]
    shape = (2, count, 2, width // 2, SHARE)
    return pl.pallas_call(
        grad_in_body,
        grid_spec=pltpu.PrefetchScalarGridSpec(
            num_scalar_prefetch=1,
            grid=(count,),
            in_specs=[
                pl.BlockSpec((row_count, width // 2), lambda e, half: (0, half[0])),
                expert_block(pre_grad.shape, first),
            ]
            + [any_block()] * len(after),
            out_specs=[pl.BlockSpec((2, 1) + shape[2:], lambda e, *_: (0, e, 0, 0, 0))] * 2,
            scratch_shapes=[pltpu.VMEM((width // 2, row_count), BF16)],
        ),
        out_shape=[jax.ShapeDtypeStruct(shape, BF16)] * 2,
        name="grad_expert_in",
    )(half_index, rows, pre_grad, *after)


def fold_body(keep_ref, got_ref, *refs):
    near_ref, far_ref = refs[-2:]
    near_ref[...] = keep_ref[0].astype(F32) + got_ref[0].astype(F32)
    far_ref[...] = (keep_ref[1].astype(F32) + got_ref[1].astype(F32)).astype(BF16)


def fold_pairs(keep, got, *after):
    shape = keep.shape
    rest = (0,) * (len(shape) - 2)
    pair = pl.BlockSpec((2, 1) + shape[2:], lambda e: (0, e) + rest)
    single = pl.BlockSpec((1,) + shape[2:], lambda e: (e,) + rest)
    return pl.pallas_call(
        fold_body,
        grid=(shape[1],),
        in_specs=[pair, pair] + [any_block()] * len(after),
        out_specs=[single, single],
        out_shape=[
            jax.ShapeDtypeStruct(shape[1:], F32),
            jax.ShapeDtypeStruct(shape[1:], BF16),
        ],
        name="fold_pairs",
    )(keep, got, *after)


def finish_body(keep, near, four, two, extra, unit, scale, gain, grad_out, *refs):
    hidden_ref, attn_ref, gain_ref = refs[-3:]
    total = keep[...] + near[...].astype(F32) + extra[...]
    for part in (four, two):
        total = total + part[...].astype(F32)
    gain_ref[...] = jnp.sum((total * unit[...]).reshape(-1, 8, total.shape[1]), 0)
    weighted = total * gain[...]
    mean = jnp.mean(weighted * unit[...], -1, keepdims=True)
    hidden = grad_out[...] + scale[...] * (weighted - unit[...] * mean)
    hidden_ref[...] = hidden
    attn_ref[...] = (RESIDUAL * hidden).astype(BF16)


def finish_rows(keep, near, four, two, extra, unit, scale, gain, grad_out, *after):
    size, width = unit.shape
    block = pl.BlockSpec((size, width), lambda e: (0, 0))
    return pl.pallas_call(
        finish_body,
        grid=(1,),
        in_specs=[block] * 6
        + [whole_block((size, 1)), whole_block((1, width)), block]
        + [any_block()] * len(after),
        out_specs=[block, block, whole_block((8, width))],
        out_shape=[
            jax.ShapeDtypeStruct((size, width), F32),
            jax.ShapeDtypeStruct((size, width), BF16),
            jax.ShapeDtypeStruct((8, width), F32),
        ],
        name="finish_rows",
    )(keep, near, four, two, extra, unit, scale, gain, grad_out, *after)


def rotated(values, cosine, sine, sign):
    width = values.shape[1]
    lane = lax.broadcasted_iota(jnp.int32, values.shape, 1)
    lower = lax.rem(lane, HEAD_DIM) < HEAD_DIM // 2
    ahead = pltpu.roll(values, width - HEAD_DIM // 2, 1)
    behind = pltpu.roll(values, HEAD_DIM // 2, 1)
    turned = jnp.where(lower, -ahead, behind)
    repeat = width // cosine.shape[1]
    cosine = jnp.concatenate([cosine] * repeat, 1)
    sine = jnp.concatenate([sine] * repeat, 1)
    return values * cosine + sign * (turned * sine)


def head(values, index, start=0, stop=None):
    return values[start:stop, index * HEAD_DIM : (index + 1) * HEAD_DIM]


def probabilities(query, keys):
    scores = lax.dot_general(query, keys, NT, preferred_element_type=F32) * ATTN_SCALE
    powers = jnp.exp(scores - jnp.max(scores, -1, keepdims=True))
    return powers / jnp.sum(powers, -1, keepdims=True)


def attention_forward_body(
    core_ref, tokens, gain, query_w, key_w, value_w, output_w, cosine, sine, *refs
):
    normed, query, keys, values, attended, keep, send = refs[-7:]
    x = tokens[...].astype(F32)
    scale = lax.rsqrt(jnp.mean(x * x, -1, keepdims=True) + EPS)
    normed[...] = (x * scale * gain[...]).astype(BF16)
    low = normed[...]
    linear = jnp.dot(low, query_w[...], preferred_element_type=F32)
    query[...] = rotated(linear, cosine[...], sine[...], 1.0).astype(BF16)
    linear = jnp.dot(low, key_w[...], preferred_element_type=F32)
    keys[...] = rotated(linear, cosine[...], sine[...], 1.0).astype(BF16)
    values[...] = jnp.dot(low, value_w[...], preferred_element_type=F32).astype(BF16)
    group = query.shape[1] // keys.shape[1]
    for start in range(0, tokens.shape[0], BLOCK):
        stop = start + BLOCK
        parts = []
        for h in range(query.shape[1] // HEAD_DIM):
            probs = probabilities(head(query, h, start, stop), head(keys, h // group, 0, stop))
            parts.append(
                jnp.dot(
                    probs.astype(BF16),
                    head(values, h // group, 0, stop),
                    preferred_element_type=F32,
                )
            )
        attended[start:stop, :] = jnp.concatenate(parts, 1).astype(BF16)
    size = tokens.shape[0] // 4
    for r in range(2):
        for target, core in ((keep, core_ref[0]), (send, 1 - core_ref[0])):
            rows = pl.ds(pl.multiple_of((2 * r + core) * size, size), size)
            part = jnp.dot(attended[rows, :], output_w[...], preferred_element_type=F32)
            target[r] = part.astype(target.dtype)


def scalar_call(body, name, scalar, inputs, shapes, after=(), scratch=()):
    return pl.pallas_call(
        body,
        grid_spec=pltpu.PrefetchScalarGridSpec(
            num_scalar_prefetch=1,
            grid=(1,),
            in_specs=[whole_block(v.shape) for v in inputs] + [any_block()] * len(after),
            out_specs=[whole_block(s.shape) for s in shapes],
            scratch_shapes=list(scratch),
        ),
        out_shape=shapes,
        name=name,
    )(scalar, *inputs, *after)


def attention_forward(core, tokens, gain, query_w, key_w, value_w, output_w, tables, *after):
    rows, width = tokens.shape
    shapes = [
        jax.ShapeDtypeStruct((rows, width), BF16),
        jax.ShapeDtypeStruct((rows, query_w.shape[1]), BF16),
        jax.ShapeDtypeStruct((rows, key_w.shape[1]), BF16),
        jax.ShapeDtypeStruct((rows, value_w.shape[1]), BF16),
        jax.ShapeDtypeStruct((rows, query_w.shape[1]), BF16),
        jax.ShapeDtypeStruct((2, rows // 4, width), F32),
        jax.ShapeDtypeStruct((2, rows // 4, width), BF16),
    ]
    inputs = (tokens, gain, query_w, key_w, value_w, output_w, *tables)
    return scalar_call(
        attention_forward_body, "attention_forward", core, inputs, shapes, after
    )


TN = (((0,), (0,)), ((), ()))


def attention_backward_body(
    share_ref,
    tokens,
    query_w,
    key_w,
    value_w,
    output_w,
    cosine,
    sine,
    query,
    keys,
    values,
    first,
    second,
    third,
    fourth,
    *refs,
):
    grad, grad_qkv, gain, keep, send, grad_keys, grad_values = refs[-7:]
    share = share_ref[0]
    size = first.shape[0]
    for r, piece in enumerate((first, second, third, fourth)):
        place = jnp.bitwise_xor(share, r) * size
        grad[pl.ds(pl.multiple_of(place, size), size), :] = piece[...]
    back = lax.dot_general(grad[...], output_w[...], NT, preferred_element_type=F32).astype(BF16)
    wide, narrow = (query.shape[1], keys.shape[1])
    group = wide // narrow
    grad_keys[...] = jnp.zeros_like(grad_keys)
    grad_values[...] = jnp.zeros_like(grad_values)
    for start in range(0, tokens.shape[0], BLOCK):
        stop = start + BLOCK
        parts, key_parts, value_parts = ([], [], [])
        for kv in range(narrow // HEAD_DIM):
            key, value = (head(keys, kv, 0, stop), head(values, kv, 0, stop))
            key_sum, value_sum = (0.0, 0.0)
            for h in range(kv * group, (kv + 1) * group):
                query_h = head(query, h, start, stop)
                back_h = head(back, h, start, stop)
                probs = probabilities(query_h, key)
                inner = lax.dot_general(back_h, value, NT, preferred_element_type=F32)
                scores = probs * (inner - jnp.sum(probs * inner, -1, keepdims=True))
                scores = scores.astype(BF16)
                parts.append(ATTN_SCALE * jnp.dot(scores, key, preferred_element_type=F32))
                key_sum += lax.dot_general(scores, query_h, TN, preferred_element_type=F32)
                value_sum += lax.dot_general(
                    probs.astype(BF16), back_h, TN, preferred_element_type=F32
                )
            key_parts.append(ATTN_SCALE * key_sum)
            value_parts.append(value_sum)
        turned = rotated(
            jnp.concatenate(parts, 1), cosine[start:stop, :], sine[start:stop, :], -1.0
        )
        grad_qkv[start:stop, :wide] = turned.astype(BF16)
        grad_keys[:stop, :] += jnp.concatenate(key_parts, 1)
        grad_values[:stop, :] += jnp.concatenate(value_parts, 1)
    turned = rotated(grad_keys[...], cosine[...], sine[...], -1.0)
    grad_qkv[:, wide : wide + narrow] = turned.astype(BF16)
    grad_qkv[:, wide + narrow :] = grad_values[...].astype(BF16)
    total = jnp.zeros(gain.shape, F32)
    for r in range(2):
        for target, core in ((keep, share % 2), (send, 1 - share % 2)):
            rows = pl.ds(pl.multiple_of((2 * r + core) * size, size), size)
            part = lax.dot_general(
                grad_qkv[rows, :wide], query_w[...], NT, preferred_element_type=F32
            )
            part += lax.dot_general(
                grad_qkv[rows, wide : wide + narrow], key_w[...], NT, preferred_element_type=F32
            )
            part += lax.dot_general(
                grad_qkv[rows, wide + narrow :], value_w[...], NT, preferred_element_type=F32
            )
            target[r] = part.astype(target.dtype)
            x = tokens[rows, :].astype(F32)
            x = x * lax.rsqrt(jnp.mean(x * x, -1, keepdims=True) + EPS)
            total += jnp.sum((part * x).reshape(-1, 8, x.shape[1]), 0)
    gain[...] = total


def attention_backward(share, tokens, weights, tables, saved, pieces, *after):
    rows, width = tokens.shape
    narrow = saved[1].shape[1]
    shapes = [
        jax.ShapeDtypeStruct((rows, width), BF16),
        jax.ShapeDtypeStruct((rows, saved[0].shape[1] + 2 * narrow), BF16),
        jax.ShapeDtypeStruct((8, width), F32),
        jax.ShapeDtypeStruct((2, rows // 4, width), F32),
        jax.ShapeDtypeStruct((2, rows // 4, width), BF16),
    ]
    return scalar_call(
        attention_backward_body,
        "attention_backward",
        share,
        (tokens, *weights, *tables, *saved, *pieces),
        shapes,
        after,
        [pltpu.VMEM((rows, narrow), F32), pltpu.VMEM((rows, narrow), F32)],
    )


def reduce_body(place_ref, normed, grad_qkv, grad, attended, small, gain, *refs):
    keep, near, far = refs[-3:]
    step = pl.program_id(0)
    first = lax.dot_general(normed[...], grad_qkv[...], TN, preferred_element_type=F32)
    second = lax.dot_general(grad[...], attended[...], TN, preferred_element_type=F32)
    rest = jnp.zeros((SHARE - small.shape[0] - gain.shape[0], SHARE), F32)
    third = jnp.concatenate([small[...], gain[...], rest], 0).T
    part = jnp.concatenate([first, second, third], 1)

    @pl.when(step < 4)
    def _():
        keep[...] = part

    @pl.when((step == 4) | (step == 5))
    def _():
        near[...] = part.astype(BF16)

    @pl.when(step >= 6)
    def _():
        far[...] = part.astype(BF16)


def reduce_parts(place, normed, grad_qkv, grad, attended, small, gain, *after):
    rows, width = normed.shape
    size = width // 8
    total = grad_qkv.shape[1] + attended.shape[1] + SHARE

    def shard(e, place):
        order = jnp.where(e < 4, 2 * e, 2 * e - 7)
        return jnp.bitwise_xor(place[0], order)

    columns = pl.BlockSpec((rows, size), lambda e, place: (0, shard(e, place)))
    return pl.pallas_call(
        reduce_body,
        grid_spec=pltpu.PrefetchScalarGridSpec(
            num_scalar_prefetch=1,
            grid=(8,),
            in_specs=[
                columns,
                whole_block(grad_qkv.shape),
                columns,
                whole_block(attended.shape),
                pl.BlockSpec((small.shape[0], size), lambda e, place: (0, shard(e, place))),
                pl.BlockSpec((gain.shape[0], size), lambda e, place: (0, shard(e, place))),
            ]
            + [any_block()] * len(after),
            out_specs=[
                pl.BlockSpec((size, total), lambda e, _: (jnp.minimum(e, 3), 0)),
                pl.BlockSpec((size, total), lambda e, _: (jnp.clip(e - 4, 0, 1), 0)),
                pl.BlockSpec((size, total), lambda e, _: (jnp.clip(e - 6, 0, 1), 0)),
            ],
        ),
        out_shape=[
            jax.ShapeDtypeStruct((4 * size, total), F32),
            jax.ShapeDtypeStruct((2 * size, total), BF16),
            jax.ShapeDtypeStruct((2 * size, total), BF16),
        ],
        name="reduce_parts",
    )(place, normed, grad_qkv, grad, attended, small, gain, *after)


def unpack_body(place_ref, *refs):
    pieces = refs[:8]
    query, key, value, output, small = refs[-5:]
    size = pieces[0].shape[0]
    wide, narrow = (query.shape[1], key.shape[1])
    for r, piece in zip(ORDER, pieces):
        start = pl.multiple_of(jnp.bitwise_xor(place_ref[0], r) * size, size)
        rows = pl.ds(start, size)
        part = piece[...].astype(F32)
        query[rows, :] = part[:, :wide]
        key[rows, :] = part[:, wide : wide + narrow]
        value[rows, :] = part[:, wide + narrow : wide + 2 * narrow]
        begin = wide + 2 * narrow
        output[:, rows] = part[:, begin : begin + output.shape[0]].T
        small[rows, :] = part[:, begin + output.shape[0] :]


def assemble_body(share_ref, *refs):
    target = refs[-1]
    size = refs[0].shape[0]
    for r in range(4):
        start = pl.multiple_of(jnp.bitwise_xor(share_ref[0], r) * size, size)
        target[pl.ds(start, size), :] = refs[r][...].astype(target.dtype)


def spread_tensor(value):
    across = swap_y(value)
    return [value, swap_core(value), across, swap_core(across)]


def assemble(share, pieces, dtype, *after):
    size, width = pieces[0].shape
    shapes = [jax.ShapeDtypeStruct((4 * size, width), dtype)]
    return scalar_call(assemble_body, "assemble", share, pieces, shapes, after)[0]


def trade(value, bits):
    return lax.ppermute(value, "expert", [(i, i ^ bits) for i in range(8)])


def swap_y(value):
    return lax.ppermute(value, "tensor", [(i, i ^ 2) for i in range(4)])


def swap_core(value):
    return lax.ppermute(value, "tensor", [(i, i ^ 1) for i in range(4)])


def gather_experts(value):
    column = [value] + [trade(value, bits) for bits in (2, 4, 6)]
    return column + [trade(shard, 1) for shard in column]


def scatter_steps(keep, send_near, send_far, *beside):
    size = keep.shape[0] // 4
    got_far = trade(send_far, 1)
    send_near, got_far, keep = lax.optimization_barrier((send_near, got_far, keep))
    if beside:
        got_far, *beside = lax.optimization_barrier((got_far, *beside))
    far = (keep[2 * size :] + got_far.astype(F32)).astype(BF16)
    got_near = trade(send_near, 1)
    four, six = (trade(far[:size], 4), trade(far[size:], 6))
    near = (keep[size : 2 * size] + got_near[size:].astype(F32)).astype(BF16)
    return (keep, got_near, (trade(near, 2), four, six), *beside)


def scatter_experts(keep, send_near, send_far, *beside):
    size = keep.shape[0] // 4
    keep, got_near, back, *beside = scatter_steps(keep, send_near, send_far, *beside)
    total = keep[:size] + got_near[:size].astype(F32)
    for part in back:
        total = total + part.astype(F32)
    return (total, *beside) if beside else total


def scatter_tensor(keep, send, row):
    half = keep + swap_core(send).astype(F32)
    keep = lax.dynamic_index_in_dim(half, row, 0, False)
    send = lax.dynamic_index_in_dim(half, 1 - row, 0, False)
    return keep + swap_y(send.astype(BF16)).astype(F32)


def ordered(index, first, second):
    return jnp.where(
        index == 0, jnp.concatenate([first, second], 0), jnp.concatenate([second, first], 0)
    )


def per_device(
    tokens,
    teacher,
    valid_mask,
    routes,
    first_gain,
    query_weight,
    key_matrix,
    value_matrix,
    output_weight,
    second_gain,
    router_weight,
    expert_in,
    expert_out,
):
    row_count, model_width = tokens.shape
    expert_count = router_weight.shape[1]
    senders = lax.axis_size("expert")
    shares = lax.axis_size("tensor")
    fits = (
        (senders, shares) == (8, 4)
        and expert_count == senders * shares
        and expert_in.shape == (8, 2, model_width // 2, SHARE)
        and row_count == 4 * 128
    )
    if not fits:
        return general_device(
            tokens,
            teacher,
            valid_mask,
            routes,
            first_gain,
            query_weight,
            key_matrix,
            value_matrix,
            output_weight,
            second_gain,
            router_weight,
            expert_in,
            expert_out,
        )
    quarter = row_count // shares
    place = lax.axis_index("expert")
    share = lax.axis_index("tensor")
    row, core = (share // 2, share % 2)
    half_index = place // 4
    half_arg = half_index.reshape(1)
    held = expert_in.shape[0] // 2
    base = 8 * (place % 4) + held * half_index

    share_arg, core_arg, place_arg = (share.reshape(1), core.reshape(1), place.reshape(1))

    def quarter_of(values):
        return lax.dynamic_slice_in_dim(values, share * quarter, quarter, 0)

    local_valid = jnp.sum(valid_mask)
    routes_mine = quarter_of(routes)
    note = jnp.concatenate([routes_mine.T, jnp.full((TOP, quarter), local_valid, jnp.int32)], 0)

    own_pack, near_pack, far_pack = pack_weights(half_arg, expert_in, expert_out)
    near_pack = trade(near_pack, 4)
    far_pack = trade(far_pack, 4)
    own_across = swap_y(own_pack)

    router_rel = lax.dynamic_slice_in_dim(
        jnp.concatenate([router_weight, router_weight], 1), base, expert_count, 1
    )
    router_rel = jnp.pad(
        jnp.concatenate([router_rel, router_rel], 1), ((0, 0), (0, 128 - 2 * expert_count))
    )

    tables = [
        jnp.concatenate([table[:, 0]] * (2 * SHARE // HEAD_DIM), 1)
        for table in rope_tables(row_count, HEAD_DIM)
    ]
    weights = (query_weight, key_matrix, value_matrix, output_weight)
    first_normed, query, keys, values, attended, attn_keep, attn_send = attention_forward(
        core_arg, tokens, first_gain[None], *weights, tables, own_pack
    )
    notes = [note] + [trade(note, bits) for bits in (2, 4, 6)]
    near_pack, own_across, attn_send, *notes = lax.optimization_barrier(
        (near_pack, own_across, attn_send, *notes)
    )
    notes = jnp.stack(notes)
    others = trade(notes, 1)
    own = [own_pack, swap_core(own_pack), own_across, swap_core(own_across)]
    tokens_mine = quarter_of(tokens).astype(F32)
    attn_sum = scatter_tensor(attn_keep, attn_send, row)
    near_pack, attn_sum, others = lax.optimization_barrier((near_pack, attn_sum, others))
    hidden = tokens_mine + RESIDUAL * attn_sum
    scale_two = lax.rsqrt(jnp.mean(hidden * hidden, -1, keepdims=True) + EPS)
    unit_two = hidden * scale_two
    normed_two = (unit_two * second_gain).astype(BF16)
    beside = trade(normed_two, 1)
    near_pack, beside = lax.optimization_barrier((near_pack, beside))
    near_across = swap_y(near_pack)
    column = [normed_two] + [trade(normed_two, bits) for bits in (2, 4, 6)]
    across = [trade(shard, 1) for shard in column[1:]]
    far_pack, near_across, *gathered = lax.optimization_barrier(
        (far_pack, near_across, beside, *across, *column[1:])
    )
    row_shards = [normed_two, *gathered[4:], *gathered[:4]]
    near = [near_pack, swap_core(near_pack), near_across, swap_core(near_across)]
    far = (far_pack, swap_y(far_pack))
    notes = jnp.concatenate([notes, others], 0)
    valid_total = jnp.sum(notes[:, TOP, 0]).astype(F32)
    route_rel = jnp.bitwise_and(notes[:, :TOP] - base, expert_count - 1)
    route_rel = route_rel.transpose(0, 2, 1).reshape(senders * quarter, TOP)
    keep, send_near, send_far, pre, gated, gates, expert_rows, far = experts_forward(
        half_arg,
        row_shards,
        route_rel,
        router_rel,
        own,
        near,
        far,
    )
    moe_sum = scatter_experts(keep, send_near, send_far)

    output = hidden + RESIDUAL * moe_sum
    residual_err = output - quarter_of(teacher).astype(F32)
    valid_rows = quarter_of(valid_mask).astype(F32)[:, None]
    squared_local = jnp.sum(valid_rows * residual_err * residual_err)
    token_total = senders * row_count
    grad_out = token_total / valid_total * valid_rows * residual_err
    grad_moe = (RESIDUAL * grad_out).astype(BF16)
    gate_mean = jnp.sum(grad_moe.astype(F32) * moe_sum, -1, keepdims=True)
    mean_part = -gate_mean * dense_gates(normed_two, routes_mine, router_weight)
    mean_high = mean_part.astype(BF16)
    mean_part = jnp.concatenate([mean_high, (mean_part - mean_high.astype(F32)).astype(BF16)], 1)
    router_pair = jnp.concatenate([router_weight, router_weight], 1)
    mean_rows = jnp.einsum("te,de->td", mean_part, router_pair, preferred_element_type=F32)
    out_pieces = spread_tensor(output.astype(BF16))
    shards = gather_experts(grad_moe)
    packs = (gates, router_rel, pre, own, near, far)
    send_near, send_far, *saved = experts_backward(1, half_arg, shards[4:], *packs)
    keep, pre_grad, logit_grad, grad_rows = experts_backward(
        0, half_arg, shards[:4], *packs, *saved
    )
    got_far = trade(send_far, 1)
    send_near, got_far, keep = lax.optimization_barrier((send_near, got_far, keep))
    far_rows = (keep[2 * quarter :] + got_far.astype(F32)).astype(BF16)
    back = trade(far_rows, 4)
    got_near = trade(send_near, 1)
    other = 1 - half_arg
    in_keep, in_send = grad_expert_ins(
        other, expert_rows, pre_grad, 0, 2, far_rows, *out_pieces[1:]
    )
    in_near, in_far = fold_pairs(in_keep, swap_core(in_send))
    in_ready = (in_near + swap_y(in_far).astype(F32)).astype(BF16)
    out_keep, out_send, own_out_keep, own_out_send = grad_expert_outs(
        half_arg, gated, grad_rows, in_far
    )
    late_keep, late_send = grad_expert_ins(other, expert_rows, pre_grad, 2, 2, in_far)
    router_part = jnp.einsum(
        "te,td->ed", logit_grad.astype(BF16), expert_rows, preferred_element_type=F32
    )
    router_part = router_part[:expert_count] + router_part[expert_count : 2 * expert_count]
    router_part = lax.dynamic_slice_in_dim(
        jnp.concatenate([router_part, router_part], 0),
        jnp.bitwise_and(expert_count - base, expert_count - 1),
        expert_count,
        0,
    )
    mean_router = jnp.einsum("te,td->ed", mean_part, normed_two, preferred_element_type=F32)
    router_part = router_part + mean_router[:expert_count] + mean_router[expert_count:]

    small = jnp.concatenate(
        [
            router_part,
            jnp.full((1, model_width), squared_local),
            jnp.zeros((7, model_width), F32),
        ],
        0,
    )
    small = small + swap_core(small)
    small = small + swap_y(small)
    back, out_send, late_send, small = lax.optimization_barrier(
        (back, out_send, late_send, small)
    )
    near_rows = keep[quarter : 2 * quarter] + got_near[quarter:].astype(F32)
    near_rows = (near_rows + back[quarter:].astype(F32)).astype(BF16)
    near_rows = trade(near_rows, 2)
    grad_hidden, grad_attn, grad_second_part = finish_rows(
        keep,
        got_near,
        back,
        near_rows,
        mean_rows,
        unit_two,
        scale_two,
        second_gain[None],
        grad_out,
        in_ready,
    )
    own_in_keep, own_in_send = grad_expert_ins(
        half_arg, expert_rows, pre_grad, 0, held, grad_attn
    )
    pieces = spread_tensor(grad_attn)
    late_near, late_far = fold_pairs(late_keep, swap_core(late_send), pieces[2])
    out_near, out_far = fold_pairs(out_keep, swap_core(out_send), pieces[2])
    out_ready = (out_near + swap_y(out_far).astype(F32)).astype(BF16)
    late_ready = (late_near + swap_y(late_far).astype(F32)).astype(BF16)
    in_back = trade(in_ready, 4)
    before = (late_far, out_far, own_in_send, in_back)
    grad_attn, grad_qkv, gain_part, one_keep, one_send = attention_backward(
        share_arg, tokens, weights, tables, (query, keys, values), pieces, *before
    )
    late_back = trade(late_ready, 4)
    grad_one = scatter_tensor(one_keep, one_send, row)
    own_out_near, own_out_far = fold_pairs(own_out_keep, swap_core(own_out_send), grad_one)
    own_out_across = swap_y(own_out_far)
    own_in_near, own_in_far = fold_pairs(own_in_keep, swap_core(own_in_send), grad_one)
    own_in_across = swap_y(own_in_far)
    before = (late_ready,)
    gains = jnp.concatenate([grad_second_part, gain_part], 0)
    keep, send_near, send_far = reduce_parts(
        place_arg, first_normed, grad_qkv, grad_attn, attended, small, gains, *before
    )
    out_back = trade(out_ready, 4)
    total, late_back, out_back = scatter_experts(keep, send_near, send_far, late_back, out_back)
    total = total.astype(BF16)
    shapes = [
        jax.ShapeDtypeStruct(shape, F32)
        for shape in (
            query_weight.shape,
            key_matrix.shape,
            value_matrix.shape,
            output_weight.shape,
            (model_width, 128),
        )
    ]
    shards = gather_experts(total)
    grad_query, grad_key, grad_value, grad_output, small = scalar_call(
        unpack_body, "unpack", place_arg, shards, shapes, (own_out_across, own_in_across)
    )

    gains = small[:, expert_count + 8 : expert_count + 24].reshape(model_width, 2, 8)
    gains = jnp.sum(gains, 2).T.reshape(16, -1)
    gains = gains + swap_core(gains)
    gains = (gains + swap_y(gains)).reshape(2, -1)

    scale_mine = lax.rsqrt(jnp.mean(tokens_mine * tokens_mine, -1, keepdims=True) + EPS)
    unit_mine = tokens_mine * scale_mine
    grad_unit_one = grad_one * first_gain
    grad_tokens = grad_hidden + scale_mine * (
        grad_unit_one - unit_mine * jnp.mean(grad_unit_one * unit_mine, -1, keepdims=True)
    )
    grad_tokens = assemble(share_arg, spread_tensor(grad_tokens.astype(BF16)), F32)
    layer_output = assemble(share_arg, out_pieces, BF16)
    grad_expert_out = ordered(
        half_index, own_out_near + own_out_across.astype(F32), out_back.astype(F32)
    )
    grad_expert_in = ordered(
        half_index,
        own_in_near + own_in_across.astype(F32),
        jnp.concatenate([in_back, late_back], 0).astype(F32),
    )
    return (
        layer_output,
        small[0, expert_count] / (2.0 * model_width * valid_total),
        grad_tokens,
        gains[1],
        grad_query,
        grad_key,
        grad_value,
        grad_output,
        gains[0],
        small[:, :expert_count],
        grad_expert_in,
        grad_expert_out,
    )


def solution(mesh):
    return jax.shard_map(
        per_device,
        mesh=mesh,
        in_specs=(
            P("expert", None),
            P("expert", None),
            P("expert"),
            P("expert", None),
            P(),
            P(None, "tensor"),
            P(None, "tensor"),
            P(None, "tensor"),
            P("tensor", None),
            P(),
            P(),
            P("expert", None, None, "tensor"),
            P("expert", "tensor", None),
        ),
        out_specs=(
            P("expert", None),
            P(),
            P("expert", None),
            P(),
            P(None, "tensor"),
            P(None, "tensor"),
            P(None, "tensor"),
            P("tensor", None),
            P(),
            P(),
            P("expert", None, None, "tensor"),
            P("expert", "tensor", None),
        ),
        check_vma=False,
    )
```

```python
import jax
import jax.numpy as jnp
from jax import lax
from jax.experimental import pallas as pl
from jax.experimental.pallas import tpu as pltpu
from jax.sharding import PartitionSpec as P

HEAD_DIM = 64
TOP = 8
BLOCK = 256


EPS = 1e-06
ATTN_SCALE = 0.015625
RESIDUAL = 0.22
THETA = 10000.0


def shifted(value, axis, steps):
    count = lax.axis_size(axis)
    pairs = [(source, (source + steps) % count) for source in range(count)]
    return lax.ppermute(value, axis, pairs)


def rope_tables(length, head_size):
    half_size = head_size // 2
    frequency = THETA ** (-(jnp.arange(half_size, dtype=jnp.float32) * 2.0) / head_size)
    angle_table = jnp.arange(length, dtype=jnp.float32)[:, None] * frequency[None, :]
    return (jnp.cos(angle_table)[:, None, :], jnp.sin(angle_table)[:, None, :])


def apply_rotary(values, cosine_lookup, sine_lookup):
    half_size = values.shape[-1] // 2
    lower_half, upper_half = (values[..., :half_size], values[..., half_size:])
    return jnp.concatenate(
        [
            lower_half * cosine_lookup - upper_half * sine_lookup,
            upper_half * cosine_lookup + lower_half * sine_lookup,
        ],
        -1,
    )


def unrotate(grads, cosine_lookup, sine_lookup):
    half_size = grads.shape[-1] // 2
    lower_half, upper_half = (grads[..., :half_size], grads[..., half_size:])
    return jnp.concatenate(
        [
            lower_half * cosine_lookup + upper_half * sine_lookup,
            upper_half * cosine_lookup - lower_half * sine_lookup,
        ],
        -1,
    )


def normalize(values):
    row_peak = jnp.max(values, -1, keepdims=True)
    exp_scores = jnp.exp(values - row_peak)
    return exp_scores / jnp.sum(exp_scores, -1, keepdims=True)


def slot_tables(route_ids, expert_count, capacity):
    row_count, top_count = route_ids.shape
    onehot = route_ids[:, :, None] == jnp.arange(expert_count, dtype=jnp.int32)[None, None, :]
    hit_count = jnp.sum(onehot.astype(jnp.int32), 1)
    slot_place = jnp.cumsum(hit_count, 0) - 1
    within = jnp.take_along_axis(slot_place, route_ids, 1)
    dest_slot = route_ids * capacity + within
    pair_count = row_count * top_count
    source = (
        jnp.full((expert_count * capacity,), pair_count, jnp.int32)
        .at[dest_slot.reshape(-1)]
        .set(jnp.arange(pair_count, dtype=jnp.int32))
    )
    live_slot = source < pair_count
    token_row = jnp.minimum(source, pair_count - 1) // top_count
    return (onehot, dest_slot, source, live_slot, token_row)


def general_device(
    tokens,
    teacher,
    valid_mask,
    routes,
    first_gain,
    query_weight,
    key_matrix,
    value_matrix,
    output_weight,
    second_gain,
    router_weight,
    expert_in,
    expert_out,
):
    row_count = tokens.shape[0]
    model_width = tokens.shape[1]
    half_width = model_width // 2
    local_query = query_weight.shape[1] // HEAD_DIM
    local_kv = key_matrix.shape[1] // HEAD_DIM
    query_group_size = local_query // local_kv
    expert_count = router_weight.shape[1]
    row_local = expert_in.shape[0]
    senders = lax.axis_size("expert")
    partner_step = senders // 2
    capacity = 3 * row_count * TOP // (2 * expert_count)
    pair_count = row_count * TOP
    score_rows = min(512, row_count)
    valid_total = lax.psum(jnp.sum(valid_mask).astype(jnp.float32), "expert")
    tokens_f32 = tokens.astype(jnp.float32)
    scale_one = lax.rsqrt(jnp.mean(tokens_f32 * tokens_f32, -1, keepdims=True) + EPS)
    unit_one = tokens_f32 * scale_one
    first_normed = (unit_one * first_gain).astype(jnp.bfloat16)
    cosine_lookup, sine_lookup = rope_tables(row_count, HEAD_DIM)
    query_linear = jnp.dot(first_normed, query_weight, preferred_element_type=jnp.float32).reshape(
        row_count, local_query, HEAD_DIM
    )
    keys_linear = jnp.dot(first_normed, key_matrix, preferred_element_type=jnp.float32).reshape(
        row_count, local_kv, HEAD_DIM
    )
    value_low = jnp.dot(first_normed, value_matrix, preferred_element_type=jnp.float32).astype(
        jnp.bfloat16
    )
    value_low = value_low.reshape(row_count, local_kv, HEAD_DIM)
    query_rotated = apply_rotary(query_linear, cosine_lookup, sine_lookup).astype(jnp.bfloat16)
    keys_rot = apply_rotary(keys_linear, cosine_lookup, sine_lookup).astype(jnp.bfloat16)
    block_of = jnp.arange(row_count, dtype=jnp.int32) // BLOCK

    def scores(start_row):
        stop_row = start_row + score_rows
        query_block = query_rotated.reshape(score_rows, local_kv, query_group_size, HEAD_DIM)
        score_block = (
            jnp.einsum("qhgd,khd->hgqk", query_block, keys_rot, preferred_element_type=jnp.float32)
            * ATTN_SCALE
        )
        allowed = block_of[None, :stop_row] <= block_of[start_row:stop_row, None]
        return (query_block, jnp.where(allowed, score_block, -1e30))

    attn_parts, row_peaks, row_totals = ([], [], [])
    start_row = 0
    query_block, score_block = scores(start_row)
    row_peak = jnp.max(score_block, -1, keepdims=True)
    exp_scores = jnp.exp(score_block - row_peak)
    row_total = jnp.sum(exp_scores, -1, keepdims=True)
    attn_probs = (exp_scores / row_total).astype(jnp.bfloat16)
    attn_parts.append(
        jnp.einsum("hgqk,khd->qhgd", attn_probs, value_low, preferred_element_type=jnp.float32)
    )
    row_peaks.append(row_peak)
    row_totals.append(row_total)
    attended = attn_parts[0].reshape(row_count, local_query * HEAD_DIM).astype(jnp.bfloat16)
    attn_part = jnp.dot(attended, output_weight, preferred_element_type=jnp.float32)
    attn_sum = lax.psum(attn_part, "tensor")
    hidden_state = tokens_f32 + RESIDUAL * attn_sum
    scale_two = lax.rsqrt(jnp.mean(hidden_state * hidden_state, -1, keepdims=True) + EPS)
    unit_two = hidden_state * scale_two
    normed_two = (unit_two * second_gain).astype(jnp.bfloat16)
    router_logits = jnp.dot(normed_two, router_weight, preferred_element_type=jnp.float32)
    onehot, dest_slot, source, live_slot, token_row = slot_tables(routes, expert_count, capacity)
    picked = jnp.sum(jnp.where(onehot, router_logits[:, None, :], 0.0), -1)
    gate_probs = normalize(picked)

    def slot_rows(slot_values):
        split_rows = slot_values.reshape(expert_count, capacity, 2, half_width).transpose(
            2, 0, 1, 3
        )
        return split_rows.reshape(senders, row_local, capacity, half_width)

    def slot_columns(returned, width):
        joined = returned.reshape(2, expert_count, capacity, width).transpose(1, 2, 0, 3)
        return joined.reshape(expert_count * capacity, 2, width)

    send_rows = slot_rows(
        jnp.where(live_slot[:, None], normed_two[token_row], jnp.zeros((), jnp.bfloat16))
    )
    received = lax.all_to_all(send_rows, "expert", split_axis=0, concat_axis=2, tiled=True)
    expert_rows = received.reshape(row_local, senders * capacity, half_width)
    gate_up_part = jnp.einsum(
        "rmd,rcdf->rmcf", expert_rows, expert_in, preferred_element_type=jnp.float32
    )
    gate_up_pre = gate_up_part + shifted(gate_up_part, "expert", partner_step)
    gate_pre = gate_up_pre[:, :, 0]
    up_pre = gate_up_pre[:, :, 1]
    inner_act = (jax.nn.silu(gate_pre) * up_pre).astype(jnp.bfloat16)
    expert_result = jnp.einsum(
        "rmf,rfd->rmd", inner_act, expert_out, preferred_element_type=jnp.float32
    )
    expert_result = expert_result.astype(jnp.bfloat16).reshape(
        row_local, senders, capacity, half_width
    )
    returned = lax.all_to_all(expert_result, "expert", split_axis=1, concat_axis=0, tiled=True)
    per_route = slot_columns(returned, half_width).reshape(expert_count * capacity, model_width)[
        dest_slot
    ]
    moe_part = jnp.sum(gate_probs[:, :, None] * per_route, 1)
    moe_sum = lax.psum(moe_part, "tensor")
    output = hidden_state + RESIDUAL * moe_sum
    residual_err = output - teacher.astype(jnp.float32)
    valid_rows = valid_mask.astype(jnp.float32)
    squared_local = jnp.sum(valid_rows * jnp.sum(residual_err * residual_err, -1))
    token_total = senders * row_count
    grad_out = token_total / valid_total * valid_rows[:, None] * residual_err
    grad_moe = (RESIDUAL * grad_out).astype(jnp.bfloat16)
    gate_part = jnp.einsum("td,tkd->tk", grad_moe, per_route, preferred_element_type=jnp.float32)
    gate_slot = gate_probs.reshape(pair_count)[jnp.minimum(source, pair_count - 1)]
    grad_slots = jnp.where(live_slot[:, None], gate_slot[:, None] * grad_moe[token_row], 0.0)
    grad_received = lax.all_to_all(
        slot_rows(grad_slots.astype(jnp.bfloat16)),
        "expert",
        split_axis=0,
        concat_axis=2,
        tiled=True,
    )
    grad_expert = grad_received.reshape(row_local, senders * capacity, half_width)
    grad_inner_part = jnp.einsum(
        "rmd,rfd->rmf", grad_expert, expert_out, preferred_element_type=jnp.float32
    )
    grad_inner = grad_inner_part + shifted(grad_inner_part, "expert", partner_step)
    grad_expert_out = jnp.einsum(
        "rmf,rmd->rfd", inner_act, grad_expert, preferred_element_type=jnp.float32
    )
    sigmoid_gate = jax.nn.sigmoid(gate_pre)
    grad_gate = grad_inner * up_pre * sigmoid_gate * (1.0 + gate_pre * (1.0 - sigmoid_gate))
    grad_up = grad_inner * (gate_pre * sigmoid_gate)
    grad_pre = jnp.stack([grad_gate, grad_up], 2).astype(jnp.bfloat16)
    grad_expert_in = jnp.einsum(
        "rmd,rmcf->rcdf", expert_rows, grad_pre, preferred_element_type=jnp.float32
    )
    grad_slot_rows = jnp.einsum(
        "rmcf,rcdf->rmd", grad_pre, expert_in, preferred_element_type=jnp.float32
    )
    grad_slot_rows = grad_slot_rows.astype(jnp.bfloat16).reshape(
        row_local, senders, capacity, half_width
    )
    grad_back = lax.all_to_all(grad_slot_rows, "expert", split_axis=1, concat_axis=0, tiled=True)
    grad_back = slot_columns(grad_back, half_width).reshape(expert_count * capacity, model_width)
    grad_two_part = jnp.sum(grad_back[dest_slot].astype(jnp.float32), 1)
    grad_two_experts, grad_gates = lax.psum((grad_two_part, gate_part), "tensor")
    grad_picked = gate_probs * (grad_gates - jnp.sum(gate_probs * grad_gates, -1, keepdims=True))
    grad_logits = jnp.sum(jnp.where(onehot, grad_picked[:, :, None], 0.0), 1).astype(jnp.bfloat16)
    grad_router = jnp.einsum(
        "td,te->de", normed_two, grad_logits, preferred_element_type=jnp.float32
    )
    grad_two = grad_two_experts + jnp.einsum(
        "te,de->td", grad_logits, router_weight, preferred_element_type=jnp.float32
    )
    grad_second_gain = jnp.sum(grad_two * unit_two, 0)
    grad_unit_two = grad_two * second_gain
    grad_hidden = grad_out + scale_two * (
        grad_unit_two - unit_two * jnp.mean(grad_unit_two * unit_two, -1, keepdims=True)
    )
    grad_attn = (RESIDUAL * grad_hidden).astype(jnp.bfloat16)
    grad_output = jnp.einsum("tc,td->cd", attended, grad_attn, preferred_element_type=jnp.float32)
    grad_attended = jnp.einsum(
        "td,cd->tc", grad_attn, output_weight, preferred_element_type=jnp.float32
    )
    grad_attended = grad_attended.astype(jnp.bfloat16).reshape(
        row_count, local_kv, query_group_size, HEAD_DIM
    )
    grad_query_parts = []
    grad_keys = jnp.zeros((row_count, local_kv, HEAD_DIM), jnp.float32)
    grad_values = jnp.zeros((row_count, local_kv, HEAD_DIM), jnp.float32)
    for block_index, start_row in enumerate(range(0, row_count, score_rows)):
        stop_row = start_row + score_rows
        query_block, score_block = scores(start_row)
        attn_probs = jnp.exp(score_block - row_peaks[block_index]) / row_totals[block_index]
        probs_low = attn_probs.astype(jnp.bfloat16)
        grad_probs = jnp.einsum(
            "qhgd,khd->hgqk", grad_attended, value_low, preferred_element_type=jnp.float32
        )
        grad_scores = attn_probs * (
            grad_probs - jnp.sum(attn_probs * grad_probs, -1, keepdims=True)
        )
        grad_scores = grad_scores.astype(jnp.bfloat16)
        grad_query_parts.append(
            ATTN_SCALE
            * jnp.einsum(
                "hgqk,khd->qhgd", grad_scores, keys_rot, preferred_element_type=jnp.float32
            )
        )
        grad_keys = grad_keys.at[:stop_row].add(
            ATTN_SCALE
            * jnp.einsum(
                "hgqk,qhgd->khd", grad_scores, query_block, preferred_element_type=jnp.float32
            )
        )
        grad_values = grad_values.at[:stop_row].add(
            jnp.einsum(
                "hgqk,qhgd->khd", probs_low, grad_attended, preferred_element_type=jnp.float32
            )
        )
    grad_query_rot = grad_query_parts[0].reshape(row_count, local_query, HEAD_DIM)
    grad_query_low = unrotate(grad_query_rot, cosine_lookup, sine_lookup).reshape(
        row_count, local_query * HEAD_DIM
    )
    grad_query_low = grad_query_low.astype(jnp.bfloat16)
    grad_keys_low = unrotate(grad_keys, cosine_lookup, sine_lookup).reshape(
        row_count, local_kv * HEAD_DIM
    )
    grad_keys_low = grad_keys_low.astype(jnp.bfloat16)
    grad_values_low = grad_values.reshape(row_count, local_kv * HEAD_DIM).astype(jnp.bfloat16)
    grad_query = jnp.einsum(
        "td,tc->dc", first_normed, grad_query_low, preferred_element_type=jnp.float32
    )
    grad_key = jnp.einsum(
        "td,tc->dc", first_normed, grad_keys_low, preferred_element_type=jnp.float32
    )
    grad_value = jnp.einsum(
        "td,tc->dc", first_normed, grad_values_low, preferred_element_type=jnp.float32
    )
    grad_one_part = (
        jnp.einsum("tc,dc->td", grad_query_low, query_weight, preferred_element_type=jnp.float32)
        + jnp.einsum("tc,dc->td", grad_keys_low, key_matrix, preferred_element_type=jnp.float32)
        + jnp.einsum("tc,dc->td", grad_values_low, value_matrix, preferred_element_type=jnp.float32)
    )
    grad_one = lax.psum(grad_one_part.astype(jnp.bfloat16), "tensor").astype(jnp.float32)
    grad_first_gain = jnp.sum(grad_one * unit_one, 0)
    grad_unit_one = grad_one * first_gain
    grad_tokens = grad_hidden + scale_one * (
        grad_unit_one - unit_one * jnp.mean(grad_unit_one * unit_one, -1, keepdims=True)
    )
    reduced = lax.psum(
        (
            grad_first_gain,
            grad_query,
            grad_key,
            grad_value,
            grad_output,
            grad_second_gain,
            grad_router,
            squared_local,
        ),
        "expert",
    )
    loss_value = reduced[7] / (2.0 * model_width * valid_total)
    return (
        output.astype(jnp.bfloat16),
        loss_value,
        grad_tokens,
        reduced[0],
        reduced[1],
        reduced[2],
        reduced[3],
        reduced[4],
        reduced[5],
        reduced[6],
        grad_expert_in,
        grad_expert_out,
    )


BF16 = jnp.bfloat16
F32 = jnp.float32
CHUNK = 512
SHARE = 128
PACK = 12 * SHARE
NT = (((1,), (1,)), ((), ()))
ORDER = (0, 2, 4, 6, 1, 3, 5, 7)


def whole_block(shape):
    return pl.BlockSpec(shape, lambda e, *_: (0,) * len(shape))


def any_block():
    return pl.BlockSpec(memory_space=pl.ANY)


def pack_body(half_ref, own_in, own_out, other_in, other_out, *refs):
    own, near, far = refs[-3:]
    step = pl.program_id(0)

    def fill(target, source_in, source_out):
        for c in range(2):
            target[c * 4 * SHARE : (c + 1) * 4 * SHARE, :] = source_in[0, c]
        for k in range(4):
            target[(8 + k) * SHARE : (9 + k) * SHARE, :] = source_out[
                0, :, k * SHARE : (k + 1) * SHARE
            ]

    fill(own, own_in, own_out)

    @pl.when(step < 2)
    def _():
        fill(near, other_in, other_out)

    @pl.when(step >= 2)
    def _():
        fill(far, other_in, other_out)


def pack_weights(half_index, expert_in, expert_out, *after):
    held = expert_in.shape[0] // 2
    in_shape = (1,) + expert_in.shape[1:]
    out_shape = (1,) + expert_out.shape[1:]
    shapes = [(held * PACK, SHARE), (held // 2 * PACK, SHARE), (held // 2 * PACK, SHARE)]
    block = (PACK, SHARE)
    return pl.pallas_call(
        pack_body,
        grid_spec=pltpu.PrefetchScalarGridSpec(
            num_scalar_prefetch=1,
            grid=(held,),
            in_specs=[
                pl.BlockSpec(in_shape, lambda e, half: (half[0] * held + e, 0, 0, 0)),
                pl.BlockSpec(out_shape, lambda e, half: (half[0] * held + e, 0, 0)),
                pl.BlockSpec(in_shape, lambda e, half: ((1 - half[0]) * held + e, 0, 0, 0)),
                pl.BlockSpec(out_shape, lambda e, half: ((1 - half[0]) * held + e, 0, 0)),
            ]
            + [any_block()] * len(after),
            out_specs=[
                pl.BlockSpec(block, lambda e, half: (e, 0)),
                pl.BlockSpec(block, lambda e, half: (jnp.minimum(e, 1), 0)),
                pl.BlockSpec(block, lambda e, half: (jnp.maximum(e - 2, 0), 0)),
            ],
        ),
        out_shape=[jax.ShapeDtypeStruct(shape, BF16) for shape in shapes],
        name="pack_weights",
    )(half_index, expert_in, expert_out, expert_in, expert_out, *after)


def weight_copies(own, other, own_row, other_row, half, in_buf, out_buf, sems, slot):
    copies = []
    for q in range(4):
        for pack, row, side in ((own[q], own_row, half), (other[q], other_row, 1 - half)):
            for c in range(2):
                copies.append(
                    (
                        pack.at[pl.ds(pl.multiple_of(row + c * 4 * SHARE, SHARE), 4 * SHARE)],
                        in_buf.at[
                            slot,
                            pl.ds(pl.multiple_of(side * 4 * SHARE, SHARE), 4 * SHARE),
                            pl.ds((2 * q + c) * SHARE, SHARE),
                        ],
                    )
                )
            for k in range(4):
                copies.append(
                    (
                        pack.at[pl.ds(pl.multiple_of(row + (8 + k) * SHARE, SHARE), SHARE)],
                        out_buf.at[slot, side, pl.ds(q * SHARE, SHARE), pl.ds(k * SHARE, SHARE)],
                    )
                )
    return [
        pltpu.make_async_copy(source, target, sems.at[slot, n])
        for n, (source, target) in enumerate(copies)
    ]


def stream_weights(first, packs, half, in_buf, out_buf, sems):
    step = pl.program_id(0)
    slot = lax.rem(step, 2)
    own, near, far = (packs[0:4], packs[4:8], packs[8:12])

    def start(index, target):
        expert = first + index

        def begin(other, start_row):
            for copy in weight_copies(
                own, other, expert * PACK, start_row, half, in_buf, out_buf, sems, target
            ):
                copy.start()

        if not far:
            begin(near, index * PACK)
            return

        @pl.when(expert < 2)
        def _():
            begin(near, expert * PACK)

        @pl.when(expert >= 2)
        def _():
            begin(far, (expert - 2) * PACK)

    @pl.when(step == 0)
    def _():
        start(0, 0)

    @pl.when(step + 1 < pl.num_programs(0))
    def _():
        start(step + 1, 1 - slot)

    def wait():
        for copy in weight_copies(own, near, 0, 0, half, in_buf, out_buf, sems, slot):
            copy.wait()

    return (step, slot, wait)


def weight_scratch(width, hidden):
    return [
        pltpu.VMEM((2, width, 2 * hidden), BF16),
        pltpu.VMEM((2, 2, hidden, width // 2), BF16),
        pltpu.SemaphoreType.DMA((2, 48)),
    ]


def split_pairs(values):
    blocks = [values[:, i * SHARE : (i + 1) * SHARE] for i in range(values.shape[1] // SHARE)]
    return (jnp.concatenate(blocks[0::2], 1), jnp.concatenate(blocks[1::2], 1))


def join_pairs(first, second):
    blocks = []
    for i in range(first.shape[1] // SHARE):
        blocks.append(first[:, i * SHARE : (i + 1) * SHARE])
        blocks.append(second[:, i * SHARE : (i + 1) * SHARE])
    return jnp.concatenate(blocks, 1)


def chunk_loop(row_count, body):
    def step(i, carry):
        body(pl.ds(pl.multiple_of(i * CHUNK, CHUNK), CHUNK))
        return carry

    lax.fori_loop(0, row_count // CHUNK, step, 0)


def gate_column(gates, expert):
    lane = lax.broadcasted_iota(jnp.int32, gates.shape, 1)
    return jnp.sum(jnp.where(lane == expert, gates, 0.0), -1, keepdims=True)


def dense_gates(rows, ids, router):
    logits = jnp.dot(rows, router, preferred_element_type=F32)
    lane = lax.broadcasted_iota(jnp.int32, logits.shape, 1)
    mask = ids[:, 0:1] == lane
    for k in range(1, TOP):
        mask = mask | (ids[:, k : k + 1] == lane)
    masked = jnp.where(mask, logits, -1e30)
    powers = jnp.where(mask, jnp.exp(masked - jnp.max(masked, -1, keepdims=True)), 0.0)
    return powers / jnp.sum(powers, -1, keepdims=True)


def apply_expert(rows, expert, slot, rows_ref, gate_ref, pre_ref, gated_ref, in_buf):
    pre = jnp.dot(rows_ref[rows, :], in_buf[slot], preferred_element_type=F32)
    pre_ref[0, rows, :] = pre.astype(BF16)
    gate_pre, up_pre = split_pairs(pre)
    weight = gate_column(gate_ref[rows, :], expert)
    gated = (weight * (gate_pre * jax.nn.sigmoid(gate_pre) * up_pre)).astype(BF16)
    gated_ref[0, rows, :] = gated
    return gated


def forward_first(half_ref, *refs):
    shards = refs[:8]
    route_ref, router_ref = refs[8:10]
    packs = refs[10:18]
    acc, pre_ref, gated_ref, gate_ref, rows_ref, in_buf, out_buf, sems = refs[18:]
    step, slot, wait = stream_weights(0, packs, half_ref[0], in_buf, out_buf, sems)
    row_count, width = acc.shape
    size = row_count // 8

    @pl.when(step == 0)
    def _():
        for i in range(8):
            rows_ref[i * size : (i + 1) * size, :] = shards[i][...]
        acc[...] = jnp.zeros_like(acc)

        def gating(rows):
            gate_ref[rows, :] = dense_gates(rows_ref[rows, :], route_ref[rows, :], router_ref[...])

        chunk_loop(row_count, gating)

    wait()

    def mlp(rows):
        gated = apply_expert(rows, step, slot, rows_ref, gate_ref, pre_ref, gated_ref, in_buf)
        for side in range(2):
            columns = slice(side * width // 2, (side + 1) * width // 2)
            acc[rows, columns] += jnp.dot(gated, out_buf[slot, side], preferred_element_type=F32)

    chunk_loop(row_count, mlp)


def forward_second(half_ref, *refs):
    rows_ref, gate_ref, start_ref = refs[:3]
    packs = refs[3:11]
    pre_ref, gated_ref = refs[-6:-4]
    targets = refs[13:-6]
    acc, in_buf, out_buf, sems = refs[-4:]
    step, slot, wait = stream_weights(2, packs, half_ref[0], in_buf, out_buf, sems)
    row_count, width = acc.shape

    wait()

    def mlp(rows, source):
        gated = apply_expert(rows, step + 2, slot, rows_ref, gate_ref, pre_ref, gated_ref, in_buf)
        for side in range(2):
            columns = slice(side * width // 2, (side + 1) * width // 2)
            acc[rows, columns] = source[rows, columns] + jnp.dot(
                gated, out_buf[slot, side], preferred_element_type=F32
            )

    @pl.when(step == 0)
    def _():
        acc[...] = start_ref[...]

    chunk_loop(row_count, lambda rows: mlp(rows, acc))

    @pl.when(step == pl.num_programs(0) - 1)
    def _():
        spread(acc, targets)


def spread(acc, targets):
    size = acc.shape[0] // len(targets)
    for i, target in enumerate(targets):
        target[...] = acc[i * size : (i + 1) * size, :].astype(target.dtype)


def spread_specs(part, row_count, width):
    if part == 0:
        shapes = [jax.ShapeDtypeStruct((row_count // 2, width), F32)]
    else:
        shapes = [jax.ShapeDtypeStruct((row_count // 4, width), BF16)] * 2
    return ([whole_block(s.shape) for s in shapes], shapes)


def half_rows(shape, part):
    block = (shape[0] // 2,) + shape[1:]
    return pl.BlockSpec(block, lambda e, *_: (part, 0))


def half_expert(shape, part, first=0):
    block = (1, shape[1] // 2) + shape[2:]
    return pl.BlockSpec(block, lambda e, *_: (e + first, part, 0))


def expert_block(shape, first=0):
    return pl.BlockSpec((1,) + shape[1:], lambda e, *_: (e + first,) + (0,) * (len(shape) - 1))


def experts_forward(half_index, shards, route_ids, router, own, near, far):
    size, width = shards[0].shape
    row_count = 8 * size
    local = own[0].shape[0] // PACK
    hidden = 4 * SHARE
    sums = jax.ShapeDtypeStruct((row_count, width), F32)
    pre = jax.ShapeDtypeStruct((local, row_count, 2 * hidden), BF16)
    gated = jax.ShapeDtypeStruct((local, row_count, hidden), BF16)
    gates = jax.ShapeDtypeStruct((row_count, 128), F32)
    rows = jax.ShapeDtypeStruct((row_count, width), BF16)
    sums_a, pre_a, gated_a, gates, rows = pl.pallas_call(
        forward_first,
        grid_spec=pltpu.PrefetchScalarGridSpec(
            num_scalar_prefetch=1,
            grid=(2,),
            in_specs=[whole_block(v.shape) for v in (*shards, route_ids, router)]
            + [any_block()] * 8,
            out_specs=[
                whole_block(sums.shape),
                expert_block(pre.shape),
                expert_block(gated.shape),
                whole_block(gates.shape),
                whole_block(rows.shape),
            ],
            scratch_shapes=weight_scratch(width, hidden),
        ),
        out_shape=[sums, pre, gated, gates, rows],
        name="experts_forward_a",
    )(half_index, *shards, route_ids, router, *own, *near)
    far_pack, far_across, sums_a = lax.optimization_barrier((*far, sums_a))
    far = [far_pack, swap_core(far_pack), far_across, swap_core(far_across)]

    def second(part, pre_a, gated_a):
        specs, shapes = spread_specs(part, row_count, width)
        return pl.pallas_call(
            forward_second,
            grid_spec=pltpu.PrefetchScalarGridSpec(
                num_scalar_prefetch=1,
                grid=(2,),
                in_specs=[half_rows(v.shape, part) for v in (rows, gates, sums)]
                + [any_block()] * 10,
                out_specs=specs
                + [half_expert(pre.shape, part, 2), half_expert(gated.shape, part, 2)],
                scratch_shapes=[pltpu.VMEM((row_count // 2, width), F32)]
                + weight_scratch(width, hidden),
            ),
            out_shape=shapes + [pre, gated],
            input_output_aliases={12: len(shapes), 13: len(shapes) + 1},
            name="experts_forward_b",
        )(half_index, rows, gates, sums_a, *own, *far, pre_a, gated_a)

    send_near, send_far, pre_a, gated_a = second(1, pre_a, gated_a)
    keep, pre_a, gated_a = second(0, pre_a, gated_a)
    return (keep, send_near, send_far, pre_a, gated_a, gates, rows, far)


def backward_body(half_ref, *refs):
    shards = refs[:4]
    gate_ref, router_ref, pre_ref = refs[4:7]
    packs = refs[7:19]
    pre_grad_ref, logit_ref, grad_ref = refs[-7:-4]
    acc, in_buf, out_buf, sems = refs[-4:]
    step, slot, wait = stream_weights(0, packs, half_ref[0], in_buf, out_buf, sems)
    row_count, width = grad_ref.shape
    size = row_count // 4
    targets = [ref for ref in refs[19:-7] if ref.shape[0] * 2 == row_count]
    targets = targets or [refs[-8]]

    @pl.when(step == 0)
    def _():
        for i in range(4):
            grad_ref[i * size : (i + 1) * size, :] = shards[i][...]
        acc[...] = jnp.zeros_like(acc)
        logit_ref[...] = jnp.zeros_like(logit_ref)

    wait()

    def mlp(rows):
        plain = lax.dot_general(
            grad_ref[rows, : width // 2], out_buf[slot, 0], NT, preferred_element_type=F32
        ) + lax.dot_general(
            grad_ref[rows, width // 2 :], out_buf[slot, 1], NT, preferred_element_type=F32
        )
        gate_pre, up_pre = split_pairs(pre_ref[0, rows, :].astype(F32))
        weight = gate_column(gate_ref[rows, :], step)
        sigmoid = jax.nn.sigmoid(gate_pre)
        act = gate_pre * sigmoid
        grad_weight = jnp.sum(act * up_pre * plain, -1, keepdims=True)
        scaled = weight * plain
        pre_grad = join_pairs(
            scaled * up_pre * (sigmoid + act * (1.0 - sigmoid)), scaled * act
        ).astype(BF16)
        pre_grad_ref[0, rows, :] = pre_grad
        old = logit_ref[rows, :]
        lane = lax.broadcasted_iota(jnp.int32, old.shape, 1)
        value = weight * grad_weight
        high = value.astype(BF16).astype(F32)
        logit_ref[rows, :] = jnp.where(
            lane == step, high, jnp.where(lane == step + 32, value - high, old)
        )
        acc[rows, :] += lax.dot_general(pre_grad, in_buf[slot], NT, preferred_element_type=F32)

    chunk_loop(row_count, mlp)

    @pl.when(step == pl.num_programs(0) - 1)
    def _():
        def router(rows):
            acc[rows, :] += lax.dot_general(
                logit_ref[rows, :].astype(BF16), router_ref[...], NT, preferred_element_type=F32
            )

        chunk_loop(row_count, router)
        spread(acc, targets)


def experts_backward(part, half_index, shards, gates, router, pre, own, near, far, *before):
    row_count, width = (8 * shards[0].shape[0], shards[0].shape[1])
    local = pre.shape[0]
    specs, shapes = spread_specs(part, row_count, width)
    saved = [
        jax.ShapeDtypeStruct(pre.shape, BF16),
        jax.ShapeDtypeStruct((row_count, 128), F32),
        jax.ShapeDtypeStruct((row_count, width), BF16),
    ]
    return pl.pallas_call(
        backward_body,
        grid_spec=pltpu.PrefetchScalarGridSpec(
            num_scalar_prefetch=1,
            grid=(local,),
            in_specs=[whole_block(v.shape) for v in shards]
            + [half_rows(gates.shape, part), whole_block(router.shape)]
            + [half_expert(pre.shape, part)]
            + [any_block()] * (12 + len(before)),
            out_specs=specs
            + [half_expert(pre.shape, part)]
            + [half_rows(v.shape, part) for v in saved[1:]],
            scratch_shapes=[pltpu.VMEM((row_count // 2, width), F32)]
            + weight_scratch(width, 4 * SHARE),
        ),
        out_shape=shapes + saved,
        input_output_aliases={20 + i: len(shapes) + i for i in range(len(before))},
        name="experts_backward",
    )(half_index, *shards, gates, router, pre, *own, *near, *far, *before)


def grad_out_body(half_ref, gated_ref, other_ref, mine_ref, *refs):
    *outs, turned = refs[-5:]
    turned[...] = gated_ref[0].T

    def pair(q, carry):
        for n, source in ((0, other_ref), (2, mine_ref)):
            for odd in range(2):
                rows = pl.ds(pl.multiple_of((2 * q + odd) * SHARE, SHARE), SHARE)
                product = jnp.dot(turned[rows, :], source[...], preferred_element_type=F32)
                outs[n + odd][q, 0] = product.astype(BF16)
        return carry

    lax.fori_loop(0, 2, pair, 0)


def grad_expert_outs(half_index, gated, grads, *after):
    local, row_count, hidden = gated.shape
    width = grads.shape[1]
    half_spec = (row_count, width // 2)
    shape = (2, local, SHARE, width // 2)
    return pl.pallas_call(
        grad_out_body,
        grid_spec=pltpu.PrefetchScalarGridSpec(
            num_scalar_prefetch=1,
            grid=(local,),
            in_specs=[
                expert_block(gated.shape),
                pl.BlockSpec(half_spec, lambda e, half: (0, 1 - half[0])),
                pl.BlockSpec(half_spec, lambda e, half: (0, half[0])),
            ]
            + [any_block()] * len(after),
            out_specs=[pl.BlockSpec((2, 1) + shape[2:], lambda e, *_: (0, e, 0, 0))] * 4,
            scratch_shapes=[pltpu.VMEM((hidden, row_count), BF16)],
        ),
        out_shape=[jax.ShapeDtypeStruct(shape, BF16)] * 4,
        name="grad_expert_out",
    )(half_index, gated, grads, grads, *after)


def grad_in_body(half_ref, rows_ref, pre_ref, *refs):
    keep_ref, send_ref, turned = refs[-3:]

    @pl.when(pl.program_id(0) == 0)
    def _():
        turned[...] = rows_ref[...].T

    def part(i, carry):
        rows = pl.ds(pl.multiple_of(i * CHUNK, CHUNK), CHUNK)
        product = jnp.dot(turned[rows, :], pre_ref[0], preferred_element_type=F32).astype(BF16)
        for q in range(4):
            for c in range(2):
                start = (2 * q + c) * SHARE
                (keep_ref, send_ref)[q % 2][q // 2, 0, c, rows] = product[:, start : start + SHARE]
        return carry

    lax.fori_loop(0, turned.shape[0] // CHUNK, part, 0)


def grad_expert_ins(half_index, rows, pre_grad, first, count, *after):
    local, row_count, wide = pre_grad.shape
    width = rows.shape[1]
    shape = (2, count, 2, width // 2, SHARE)
    return pl.pallas_call(
        grad_in_body,
        grid_spec=pltpu.PrefetchScalarGridSpec(
            num_scalar_prefetch=1,
            grid=(count,),
            in_specs=[
                pl.BlockSpec((row_count, width // 2), lambda e, half: (0, half[0])),
                expert_block(pre_grad.shape, first),
            ]
            + [any_block()] * len(after),
            out_specs=[pl.BlockSpec((2, 1) + shape[2:], lambda e, *_: (0, e, 0, 0, 0))] * 2,
            scratch_shapes=[pltpu.VMEM((width // 2, row_count), BF16)],
        ),
        out_shape=[jax.ShapeDtypeStruct(shape, BF16)] * 2,
        name="grad_expert_in",
    )(half_index, rows, pre_grad, *after)


def fold_body(keep_ref, got_ref, *refs):
    near_ref, far_ref = refs[-2:]
    near_ref[...] = keep_ref[0].astype(F32) + got_ref[0].astype(F32)
    far_ref[...] = (keep_ref[1].astype(F32) + got_ref[1].astype(F32)).astype(BF16)


def fold_pairs(keep, got, *after):
    shape = keep.shape
    rest = (0,) * (len(shape) - 2)
    pair = pl.BlockSpec((2, 1) + shape[2:], lambda e: (0, e) + rest)
    single = pl.BlockSpec((1,) + shape[2:], lambda e: (e,) + rest)
    return pl.pallas_call(
        fold_body,
        grid=(shape[1],),
        in_specs=[pair, pair] + [any_block()] * len(after),
        out_specs=[single, single],
        out_shape=[
            jax.ShapeDtypeStruct(shape[1:], F32),
            jax.ShapeDtypeStruct(shape[1:], BF16),
        ],
        name="fold_pairs",
    )(keep, got, *after)


def finish_body(keep, near, four, two, extra, unit, scale, gain, grad_out, *refs):
    hidden_ref, attn_ref, gain_ref = refs[-3:]
    total = keep[...] + near[...].astype(F32) + extra[...]
    for part in (four, two):
        total = total + part[...].astype(F32)
    gain_ref[...] = jnp.sum((total * unit[...]).reshape(-1, 8, total.shape[1]), 0)
    weighted = total * gain[...]
    mean = jnp.mean(weighted * unit[...], -1, keepdims=True)
    hidden = grad_out[...] + scale[...] * (weighted - unit[...] * mean)
    hidden_ref[...] = hidden
    attn_ref[...] = (RESIDUAL * hidden).astype(BF16)


def finish_rows(keep, near, four, two, extra, unit, scale, gain, grad_out, *after):
    size, width = unit.shape
    block = pl.BlockSpec((size, width), lambda e: (0, 0))
    return pl.pallas_call(
        finish_body,
        grid=(1,),
        in_specs=[block] * 6
        + [whole_block((size, 1)), whole_block((1, width)), block]
        + [any_block()] * len(after),
        out_specs=[block, block, whole_block((8, width))],
        out_shape=[
            jax.ShapeDtypeStruct((size, width), F32),
            jax.ShapeDtypeStruct((size, width), BF16),
            jax.ShapeDtypeStruct((8, width), F32),
        ],
        name="finish_rows",
    )(keep, near, four, two, extra, unit, scale, gain, grad_out, *after)


def rotated(values, cosine, sine, sign):
    width = values.shape[1]
    lane = lax.broadcasted_iota(jnp.int32, values.shape, 1)
    lower = lax.rem(lane, HEAD_DIM) < HEAD_DIM // 2
    ahead = pltpu.roll(values, width - HEAD_DIM // 2, 1)
    behind = pltpu.roll(values, HEAD_DIM // 2, 1)
    turned = jnp.where(lower, -ahead, behind)
    repeat = width // cosine.shape[1]
    cosine = jnp.concatenate([cosine] * repeat, 1)
    sine = jnp.concatenate([sine] * repeat, 1)
    return values * cosine + sign * (turned * sine)


def head(values, index, start=0, stop=None):
    return values[start:stop, index * HEAD_DIM : (index + 1) * HEAD_DIM]


def probabilities(query, keys):
    scores = lax.dot_general(query, keys, NT, preferred_element_type=F32) * ATTN_SCALE
    powers = jnp.exp(scores - jnp.max(scores, -1, keepdims=True))
    return powers / jnp.sum(powers, -1, keepdims=True)


def attention_forward_body(
    core_ref, tokens, gain, query_w, key_w, value_w, output_w, cosine, sine, *refs
):
    normed, query, keys, values, attended, keep, send = refs[-7:]
    x = tokens[...].astype(F32)
    scale = lax.rsqrt(jnp.mean(x * x, -1, keepdims=True) + EPS)
    normed[...] = (x * scale * gain[...]).astype(BF16)
    low = normed[...]
    linear = jnp.dot(low, query_w[...], preferred_element_type=F32)
    query[...] = rotated(linear, cosine[...], sine[...], 1.0).astype(BF16)
    linear = jnp.dot(low, key_w[...], preferred_element_type=F32)
    keys[...] = rotated(linear, cosine[...], sine[...], 1.0).astype(BF16)
    values[...] = jnp.dot(low, value_w[...], preferred_element_type=F32).astype(BF16)
    group = query.shape[1] // keys.shape[1]
    for start in range(0, tokens.shape[0], BLOCK):
        stop = start + BLOCK
        parts = []
        for h in range(query.shape[1] // HEAD_DIM):
            probs = probabilities(head(query, h, start, stop), head(keys, h // group, 0, stop))
            parts.append(
                jnp.dot(
                    probs.astype(BF16),
                    head(values, h // group, 0, stop),
                    preferred_element_type=F32,
                )
            )
        attended[start:stop, :] = jnp.concatenate(parts, 1).astype(BF16)
    size = tokens.shape[0] // 4
    for r in range(2):
        for target, core in ((keep, core_ref[0]), (send, 1 - core_ref[0])):
            rows = pl.ds(pl.multiple_of((2 * r + core) * size, size), size)
            part = jnp.dot(attended[rows, :], output_w[...], preferred_element_type=F32)
            target[r] = part.astype(target.dtype)


def scalar_call(body, name, scalar, inputs, shapes, after=(), scratch=()):
    return pl.pallas_call(
        body,
        grid_spec=pltpu.PrefetchScalarGridSpec(
            num_scalar_prefetch=1,
            grid=(1,),
            in_specs=[whole_block(v.shape) for v in inputs] + [any_block()] * len(after),
            out_specs=[whole_block(s.shape) for s in shapes],
            scratch_shapes=list(scratch),
        ),
        out_shape=shapes,
        name=name,
    )(scalar, *inputs, *after)


def attention_forward(core, tokens, gain, query_w, key_w, value_w, output_w, tables, *after):
    rows, width = tokens.shape
    shapes = [
        jax.ShapeDtypeStruct((rows, width), BF16),
        jax.ShapeDtypeStruct((rows, query_w.shape[1]), BF16),
        jax.ShapeDtypeStruct((rows, key_w.shape[1]), BF16),
        jax.ShapeDtypeStruct((rows, value_w.shape[1]), BF16),
        jax.ShapeDtypeStruct((rows, query_w.shape[1]), BF16),
        jax.ShapeDtypeStruct((2, rows // 4, width), F32),
        jax.ShapeDtypeStruct((2, rows // 4, width), BF16),
    ]
    inputs = (tokens, gain, query_w, key_w, value_w, output_w, *tables)
    return scalar_call(
        attention_forward_body, "attention_forward", core, inputs, shapes, after
    )


TN = (((0,), (0,)), ((), ()))


def attention_backward_body(
    share_ref,
    tokens,
    query_w,
    key_w,
    value_w,
    output_w,
    cosine,
    sine,
    query,
    keys,
    values,
    first,
    second,
    third,
    fourth,
    *refs,
):
    grad, grad_qkv, gain, keep, send, grad_keys, grad_values = refs[-7:]
    share = share_ref[0]
    size = first.shape[0]
    for r, piece in enumerate((first, second, third, fourth)):
        place = jnp.bitwise_xor(share, r) * size
        grad[pl.ds(pl.multiple_of(place, size), size), :] = piece[...]
    back = lax.dot_general(grad[...], output_w[...], NT, preferred_element_type=F32).astype(BF16)
    wide, narrow = (query.shape[1], keys.shape[1])
    group = wide // narrow
    grad_keys[...] = jnp.zeros_like(grad_keys)
    grad_values[...] = jnp.zeros_like(grad_values)
    for start in range(0, tokens.shape[0], BLOCK):
        stop = start + BLOCK
        parts, key_parts, value_parts = ([], [], [])
        for kv in range(narrow // HEAD_DIM):
            key, value = (head(keys, kv, 0, stop), head(values, kv, 0, stop))
            key_sum, value_sum = (0.0, 0.0)
            for h in range(kv * group, (kv + 1) * group):
                query_h = head(query, h, start, stop)
                back_h = head(back, h, start, stop)
                probs = probabilities(query_h, key)
                inner = lax.dot_general(back_h, value, NT, preferred_element_type=F32)
                scores = probs * (inner - jnp.sum(probs * inner, -1, keepdims=True))
                scores = scores.astype(BF16)
                parts.append(ATTN_SCALE * jnp.dot(scores, key, preferred_element_type=F32))
                key_sum += lax.dot_general(scores, query_h, TN, preferred_element_type=F32)
                value_sum += lax.dot_general(
                    probs.astype(BF16), back_h, TN, preferred_element_type=F32
                )
            key_parts.append(ATTN_SCALE * key_sum)
            value_parts.append(value_sum)
        turned = rotated(
            jnp.concatenate(parts, 1), cosine[start:stop, :], sine[start:stop, :], -1.0
        )
        grad_qkv[start:stop, :wide] = turned.astype(BF16)
        grad_keys[:stop, :] += jnp.concatenate(key_parts, 1)
        grad_values[:stop, :] += jnp.concatenate(value_parts, 1)
    turned = rotated(grad_keys[...], cosine[...], sine[...], -1.0)
    grad_qkv[:, wide : wide + narrow] = turned.astype(BF16)
    grad_qkv[:, wide + narrow :] = grad_values[...].astype(BF16)
    total = jnp.zeros(gain.shape, F32)
    for r in range(2):
        for target, core in ((keep, share % 2), (send, 1 - share % 2)):
            rows = pl.ds(pl.multiple_of((2 * r + core) * size, size), size)
            part = lax.dot_general(
                grad_qkv[rows, :wide], query_w[...], NT, preferred_element_type=F32
            )
            part += lax.dot_general(
                grad_qkv[rows, wide : wide + narrow], key_w[...], NT, preferred_element_type=F32
            )
            part += lax.dot_general(
                grad_qkv[rows, wide + narrow :], value_w[...], NT, preferred_element_type=F32
            )
            target[r] = part.astype(target.dtype)
            x = tokens[rows, :].astype(F32)
            x = x * lax.rsqrt(jnp.mean(x * x, -1, keepdims=True) + EPS)
            total += jnp.sum((part * x).reshape(-1, 8, x.shape[1]), 0)
    gain[...] = total


def attention_backward(share, tokens, weights, tables, saved, pieces, *after):
    rows, width = tokens.shape
    narrow = saved[1].shape[1]
    shapes = [
        jax.ShapeDtypeStruct((rows, width), BF16),
        jax.ShapeDtypeStruct((rows, saved[0].shape[1] + 2 * narrow), BF16),
        jax.ShapeDtypeStruct((8, width), F32),
        jax.ShapeDtypeStruct((2, rows // 4, width), F32),
        jax.ShapeDtypeStruct((2, rows // 4, width), BF16),
    ]
    return scalar_call(
        attention_backward_body,
        "attention_backward",
        share,
        (tokens, *weights, *tables, *saved, *pieces),
        shapes,
        after,
        [pltpu.VMEM((rows, narrow), F32), pltpu.VMEM((rows, narrow), F32)],
    )


def reduce_body(place_ref, normed, grad_qkv, grad, attended, small, gain, *refs):
    keep, near, far = refs[-3:]
    step = pl.program_id(0)
    first = lax.dot_general(normed[...], grad_qkv[...], TN, preferred_element_type=F32)
    second = lax.dot_general(grad[...], attended[...], TN, preferred_element_type=F32)
    rest = jnp.zeros((SHARE - small.shape[0] - gain.shape[0], SHARE), F32)
    third = jnp.concatenate([small[...], gain[...], rest], 0).T
    part = jnp.concatenate([first, second, third], 1)

    @pl.when(step < 4)
    def _():
        keep[...] = part

    @pl.when((step == 4) | (step == 5))
    def _():
        near[...] = part.astype(BF16)

    @pl.when(step >= 6)
    def _():
        far[...] = part.astype(BF16)


def reduce_parts(place, normed, grad_qkv, grad, attended, small, gain, *after):
    rows, width = normed.shape
    size = width // 8
    total = grad_qkv.shape[1] + attended.shape[1] + SHARE

    def shard(e, place):
        order = jnp.where(e < 4, 2 * e, 2 * e - 7)
        return jnp.bitwise_xor(place[0], order)

    columns = pl.BlockSpec((rows, size), lambda e, place: (0, shard(e, place)))
    return pl.pallas_call(
        reduce_body,
        grid_spec=pltpu.PrefetchScalarGridSpec(
            num_scalar_prefetch=1,
            grid=(8,),
            in_specs=[
                columns,
                whole_block(grad_qkv.shape),
                columns,
                whole_block(attended.shape),
                pl.BlockSpec((small.shape[0], size), lambda e, place: (0, shard(e, place))),
                pl.BlockSpec((gain.shape[0], size), lambda e, place: (0, shard(e, place))),
            ]
            + [any_block()] * len(after),
            out_specs=[
                pl.BlockSpec((size, total), lambda e, _: (jnp.minimum(e, 3), 0)),
                pl.BlockSpec((size, total), lambda e, _: (jnp.clip(e - 4, 0, 1), 0)),
                pl.BlockSpec((size, total), lambda e, _: (jnp.clip(e - 6, 0, 1), 0)),
            ],
        ),
        out_shape=[
            jax.ShapeDtypeStruct((4 * size, total), F32),
            jax.ShapeDtypeStruct((2 * size, total), BF16),
            jax.ShapeDtypeStruct((2 * size, total), BF16),
        ],
        name="reduce_parts",
    )(place, normed, grad_qkv, grad, attended, small, gain, *after)


def unpack_body(place_ref, *refs):
    pieces = refs[:8]
    query, key, value, output, small = refs[-5:]
    size = pieces[0].shape[0]
    wide, narrow = (query.shape[1], key.shape[1])
    for r, piece in zip(ORDER, pieces):
        start = pl.multiple_of(jnp.bitwise_xor(place_ref[0], r) * size, size)
        rows = pl.ds(start, size)
        part = piece[...].astype(F32)
        query[rows, :] = part[:, :wide]
        key[rows, :] = part[:, wide : wide + narrow]
        value[rows, :] = part[:, wide + narrow : wide + 2 * narrow]
        begin = wide + 2 * narrow
        output[:, rows] = part[:, begin : begin + output.shape[0]].T
        small[rows, :] = part[:, begin + output.shape[0] :]


def assemble_body(share_ref, *refs):
    target = refs[-1]
    size = refs[0].shape[0]
    for r in range(4):
        start = pl.multiple_of(jnp.bitwise_xor(share_ref[0], r) * size, size)
        target[pl.ds(start, size), :] = refs[r][...].astype(target.dtype)


def spread_tensor(value):
    across = swap_y(value)
    return [value, swap_core(value), across, swap_core(across)]


def assemble(share, pieces, dtype, *after):
    size, width = pieces[0].shape
    shapes = [jax.ShapeDtypeStruct((4 * size, width), dtype)]
    return scalar_call(assemble_body, "assemble", share, pieces, shapes, after)[0]


def trade(value, bits):
    return lax.ppermute(value, "expert", [(i, i ^ bits) for i in range(8)])


def swap_y(value):
    return lax.ppermute(value, "tensor", [(i, i ^ 2) for i in range(4)])


def swap_core(value):
    return lax.ppermute(value, "tensor", [(i, i ^ 1) for i in range(4)])


def gather_experts(value):
    column = [value] + [trade(value, bits) for bits in (2, 4, 6)]
    return column + [trade(shard, 1) for shard in column]


def scatter_steps(keep, send_near, send_far, *beside):
    size = keep.shape[0] // 4
    got_far = trade(send_far, 1)
    send_near, got_far, keep = lax.optimization_barrier((send_near, got_far, keep))
    if beside:
        got_far, *beside = lax.optimization_barrier((got_far, *beside))
    far = (keep[2 * size :] + got_far.astype(F32)).astype(BF16)
    got_near = trade(send_near, 1)
    four, six = (trade(far[:size], 4), trade(far[size:], 6))
    near = (keep[size : 2 * size] + got_near[size:].astype(F32)).astype(BF16)
    return (keep, got_near, (trade(near, 2), four, six), *beside)


def scatter_experts(keep, send_near, send_far, *beside):
    size = keep.shape[0] // 4
    keep, got_near, back, *beside = scatter_steps(keep, send_near, send_far, *beside)
    total = keep[:size] + got_near[:size].astype(F32)
    for part in back:
        total = total + part.astype(F32)
    return (total, *beside) if beside else total


def scatter_tensor(keep, send, row):
    half = keep + swap_core(send).astype(F32)
    keep = lax.dynamic_index_in_dim(half, row, 0, False)
    send = lax.dynamic_index_in_dim(half, 1 - row, 0, False)
    return keep + swap_y(send.astype(BF16)).astype(F32)


def ordered(index, first, second):
    return jnp.where(
        index == 0, jnp.concatenate([first, second], 0), jnp.concatenate([second, first], 0)
    )


def per_device(
    tokens,
    teacher,
    valid_mask,
    routes,
    first_gain,
    query_weight,
    key_matrix,
    value_matrix,
    output_weight,
    second_gain,
    router_weight,
    expert_in,
    expert_out,
):
    row_count, model_width = tokens.shape
    expert_count = router_weight.shape[1]
    senders = lax.axis_size("expert")
    shares = lax.axis_size("tensor")
    fits = (
        (senders, shares) == (8, 4)
        and expert_count == senders * shares
        and expert_in.shape == (8, 2, model_width // 2, SHARE)
        and row_count == 4 * 128
    )
    if not fits:
        return general_device(
            tokens,
            teacher,
            valid_mask,
            routes,
            first_gain,
            query_weight,
            key_matrix,
            value_matrix,
            output_weight,
            second_gain,
            router_weight,
            expert_in,
            expert_out,
        )
    quarter = row_count // shares
    place = lax.axis_index("expert")
    share = lax.axis_index("tensor")
    row, core = (share // 2, share % 2)
    half_index = place // 4
    half_arg = half_index.reshape(1)
    held = expert_in.shape[0] // 2
    base = 8 * (place % 4) + held * half_index

    share_arg, core_arg, place_arg = (share.reshape(1), core.reshape(1), place.reshape(1))

    def quarter_of(values):
        return lax.dynamic_slice_in_dim(values, share * quarter, quarter, 0)

    local_valid = jnp.sum(valid_mask)
    routes_mine = quarter_of(routes)
    note = jnp.concatenate([routes_mine.T, jnp.full((TOP, quarter), local_valid, jnp.int32)], 0)

    own_pack, near_pack, far_pack = pack_weights(half_arg, expert_in, expert_out)
    near_pack = trade(near_pack, 4)
    far_pack = trade(far_pack, 4)
    own_across = swap_y(own_pack)

    router_rel = lax.dynamic_slice_in_dim(
        jnp.concatenate([router_weight, router_weight], 1), base, expert_count, 1
    )
    router_rel = jnp.pad(
        jnp.concatenate([router_rel, router_rel], 1), ((0, 0), (0, 128 - 2 * expert_count))
    )

    tables = [
        jnp.concatenate([table[:, 0]] * (2 * SHARE // HEAD_DIM), 1)
        for table in rope_tables(row_count, HEAD_DIM)
    ]
    weights = (query_weight, key_matrix, value_matrix, output_weight)
    first_normed, query, keys, values, attended, attn_keep, attn_send = attention_forward(
        core_arg, tokens, first_gain[None], *weights, tables, own_pack
    )
    notes = [note] + [trade(note, bits) for bits in (2, 4, 6)]
    near_pack, own_across, attn_send, *notes = lax.optimization_barrier(
        (near_pack, own_across, attn_send, *notes)
    )
    notes = jnp.stack(notes)
    others = trade(notes, 1)
    own = [own_pack, swap_core(own_pack), own_across, swap_core(own_across)]
    tokens_mine = quarter_of(tokens).astype(F32)
    attn_sum = scatter_tensor(attn_keep, attn_send, row)
    near_pack, attn_sum, others = lax.optimization_barrier((near_pack, attn_sum, others))
    hidden = tokens_mine + RESIDUAL * attn_sum
    scale_two = lax.rsqrt(jnp.mean(hidden * hidden, -1, keepdims=True) + EPS)
    unit_two = hidden * scale_two
    normed_two = (unit_two * second_gain).astype(BF16)
    beside = trade(normed_two, 1)
    near_pack, beside = lax.optimization_barrier((near_pack, beside))
    near_across = swap_y(near_pack)
    column = [normed_two] + [trade(normed_two, bits) for bits in (2, 4, 6)]
    across = [trade(shard, 1) for shard in column[1:]]
    far_pack, near_across, *gathered = lax.optimization_barrier(
        (far_pack, near_across, beside, *across, *column[1:])
    )
    row_shards = [normed_two, *gathered[4:], *gathered[:4]]
    near = [near_pack, swap_core(near_pack), near_across, swap_core(near_across)]
    far = (far_pack, swap_y(far_pack))
    notes = jnp.concatenate([notes, others], 0)
    valid_total = jnp.sum(notes[:, TOP, 0]).astype(F32)
    route_rel = jnp.bitwise_and(notes[:, :TOP] - base, expert_count - 1)
    route_rel = route_rel.transpose(0, 2, 1).reshape(senders * quarter, TOP)
    keep, send_near, send_far, pre, gated, gates, expert_rows, far = experts_forward(
        half_arg,
        row_shards,
        route_rel,
        router_rel,
        own,
        near,
        far,
    )
    moe_sum = scatter_experts(keep, send_near, send_far)

    output = hidden + RESIDUAL * moe_sum
    residual_err = output - quarter_of(teacher).astype(F32)
    valid_rows = quarter_of(valid_mask).astype(F32)[:, None]
    squared_local = jnp.sum(valid_rows * residual_err * residual_err)
    token_total = senders * row_count
    grad_out = token_total / valid_total * valid_rows * residual_err
    grad_moe = (RESIDUAL * grad_out).astype(BF16)
    gate_mean = jnp.sum(grad_moe.astype(F32) * moe_sum, -1, keepdims=True)
    mean_part = -gate_mean * dense_gates(normed_two, routes_mine, router_weight)
    mean_high = mean_part.astype(BF16)
    mean_part = jnp.concatenate([mean_high, (mean_part - mean_high.astype(F32)).astype(BF16)], 1)
    router_pair = jnp.concatenate([router_weight, router_weight], 1)
    mean_rows = jnp.einsum("te,de->td", mean_part, router_pair, preferred_element_type=F32)
    out_pieces = spread_tensor(output.astype(BF16))
    shards = gather_experts(grad_moe)
    packs = (gates, router_rel, pre, own, near, far)
    send_near, send_far, *saved = experts_backward(1, half_arg, shards[4:], *packs)
    keep, pre_grad, logit_grad, grad_rows = experts_backward(
        0, half_arg, shards[:4], *packs, *saved
    )
    got_far = trade(send_far, 1)
    send_near, got_far, keep = lax.optimization_barrier((send_near, got_far, keep))
    far_rows = (keep[2 * quarter :] + got_far.astype(F32)).astype(BF16)
    back = trade(far_rows, 4)
    got_near = trade(send_near, 1)
    other = 1 - half_arg
    in_keep, in_send = grad_expert_ins(
        other, expert_rows, pre_grad, 0, 3, far_rows, *out_pieces[1:]
    )
    in_near, in_far = fold_pairs(in_keep, swap_core(in_send))
    in_ready = (in_near + swap_y(in_far).astype(F32)).astype(BF16)
    out_keep, out_send, own_out_keep, own_out_send = grad_expert_outs(
        half_arg, gated, grad_rows, in_far
    )
    late_keep, late_send = grad_expert_ins(other, expert_rows, pre_grad, 3, 1, in_far)
    router_part = jnp.einsum(
        "te,td->ed", logit_grad.astype(BF16), expert_rows, preferred_element_type=F32
    )
    router_part = router_part[:expert_count] + router_part[expert_count : 2 * expert_count]
    router_part = lax.dynamic_slice_in_dim(
        jnp.concatenate([router_part, router_part], 0),
        jnp.bitwise_and(expert_count - base, expert_count - 1),
        expert_count,
        0,
    )
    mean_router = jnp.einsum("te,td->ed", mean_part, normed_two, preferred_element_type=F32)
    router_part = router_part + mean_router[:expert_count] + mean_router[expert_count:]

    small = jnp.concatenate(
        [
            router_part,
            jnp.full((1, model_width), squared_local),
            jnp.zeros((7, model_width), F32),
        ],
        0,
    )
    small = small + swap_core(small)
    small = small + swap_y(small)
    back, out_send, late_send, small = lax.optimization_barrier(
        (back, out_send, late_send, small)
    )
    near_rows = keep[quarter : 2 * quarter] + got_near[quarter:].astype(F32)
    near_rows = (near_rows + back[quarter:].astype(F32)).astype(BF16)
    near_rows = trade(near_rows, 2)
    grad_hidden, grad_attn, grad_second_part = finish_rows(
        keep,
        got_near,
        back,
        near_rows,
        mean_rows,
        unit_two,
        scale_two,
        second_gain[None],
        grad_out,
        in_ready,
    )
    own_in_keep, own_in_send = grad_expert_ins(
        half_arg, expert_rows, pre_grad, 0, held, grad_attn
    )
    pieces = spread_tensor(grad_attn)
    late_near, late_far = fold_pairs(late_keep, swap_core(late_send), pieces[2])
    out_near, out_far = fold_pairs(out_keep, swap_core(out_send), pieces[2])
    out_ready = (out_near + swap_y(out_far).astype(F32)).astype(BF16)
    late_ready = (late_near + swap_y(late_far).astype(F32)).astype(BF16)
    in_back = trade(in_ready, 4)
    before = (late_far, out_far, own_in_send, in_back)
    grad_attn, grad_qkv, gain_part, one_keep, one_send = attention_backward(
        share_arg, tokens, weights, tables, (query, keys, values), pieces, *before
    )
    late_back = trade(late_ready, 4)
    grad_one = scatter_tensor(one_keep, one_send, row)
    own_out_near, own_out_far = fold_pairs(own_out_keep, swap_core(own_out_send), grad_one)
    own_out_across = swap_y(own_out_far)
    own_in_near, own_in_far = fold_pairs(own_in_keep, swap_core(own_in_send), grad_one)
    own_in_across = swap_y(own_in_far)
    before = (late_ready,)
    gains = jnp.concatenate([grad_second_part, gain_part], 0)
    keep, send_near, send_far = reduce_parts(
        place_arg, first_normed, grad_qkv, grad_attn, attended, small, gains, *before
    )
    out_back = trade(out_ready, 4)
    total, late_back, out_back = scatter_experts(keep, send_near, send_far, late_back, out_back)
    total = total.astype(BF16)
    shapes = [
        jax.ShapeDtypeStruct(shape, F32)
        for shape in (
            query_weight.shape,
            key_matrix.shape,
            value_matrix.shape,
            output_weight.shape,
            (model_width, 128),
        )
    ]
    shards = gather_experts(total)
    grad_query, grad_key, grad_value, grad_output, small = scalar_call(
        unpack_body, "unpack", place_arg, shards, shapes, (own_out_across, own_in_across)
    )

    gains = small[:, expert_count + 8 : expert_count + 24].reshape(model_width, 2, 8)
    gains = jnp.sum(gains, 2).T.reshape(16, -1)
    gains = gains + swap_core(gains)
    gains = (gains + swap_y(gains)).reshape(2, -1)

    scale_mine = lax.rsqrt(jnp.mean(tokens_mine * tokens_mine, -1, keepdims=True) + EPS)
    unit_mine = tokens_mine * scale_mine
    grad_unit_one = grad_one * first_gain
    grad_tokens = grad_hidden + scale_mine * (
        grad_unit_one - unit_mine * jnp.mean(grad_unit_one * unit_mine, -1, keepdims=True)
    )
    grad_tokens = assemble(share_arg, spread_tensor(grad_tokens.astype(BF16)), F32)
    layer_output = assemble(share_arg, out_pieces, BF16)
    grad_expert_out = ordered(
        half_index, own_out_near + own_out_across.astype(F32), out_back.astype(F32)
    )
    grad_expert_in = ordered(
        half_index,
        own_in_near + own_in_across.astype(F32),
        jnp.concatenate([in_back, late_back], 0).astype(F32),
    )
    return (
        layer_output,
        small[0, expert_count] / (2.0 * model_width * valid_total),
        grad_tokens,
        gains[1],
        grad_query,
        grad_key,
        grad_value,
        grad_output,
        gains[0],
        small[:, :expert_count],
        grad_expert_in,
        grad_expert_out,
    )


def solution(mesh):
    return jax.shard_map(
        per_device,
        mesh=mesh,
        in_specs=(
            P("expert", None),
            P("expert", None),
            P("expert"),
            P("expert", None),
            P(),
            P(None, "tensor"),
            P(None, "tensor"),
            P(None, "tensor"),
            P("tensor", None),
            P(),
            P(),
            P("expert", None, None, "tensor"),
            P("expert", "tensor", None),
        ),
        out_specs=(
            P("expert", None),
            P(),
            P("expert", None),
            P(),
            P(None, "tensor"),
            P(None, "tensor"),
            P(None, "tensor"),
            P("tensor", None),
            P(),
            P(),
            P("expert", None, None, "tensor"),
            P("expert", "tensor", None),
        ),
        check_vma=False,
    )
```
